32 devices in a mesh: grp: 4 (over y, x), fsdp: 8 (over z, core).
Axes of the slice: x: 2, y: 2, z: 4, core: 2. Of those that a mesh axis runs over, the one named last changes fastest.
Arguments:
- content_in: bfloat16 [2, 12288, 768], P(None, ('grp', 'fsdp')), may hold values from -6 to 6
- query_in: bfloat16 [2, 1792, 768], P(None, ('grp', 'fsdp')), may hold values from -6 to 6
- pred_order: int32 [2, 32, 56], P(None, ('grp', 'fsdp')), may hold values from 0 to 383, as said below
- cont_prompt: int32 [2, 4, 4], P(None, 'grp'), may hold values from 0 to 1
- rel_bucket: int32 [128], replicated, may hold values from 0 to 31
- w_query: bfloat16 [768, 768], P('fsdp'), may hold values from -0.21875 to 0.21875
- b_query: bfloat16 [768], P('fsdp'), may hold values from -3 to 3
- w_key: bfloat16 [768, 768], P('fsdp'), may hold values from -0.21875 to 0.21875
- w_value: bfloat16 [768, 768], P('fsdp'), may hold values from -0.21875 to 0.21875
- b_value: bfloat16 [768], P('fsdp'), may hold values from -1.1953125 to 1.1953125
- w_out: bfloat16 [768, 768], P('fsdp'), may hold values from -3.5 to 3.5
- b_out: bfloat16 [768], P('fsdp'), may hold values from -3 to 3
- ln1_gain: bfloat16 [768], P('fsdp'), may hold values from 0.5 to 1.5
- ln1_bias: bfloat16 [768], P('fsdp'), may hold values from -2 to 2
- w_up: bfloat16 [768, 3072], P('fsdp'), may hold values from -0.21875 to 0.21875
- b_up: bfloat16 [3072], P('fsdp'), may hold values from -3 to 3
- w_down: bfloat16 [3072, 768], P('fsdp'), may hold values from -0.109375 to 0.109375
- b_down: bfloat16 [768], P('fsdp'), may hold values from -3 to 3
- ln2_gain: bfloat16 [768], P('fsdp'), may hold values from 0.5 to 1.5
- ln2_bias: bfloat16 [768], P('fsdp'), may hold values from -2 to 2
- bias_table: bfloat16 [32, 12], replicated, may hold values from -4 to 4
- cot_content: bfloat16 [2, 12288, 768], P(None, ('grp', 'fsdp')), may hold values from -6 to 6
- cot_query: bfloat16 [2, 1792, 768], P(None, ('grp', 'fsdp')), may hold values from -6 to 6
Outputs:
- content_out: float32 [2, 12288, 768], P(None, ('grp', 'fsdp'))
- query_out: float32 [2, 1792, 768], P(None, ('grp', 'fsdp'))
- content_grad: float32 [2, 12288, 768], P(None, ('grp', 'fsdp'))
- query_grad: float32 [2, 1792, 768], P(None, ('grp', 'fsdp'))
- grad_w_query: float32 [768, 768], P('fsdp')
- grad_b_query: float32 [768], P('fsdp')
- grad_w_key: float32 [768, 768], P('fsdp')
- grad_w_value: float32 [768, 768], P('fsdp')
- grad_b_value: float32 [768], P('fsdp')
- grad_w_out: float32 [768, 768], P('fsdp')
- grad_b_out: float32 [768], P('fsdp')
- grad_ln1_gain: float32 [768], P('fsdp')
- grad_ln1_bias: float32 [768], P('fsdp')
- grad_w_up: float32 [768, 3072], P('fsdp')
- grad_b_up: float32 [3072], P('fsdp')
- grad_w_down: float32 [3072, 768], P('fsdp')
- grad_b_down: float32 [768], P('fsdp')
- grad_ln2_gain: float32 [768], P('fsdp')
- grad_ln2_bias: float32 [768], P('fsdp')
- grad_bias_table: float32 [32, 12], P('fsdp')
The draws below stay inside these ranges and needn't reach their ends.
Inputs may be any that keep to these rules, and one draw needn't show every extreme that they name: `pred_order`: each row of 56 entries names distinct content rows of one device.
All inputs are finite; a program needn't handle non-finite values.
Results may differ from the reference program's by a relative error of at most 0.025.
Values may be sent and summed in bfloat16 or wider, within the bound.
A program may use at most 320 MiB of HBM per device.

```python
import jax
import jax.numpy as jnp
from jax import lax

D = 768
H = 12
HD = 64
FF = 3072
BUCKETS = 32
DIST = 128
PD = 128
CH = 256
MICRO = 2
TD = 384
QD = 56
CONTS = 4
SHARDS = 32
TOKENS = 12288
QTOKENS = 1792
N_GRP = 4
N_FSDP = 8


def draw_pred_order(key, part):
    streams = jax.random.split(key, MICRO * SHARDS)
    shuffled = jax.vmap(lambda stream: jax.random.permutation(stream, TD))(streams)
    return shuffled[:, :QD].reshape(MICRO, SHARDS, QD).astype(jnp.int32)


def place_ends(drawn, stream_key, low, largest):
    longest = drawn.shape.index(max(drawn.shape))
    spots = []
    for shift in (0, 1):
        where = [jax.random.randint(jax.random.fold_in(stream_key, axis), (), 0, length) for axis, length in enumerate(drawn.shape)]
        where[longest] = (where[longest] + shift) % drawn.shape[longest]
        spots.append(tuple(where))
    return drawn.at[spots[0]].set(low).at[spots[1]].set(largest)


def block_levels(own_key, shape, pieces, least, top_value):
    loudness, own = 1.0, jax.random.fold_in(own_key, 6)
    for axis_at, blocks in pieces:
        heights = jnp.exp(jax.random.uniform(jax.random.fold_in(own, axis_at), (blocks,), jnp.float32, least / len(pieces), top_value / len(pieces)))
        loudness = loudness * jnp.repeat(heights, shape[axis_at] // blocks).reshape([-1 if axis == axis_at else 1 for axis in range(len(shape))])
    return loudness


def scatter_about(key, extent, scale, bound, cuts=(), kind=jnp.bfloat16):
    entries = scale * jax.random.normal(key, extent, jnp.float32)
    if cuts:
        entries = entries * block_levels(key, extent, cuts, -0.22, 0.18)
    return jnp.clip(entries, -bound, bound).astype(kind)


def setup_inputs(seed: int = 0) -> dict:
    seeds = jax.random.split(jax.random.key(seed), 24)
    return {
        "content_in": scatter_about(seeds[0], (MICRO, TOKENS, D), 1.0, 6.0, ((1, 32),)),
        "query_in": scatter_about(seeds[1], (MICRO, QTOKENS, D), 1.0, 6.0, ((1, 32),)),
        "pred_order": draw_pred_order(jax.random.fold_in(seeds[23], 71), 0),
        "cont_prompt": place_ends(jax.random.randint(seeds[3], (MICRO, N_GRP, CONTS), 0, 2), jax.random.fold_in(seeds[3], 1), 0, 1).astype(jnp.int32),
        "rel_bucket": place_ends(jax.random.randint(seeds[4], (DIST,), 0, BUCKETS), jax.random.fold_in(seeds[4], 1), 0, BUCKETS - 1).astype(jnp.int32),
        "w_query": scatter_about(seeds[5], (D, D), D ** -0.5, 0.21875, ((0, 8),)),
        "b_query": scatter_about(seeds[6], (D,), 0.5, 3.0, ((0, 8),)),
        "w_key": scatter_about(seeds[7], (D, D), D ** -0.5, 0.21875, ((0, 8),)),
        "w_value": scatter_about(seeds[8], (D, D), D ** -0.5, 0.21875, ((0, 8),)),
        "b_value": scatter_about(seeds[9], (D,), 0.2, 1.1953125, ((0, 8),)),
        "w_out": scatter_about(seeds[10], (D, D), (max(1, D // 256)) ** -0.5, 3.5, ((0, 8),)),
        "b_out": scatter_about(seeds[11], (D,), 0.5, 3.0, ((0, 8),)),
        "ln1_gain": jnp.clip(1.0 + 0.1 * jax.random.normal(seeds[12], (D,), jnp.float32), 0.5, 1.5).astype(jnp.bfloat16),
        "ln1_bias": scatter_about(seeds[13], (D,), 0.3, 2.0, ((0, 8),)),
        "w_up": scatter_about(seeds[14], (D, FF), D ** -0.5, 0.21875, ((0, 8),)),
        "b_up": scatter_about(seeds[15], (FF,), 0.5, 3.0, ((0, 8),)),
        "w_down": scatter_about(seeds[16], (FF, D), FF ** -0.5, 0.109375, ((0, 8),)),
        "b_down": scatter_about(seeds[17], (D,), 0.5, 3.0, ((0, 8),)),
        "ln2_gain": jnp.clip(1.0 + 0.1 * jax.random.normal(seeds[18], (D,), jnp.float32), 0.5, 1.5).astype(jnp.bfloat16),
        "ln2_bias": scatter_about(seeds[19], (D,), 0.3, 2.0, ((0, 8),)),
        "bias_table": scatter_about(seeds[20], (BUCKETS, H), 1.0, 4.0),
        "cot_content": scatter_about(seeds[21], (MICRO, TOKENS, D), 1.0, 6.0, ((1, 32),)),
        "cot_query": scatter_about(seeds[22], (MICRO, QTOKENS, D), 1.0, 6.0, ((1, 32),)),
    }


PRECISE = lax.Precision.HIGHEST
MASKED = -1e+30

@jax.custom_vjp
def low(v):
    return lax.optimization_barrier(v.astype(jnp.bfloat16)).astype(jnp.float32)

@jax.custom_vjp
def low_back(v):
    return v

def low_keep(v):
    return (low(v), None)

def low_pass(kept, grad):
    return (grad,)

def back_keep(v):
    return (v, None)

def back_low(kept, grad):
    return (low(grad),)
low.defvjp(low_keep, low_pass)
low_back.defvjp(back_keep, back_low)

def matmul_hi(left, right):
    return jnp.matmul(left, right, precision=PRECISE)

def layer_norm(value, gain, shift):
    centred = value - lax.optimization_barrier(jnp.mean(value, axis=-1, keepdims=True))
    return centred * lax.rsqrt(lax.optimization_barrier(jnp.mean(centred * centred, axis=-1, keepdims=True)) + 1e-05) * gain + shift

def reference(content_in, query_in, pred_order, cont_prompt, rel_bucket, w_query, b_query, w_key, w_value, b_value, w_out, b_out, ln1_gain, ln1_bias, w_up, b_up, w_down, b_down, ln2_gain, ln2_bias, bias_table, cot_content, cot_query):
    halfway = N_FSDP // 2
    plength = PD * halfway
    prompt_keys = PD * N_FSDP
    cont_keys = N_FSDP * CH
    groups = MICRO * N_GRP
    index_p = jnp.arange(prompt_keys, dtype=jnp.int32)
    index_c = jnp.arange(cont_keys, dtype=jnp.int32)
    key_prompt = jnp.concatenate([index_p // plength, jnp.full((cont_keys,), -1, jnp.int32)])
    key_cont = jnp.concatenate([jnp.full((prompt_keys,), -1, jnp.int32), index_c // CH // 2])
    key_pos = jnp.concatenate([index_p % plength, plength + 2 * (index_c % CH) + index_c // CH % 2])
    orders = pred_order.reshape(groups, N_FSDP, QD)
    prompt_maps = cont_prompt.reshape(groups, N_FSDP // 2)
    ranks = jnp.arange(N_FSDP, dtype=jnp.int32)
    row_ids = jnp.arange(TD, dtype=jnp.int32)

    def forward(content_x, query_x, query_weight, query_bias, key_weight, value_weight, value_bias, out_weight, out_bias, gain_one, shift_one, up_weight, up_bias, down_weight, down_bias, gain_two, shift_two, bias_grid):
        dist_table = bias_grid[rel_bucket]

        def group_pass(item):
            tokens_x, extra_x, order_ids, prompt_map = item
            queries = low(low_back(matmul_hi(tokens_x, query_weight) + query_bias))
            key_rows = low(low_back(matmul_hi(tokens_x, key_weight)))
            value_rows = low(low_back(matmul_hi(tokens_x, value_weight) + value_bias))
            extra_q = low(low_back(matmul_hi(extra_x, query_weight) + query_bias))
            key_heads = jnp.concatenate([key_rows[:, :PD].reshape(prompt_keys, D), key_rows[:, PD:].reshape(cont_keys, D)]).reshape(-1, H, HD)
            value_heads = jnp.concatenate([value_rows[:, :PD].reshape(prompt_keys, D), value_rows[:, PD:].reshape(cont_keys, D)]).reshape(-1, H, HD)

            def device_pass(inner):
                own_rank, own_q, own_extra, own_order = inner
                rows = jnp.concatenate([row_ids, own_order])
                in_prompt = rows < PD
                query_ref = jnp.where(in_prompt, own_rank // halfway, prompt_map[own_rank // 2])
                query_cont = jnp.where(in_prompt, -1, own_rank // 2)
                query_pos = jnp.where(in_prompt, own_rank % halfway * PD + rows, plength + 2 * (rows - PD) + own_rank % 2)
                limits = jnp.concatenate([query_pos[:TD] + 1, jnp.maximum(query_pos[TD:], 1)])
                same_seq = (key_prompt[None, :] == query_ref[:, None]) | (key_cont[None, :] == query_cont[:, None]) & (query_cont[:, None] >= 0)
                visible = same_seq & (key_pos[None, :] < limits[:, None])
                query_heads = jnp.concatenate([own_q, own_extra]).reshape(-1, H, HD)
                raw = low_back(jnp.einsum('qhd,khd->hqk', query_heads, key_heads, precision=PRECISE) / 8.0)
                relative = jnp.clip(query_pos[:, None] - key_pos[None, :], 0, DIST - 1)
                scores = jnp.where(visible[None], raw + jnp.transpose(dist_table[relative], (2, 0, 1)), MASKED)
                chance = low(jax.nn.softmax(scores, axis=-1))
                context = jnp.einsum('hqk,khd->qhd', chance, value_heads, precision=PRECISE)
                return low(low_back(context.reshape(-1, D)))
            context = lax.map(jax.checkpoint(device_pass), (ranks, queries, extra_q, order_ids))
            residual = jnp.concatenate([tokens_x, extra_x], axis=1)
            first = layer_norm(residual + low_back(matmul_hi(context, out_weight)) + out_bias, gain_one, shift_one)
            hidden = low_back(matmul_hi(low(first), up_weight) + up_bias)
            active = low(low_back(jax.nn.gelu(hidden, approximate=False)))
            final = layer_norm(first + low_back(matmul_hi(active, down_weight)) + down_bias, gain_two, shift_two)
            return (final[:, :TD], final[:, TD:])
        return lax.map(jax.checkpoint(group_pass), (content_x, query_x, orders, prompt_maps))

    def floats(array_in):
        return array_in.astype(jnp.float32)
    content_x = floats(content_in).reshape(groups, N_FSDP, TD, D)
    query_x = floats(query_in).reshape(groups, N_FSDP, QD, D)
    params = [floats(entry) for entry in (w_query, b_query, w_key, w_value, b_value, w_out, b_out, ln1_gain, ln1_bias, w_up, b_up, w_down, b_down, ln2_gain, ln2_bias, bias_table)]
    outputs, pullback = jax.vjp(forward, content_x, query_x, *params)
    grads = pullback((floats(cot_content).reshape(groups, N_FSDP, TD, D), floats(cot_query).reshape(groups, N_FSDP, QD, D)))
    content_rows = N_GRP * N_FSDP * TD
    query_rows = N_GRP * N_FSDP * QD
    return (outputs[0].reshape(MICRO, content_rows, D), outputs[1].reshape(MICRO, query_rows, D), grads[0].reshape(MICRO, content_rows, D), grads[1].reshape(MICRO, query_rows, D), grads[2], grads[3], grads[4], grads[5], grads[6], grads[7], grads[8], grads[9], grads[10], grads[11], grads[12], grads[13], grads[14], grads[15], grads[16], grads[17])
```

```python
import functools

import jax
import jax.numpy as jnp
from jax import lax
from jax.experimental import pallas as pl
from jax.experimental.pallas import tpu as pltpu
from jax.sharding import PartitionSpec as P

D = 768
PD = 128
CH = 256
MICRO = 2
TD = 384
QP = 64
HD = 64
LANES = 128
PAIRS = D // LANES

PRECISE = lax.Precision.HIGHEST
MASKED = -1e30
VMEM_LIMIT = 56 * 1024 * 1024


def dot_nt(left, right):
    return lax.dot_general(
        left, right, (((1,), (1,)), ((), ())), preferred_element_type=jnp.float32
    )


def dot_tn(left, right):
    return lax.dot_general(
        left, right, (((0,), (0,)), ((), ())), preferred_element_type=jnp.float32
    )


def dot_nn(left, right):
    return jnp.dot(left, right, preferred_element_type=jnp.float32)


def head_stack(block):
    lane = lax.broadcasted_iota(jnp.int32, block.shape, 1)
    zero = jnp.zeros_like(block)
    return jnp.concatenate(
        [jnp.where(lane < HD, block, zero), jnp.where(lane < HD, zero, block)], axis=0
    )


def head_merge(stacked):
    rows = stacked.shape[0] // 2
    lane = lax.broadcasted_iota(jnp.int32, (rows, LANES), 1)
    return jnp.where(lane < HD, stacked[:rows], stacked[rows:])


def lookup(table, index):
    return jnp.take_along_axis(table, index, axis=1, mode="promise_in_bounds")


def near_index(distance):
    return jnp.clip(distance, 0, LANES - 1)


def fill_keys(scratch, own_ref, map_ref, near_ref, cont_ref, plength):
    scratch[0:plength] = own_ref[...].reshape(plength, LANES)
    scratch[plength : 2 * plength] = map_ref[...].reshape(plength, LANES)
    near = near_ref[...].reshape(CH, LANES)
    at = 2 * plength
    scratch[at : at + 128] = near[0:128]
    scratch[at + 128 : at + 256] = cont_ref[PD : PD + 128]
    scratch[at + 256 : at + 384] = near[128:256]
    scratch[at + 384 : at + 512] = cont_ref[PD + 128 : PD + 256]


def attend_kernel(
    plength,
    meta,
    qc,
    qx,
    ko,
    vo,
    km,
    vm,
    kn,
    vn,
    kc,
    vc,
    table,
    xcol,
    ctx_c,
    ctx_x,
    full_c,
    full_x,
    lse_ref,
    keys,
    vals,
    scores,
    probs,
):
    base = meta[1]
    side = meta[2]
    blocks = plength // 128
    fill_keys(keys, ko, km, kn, kc, plength)
    fill_keys(vals, vo, vm, vn, vc, plength)
    row = lax.broadcasted_iota(jnp.int32, (128, 128), 0)
    col = lax.broadcasted_iota(jnp.int32, (128, 128), 1)
    tab_a = jnp.broadcast_to(table[0, 0:1, :], (128, 128))
    tab_b = jnp.broadcast_to(table[0, 1:2, :], (128, 128))
    tab_x = jnp.where(row < QP, tab_a, tab_b)
    lse_ref[...] = jnp.zeros_like(lse_ref)

    def solve(stack, first, plan, tables, lse_rows):
        count = len(plan)
        span = slice(first, first + 128 * count)
        halves = len(tables)
        width = 128 * count
        scores[0 : 128 * halves, 0:width] = dot_nt(stack, keys[span])
        for half in range(halves):
            rows = slice(128 * half, 128 * half + 128)
            peak = None
            for at, (index, visible) in enumerate(plan):
                cols = slice(128 * at, 128 * at + 128)
                s = scores[rows, cols]
                if index is not None:
                    s = s + lookup(tables[half], index)
                if visible is not None:
                    s = jnp.where(visible, s, MASKED)
                if index is not None or visible is not None:
                    scores[rows, cols] = s
                peak = s if peak is None else jnp.maximum(peak, s)
            top = jnp.max(peak, axis=1, keepdims=True)
            total = None
            for at in range(count):
                cols = slice(128 * at, 128 * at + 128)
                p = jnp.exp(scores[rows, cols] - top)
                total = p if total is None else total + p
                probs[rows, cols] = p.astype(jnp.bfloat16)
            total = jnp.sum(total, axis=1, keepdims=True)
            log_total = top + jnp.log(total)
            lse_ref[0, 0, lse_rows[half] : lse_rows[half] + 1, :] = jnp.transpose(
                jnp.broadcast_to(log_total, (128, 128))
            )[0:1, :]
            scores[rows, 0:128] = jnp.broadcast_to(1.0 / total, (128, 128))
        out = dot_nn(probs[0 : 128 * halves, 0:width], vals[span])
        return out * scores[0 : 128 * halves, 0:128]

    scale = jnp.asarray(0.125, jnp.bfloat16)
    q_p = head_stack(qc[0:PD] * scale)
    q_0 = head_stack(qc[PD : PD + 128] * scale)
    q_1 = head_stack(qc[PD + 128 : PD + 256] * scale)
    q_x = head_stack(qx[...] * scale)

    plan_p = []
    for b in range(blocks):
        d = base + row - (col + 128 * b)
        plan_p.append((near_index(d), d >= 0))
    out = head_merge(solve(q_p, 0, plan_p, (tab_a, tab_b), (0, 3)))
    ctx_c[0:PD] = out.astype(jnp.bfloat16)
    full_c[0:PD] = out

    far = (None, None)
    last = 128 + 2 * row + side - col
    near_d = 2 * (row - col) + 2 * side - 1
    own_d = 2 * (row - col)
    plan_0 = [far] * (blocks - 1) + [
        (near_index(last), None),
        (near_index(near_d), near_d >= 0),
        (near_index(own_d), own_d >= 0),
    ]
    out = head_merge(solve(q_0, plength, plan_0, (tab_a, tab_b), (1, 4)))
    ctx_c[PD : PD + 128] = out.astype(jnp.bfloat16)
    full_c[PD : PD + 128] = out
    plan_1 = [far] * blocks + [
        (near_index(near_d + 256), None),
        (near_index(own_d + 256), None),
        (near_index(near_d), near_d >= 0),
        (near_index(own_d), own_d >= 0),
    ]
    out = head_merge(solve(q_1, plength, plan_1, (tab_a, tab_b), (2, 5)))
    ctx_c[PD + 128 : PD + 256] = out.astype(jnp.bfloat16)
    full_c[PD + 128 : PD + 256] = out

    pos = jnp.broadcast_to(xcol[0, :, 0:1], (128, 128))
    lim_p = jnp.broadcast_to(xcol[0, :, 1:2], (128, 128))
    lim_c = jnp.broadcast_to(xcol[0, :, 2:3], (128, 128))
    plan_x = []
    for b in range(blocks):
        key = col + 128 * b
        plan_x.append((near_index(pos - key), key < lim_p))
    in_cont = lim_c > 0
    for b in range(blocks - 1):
        plan_x.append((None, in_cont))
    key = col + 128 * (blocks - 1)
    plan_x.append((near_index(pos - key), in_cont))
    for b in range(2):
        for offset in (1 - side, side):
            key = plength + 2 * (col + 128 * b) + offset
            plan_x.append((near_index(pos - key), key < lim_c))
    out = solve(q_x, 0, plan_x, (tab_x,), (6,))
    lane = lax.broadcasted_iota(jnp.int32, (QP, LANES), 1)
    out = jnp.where(lane < HD, out[0:QP], out[QP:])
    ctx_x[...] = out.astype(jnp.bfloat16)
    full_x[...] = out


def pair_column(shift):
    return lambda m, j, meta: (m, shift * PAIRS + j)


def prompt_specs(half):
    def at(kv, mapped):
        def index(m, j, meta):
            return (meta[3 + m] if mapped else meta[0], kv, m, 0, j)

        return pl.BlockSpec((half, 1, 1, PD, LANES), index)

    return [at(0, False), at(1, False), at(0, True), at(1, True)]


def near_spec(kv):
    return pl.BlockSpec((1, 1, CH, LANES), lambda m, j, meta: (kv, m, 0, j))


TABLE_SPEC = pl.BlockSpec((1, 8, LANES), lambda m, j, meta: (j, 0, 0))


def attend(meta, qkv, extra_q, prompt_kv, near_kv, table, xcol):
    half = prompt_kv.shape[0] // 2
    plength = half * PD
    n_keys = 2 * plength + 2 * CH
    content = pl.BlockSpec((TD, LANES), pair_column(0))
    extra = pl.BlockSpec((QP, LANES), pair_column(0))
    own_row = plength + 2 * CH
    pairs = MICRO * PAIRS * 2 * (128 * plength + 256 * own_row) + MICRO * PAIRS * 128 * n_keys
    return pl.pallas_call(
        functools.partial(attend_kernel, plength),
        name="attend",
        grid_spec=pltpu.PrefetchScalarGridSpec(
            num_scalar_prefetch=1,
            grid=(MICRO, PAIRS),
            in_specs=[content, extra]
            + prompt_specs(half)
            + [
                near_spec(0),
                near_spec(1),
                pl.BlockSpec((TD, LANES), pair_column(1)),
                pl.BlockSpec((TD, LANES), pair_column(2)),
                TABLE_SPEC,
                pl.BlockSpec((1, 128, 8), lambda m, j, meta: (m, 0, 0)),
            ],
            out_specs=[
                content,
                extra,
                content,
                extra,
                pl.BlockSpec((1, 1, 8, LANES), lambda m, j, meta: (m, j, 0, 0)),
            ],
            scratch_shapes=[
                pltpu.VMEM((n_keys, LANES), jnp.bfloat16),
                pltpu.VMEM((n_keys, LANES), jnp.bfloat16),
                pltpu.VMEM((256, n_keys), jnp.float32),
                pltpu.VMEM((256, n_keys), jnp.bfloat16),
            ],
        ),
        out_shape=[
            jax.ShapeDtypeStruct((MICRO * TD, D), jnp.bfloat16),
            jax.ShapeDtypeStruct((MICRO * QP, D), jnp.bfloat16),
            jax.ShapeDtypeStruct((MICRO * TD, D), jnp.float32),
            jax.ShapeDtypeStruct((MICRO * QP, D), jnp.float32),
            jax.ShapeDtypeStruct((MICRO, PAIRS, 8, LANES), jnp.float32),
        ],
        compiler_params=pltpu.CompilerParams(vmem_limit_bytes=VMEM_LIMIT),
        cost_estimate=pl.CostEstimate(
            flops=4 * pairs * LANES, bytes_accessed=16 * 1024 * 1024, transcendentals=pairs
        ),
    )(
        meta,
        qkv,
        extra_q,
        prompt_kv,
        prompt_kv,
        prompt_kv,
        prompt_kv,
        near_kv,
        near_kv,
        qkv,
        qkv,
        table,
        xcol,
    )


def attend_back_kernel(
    plength,
    meta,
    qc,
    qx,
    ko,
    vo,
    km,
    vm,
    kn,
    vn,
    kc,
    vc,
    table,
    xcol,
    xrow,
    lse_ref,
    dc,
    dx,
    full_c,
    full_x,
    dq_c,
    dq_x,
    dkv_prompt,
    dkv_near,
    dkv_own,
    hist,
    keys,
    vals,
    q_all,
    d_all,
    scores,
    dprobs,
    probs_t,
    dscores_t,
    ds_p,
    dk_acc,
    dv_acc,
    d_prompt,
):
    own_prompt = meta[0]
    base = meta[1]
    side = meta[2]
    mapped = meta[3 + pl.program_id(0)]
    blocks = plength // 128
    at_k1 = 2 * plength + 256
    n_keys = 2 * plength + 512
    fill_keys(keys, ko, km, kn, kc, plength)
    fill_keys(vals, vo, vm, vn, vc, plength)
    row = lax.broadcasted_iota(jnp.int32, (128, 128), 0)
    col = lax.broadcasted_iota(jnp.int32, (128, 128), 1)
    tab_a = jnp.broadcast_to(table[0, 0:1, :], (128, 128))
    tab_b = jnp.broadcast_to(table[0, 1:2, :], (128, 128))
    scale = jnp.asarray(0.125, jnp.bfloat16)

    p_at, x_at, c1_at, c0_at = 0, 256, 384, 640
    q_all[0:256] = head_stack(qc[0:PD] * scale)
    q_all[256:384] = head_stack(qx[...] * scale)
    q_all[384:640] = head_stack(qc[PD + 128 : PD + 256] * scale)
    q_all[640:896] = head_stack(qc[PD : PD + 128] * scale)
    d_all[0:256] = head_stack(dc[0:PD])
    d_all[256:384] = head_stack(dx[...])
    d_all[384:640] = head_stack(dc[PD + 128 : PD + 256])
    d_all[640:896] = head_stack(dc[PD : PD + 128])

    ones_lane = lax.broadcasted_iota(jnp.int32, (8, LANES), 1)
    ones_row = lax.broadcasted_iota(jnp.int32, (8, LANES), 0)
    pick = jnp.where((ones_lane < HD) == (ones_row == 0), 1.0, 0.0)
    pick = jnp.where(ones_row < 2, pick, 0.0)

    def deltas(upstream, context):
        product = upstream.astype(jnp.float32) * context
        return lax.dot_general(
            pick,
            product,
            (((1,), (1,)), ((), ())),
            precision=PRECISE,
            preferred_element_type=jnp.float32,
        )

    delta_p = deltas(dc[0:PD], full_c[0:PD])
    delta_0 = deltas(dc[PD : PD + 128], full_c[PD : PD + 128])
    delta_1 = deltas(dc[PD + 128 : PD + 256], full_c[PD + 128 : PD + 256])
    delta_x = deltas(dx[...], full_x[...])
    delta_x = jnp.concatenate([delta_x[0:1], delta_x[1:2]], axis=1)

    def block_back(first, plan, at_col, halves):
        count = len(plan)
        width = 128 * len(halves)
        span = slice(first, first + 128 * count)
        cols = slice(at_col, at_col + width)
        scores[0 : 128 * count, 0:width] = dot_nt(keys[span], q_all[cols])
        dprobs[0 : 128 * count, 0:width] = dot_nt(vals[span], d_all[cols])
        for half, (tables, lse_row, delta) in enumerate(halves):
            lane = slice(128 * half, 128 * half + 128)
            out_lane = slice(at_col + 128 * half, at_col + 128 * half + 128)
            lse = lse_ref[0, 0, lse_row : lse_row + 1, :]
            for at, (index, visible) in enumerate(plan):
                rows = slice(128 * at, 128 * at + 128)
                out_rows = slice(first + 128 * at, first + 128 * at + 128)
                s = scores[rows, lane]
                if index is not None:
                    bias = lookup(tables[0], index)
                    if len(tables) > 1:
                        bias = jnp.where(col < QP, bias, lookup(tables[1], index))
                    s = s + bias
                if visible is not None:
                    s = jnp.where(visible, s, MASKED)
                p = jnp.exp(s - lse)
                ds = p * (dprobs[rows, lane] - delta)
                probs_t[out_rows, out_lane] = p.astype(jnp.bfloat16)
                dscores_t[out_rows, out_lane] = ds.astype(jnp.bfloat16)
                yield half, at, ds

    extra_a = jnp.where(
        (xcol[0, :, 3:4] == lax.broadcasted_iota(jnp.int32, (128, TD), 1))
        & (lax.broadcasted_iota(jnp.int32, (128, TD), 0) < QP),
        1.0,
        0.0,
    ).astype(jnp.bfloat16)
    extra_b = jnp.where(
        (xcol[0, :, 3:4] == lax.broadcasted_iota(jnp.int32, (128, TD), 1))
        & (lax.broadcasted_iota(jnp.int32, (128, TD), 0) >= QP),
        1.0,
        0.0,
    ).astype(jnp.bfloat16)
    spread = (extra_a, extra_b)

    pos = xrow[0, 0:1, :]
    lim_p = xrow[0, 1:2, :]
    lim_c = xrow[0, 2:3, :]
    plan = []
    for b in range(blocks):
        key = row + 128 * b
        plan.append((near_index(pos - key), key < lim_p))
    in_cont = jnp.broadcast_to(lim_c > 0, (128, 128))
    for b in range(blocks - 1):
        plan.append((None, in_cont))
    plan.append((near_index(pos - (row + 128 * (blocks - 1))), in_cont))
    for b in range(2):
        for offset in (1 - side, side):
            key = plength + 2 * (row + 128 * b) + offset
            plan.append((near_index(pos - key), key < lim_c))
    for _ in block_back(0, plan, x_at, [((tab_a, tab_b), 6, delta_x)]):
        pass

    def spread_block(head, key_at, content_at):
        return dot_nn(
            dscores_t[pl.ds(key_at, 128), x_at : x_at + 128],
            spread[head][:, content_at : content_at + 128],
        )

    turn = (col + row) % 128
    turn_half = (col + row // 2) % 128

    def fold(block):
        return jnp.sum(block.reshape(16, 8, LANES), axis=0)

    plan = []
    for b in range(blocks):
        d = base + col - (row + 128 * b)
        plan.append((near_index(d), d >= 0))
    halves = [((tab_a,), 0, delta_p[0:1]), ((tab_b,), 3, delta_p[1:2])]
    for half, at, ds in block_back(0, plan, p_at, halves):
        ds_p[128 * at : 128 * at + 128, 128 * half : 128 * half + 128] = ds
    before = jnp.maximum(base - 128, 0)
    base_at = pl.multiple_of(base, 128)
    before_at = pl.multiple_of(before, 128)
    for head in range(2):
        lane = slice(128 * head, 128 * head + 128)
        here = ds_p[pl.ds(base_at, 128), lane] + spread_block(head, base_at, 0)
        prior = ds_p[pl.ds(before_at, 128), lane] + spread_block(head, before_at, 0)
        prior = jnp.where(base > 0, prior, 0.0)
        both = jnp.where(col >= row, here, prior)
        hist[0, 0, 32 * head : 32 * head + 8] = fold(lookup(both, turn))

    last = 128 + 2 * col + side - row
    near_d = 2 * (col - row) + 2 * side - 1
    own_d = 2 * (col - row)
    far = (None, None)
    plan_0 = [far] * (blocks - 1) + [
        (near_index(last), None),
        (near_index(near_d), near_d >= 0),
        (near_index(own_d), own_d >= 0),
    ]
    plan_1 = [far] * blocks + [
        (near_index(near_d + 256), None),
        (near_index(own_d + 256), None),
        (near_index(near_d), near_d >= 0),
        (near_index(own_d), own_d >= 0),
    ]
    halves = [((tab_a,), 1, delta_0[0:1]), ((tab_b,), 4, delta_0[1:2])]
    near_sum = {}
    own_sum = {}
    last_key = 2 * plength - 128
    for half, at, ds in block_back(plength, plan_0, c0_at, halves):
        if at == blocks - 1:
            ds = ds + spread_block(half, last_key, PD)
            ds = jnp.where(col < 64, ds, 0.0)
            hist[0, 0, 32 * half + 8 : 32 * half + 16] = fold(lookup(ds, turn_half))
        if at == blocks:
            ds = ds + spread_block(half, 2 * plength, PD)
            near_sum[half] = jnp.where(col >= row, ds, 0.0)
        if at == blocks + 1:
            ds = ds + spread_block(half, 2 * plength + 128, PD)
            own_sum[half] = jnp.where(col >= row, ds, 0.0)
    for half in range(2):
        lane = slice(128 * half, 128 * half + 128)
        ds_p[0:128, lane] = near_sum[half]
        ds_p[128:256, lane] = own_sum[half]
    halves = [((tab_a,), 2, delta_1[0:1]), ((tab_b,), 5, delta_1[1:2])]
    for half, at, ds in block_back(plength, plan_1, c1_at, halves):
        lane = slice(128 * half, 128 * half + 128)
        if at == blocks:
            ds = ds + spread_block(half, 2 * plength, PD + 128)
            ds_p[0:128, lane] = ds_p[0:128, lane] + jnp.where(col < row, ds, 0.0)
        if at == blocks + 1:
            ds = ds + spread_block(half, 2 * plength + 128, PD + 128)
            ds_p[128:256, lane] = ds_p[128:256, lane] + jnp.where(col < row, ds, 0.0)
        if at == blocks + 2:
            ds = ds + spread_block(half, at_k1, PD + 128)
            ds = ds_p[0:128, lane] + jnp.where(col >= row, ds, 0.0)
            hist[0, 0, 32 * half + 16 : 32 * half + 24] = fold(lookup(ds, turn))
        if at == blocks + 3:
            ds = ds + spread_block(half, at_k1 + 128, PD + 128)
            ds = ds_p[128:256, lane] + jnp.where(col >= row, ds, 0.0)
            hist[0, 0, 32 * half + 24 : 32 * half + 32] = fold(lookup(ds, turn))

    own = slice(0, plength)
    middle = slice(plength, at_k1)
    end = slice(at_k1, n_keys)
    for acc, left, right in ((dk_acc, dscores_t, q_all), (dv_acc, probs_t, d_all)):
        acc[own] = dot_nn(left[own, 0:384], right[0:384])
        acc[middle] = dot_nn(left[middle, 256:896], right[256:896])
        acc[end] = dot_nn(left[end, 256:640], right[256:640])

    dq_c[0:PD] = (
        head_merge(dot_tn(dscores_t[own, p_at : p_at + 256], keys[own])) * 0.125
    ).astype(jnp.bfloat16)
    dq_c[PD : PD + 128] = (
        head_merge(dot_tn(dscores_t[middle, c0_at : c0_at + 256], keys[middle])) * 0.125
    ).astype(jnp.bfloat16)
    cont = slice(plength, n_keys)
    dq_c[PD + 128 : PD + 256] = (
        head_merge(dot_tn(dscores_t[cont, c1_at : c1_at + 256], keys[cont])) * 0.125
    ).astype(jnp.bfloat16)
    out = dot_tn(dscores_t[:, x_at : x_at + 128], keys[...])
    lane = lax.broadcasted_iota(jnp.int32, (QP, LANES), 1)
    dq_x[...] = (jnp.where(lane < HD, out[0:QP], out[QP:]) * 0.125).astype(jnp.bfloat16)

    for kv, acc in ((0, dk_acc), (1, dv_acc)):
        near = jnp.concatenate([acc[at_k1 - 256 : at_k1 - 128], acc[at_k1 : at_k1 + 128]], axis=0)
        dkv_near[kv, 0] = near.astype(jnp.bfloat16)
        dkv_own[kv, 0, 0:128] = acc[at_k1 - 128 : at_k1]
        dkv_own[kv, 0, 128:256] = acc[at_k1 + 128 : at_k1 + 256]
        d_prompt[...] = jnp.zeros_like(d_prompt)
        own_at = pl.multiple_of(own_prompt * plength, 128)
        map_at = pl.multiple_of(mapped * plength, 128)
        d_prompt[pl.ds(own_at, plength), :] = acc[own]
        d_prompt[pl.ds(map_at, plength), :] = (
            d_prompt[pl.ds(map_at, plength), :] + acc[plength : 2 * plength]
        )
        dkv_prompt[:, kv, 0] = (
            d_prompt[...].astype(jnp.bfloat16).reshape(2 * blocks, PD, LANES)
        )


def attend_back(meta, qkv, extra_q, prompt_kv, near_kv, table, xcol, xrow, lse, dc, dx, fc, fx):
    devices = prompt_kv.shape[0]
    half = devices // 2
    plength = half * PD
    n_keys = 2 * plength + 2 * CH
    content = pl.BlockSpec((TD, LANES), pair_column(0))
    extra = pl.BlockSpec((QP, LANES), pair_column(0))
    own_row = plength + 2 * CH
    pairs = MICRO * PAIRS * 2 * (128 * plength + 256 * own_row) + MICRO * PAIRS * 128 * n_keys
    return pl.pallas_call(
        functools.partial(attend_back_kernel, plength),
        name="attend_back",
        grid_spec=pltpu.PrefetchScalarGridSpec(
            num_scalar_prefetch=1,
            grid=(MICRO, PAIRS),
            in_specs=[content, extra]
            + prompt_specs(half)
            + [
                near_spec(0),
                near_spec(1),
                pl.BlockSpec((TD, LANES), pair_column(1)),
                pl.BlockSpec((TD, LANES), pair_column(2)),
                TABLE_SPEC,
                pl.BlockSpec((1, 128, 8), lambda m, j, meta: (m, 0, 0)),
                pl.BlockSpec((1, 8, 128), lambda m, j, meta: (m, 0, 0)),
                pl.BlockSpec((1, 1, 8, LANES), lambda m, j, meta: (m, j, 0, 0)),
                content,
                extra,
                content,
                extra,
            ],
            out_specs=[
                content,
                extra,
                pl.BlockSpec((devices, 2, 1, PD, LANES), lambda m, j, meta: (0, 0, m, 0, j)),
                pl.BlockSpec((2, 1, CH, LANES), lambda m, j, meta: (0, m, 0, j)),
                pl.BlockSpec((2, 1, CH, LANES), lambda m, j, meta: (0, m, 0, j)),
                pl.BlockSpec((1, 1, 64, LANES), lambda m, j, meta: (m, j, 0, 0)),
            ],
            scratch_shapes=[
                pltpu.VMEM((n_keys, LANES), jnp.bfloat16),
                pltpu.VMEM((n_keys, LANES), jnp.bfloat16),
                pltpu.VMEM((896, LANES), jnp.bfloat16),
                pltpu.VMEM((896, LANES), jnp.bfloat16),
                pltpu.VMEM((n_keys, 256), jnp.float32),
                pltpu.VMEM((n_keys, 256), jnp.float32),
                pltpu.VMEM((n_keys, 896), jnp.bfloat16),
                pltpu.VMEM((n_keys, 896), jnp.bfloat16),
                pltpu.VMEM((plength, 256), jnp.float32),
                pltpu.VMEM((n_keys, LANES), jnp.float32),
                pltpu.VMEM((n_keys, LANES), jnp.float32),
                pltpu.VMEM((2 * plength, LANES), jnp.float32),
            ],
        ),
        out_shape=[
            jax.ShapeDtypeStruct((MICRO * TD, D), jnp.bfloat16),
            jax.ShapeDtypeStruct((MICRO * QP, D), jnp.bfloat16),
            jax.ShapeDtypeStruct((devices, 2, MICRO, PD, D), jnp.bfloat16),
            jax.ShapeDtypeStruct((2, MICRO, CH, D), jnp.bfloat16),
            jax.ShapeDtypeStruct((2, MICRO, CH, D), jnp.float32),
            jax.ShapeDtypeStruct((MICRO, PAIRS, 64, LANES), jnp.float32),
        ],
        compiler_params=pltpu.CompilerParams(vmem_limit_bytes=VMEM_LIMIT),
        cost_estimate=pl.CostEstimate(
            flops=10 * pairs * LANES, bytes_accessed=32 * 1024 * 1024, transcendentals=pairs
        ),
    )(
        meta,
        qkv,
        extra_q,
        prompt_kv,
        prompt_kv,
        prompt_kv,
        prompt_kv,
        near_kv,
        near_kv,
        qkv,
        qkv,
        table,
        xcol,
        xrow,
        lse,
        dc,
        dx,
        fc,
        fx,
    )


def from_partner(block, axis):
    count = lax.axis_size(axis)
    return lax.ppermute(block, axis, [(i, i ^ 1) for i in range(count)])


def layer_norm(value, gain, shift):
    centred = value - jnp.mean(value, axis=-1, keepdims=True)
    inverse = lax.rsqrt(jnp.mean(centred * centred, axis=-1, keepdims=True) + 1e-05)
    normed = centred * inverse
    return (normed * gain + shift, normed, inverse)


def norm_back(upstream, normed, inverse, gain):
    scaled = upstream * gain
    inner = (
        scaled
        - jnp.mean(scaled, axis=-1, keepdims=True)
        - normed * jnp.mean(scaled * normed, axis=-1, keepdims=True)
    )
    return (inverse * inner, jnp.sum(upstream * normed, axis=0), jnp.sum(upstream, axis=0))


def gelu_slope(hidden):
    return (
        0.5 * (1.0 + lax.erf(hidden * 0.7071067811865476))
        + hidden * jnp.exp(-0.5 * hidden * hidden) * 0.3989422804014327
    )


def pad_rows(block):
    return jnp.pad(block, ((0, 0), (0, QP - block.shape[1]), (0, 0))).reshape(MICRO * QP, D)


def table_gradient(hist, rel_bucket, buckets, side, heads):
    summed = jnp.sum(hist, axis=0).reshape(PAIRS, 2, 4, 8, LANES)
    prompt = jnp.sum(summed[:, :, 0], axis=2)
    even = jnp.sum(summed[:, :, 1, 0::2], axis=2)
    odd = jnp.sum(summed[:, :, 1, 1::2], axis=2)
    near = jnp.sum(summed[:, :, 2], axis=2)
    own = jnp.sum(summed[:, :, 3], axis=2)
    lanes = jnp.arange(LANES, dtype=jnp.int32)
    signed = jnp.where(lanes < 64, lanes, lanes - 128)
    distance = jnp.stack(
        [
            lanes,
            128 + side + 2 * signed,
            127 + side + 2 * signed,
            2 * lanes + 2 * side - 1,
            2 * lanes,
        ]
    ).reshape(-1)
    hot = (distance[:, None] == lanes[None, :]) & (lanes[None, :] < LANES - 1)
    parts = jnp.stack([prompt, even, odd, near, own], axis=2).reshape(heads, 5 * LANES)
    close = jnp.dot(parts, hot.astype(jnp.float32), precision=PRECISE)
    close = jnp.where(
        lanes[None, :] == LANES - 1, -jnp.sum(close, axis=1, keepdims=True), close
    )
    bucket_hot = (rel_bucket[:, None] == jnp.arange(buckets, dtype=jnp.int32)[None, :]).astype(
        jnp.float32
    )
    return jnp.dot(bucket_hot.T, close.T, precision=PRECISE)


def on_device(
    content_in,
    query_in,
    pred_order,
    cont_prompt,
    rel_bucket,
    w_query,
    b_query,
    w_key,
    w_value,
    b_value,
    w_out,
    b_out,
    ln1_gain,
    ln1_bias,
    w_up,
    b_up,
    w_down,
    b_down,
    ln2_gain,
    ln2_bias,
    bias_table,
    cot_content,
    cot_query,
):
    devices = lax.axis_size("fsdp")
    halfway = devices // 2
    own_rank = lax.axis_index("fsdp")
    plength = PD * halfway
    heads = bias_table.shape[1]
    extra_rows = query_in.shape[1]
    own_prompt = own_rank // halfway
    prompt_base = own_rank % halfway * PD
    cont_index = own_rank // 2
    side = own_rank % 2

    def gather(entry):
        return lax.all_gather(entry, "fsdp", axis=0, tiled=True)

    vectors = jnp.concatenate(
        [b_query, b_value, b_out, b_down, ln1_gain, ln1_bias, ln2_gain, ln2_bias, b_up]
    )
    query_weight, key_weight, value_weight = gather(w_query), gather(w_key), gather(w_value)
    all_vectors = gather(vectors[None])
    shard = b_query.shape[0]
    singles = [
        all_vectors[:, shard * i : shard * i + shard].reshape(-1).astype(jnp.float32)
        for i in range(8)
    ]
    (
        query_bias,
        value_bias,
        out_bias,
        down_bias,
        gain_one,
        shift_one,
        gain_two,
        shift_two,
    ) = singles
    up_bias = all_vectors[:, 8 * shard :].reshape(-1).astype(jnp.float32)
    out_weight, up_weight, down_weight = gather(w_out), gather(w_up), gather(w_down)

    prompt_map = cont_prompt[:, 0, :]
    prompt_ref = jnp.sum(
        jnp.where(
            jnp.arange(prompt_map.shape[1], dtype=jnp.int32)[None, :] == cont_index, prompt_map, 0
        ),
        axis=1,
    )
    meta = jnp.concatenate([jnp.stack([own_prompt, prompt_base, side]), prompt_ref]).astype(
        jnp.int32
    )
    order = jnp.pad(pred_order[:, 0, :], ((0, 0), (0, QP - extra_rows)), constant_values=-1)
    real = order >= 0
    in_prompt = order < PD
    position = jnp.where(
        in_prompt, prompt_base + order, plength + 2 * (order - PD) + side
    )
    limit_p = jnp.where(real & in_prompt, jnp.maximum(position, 1), -1)
    limit_c = jnp.where(real & ~in_prompt, position, -1)
    info = jnp.stack([position, limit_p, limit_c, order], axis=1)
    info = jnp.concatenate([info, info], axis=2)
    xrow = jnp.pad(info, ((0, 0), (0, 4), (0, 0))).astype(jnp.int32)
    xcol = jnp.swapaxes(xrow, 1, 2)
    dist = bias_table.astype(jnp.float32)[rel_bucket].T
    dist = dist - dist[:, LANES - 1 :]
    table = jnp.pad(dist.reshape(PAIRS, 2, LANES), ((0, 0), (0, 6), (0, 0)))

    tokens_x = content_in.reshape(MICRO * TD, D)
    extra_x = pad_rows(query_in)
    x_all = jnp.concatenate([tokens_x, extra_x])
    qkv_weight = jnp.concatenate([query_weight, key_weight, value_weight], axis=1)
    qkv_bias = jnp.concatenate([query_bias, jnp.zeros((D,), jnp.float32), value_bias])
    qkv = (
        jnp.dot(tokens_x, qkv_weight, preferred_element_type=jnp.float32) + qkv_bias
    ).astype(jnp.bfloat16)
    extra_q = (
        jnp.dot(extra_x, query_weight, preferred_element_type=jnp.float32) + query_bias
    ).astype(jnp.bfloat16)
    kv = qkv[:, D:].reshape(MICRO, TD, 2, D)
    kv = jnp.transpose(kv, (2, 0, 1, 3))
    prompt_kv = lax.all_gather(kv[:, :, :PD], "fsdp", axis=0)
    near_kv = from_partner(kv[:, :, PD:], "fsdp")

    ctx_c, ctx_x, full_c, full_x, lse = attend(
        meta, qkv, extra_q, prompt_kv, near_kv, table, xcol
    )
    context = jnp.concatenate([ctx_c, ctx_x])
    first, normed_one, inverse_one = layer_norm(
        x_all.astype(jnp.float32)
        + jnp.dot(context, out_weight, preferred_element_type=jnp.float32)
        + out_bias,
        gain_one,
        shift_one,
    )
    first_b = first.astype(jnp.bfloat16)
    hidden = jnp.dot(first_b, up_weight, preferred_element_type=jnp.float32) + up_bias
    active = jax.nn.gelu(hidden, approximate=False).astype(jnp.bfloat16)
    final, normed_two, inverse_two = layer_norm(
        first + jnp.dot(active, down_weight, preferred_element_type=jnp.float32) + down_bias,
        gain_two,
        shift_two,
    )
    rows_c = MICRO * TD
    out_content = final[:rows_c].reshape(MICRO, TD, D)
    out_query = final[rows_c:].reshape(MICRO, QP, D)[:, :extra_rows]

    upstream = jnp.concatenate(
        [cot_content.reshape(rows_c, D), pad_rows(cot_query)]
    ).astype(jnp.float32)
    dres_two, dgain_two, dshift_two = norm_back(upstream, normed_two, inverse_two, gain_two)
    dbias_down = jnp.sum(dres_two, axis=0)
    dres_two_b = dres_two.astype(jnp.bfloat16)
    dweight_down = dot_tn(active, dres_two_b)
    dactive = dot_nt(dres_two_b, down_weight).astype(jnp.bfloat16)
    dhidden = (dactive.astype(jnp.float32) * gelu_slope(hidden)).astype(jnp.bfloat16)
    dbias_up = jnp.sum(dhidden.astype(jnp.float32), axis=0)
    dweight_up = dot_tn(first_b, dhidden)
    dfirst = dres_two + dot_nt(dhidden, up_weight)
    dres_one, dgain_one, dshift_one = norm_back(dfirst, normed_one, inverse_one, gain_one)
    dbias_out = jnp.sum(dres_one, axis=0)
    dres_one_b = dres_one.astype(jnp.bfloat16)
    dweight_out = dot_tn(context, dres_one_b)
    dcontext = dot_nt(dres_one_b, out_weight).astype(jnp.bfloat16)

    dq_c, dq_x, dkv_prompt, dkv_near, dkv_own, hist = attend_back(
        meta,
        qkv,
        extra_q,
        prompt_kv,
        near_kv,
        table,
        xcol,
        xrow,
        lse,
        dcontext[:rows_c],
        dcontext[rows_c:],
        full_c,
        full_x,
    )
    own_prompt_grad = lax.psum_scatter(dkv_prompt, "fsdp", scatter_dimension=0)
    from_near = from_partner(dkv_near, "fsdp").astype(jnp.float32)
    dkv = jnp.concatenate(
        [own_prompt_grad, (dkv_own + from_near).astype(jnp.bfloat16)], axis=2
    ).reshape(2, rows_c, D)
    dqkv = jnp.concatenate([dq_c, dkv[0], dkv[1]], axis=1)
    dq_all = jnp.concatenate([dq_c, dq_x])
    dweight_query = dot_tn(x_all, dq_all)
    dbias_query = jnp.sum(dq_all.astype(jnp.float32), axis=0)
    dweight_kv = dot_tn(tokens_x, dqkv[:, D:])
    dbias_value = jnp.sum(dkv[1].astype(jnp.float32), axis=0)
    dtokens = dres_one[:rows_c] + dot_nt(dqkv, qkv_weight)
    dextra = dres_one[rows_c:] + dot_nt(dq_x, query_weight)
    grad_content = dtokens.reshape(MICRO, TD, D)
    grad_query = dextra.reshape(MICRO, QP, D)[:, :extra_rows]
    dtable = table_gradient(hist, rel_bucket, bias_table.shape[0], side, heads)

    def scatter(piece):
        return lax.psum_scatter(
            piece.astype(jnp.bfloat16), "fsdp", scatter_dimension=0, tiled=True
        )

    small = jnp.concatenate(
        [
            entry.reshape(devices, -1)
            for entry in (
                dbias_query,
                dbias_value,
                dbias_out,
                dbias_down,
                dgain_one,
                dshift_one,
                dgain_two,
                dshift_two,
                dbias_up,
                dtable,
            )
        ],
        axis=1,
    )
    shares = (
        scatter(dweight_down),
        scatter(dweight_up),
        scatter(dweight_out),
        scatter(dweight_query),
        scatter(dweight_kv),
        scatter(small),
    )
    totals = [lax.psum(entry, "grp").astype(jnp.float32) for entry in shares]
    t_down, t_up, t_out, t_query, t_kv, t_small = totals
    t_small = t_small.reshape(-1)
    pieces = [t_small[shard * i : shard * i + shard] for i in range(8)]
    up_at = 8 * shard
    up_size = b_up.shape[0]
    t_table = t_small[up_at + up_size :].reshape(-1, heads)
    return (
        out_content,
        out_query,
        grad_content,
        grad_query,
        t_query,
        pieces[0],
        t_kv[:, :D],
        t_kv[:, D:],
        pieces[1],
        t_out,
        pieces[2],
        pieces[4],
        pieces[5],
        t_up,
        t_small[up_at : up_at + up_size],
        t_down,
        pieces[3],
        pieces[6],
        pieces[7],
        t_table,
    )


def solution(mesh):
    rows = P(None, ("grp", "fsdp"), None)
    matrix = P("fsdp", None)
    vector = P("fsdp")
    in_specs = (
        rows,
        rows,
        rows,
        P(None, "grp", None),
        P(),
        matrix,
        vector,
        matrix,
        matrix,
        vector,
        matrix,
        vector,
        vector,
        vector,
        matrix,
        vector,
        matrix,
        vector,
        vector,
        vector,
        P(),
        rows,
        rows,
    )
    out_specs = (
        rows,
        rows,
        rows,
        rows,
        matrix,
        vector,
        matrix,
        matrix,
        vector,
        matrix,
        vector,
        vector,
        vector,
        matrix,
        vector,
        matrix,
        vector,
        vector,
        vector,
        matrix,
    )
    return jax.shard_map(
        on_device, mesh=mesh, in_specs=in_specs, out_specs=out_specs, check_vma=False
    )
```

```python
import functools

import jax
import jax.numpy as jnp
from jax import lax
from jax.experimental import pallas as pl
from jax.experimental.pallas import tpu as pltpu
from jax.sharding import PartitionSpec as P

D = 768
PD = 128
CH = 256
MICRO = 2
TD = 384
QP = 64
HD = 64
LANES = 128
PAIRS = D // LANES

PRECISE = lax.Precision.HIGHEST
MASKED = -1e30
VMEM_LIMIT = 56 * 1024 * 1024


def dot_nt(left, right):
    return lax.dot_general(
        left, right, (((1,), (1,)), ((), ())), preferred_element_type=jnp.float32
    )


def dot_tn(left, right):
    return lax.dot_general(
        left, right, (((0,), (0,)), ((), ())), preferred_element_type=jnp.float32
    )


def dot_nn(left, right):
    return jnp.dot(left, right, preferred_element_type=jnp.float32)


def head_stack(block):
    lane = lax.broadcasted_iota(jnp.int32, block.shape, 1)
    zero = jnp.zeros_like(block)
    return jnp.concatenate(
        [jnp.where(lane < HD, block, zero), jnp.where(lane < HD, zero, block)], axis=0
    )


def head_merge(stacked):
    rows = stacked.shape[0] // 2
    lane = lax.broadcasted_iota(jnp.int32, (rows, LANES), 1)
    return jnp.where(lane < HD, stacked[:rows], stacked[rows:])


def lookup(table, index):
    return jnp.take_along_axis(table, index, axis=1, mode="promise_in_bounds")


def near_index(distance):
    return jnp.clip(distance, 0, LANES - 1)


def fill_keys(scratch, rows_ref, own_prompt, mapped, plength):
    own_at = pl.multiple_of(own_prompt * plength, 128)
    scratch[0:plength] = rows_ref[pl.ds(own_at, plength), :]
    scratch[plength : 2 * plength] = jnp.where(
        mapped == 0, rows_ref[0:plength], rows_ref[plength : 2 * plength]
    )
    scratch[2 * plength :] = rows_ref[2 * plength :]


def place(plength):
    rank = lax.axis_index("fsdp")
    halfway = plength // PD
    return rank // halfway, rank % halfway * PD, rank % 2


def attend_kernel(
    plength,
    meta,
    qc,
    qx,
    k_rows,
    v_rows,
    table,
    xcol,
    w_ref,
    ctx_c,
    ctx_x,
    full_c,
    full_x,
    lse_ref,
    w_all,
    keys,
    vals,
    scores,
    probs,
    send_sem,
    recv_sem,
    local_sem,
):
    step = pl.program_id(0) * PAIRS + pl.program_id(1)
    grp = lax.axis_index("grp")
    rank = lax.axis_index("fsdp")
    core_mate = (grp, rank ^ 1)
    x_mate = (grp ^ 1, rank)
    local = pltpu.make_async_copy(w_ref, w_all.at[0], local_sem)
    swap = pltpu.make_async_remote_copy(
        w_ref, w_all.at[1], send_sem.at[0], recv_sem.at[0], device_id=core_mate,
        device_id_type=pl.DeviceIdType.MESH,
    )
    cross = pltpu.make_async_remote_copy(
        w_all.at[0:2], w_all.at[2:4], send_sem.at[1], recv_sem.at[1], device_id=x_mate,
        device_id_type=pl.DeviceIdType.MESH,
    )

    @pl.when(step == 0)
    def _():
        barrier = pltpu.get_barrier_semaphore()
        for mate in (core_mate, x_mate):
            pl.semaphore_signal(
                barrier, inc=1, device_id=mate, device_id_type=pl.DeviceIdType.MESH
            )
        pl.semaphore_wait(barrier, 2)
        local.start()
        swap.start()

    @pl.when(step == 5)
    def _():
        local.wait()
        swap.wait()
        cross.start()

    @pl.when(step == 11)
    def _():
        cross.wait()

    own_prompt, base, side = place(plength)
    mapped = meta[pl.program_id(0)]
    blocks = plength // 128
    fill_keys(keys, k_rows, own_prompt, mapped, plength)
    fill_keys(vals, v_rows, own_prompt, mapped, plength)
    row = lax.broadcasted_iota(jnp.int32, (128, 128), 0)
    col = lax.broadcasted_iota(jnp.int32, (128, 128), 1)
    tab_a = jnp.broadcast_to(table[0, 0:1, :], (128, 128))
    tab_b = jnp.broadcast_to(table[0, 1:2, :], (128, 128))
    tab_x = jnp.where(row < QP, tab_a, tab_b)
    lse_ref[...] = jnp.zeros_like(lse_ref)

    def solve(stack, first, plan, tables, lse_rows):
        count = len(plan)
        span = slice(first, first + 128 * count)
        halves = len(tables)
        width = 128 * count
        scores[0 : 128 * halves, 0:width] = dot_nt(stack, keys[span])
        for half in range(halves):
            rows = slice(128 * half, 128 * half + 128)
            peak = None
            for at, (index, visible) in enumerate(plan):
                cols = slice(128 * at, 128 * at + 128)
                s = scores[rows, cols]
                if index is not None:
                    s = s + lookup(tables[half], index)
                if visible is not None:
                    s = jnp.where(visible, s, MASKED)
                if index is not None or visible is not None:
                    scores[rows, cols] = s
                peak = s if peak is None else jnp.maximum(peak, s)
            top = jnp.max(peak, axis=1, keepdims=True)
            total = None
            for at in range(count):
                cols = slice(128 * at, 128 * at + 128)
                p = jnp.exp(scores[rows, cols] - top)
                total = p if total is None else total + p
                probs[rows, cols] = p.astype(jnp.bfloat16)
            total = jnp.sum(total, axis=1, keepdims=True)
            log_total = top + jnp.log(total)
            lse_ref[0, 0, lse_rows[half] : lse_rows[half] + 1, :] = jnp.transpose(
                jnp.broadcast_to(log_total, (128, 128))
            )[0:1, :]
            scores[rows, 0:128] = jnp.broadcast_to(1.0 / total, (128, 128))
        out = dot_nn(probs[0 : 128 * halves, 0:width], vals[span])
        return out * scores[0 : 128 * halves, 0:128]

    scale = jnp.asarray(0.125, jnp.bfloat16)
    q_p = head_stack(qc[0:PD] * scale)
    q_0 = head_stack(qc[PD : PD + 128] * scale)
    q_1 = head_stack(qc[PD + 128 : PD + 256] * scale)
    q_x = head_stack(qx[...] * scale)

    plan_p = []
    for b in range(blocks):
        d = base + row - (col + 128 * b)
        plan_p.append((near_index(d), d >= 0))
    out = head_merge(solve(q_p, 0, plan_p, (tab_a, tab_b), (0, 3)))
    ctx_c[0:PD] = out.astype(jnp.bfloat16)
    full_c[0:PD] = out

    far = (None, None)
    last = 128 + 2 * row + side - col
    near_d = 2 * (row - col) + 2 * side - 1
    own_d = 2 * (row - col)
    plan_0 = [far] * (blocks - 1) + [
        (near_index(last), None),
        (near_index(near_d), near_d >= 0),
        (near_index(own_d), own_d >= 0),
    ]
    out = head_merge(solve(q_0, plength, plan_0, (tab_a, tab_b), (1, 4)))
    ctx_c[PD : PD + 128] = out.astype(jnp.bfloat16)
    full_c[PD : PD + 128] = out
    plan_1 = [far] * blocks + [
        (near_index(near_d + 256), None),
        (near_index(own_d + 256), None),
        (near_index(near_d), near_d >= 0),
        (near_index(own_d), own_d >= 0),
    ]
    out = head_merge(solve(q_1, plength, plan_1, (tab_a, tab_b), (2, 5)))
    ctx_c[PD + 128 : PD + 256] = out.astype(jnp.bfloat16)
    full_c[PD + 128 : PD + 256] = out

    pos = jnp.broadcast_to(xcol[0, :, 0:1], (128, 128))
    lim_p = jnp.broadcast_to(xcol[0, :, 1:2], (128, 128))
    lim_c = jnp.broadcast_to(xcol[0, :, 2:3], (128, 128))
    plan_x = []
    for b in range(blocks):
        key = col + 128 * b
        plan_x.append((near_index(pos - key), key < lim_p))
    in_cont = lim_c > 0
    for b in range(blocks - 1):
        plan_x.append((None, in_cont))
    key = col + 128 * (blocks - 1)
    plan_x.append((near_index(pos - key), in_cont))
    for b in range(2):
        for offset in (1 - side, side):
            key = plength + 2 * (col + 128 * b) + offset
            plan_x.append((near_index(pos - key), key < lim_c))
    out = solve(q_x, 0, plan_x, (tab_x,), (6,))
    lane = lax.broadcasted_iota(jnp.int32, (QP, LANES), 1)
    out = jnp.where(lane < HD, out[0:QP], out[QP:])
    ctx_x[...] = out.astype(jnp.bfloat16)
    full_x[...] = out


def pair_column(shift):
    return lambda m, j, meta: (m, shift * PAIRS + j)


def key_spec(n_keys, shift):
    return pl.BlockSpec((n_keys, LANES), lambda m, j, meta: (m, shift * PAIRS + j))


TABLE_SPEC = pl.BlockSpec((1, 8, LANES), lambda m, j, meta: (j, 0, 0))


def attend(meta, queries, extra_q, key_rows, table, xcol, weight):
    n_keys = key_rows.shape[0] // MICRO
    plength = (n_keys - 2 * CH) // 2
    content = pl.BlockSpec((TD, LANES), pair_column(0))
    extra = pl.BlockSpec((QP, LANES), pair_column(0))
    own_row = plength + 2 * CH
    pairs = MICRO * PAIRS * 2 * (128 * plength + 256 * own_row) + MICRO * PAIRS * 128 * n_keys
    return pl.pallas_call(
        functools.partial(attend_kernel, plength),
        name="attend",
        grid_spec=pltpu.PrefetchScalarGridSpec(
            num_scalar_prefetch=1,
            grid=(MICRO, PAIRS),
            in_specs=[content, extra]
            + [
                key_spec(n_keys, 0),
                key_spec(n_keys, 1),
                TABLE_SPEC,
                pl.BlockSpec((1, 128, 8), lambda m, j, meta: (m, 0, 0)),
                pl.BlockSpec(memory_space=pl.ANY),
            ],
            out_specs=[
                content,
                extra,
                content,
                extra,
                pl.BlockSpec((1, 1, 8, LANES), lambda m, j, meta: (m, j, 0, 0)),
                pl.BlockSpec(memory_space=pl.ANY),
            ],
            scratch_shapes=[
                pltpu.VMEM((n_keys, LANES), jnp.bfloat16),
                pltpu.VMEM((n_keys, LANES), jnp.bfloat16),
                pltpu.VMEM((256, n_keys), jnp.float32),
                pltpu.VMEM((256, n_keys), jnp.bfloat16),
                pltpu.SemaphoreType.DMA((2,)),
                pltpu.SemaphoreType.DMA((2,)),
                pltpu.SemaphoreType.DMA,
            ],
        ),
        out_shape=[
            jax.ShapeDtypeStruct((MICRO * TD, D), jnp.bfloat16),
            jax.ShapeDtypeStruct((MICRO * QP, D), jnp.bfloat16),
            jax.ShapeDtypeStruct((MICRO * TD, D), jnp.float32),
            jax.ShapeDtypeStruct((MICRO * QP, D), jnp.float32),
            jax.ShapeDtypeStruct((MICRO, PAIRS, 8, LANES), jnp.float32),
            jax.ShapeDtypeStruct((4,) + weight.shape, weight.dtype),
        ],
        compiler_params=pltpu.CompilerParams(
            vmem_limit_bytes=VMEM_LIMIT, collective_id=1, has_side_effects=True
        ),
        cost_estimate=pl.CostEstimate(
            flops=4 * pairs * LANES, bytes_accessed=16 * 1024 * 1024, transcendentals=pairs
        ),
    )(
        meta,
        queries,
        extra_q,
        key_rows,
        key_rows,
        table,
        xcol,
        weight,
    )


def attend_back_kernel(
    plength,
    meta,
    qc,
    qx,
    k_rows,
    v_rows,
    table,
    xcol,
    xrow,
    lse_ref,
    dc,
    dx,
    full_c,
    full_x,
    dq_c,
    dq_x,
    dk_rows,
    dv_rows,
    hist,
    keys,
    vals,
    q_all,
    d_all,
    scores,
    dprobs,
    probs_t,
    dscores_t,
    ds_p,
    dk_acc,
    dv_acc,
):
    own_prompt, base, side = place(plength)
    mapped = meta[pl.program_id(0)]
    blocks = plength // 128
    at_k1 = 2 * plength + 256
    n_keys = 2 * plength + 512
    fill_keys(keys, k_rows, own_prompt, mapped, plength)
    fill_keys(vals, v_rows, own_prompt, mapped, plength)
    row = lax.broadcasted_iota(jnp.int32, (128, 128), 0)
    col = lax.broadcasted_iota(jnp.int32, (128, 128), 1)
    tab_a = jnp.broadcast_to(table[0, 0:1, :], (128, 128))
    tab_b = jnp.broadcast_to(table[0, 1:2, :], (128, 128))
    scale = jnp.asarray(0.125, jnp.bfloat16)

    p_at, x_at, c1_at, c0_at = 0, 256, 384, 640
    q_all[0:256] = head_stack(qc[0:PD] * scale)
    q_all[256:384] = head_stack(qx[...] * scale)
    q_all[384:640] = head_stack(qc[PD + 128 : PD + 256] * scale)
    q_all[640:896] = head_stack(qc[PD : PD + 128] * scale)
    d_all[0:256] = head_stack(dc[0:PD])
    d_all[256:384] = head_stack(dx[...])
    d_all[384:640] = head_stack(dc[PD + 128 : PD + 256])
    d_all[640:896] = head_stack(dc[PD : PD + 128])

    ones_lane = lax.broadcasted_iota(jnp.int32, (8, LANES), 1)
    ones_row = lax.broadcasted_iota(jnp.int32, (8, LANES), 0)
    pick = jnp.where((ones_lane < HD) == (ones_row == 0), 1.0, 0.0)
    pick = jnp.where(ones_row < 2, pick, 0.0)

    def deltas(upstream, context):
        product = upstream.astype(jnp.float32) * context
        return lax.dot_general(
            pick,
            product,
            (((1,), (1,)), ((), ())),
            precision=PRECISE,
            preferred_element_type=jnp.float32,
        )

    delta_p = deltas(dc[0:PD], full_c[0:PD])
    delta_0 = deltas(dc[PD : PD + 128], full_c[PD : PD + 128])
    delta_1 = deltas(dc[PD + 128 : PD + 256], full_c[PD + 128 : PD + 256])
    delta_x = deltas(dx[...], full_x[...])
    delta_x = jnp.concatenate([delta_x[0:1], delta_x[1:2]], axis=1)

    def block_back(first, plan, at_col, halves):
        count = len(plan)
        width = 128 * len(halves)
        span = slice(first, first + 128 * count)
        cols = slice(at_col, at_col + width)
        scores[0 : 128 * count, 0:width] = dot_nt(keys[span], q_all[cols])
        dprobs[0 : 128 * count, 0:width] = dot_nt(vals[span], d_all[cols])
        for half, (tables, lse_row, delta) in enumerate(halves):
            lane = slice(128 * half, 128 * half + 128)
            out_lane = slice(at_col + 128 * half, at_col + 128 * half + 128)
            lse = lse_ref[0, 0, lse_row : lse_row + 1, :]
            for at, (index, visible) in enumerate(plan):
                rows = slice(128 * at, 128 * at + 128)
                out_rows = slice(first + 128 * at, first + 128 * at + 128)
                s = scores[rows, lane]
                if index is not None:
                    bias = lookup(tables[0], index)
                    if len(tables) > 1:
                        bias = jnp.where(col < QP, bias, lookup(tables[1], index))
                    s = s + bias
                if visible is not None:
                    s = jnp.where(visible, s, MASKED)
                p = jnp.exp(s - lse)
                ds = p * (dprobs[rows, lane] - delta)
                probs_t[out_rows, out_lane] = p.astype(jnp.bfloat16)
                dscores_t[out_rows, out_lane] = ds.astype(jnp.bfloat16)
                yield half, at, ds

    extra_a = jnp.where(
        (xcol[0, :, 3:4] == lax.broadcasted_iota(jnp.int32, (128, TD), 1))
        & (lax.broadcasted_iota(jnp.int32, (128, TD), 0) < QP),
        1.0,
        0.0,
    ).astype(jnp.bfloat16)
    extra_b = jnp.where(
        (xcol[0, :, 3:4] == lax.broadcasted_iota(jnp.int32, (128, TD), 1))
        & (lax.broadcasted_iota(jnp.int32, (128, TD), 0) >= QP),
        1.0,
        0.0,
    ).astype(jnp.bfloat16)
    spread = (extra_a, extra_b)

    pos = xrow[0, 0:1, :]
    lim_p = xrow[0, 1:2, :]
    lim_c = xrow[0, 2:3, :]
    plan = []
    for b in range(blocks):
        key = row + 128 * b
        plan.append((near_index(pos - key), key < lim_p))
    in_cont = jnp.broadcast_to(lim_c > 0, (128, 128))
    for b in range(blocks - 1):
        plan.append((None, in_cont))
    plan.append((near_index(pos - (row + 128 * (blocks - 1))), in_cont))
    for b in range(2):
        for offset in (1 - side, side):
            key = plength + 2 * (row + 128 * b) + offset
            plan.append((near_index(pos - key), key < lim_c))
    for _ in block_back(0, plan, x_at, [((tab_a, tab_b), 6, delta_x)]):
        pass

    def spread_block(head, key_at, content_at):
        return dot_nn(
            dscores_t[pl.ds(key_at, 128), x_at : x_at + 128],
            spread[head][:, content_at : content_at + 128],
        )

    turn = (col + row) % 128
    turn_half = (col + row // 2) % 128

    def fold(block):
        return jnp.sum(block.reshape(16, 8, LANES), axis=0)

    plan = []
    for b in range(blocks):
        d = base + col - (row + 128 * b)
        plan.append((near_index(d), d >= 0))
    halves = [((tab_a,), 0, delta_p[0:1]), ((tab_b,), 3, delta_p[1:2])]
    for half, at, ds in block_back(0, plan, p_at, halves):
        ds_p[128 * at : 128 * at + 128, 128 * half : 128 * half + 128] = ds
    before = jnp.maximum(base - 128, 0)
    base_at = pl.multiple_of(base, 128)
    before_at = pl.multiple_of(before, 128)
    for head in range(2):
        lane = slice(128 * head, 128 * head + 128)
        here = ds_p[pl.ds(base_at, 128), lane] + spread_block(head, base_at, 0)
        prior = ds_p[pl.ds(before_at, 128), lane] + spread_block(head, before_at, 0)
        prior = jnp.where(base > 0, prior, 0.0)
        both = jnp.where(col >= row, here, prior)
        hist[0, 0, 32 * head : 32 * head + 8] = fold(lookup(both, turn))

    last = 128 + 2 * col + side - row
    near_d = 2 * (col - row) + 2 * side - 1
    own_d = 2 * (col - row)
    far = (None, None)
    plan_0 = [far] * (blocks - 1) + [
        (near_index(last), None),
        (near_index(near_d), near_d >= 0),
        (near_index(own_d), own_d >= 0),
    ]
    plan_1 = [far] * blocks + [
        (near_index(near_d + 256), None),
        (near_index(own_d + 256), None),
        (near_index(near_d), near_d >= 0),
        (near_index(own_d), own_d >= 0),
    ]
    halves = [((tab_a,), 1, delta_0[0:1]), ((tab_b,), 4, delta_0[1:2])]
    near_sum = {}
    own_sum = {}
    last_key = 2 * plength - 128
    for half, at, ds in block_back(plength, plan_0, c0_at, halves):
        if at == blocks - 1:
            ds = ds + spread_block(half, last_key, PD)
            ds = jnp.where(col < 64, ds, 0.0)
            hist[0, 0, 32 * half + 8 : 32 * half + 16] = fold(lookup(ds, turn_half))
        if at == blocks:
            ds = ds + spread_block(half, 2 * plength, PD)
            near_sum[half] = jnp.where(col >= row, ds, 0.0)
        if at == blocks + 1:
            ds = ds + spread_block(half, 2 * plength + 128, PD)
            own_sum[half] = jnp.where(col >= row, ds, 0.0)
    for half in range(2):
        lane = slice(128 * half, 128 * half + 128)
        ds_p[0:128, lane] = near_sum[half]
        ds_p[128:256, lane] = own_sum[half]
    halves = [((tab_a,), 2, delta_1[0:1]), ((tab_b,), 5, delta_1[1:2])]
    for half, at, ds in block_back(plength, plan_1, c1_at, halves):
        lane = slice(128 * half, 128 * half + 128)
        if at == blocks:
            ds = ds + spread_block(half, 2 * plength, PD + 128)
            ds_p[0:128, lane] = ds_p[0:128, lane] + jnp.where(col < row, ds, 0.0)
        if at == blocks + 1:
            ds = ds + spread_block(half, 2 * plength + 128, PD + 128)
            ds_p[128:256, lane] = ds_p[128:256, lane] + jnp.where(col < row, ds, 0.0)
        if at == blocks + 2:
            ds = ds + spread_block(half, at_k1, PD + 128)
            ds = ds_p[0:128, lane] + jnp.where(col >= row, ds, 0.0)
            hist[0, 0, 32 * half + 16 : 32 * half + 24] = fold(lookup(ds, turn))
        if at == blocks + 3:
            ds = ds + spread_block(half, at_k1 + 128, PD + 128)
            ds = ds_p[128:256, lane] + jnp.where(col >= row, ds, 0.0)
            hist[0, 0, 32 * half + 24 : 32 * half + 32] = fold(lookup(ds, turn))

    own = slice(0, plength)
    middle = slice(plength, at_k1)
    end = slice(at_k1, n_keys)
    for acc, left, right in ((dk_acc, dscores_t, q_all), (dv_acc, probs_t, d_all)):
        acc[own] = dot_nn(left[own, 0:384], right[0:384])
        acc[middle] = dot_nn(left[middle, 256:896], right[256:896])
        acc[end] = dot_nn(left[end, 256:640], right[256:640])

    dq_c[0:PD] = (
        head_merge(dot_tn(dscores_t[own, p_at : p_at + 256], keys[own])) * 0.125
    ).astype(jnp.bfloat16)
    dq_c[PD : PD + 128] = (
        head_merge(dot_tn(dscores_t[middle, c0_at : c0_at + 256], keys[middle])) * 0.125
    ).astype(jnp.bfloat16)
    cont = slice(plength, n_keys)
    dq_c[PD + 128 : PD + 256] = (
        head_merge(dot_tn(dscores_t[cont, c1_at : c1_at + 256], keys[cont])) * 0.125
    ).astype(jnp.bfloat16)
    out = dot_tn(dscores_t[:, x_at : x_at + 128], keys[...])
    lane = lax.broadcasted_iota(jnp.int32, (QP, LANES), 1)
    dq_x[...] = (jnp.where(lane < HD, out[0:QP], out[QP:]) * 0.125).astype(jnp.bfloat16)

    for out_ref, acc in ((dk_rows, dk_acc), (dv_rows, dv_acc)):
        for p in range(2):
            mine = jnp.where(own_prompt == p, acc[own], 0.0)
            other = jnp.where(mapped == p, acc[plength : 2 * plength], 0.0)
            out_ref[p * plength : (p + 1) * plength] = (mine + other).astype(jnp.bfloat16)
        out_ref[2 * plength :] = acc[2 * plength :].astype(jnp.bfloat16)


def attend_back(meta, queries, extra_q, key_rows, table, xcol, xrow, lse, dc, dx, fc, fx):
    n_keys = key_rows.shape[0] // MICRO
    plength = (n_keys - 2 * CH) // 2
    content = pl.BlockSpec((TD, LANES), pair_column(0))
    extra = pl.BlockSpec((QP, LANES), pair_column(0))
    own_row = plength + 2 * CH
    pairs = MICRO * PAIRS * 2 * (128 * plength + 256 * own_row) + MICRO * PAIRS * 128 * n_keys
    return pl.pallas_call(
        functools.partial(attend_back_kernel, plength),
        name="attend_back",
        grid_spec=pltpu.PrefetchScalarGridSpec(
            num_scalar_prefetch=1,
            grid=(MICRO, PAIRS),
            in_specs=[content, extra]
            + [
                key_spec(n_keys, 0),
                key_spec(n_keys, 1),
                TABLE_SPEC,
                pl.BlockSpec((1, 128, 8), lambda m, j, meta: (m, 0, 0)),
                pl.BlockSpec((1, 8, 128), lambda m, j, meta: (m, 0, 0)),
                pl.BlockSpec((1, 1, 8, LANES), lambda m, j, meta: (m, j, 0, 0)),
                content,
                extra,
                content,
                extra,
            ],
            out_specs=[
                content,
                extra,
                key_spec(n_keys, 0),
                key_spec(n_keys, 0),
                pl.BlockSpec((1, 1, 64, LANES), lambda m, j, meta: (m, j, 0, 0)),
            ],
            scratch_shapes=[
                pltpu.VMEM((n_keys, LANES), jnp.bfloat16),
                pltpu.VMEM((n_keys, LANES), jnp.bfloat16),
                pltpu.VMEM((896, LANES), jnp.bfloat16),
                pltpu.VMEM((896, LANES), jnp.bfloat16),
                pltpu.VMEM((n_keys, 256), jnp.float32),
                pltpu.VMEM((n_keys, 256), jnp.float32),
                pltpu.VMEM((n_keys, 896), jnp.bfloat16),
                pltpu.VMEM((n_keys, 896), jnp.bfloat16),
                pltpu.VMEM((plength, 256), jnp.float32),
                pltpu.VMEM((n_keys, LANES), jnp.float32),
                pltpu.VMEM((n_keys, LANES), jnp.float32),
            ],
        ),
        out_shape=[
            jax.ShapeDtypeStruct((MICRO * TD, D), jnp.bfloat16),
            jax.ShapeDtypeStruct((MICRO * QP, D), jnp.bfloat16),
            jax.ShapeDtypeStruct((MICRO * n_keys, D), jnp.bfloat16),
            jax.ShapeDtypeStruct((MICRO * n_keys, D), jnp.bfloat16),
            jax.ShapeDtypeStruct((MICRO, PAIRS, 64, LANES), jnp.float32),
        ],
        compiler_params=pltpu.CompilerParams(vmem_limit_bytes=VMEM_LIMIT),
        cost_estimate=pl.CostEstimate(
            flops=10 * pairs * LANES, bytes_accessed=32 * 1024 * 1024, transcendentals=pairs
        ),
    )(
        meta,
        queries,
        extra_q,
        key_rows,
        key_rows,
        table,
        xcol,
        xrow,
        lse,
        dc,
        dx,
        fc,
        fx,
    )


def from_partner(block, axis):
    count = lax.axis_size(axis)
    return lax.ppermute(block, axis, [(i, i ^ 1) for i in range(count)])


def layer_norm(value, gain, shift):
    centred = value - jnp.mean(value, axis=-1, keepdims=True)
    inverse = lax.rsqrt(jnp.mean(centred * centred, axis=-1, keepdims=True) + 1e-05)
    normed = centred * inverse
    return (normed * gain + shift, normed, inverse)


def norm_back(upstream, normed, inverse, gain):
    scaled = upstream * gain
    inner = (
        scaled
        - jnp.mean(scaled, axis=-1, keepdims=True)
        - normed * jnp.mean(scaled * normed, axis=-1, keepdims=True)
    )
    return (inverse * inner, jnp.sum(upstream * normed, axis=0), jnp.sum(upstream, axis=0))


def gelu_slope(hidden):
    return (
        0.5 * (1.0 + lax.erf(hidden * 0.7071067811865476))
        + hidden * jnp.exp(-0.5 * hidden * hidden) * 0.3989422804014327
    )


def pad_rows(block):
    return jnp.pad(block, ((0, 0), (0, QP - block.shape[1]), (0, 0))).reshape(MICRO * QP, D)


def table_gradient(hist, rel_bucket, buckets, side, heads):
    summed = jnp.sum(hist, axis=0).reshape(PAIRS, 2, 4, 8, LANES)
    prompt = jnp.sum(summed[:, :, 0], axis=2)
    even = jnp.sum(summed[:, :, 1, 0::2], axis=2)
    odd = jnp.sum(summed[:, :, 1, 1::2], axis=2)
    near = jnp.sum(summed[:, :, 2], axis=2)
    own = jnp.sum(summed[:, :, 3], axis=2)
    lanes = jnp.arange(LANES, dtype=jnp.int32)
    signed = jnp.where(lanes < 64, lanes, lanes - 128)
    distance = jnp.stack(
        [
            lanes,
            128 + side + 2 * signed,
            127 + side + 2 * signed,
            2 * lanes + 2 * side - 1,
            2 * lanes,
        ]
    ).reshape(-1)
    hot = (distance[:, None] == lanes[None, :]) & (lanes[None, :] < LANES - 1)
    parts = jnp.stack([prompt, even, odd, near, own], axis=2).reshape(heads, 5 * LANES)
    close = jnp.dot(parts, hot.astype(jnp.float32), precision=PRECISE)
    close = jnp.where(
        lanes[None, :] == LANES - 1, -jnp.sum(close, axis=1, keepdims=True), close
    )
    bucket_hot = (rel_bucket[:, None] == jnp.arange(buckets, dtype=jnp.int32)[None, :]).astype(
        jnp.float32
    )
    return jnp.dot(bucket_hot.T, close.T, precision=PRECISE)


def on_device(
    content_in,
    query_in,
    pred_order,
    cont_prompt,
    rel_bucket,
    w_query,
    b_query,
    w_key,
    w_value,
    b_value,
    w_out,
    b_out,
    ln1_gain,
    ln1_bias,
    w_up,
    b_up,
    w_down,
    b_down,
    ln2_gain,
    ln2_bias,
    bias_table,
    cot_content,
    cot_query,
):
    devices = lax.axis_size("fsdp")
    halfway = devices // 2
    own_rank = lax.axis_index("fsdp")
    plength = PD * halfway
    heads = bias_table.shape[1]
    extra_rows = query_in.shape[1]
    prompt_base = own_rank % halfway * PD
    cont_index = own_rank // 2
    side = own_rank % 2

    def gather(entry):
        return lax.all_gather(entry, "fsdp", axis=0, tiled=True)

    vectors = jnp.concatenate(
        [b_query, b_value, b_out, b_down, ln1_gain, ln1_bias, ln2_gain, ln2_bias, b_up]
    )
    query_weight, key_weight, value_weight = gather(w_query), gather(w_key), gather(w_value)
    all_vectors = gather(vectors[None])
    shard = b_query.shape[0]
    singles = [
        all_vectors[:, shard * i : shard * i + shard].reshape(-1).astype(jnp.float32)
        for i in range(8)
    ]
    (
        query_bias,
        value_bias,
        out_bias,
        down_bias,
        gain_one,
        shift_one,
        gain_two,
        shift_two,
    ) = singles
    up_bias = all_vectors[:, 8 * shard :].reshape(-1).astype(jnp.float32)
    out_weight, up_weight, down_weight = gather(w_out), gather(w_up), gather(w_down)

    prompt_map = cont_prompt[:, 0, :]
    prompt_ref = jnp.sum(
        jnp.where(
            jnp.arange(prompt_map.shape[1], dtype=jnp.int32)[None, :] == cont_index, prompt_map, 0
        ),
        axis=1,
    )
    meta = prompt_ref.astype(jnp.int32)
    order = jnp.pad(pred_order[:, 0, :], ((0, 0), (0, QP - extra_rows)), constant_values=-1)
    real = order >= 0
    in_prompt = order < PD
    position = jnp.where(
        in_prompt, prompt_base + order, plength + 2 * (order - PD) + side
    )
    limit_p = jnp.where(real & in_prompt, jnp.maximum(position, 1), -1)
    limit_c = jnp.where(real & ~in_prompt, position, -1)
    info = jnp.stack([position, limit_p, limit_c, order], axis=1)
    info = jnp.concatenate([info, info], axis=2)
    xrow = jnp.pad(info, ((0, 0), (0, 4), (0, 0))).astype(jnp.int32)
    xcol = jnp.swapaxes(xrow, 1, 2)
    dist = bias_table.astype(jnp.float32)[rel_bucket].T
    dist = dist - dist[:, LANES - 1 :]
    table = jnp.pad(dist.reshape(PAIRS, 2, LANES), ((0, 0), (0, 6), (0, 0)))

    tokens_x = content_in.reshape(MICRO * TD, D)
    extra_x = pad_rows(query_in)
    x_all = jnp.concatenate([tokens_x, extra_x])
    n_keys = 2 * plength + 2 * CH
    prompt_x = lax.all_gather(content_in[:, :PD], "fsdp", axis=1, tiled=True)
    near_x = from_partner(content_in[:, PD:], "fsdp").reshape(MICRO, 2, 1, 128, D)
    own_x = content_in[:, PD:].reshape(MICRO, 2, 1, 128, D)
    cont_x = jnp.concatenate([near_x, own_x], axis=2).reshape(MICRO, 2 * CH, D)
    keys_x = jnp.concatenate([prompt_x, cont_x], axis=1).reshape(MICRO * n_keys, D)
    kv_weight = jnp.concatenate([key_weight, value_weight], axis=1)
    kv_bias = jnp.concatenate([jnp.zeros((D,), jnp.float32), value_bias])
    key_rows = (
        jnp.dot(keys_x, kv_weight, preferred_element_type=jnp.float32) + kv_bias
    ).astype(jnp.bfloat16)
    q_all = (
        jnp.dot(x_all, query_weight, preferred_element_type=jnp.float32) + query_bias
    ).astype(jnp.bfloat16)
    queries = q_all[: MICRO * TD]
    extra_q = q_all[MICRO * TD :]

    ctx_c, ctx_x, full_c, full_x, lse, _ = attend(
        meta, queries, extra_q, key_rows, table, xcol, w_out
    )
    context = jnp.concatenate([ctx_c, ctx_x])
    first, normed_one, inverse_one = layer_norm(
        x_all.astype(jnp.float32)
        + jnp.dot(context, out_weight, preferred_element_type=jnp.float32)
        + out_bias,
        gain_one,
        shift_one,
    )
    first_b = first.astype(jnp.bfloat16)
    hidden = jnp.dot(first_b, up_weight, preferred_element_type=jnp.float32) + up_bias
    active = jax.nn.gelu(hidden, approximate=False).astype(jnp.bfloat16)
    final, normed_two, inverse_two = layer_norm(
        first + jnp.dot(active, down_weight, preferred_element_type=jnp.float32) + down_bias,
        gain_two,
        shift_two,
    )
    rows_c = MICRO * TD
    out_content = final[:rows_c].reshape(MICRO, TD, D)
    out_query = final[rows_c:].reshape(MICRO, QP, D)[:, :extra_rows]

    upstream = jnp.concatenate(
        [cot_content.reshape(rows_c, D), pad_rows(cot_query)]
    ).astype(jnp.float32)
    dres_two, dgain_two, dshift_two = norm_back(upstream, normed_two, inverse_two, gain_two)
    dbias_down = jnp.sum(dres_two, axis=0)
    dres_two_b = dres_two.astype(jnp.bfloat16)
    dweight_down = dot_tn(active, dres_two_b)
    dactive = dot_nt(dres_two_b, down_weight).astype(jnp.bfloat16)
    dhidden = (dactive.astype(jnp.float32) * gelu_slope(hidden)).astype(jnp.bfloat16)
    dbias_up = jnp.sum(dhidden.astype(jnp.float32), axis=0)
    dweight_up = dot_tn(first_b, dhidden)
    dfirst = dres_two + dot_nt(dhidden, up_weight)
    dres_one, dgain_one, dshift_one = norm_back(dfirst, normed_one, inverse_one, gain_one)
    dbias_out = jnp.sum(dres_one, axis=0)
    dres_one_b = dres_one.astype(jnp.bfloat16)
    dweight_out = dot_tn(context, dres_one_b)
    dcontext = dot_nt(dres_one_b, out_weight).astype(jnp.bfloat16)

    dq_c, dq_x, dk_rows, dv_rows, hist = attend_back(
        meta,
        queries,
        extra_q,
        key_rows,
        table,
        xcol,
        xrow,
        lse,
        dcontext[:rows_c],
        dcontext[rows_c:],
        full_c,
        full_x,
    )
    dkv_rows = jnp.concatenate([dk_rows, dv_rows], axis=1)
    dq_all = jnp.concatenate([dq_c, dq_x])
    dweight_query = dot_tn(x_all, dq_all)
    dbias_query = jnp.sum(dq_all.astype(jnp.float32), axis=0)
    dweight_kv = dot_tn(keys_x, dkv_rows)
    dbias_value = jnp.sum(dv_rows.astype(jnp.float32), axis=0)
    dkeys_x = dot_nt(dkv_rows, kv_weight).reshape(MICRO, n_keys, D)
    from_prompts = lax.psum_scatter(
        dkeys_x[:, : 2 * plength].astype(jnp.bfloat16), "fsdp", scatter_dimension=1, tiled=True
    ).astype(jnp.float32)
    dcont = dkeys_x[:, 2 * plength :].reshape(MICRO, 2, 2, 128, D)
    from_near = from_partner(dcont[:, :, 0].astype(jnp.bfloat16), "fsdp").astype(jnp.float32)
    dcont = (dcont[:, :, 1] + from_near).reshape(MICRO, CH, D)
    dx_all = dres_one + dot_nt(dq_all, query_weight)
    dtokens = dx_all[:rows_c].reshape(MICRO, TD, D) + jnp.concatenate(
        [from_prompts, dcont], axis=1
    )
    dextra = dx_all[rows_c:]
    grad_content = dtokens
    grad_query = dextra.reshape(MICRO, QP, D)[:, :extra_rows]
    dtable = table_gradient(hist, rel_bucket, bias_table.shape[0], side, heads)

    def scatter(piece):
        return lax.psum_scatter(
            piece.astype(jnp.bfloat16), "fsdp", scatter_dimension=0, tiled=True
        )

    small = jnp.concatenate(
        [
            entry.reshape(devices, -1)
            for entry in (
                dbias_query,
                dbias_value,
                dbias_out,
                dbias_down,
                dgain_one,
                dshift_one,
                dgain_two,
                dshift_two,
                dbias_up,
                dtable,
            )
        ],
        axis=1,
    )
    shares = (
        scatter(dweight_down),
        scatter(dweight_up),
        scatter(dweight_out),
        scatter(dweight_query),
        scatter(dweight_kv),
        scatter(small),
    )
    totals = [lax.psum(entry, "grp").astype(jnp.float32) for entry in shares]
    t_down, t_up, t_out, t_query, t_kv, t_small = totals
    t_small = t_small.reshape(-1)
    pieces = [t_small[shard * i : shard * i + shard] for i in range(8)]
    up_at = 8 * shard
    up_size = b_up.shape[0]
    t_table = t_small[up_at + up_size :].reshape(-1, heads)
    return (
        out_content,
        out_query,
        grad_content,
        grad_query,
        t_query,
        pieces[0],
        t_kv[:, :D],
        t_kv[:, D:],
        pieces[1],
        t_out,
        pieces[2],
        pieces[4],
        pieces[5],
        t_up,
        t_small[up_at : up_at + up_size],
        t_down,
        pieces[3],
        pieces[6],
        pieces[7],
        t_table,
    )


def solution(mesh):
    rows = P(None, ("grp", "fsdp"), None)
    matrix = P("fsdp", None)
    vector = P("fsdp")
    in_specs = (
        rows,
        rows,
        rows,
        P(None, "grp", None),
        P(),
        matrix,
        vector,
        matrix,
        matrix,
        vector,
        matrix,
        vector,
        vector,
        vector,
        matrix,
        vector,
        matrix,
        vector,
        vector,
        vector,
        P(),
        rows,
        rows,
    )
    out_specs = (
        rows,
        rows,
        rows,
        rows,
        matrix,
        vector,
        matrix,
        matrix,
        vector,
        matrix,
        vector,
        vector,
        vector,
        matrix,
        vector,
        matrix,
        vector,
        vector,
        vector,
        matrix,
    )
    return jax.shard_map(
        on_device, mesh=mesh, in_specs=in_specs, out_specs=out_specs, check_vma=False
    )
```

```python
import functools

import jax
import jax.numpy as jnp
from jax import lax
from jax.experimental import pallas as pl
from jax.experimental.pallas import tpu as pltpu
from jax.sharding import PartitionSpec as P

D = 768
PD = 128
CH = 256
MICRO = 2
TD = 384
QP = 64
HD = 64
LANES = 128
PAIRS = D // LANES

PRECISE = lax.Precision.HIGHEST
MASKED = -1e30
VMEM_LIMIT = 56 * 1024 * 1024


def dot_nt(left, right):
    return lax.dot_general(
        left, right, (((1,), (1,)), ((), ())), preferred_element_type=jnp.float32
    )


def dot_tn(left, right):
    return lax.dot_general(
        left, right, (((0,), (0,)), ((), ())), preferred_element_type=jnp.float32
    )


def dot_nn(left, right):
    return jnp.dot(left, right, preferred_element_type=jnp.float32)


def head_stack(block):
    lane = lax.broadcasted_iota(jnp.int32, block.shape, 1)
    zero = jnp.zeros_like(block)
    return jnp.concatenate(
        [jnp.where(lane < HD, block, zero), jnp.where(lane < HD, zero, block)], axis=0
    )


def head_merge(stacked):
    rows = stacked.shape[0] // 2
    lane = lax.broadcasted_iota(jnp.int32, (rows, LANES), 1)
    return jnp.where(lane < HD, stacked[:rows], stacked[rows:])


def lookup(table, index):
    return jnp.take_along_axis(table, index, axis=1, mode="promise_in_bounds")


def near_index(distance):
    return jnp.clip(distance, 0, LANES - 1)


def fill_keys(scratch, rows_ref, own_prompt, mapped, plength):
    own_at = pl.multiple_of(own_prompt * plength, 128)
    scratch[0:plength] = rows_ref[pl.ds(own_at, plength), :]
    scratch[plength : 2 * plength] = jnp.where(
        mapped == 0, rows_ref[0:plength], rows_ref[plength : 2 * plength]
    )
    scratch[2 * plength :] = rows_ref[2 * plength :]


MESH = pl.DeviceIdType.MESH
ANY_SPEC = pl.BlockSpec(memory_space=pl.ANY)


class Net:
    def __init__(self):
        self.g = lax.axis_index("grp")
        self.f = lax.axis_index("fsdp")
        self.x = self.g % 2
        self.y = self.g // 2
        self.z = self.f // 2
        self.c = self.f % 2
        self.gx = self.g + 1 - 2 * self.x
        self.gy = self.g + 2 - 4 * self.y
        self.mate = self.f + 1 - 2 * self.c
        self.z_of = [
            self.z + 1 - 2 * (self.z % 2),
            (self.z + 2) % 4,
            3 - self.z,
        ]
        self.f_of = [2 * other + self.c for other in self.z_of]
        self.to_x = (self.gx, self.f)
        self.to_y = (self.gy, self.f)
        self.to_mate = (self.g, self.mate)
        self.to_z = [(self.g, other) for other in self.f_of]

    def greet(self):
        barrier = pltpu.get_barrier_semaphore()
        everyone = [self.to_x, self.to_y, self.to_mate] + self.to_z
        for device in everyone:
            pl.semaphore_signal(barrier, inc=1, device_id=device, device_id_type=MESH)
        pl.semaphore_wait(barrier, len(everyone))


class Copies:
    def __init__(self, sends, recvs):
        self.sends = sends
        self.recvs = recvs
        self.used = 0
        self.all = []

    def to(self, device, src, dst):
        copy = pltpu.make_async_remote_copy(
            src_ref=src,
            dst_ref=dst,
            send_sem=self.sends.at[self.used],
            recv_sem=self.recvs.at[self.used],
            device_id=device,
            device_id_type=MESH,
        )
        self.used += 1
        self.all.append(copy)
        return copy

    def finish(self):
        for copy in self.all:
            copy.wait_send()


def start(copies):
    for copy in copies:
        copy.start()


def arrive(copies):
    for copy in copies:
        copy.wait_recv()


GATHER_COPIES = 19


def gather_stages(net, copies, local_sem, shard, full):
    part, width = shard.shape[1:]
    half = width // 2

    def rows(owner, quarter):
        return 4 * owner + quarter

    def whole(owner):
        return pl.ds(4 * owner, 4)

    local = pltpu.make_async_copy(shard, full.at[whole(net.f)], local_sem)
    mine = shard.at[net.g]
    along_z = [copies.to(device, mine, full.at[rows(net.f, net.g)]) for device in net.to_z]
    to_mate = [copies.to(net.to_mate, shard, full.at[whole(net.f)])]
    to_x, to_y, on_x, on_y, later = [], [], [], [], []
    for owner in net.f_of:
        got = full.at[rows(owner, net.g)]
        to_x.append(copies.to(net.to_x, got, got))
        to_y.append(copies.to(net.to_y, got, got))
        left = full.at[rows(owner, net.gx), :, pl.ds(0, half)]
        on_y.append(copies.to(net.to_y, left, left))
        right = full.at[rows(owner, net.gy), :, pl.ds(half, half)]
        on_x.append(copies.to(net.to_x, right, right))
        shared = full.at[whole(owner)]
        later.append(copies.to(net.to_mate, shared, shared))

    def begin():
        local.start()
        start(along_z)
        start(to_mate)

    def plane():
        arrive(along_z)
        start(to_x + to_y)

    def corners():
        arrive(to_x + to_y)
        start(on_y + on_x)

    def mates():
        arrive(on_y + on_x)
        start(later)

    def end():
        arrive(to_mate + later)
        local.wait()
        for copy in along_z + to_mate + to_x + to_y + on_x + on_y + later:
            copy.wait_send()

    return [begin, plane, corners, mates, end]


REDUCE_COPIES = 19


def reduce_buffers(size, width):
    part, half = size // 4, width // 2
    return [
        pltpu.VMEM((4, 4, part, width), jnp.bfloat16),
        pltpu.VMEM((4, 4, part, width), jnp.bfloat16),
        pltpu.VMEM((4, 2, part, half), jnp.bfloat16),
        pltpu.VMEM((4, 2, part, half), jnp.bfloat16),
        pltpu.VMEM((2, 4, part, half), jnp.bfloat16),
        pltpu.VMEM((2, 3, part, half), jnp.bfloat16),
        pltpu.VMEM((2, 4, part, half), jnp.bfloat16),
        pltpu.SemaphoreType.DMA((2,)),
        pltpu.SemaphoreType.DMA((REDUCE_COPIES,)),
        pltpu.SemaphoreType.DMA((REDUCE_COPIES,)),
    ]


def reduce_stages(net, grad, share, buffers):
    own, other, side_a, side_b, line, along, done, local_sem, sends, recvs = buffers
    copies = Copies(sends, recvs)
    half = grad.shape[4] // 2
    left, right = pl.ds(0, half), pl.ds(half, half)
    load = pltpu.make_async_copy(grad.at[:, net.c], own, local_sem.at[0])
    to_mate = [copies.to(net.to_mate, grad.at[:, 1 - net.c], other)]
    first = []
    for i in range(2):
        first.append(
            copies.to(net.to_x, own.at[:, 2 * i + 1 - net.x, :, left], side_a.at[:, i])
        )
        first.append(
            copies.to(net.to_y, own.at[:, 2 - 2 * net.y + i, :, right], side_b.at[:, i])
        )
    second = [
        copies.to(net.to_y, side_a.at[:, 1 - net.y], line.at[0]),
        copies.to(net.to_x, side_b.at[:, 1 - net.x], line.at[1]),
    ]
    third = []
    for k in range(3):
        for h in range(2):
            third.append(
                copies.to(net.to_z[k], line.at[h, net.z_of[k]], along.at[h, k])
            )
    fourth = []
    fifth = []
    for h in range(2):
        fourth.append(copies.to(net.to_x, done.at[h, net.g], done.at[h, net.g]))
        fourth.append(copies.to(net.to_y, done.at[h, net.g], done.at[h, net.g]))
    fifth.append(copies.to(net.to_y, done.at[0, net.gx], done.at[0, net.gx]))
    fifth.append(copies.to(net.to_x, done.at[1, net.gy], done.at[1, net.gy]))
    store = [
        pltpu.make_async_copy(done.at[0], share.at[:, :, left], local_sem.at[0]),
        pltpu.make_async_copy(done.at[1], share.at[:, :, right], local_sem.at[1]),
    ]

    def begin():
        load.start()
        start(to_mate)

    def plane():
        load.wait()
        arrive(to_mate)

        @pl.loop(0, 16)
        def _(i):
            zi, qi = i // 4, i % 4
            own[zi, qi] = own[zi, qi] + other[zi, qi]

        start(first)

    def cross():
        arrive(first)

        @pl.loop(0, 8)
        def _(i):
            zi, qi = i // 2, i % 2
            side_a[zi, qi] = side_a[zi, qi] + own[zi, 2 * qi + net.x, :, 0:half]
            side_b[zi, qi] = side_b[zi, qi] + own[zi, 2 * net.y + qi, :, half : 2 * half]

        start(second)

    def column():
        arrive(second)

        @pl.loop(0, 4)
        def _(zi):
            line[0, zi] = line[0, zi] + side_a[zi, net.y]
            line[1, zi] = line[1, zi] + side_b[zi, net.x]

        start(third)

    def spread():
        arrive(third)

        @pl.loop(0, 2)
        def _(h):
            total = line[h, net.z].astype(jnp.float32)
            for k in range(3):
                total = total + along[h, k].astype(jnp.float32)
            done[h, net.g] = total.astype(jnp.bfloat16)

        start(fourth)

    def corners():
        arrive(fourth)
        start(fifth)

    def end():
        arrive(fifth)
        start(store)
        for copy in store:
            copy.wait()
        copies.finish()

    return [begin, plane, cross, column, spread, corners, end]


def gather_first_kernel(
    w_ref, v_ref, x_ref, w_full, v_full, keys_x, w_s, w_r, v_s, v_r, x_s, x_r, local_sem
):
    net = Net()
    net.greet()
    weights = gather_stages(net, Copies(w_s, w_r), local_sem.at[0], w_ref, w_full)
    vectors = gather_stages(net, Copies(v_s, v_r), local_sem.at[1], v_ref, v_full)
    plength = PD * 4
    at = 2 * plength

    def block(owner):
        return pl.ds(pl.multiple_of(owner * PD, 128), PD)

    prompt = x_ref.at[:, pl.ds(0, PD)]
    cont = [x_ref.at[:, pl.ds(PD + 128 * i, 128)] for i in range(2)]
    near = [keys_x.at[:, pl.ds(at + 256 * i, 128)] for i in range(2)]
    here = [keys_x.at[:, pl.ds(at + 256 * i + 128, 128)] for i in range(2)]
    copies = Copies(x_s, x_r)
    local = [pltpu.make_async_copy(prompt, keys_x.at[:, block(net.f)], local_sem.at[2])]
    local += [
        pltpu.make_async_copy(cont[i], here[i], local_sem.at[3 + i]) for i in range(2)
    ]
    to_mate = [copies.to(net.to_mate, prompt, keys_x.at[:, block(net.f)])]
    to_mate += [copies.to(net.to_mate, cont[i], near[i]) for i in range(2)]
    along_z = [copies.to(device, prompt, keys_x.at[:, block(net.f)]) for device in net.to_z]
    later = [
        copies.to(net.to_mate, keys_x.at[:, block(owner)], keys_x.at[:, block(owner)])
        for owner in net.f_of
    ]
    weights[0]()
    vectors[0]()
    start(local)
    start(to_mate)
    weights[1]()
    start(along_z)
    vectors[1]()
    weights[2]()
    vectors[2]()
    weights[3]()
    vectors[3]()
    arrive(along_z)
    start(later)
    weights[4]()
    vectors[4]()
    arrive(to_mate + later)
    for copy in local:
        copy.wait()
    copies.finish()


def gather_first(w_shard, v_shard, content_in):
    def sems(count):
        return [pltpu.SemaphoreType.DMA((count,))] * 2

    return pl.pallas_call(
        gather_first_kernel,
        name="gather_first",
        in_specs=[ANY_SPEC] * 3,
        out_specs=[ANY_SPEC] * 3,
        out_shape=[
            jax.ShapeDtypeStruct((8 * 4,) + w_shard.shape[1:], jnp.bfloat16),
            jax.ShapeDtypeStruct((8 * 4,) + v_shard.shape[1:], jnp.bfloat16),
            jax.ShapeDtypeStruct((MICRO, 8 * PD + 2 * CH, D), jnp.bfloat16),
        ],
        scratch_shapes=sems(GATHER_COPIES)
        + sems(GATHER_COPIES)
        + sems(9)
        + [pltpu.SemaphoreType.DMA((5,))],
        compiler_params=pltpu.CompilerParams(collective_id=1, has_side_effects=True),
    )(w_shard, v_shard, content_in)


def reduce_last_kernel(w_ref, v_ref, p_ref, n_ref, w_out, v_out, p_out, n_out, *scratch):
    w_buf, v_buf = scratch[:10], scratch[10:20]
    mine, theirs, along, total, n_buf, x_s, x_r, x_local = scratch[20:]
    net = Net()
    net.greet()
    weights = reduce_stages(net, w_ref, w_out, w_buf)
    vectors = reduce_stages(net, v_ref, v_out, v_buf)
    copies = Copies(x_s, x_r)
    load = pltpu.make_async_copy(p_ref.at[:, :, net.c], mine, x_local)
    to_mate = [
        copies.to(net.to_mate, p_ref.at[:, :, 1 - net.c], theirs),
        copies.to(net.to_mate, n_ref, n_buf),
    ]
    third = [
        copies.to(net.to_z[k], mine.at[:, net.z_of[k]], along.at[k]) for k in range(3)
    ]
    weights[0]()
    vectors[0]()
    load.start()
    start(to_mate)
    weights[1]()
    vectors[1]()
    load.wait()
    arrive(to_mate)

    @pl.loop(0, 8)
    def _(i):
        m, zi = i // 4, i % 4
        mine[m, zi] = mine[m, zi] + theirs[m, zi]

    start(third)
    for i in range(2, 4):
        weights[i]()
        vectors[i]()
    arrive(third)
    weights[4]()
    vectors[4]()

    @pl.loop(0, 2)
    def _(m):
        s = mine[m, net.z].astype(jnp.float32)
        for k in range(3):
            s = s + along[k, m].astype(jnp.float32)
        total[m] = s

    out = pltpu.make_async_copy(total, p_out, x_local)
    out.start()
    out.wait()
    out = pltpu.make_async_copy(n_buf, n_out, x_local)
    out.start()
    out.wait()
    for i in range(5, 7):
        weights[i]()
        vectors[i]()
    copies.finish()


def reduce_last(w_grad, v_grad, p_grad, n_grad):
    def buffers(grad):
        return reduce_buffers(4 * grad.shape[3], grad.shape[4])

    return pl.pallas_call(
        reduce_last_kernel,
        name="reduce_last",
        in_specs=[ANY_SPEC] * 4,
        out_specs=[ANY_SPEC] * 4,
        out_shape=[
            jax.ShapeDtypeStruct(w_grad.shape[2:], jnp.bfloat16),
            jax.ShapeDtypeStruct(v_grad.shape[2:], jnp.bfloat16),
            jax.ShapeDtypeStruct((MICRO, PD, D), jnp.float32),
            jax.ShapeDtypeStruct(n_grad.shape, jnp.bfloat16),
        ],
        scratch_shapes=buffers(w_grad)
        + buffers(v_grad)
        + [
            pltpu.VMEM((MICRO, 4, PD, D), jnp.bfloat16),
            pltpu.VMEM((MICRO, 4, PD, D), jnp.bfloat16),
            pltpu.VMEM((3, MICRO, PD, D), jnp.bfloat16),
            pltpu.VMEM((MICRO, PD, D), jnp.float32),
            pltpu.VMEM(n_grad.shape, jnp.bfloat16),
            pltpu.SemaphoreType.DMA((5,)),
            pltpu.SemaphoreType.DMA((5,)),
            pltpu.SemaphoreType.DMA,
        ],
        compiler_params=pltpu.CompilerParams(
            collective_id=4, has_side_effects=True, vmem_limit_bytes=VMEM_LIMIT
        ),
    )(w_grad, v_grad, p_grad, n_grad)


def hosted(plan, step):
    for at, stage in plan:

        @pl.when(step == at)
        def _():
            stage()


def place(plength):
    rank = lax.axis_index("fsdp")
    halfway = plength // PD
    return rank // halfway, rank % halfway * PD, rank % 2


def attend_kernel(plength, carried, *refs):
    (meta, qc, qx, k_rows, v_rows, table, xcol), refs = refs[:7], refs[7:]
    shards, refs = refs[:carried], refs[carried:]
    (ctx_c, ctx_x, full_c, full_x, lse_ref), refs = refs[:5], refs[5:]
    fulls, refs = refs[:carried], refs[carried:]
    keys, vals, scores, probs = refs[:4]
    step = pl.program_id(0) * PAIRS + pl.program_id(1)
    stages = []
    if carried:
        net = Net()
        for i in range(carried):
            sends, recvs = refs[4 + 2 * i : 6 + 2 * i]
            stages.append(
                gather_stages(
                    net, Copies(sends, recvs), refs[-1].at[i], shards[i], fulls[i]
                )
            )
        up, down, proj = stages
        hosted([(0, net.greet)], step)
        hosted(
            [
                (0, up[0]),
                (3, up[1]),
                (3, down[0]),
                (6, up[2]),
                (7, down[1]),
                (7, proj[0]),
                (8, up[3]),
                (8, proj[1]),
                (10, down[2]),
                (10, proj[2]),
            ],
            step,
        )
    own_prompt, base, side = place(plength)
    mapped = meta[pl.program_id(0)]
    blocks = plength // 128
    fill_keys(keys, k_rows, own_prompt, mapped, plength)
    fill_keys(vals, v_rows, own_prompt, mapped, plength)
    row = lax.broadcasted_iota(jnp.int32, (128, 128), 0)
    col = lax.broadcasted_iota(jnp.int32, (128, 128), 1)
    tab_a = jnp.broadcast_to(table[0, 0:1, :], (128, 128))
    tab_b = jnp.broadcast_to(table[0, 1:2, :], (128, 128))
    tab_x = jnp.where(row < QP, tab_a, tab_b)
    lse_ref[...] = jnp.zeros_like(lse_ref)

    def solve(stack, first, plan, tables, lse_rows):
        count = len(plan)
        span = slice(first, first + 128 * count)
        halves = len(tables)
        width = 128 * count
        scores[0 : 128 * halves, 0:width] = dot_nt(stack, keys[span])
        for half in range(halves):
            rows = slice(128 * half, 128 * half + 128)
            peak = None
            for at, (index, visible) in enumerate(plan):
                cols = slice(128 * at, 128 * at + 128)
                s = scores[rows, cols]
                if index is not None:
                    s = s + lookup(tables[half], index)
                if visible is not None:
                    s = jnp.where(visible, s, MASKED)
                if index is not None or visible is not None:
                    scores[rows, cols] = s
                peak = s if peak is None else jnp.maximum(peak, s)
            top = jnp.max(peak, axis=1, keepdims=True)
            total = None
            for at in range(count):
                cols = slice(128 * at, 128 * at + 128)
                p = jnp.exp(scores[rows, cols] - top)
                total = p if total is None else total + p
                probs[rows, cols] = p.astype(jnp.bfloat16)
            total = jnp.sum(total, axis=1, keepdims=True)
            log_total = top + jnp.log(total)
            lse_ref[0, 0, lse_rows[half] : lse_rows[half] + 1, :] = jnp.transpose(
                jnp.broadcast_to(log_total, (128, 128))
            )[0:1, :]
            scores[rows, 0:128] = jnp.broadcast_to(1.0 / total, (128, 128))
        out = dot_nn(probs[0 : 128 * halves, 0:width], vals[span])
        return out * scores[0 : 128 * halves, 0:128]

    scale = jnp.asarray(0.125, jnp.bfloat16)
    q_p = head_stack(qc[0:PD] * scale)
    q_0 = head_stack(qc[PD : PD + 128] * scale)
    q_1 = head_stack(qc[PD + 128 : PD + 256] * scale)
    q_x = head_stack(qx[...] * scale)

    plan_p = []
    for b in range(blocks):
        d = base + row - (col + 128 * b)
        plan_p.append((near_index(d), d >= 0))
    out = head_merge(solve(q_p, 0, plan_p, (tab_a, tab_b), (0, 3)))
    ctx_c[0:PD] = out.astype(jnp.bfloat16)
    full_c[0:PD] = out

    far = (None, None)
    last = 128 + 2 * row + side - col
    near_d = 2 * (row - col) + 2 * side - 1
    own_d = 2 * (row - col)
    plan_0 = [far] * (blocks - 1) + [
        (near_index(last), None),
        (near_index(near_d), near_d >= 0),
        (near_index(own_d), own_d >= 0),
    ]
    out = head_merge(solve(q_0, plength, plan_0, (tab_a, tab_b), (1, 4)))
    ctx_c[PD : PD + 128] = out.astype(jnp.bfloat16)
    full_c[PD : PD + 128] = out
    plan_1 = [far] * blocks + [
        (near_index(near_d + 256), None),
        (near_index(own_d + 256), None),
        (near_index(near_d), near_d >= 0),
        (near_index(own_d), own_d >= 0),
    ]
    out = head_merge(solve(q_1, plength, plan_1, (tab_a, tab_b), (2, 5)))
    ctx_c[PD + 128 : PD + 256] = out.astype(jnp.bfloat16)
    full_c[PD + 128 : PD + 256] = out

    pos = jnp.broadcast_to(xcol[0, :, 0:1], (128, 128))
    lim_p = jnp.broadcast_to(xcol[0, :, 1:2], (128, 128))
    lim_c = jnp.broadcast_to(xcol[0, :, 2:3], (128, 128))
    plan_x = []
    for b in range(blocks):
        key = col + 128 * b
        plan_x.append((near_index(pos - key), key < lim_p))
    in_cont = lim_c > 0
    for b in range(blocks - 1):
        plan_x.append((None, in_cont))
    key = col + 128 * (blocks - 1)
    plan_x.append((near_index(pos - key), in_cont))
    for b in range(2):
        for offset in (1 - side, side):
            key = plength + 2 * (col + 128 * b) + offset
            plan_x.append((near_index(pos - key), key < lim_c))
    out = solve(q_x, 0, plan_x, (tab_x,), (6,))
    lane = lax.broadcasted_iota(jnp.int32, (QP, LANES), 1)
    out = jnp.where(lane < HD, out[0:QP], out[QP:])
    ctx_x[...] = out.astype(jnp.bfloat16)
    full_x[...] = out
    if carried:
        hosted([(11, s) for s in (down[3], proj[3], up[4], down[4], proj[4])], step)


def pair_column(shift):
    return lambda m, j, meta: (m, shift * PAIRS + j)


def key_spec(n_keys, shift):
    return pl.BlockSpec((n_keys, LANES), lambda m, j, meta: (m, shift * PAIRS + j))


TABLE_SPEC = pl.BlockSpec((1, 8, LANES), lambda m, j, meta: (j, 0, 0))


def host_params(collective_id, carried):
    if carried:
        return pltpu.CompilerParams(
            vmem_limit_bytes=VMEM_LIMIT, collective_id=collective_id, has_side_effects=True
        )
    return pltpu.CompilerParams(vmem_limit_bytes=VMEM_LIMIT)


def attend(meta, queries, extra_q, key_rows, table, xcol, shards):
    carried = len(shards)
    n_keys = key_rows.shape[0] // MICRO
    plength = (n_keys - 2 * CH) // 2
    content = pl.BlockSpec((TD, LANES), pair_column(0))
    extra = pl.BlockSpec((QP, LANES), pair_column(0))
    own_row = plength + 2 * CH
    pairs = MICRO * PAIRS * 2 * (128 * plength + 256 * own_row) + MICRO * PAIRS * 128 * n_keys
    return pl.pallas_call(
        functools.partial(attend_kernel, plength, carried),
        name="attend",
        grid_spec=pltpu.PrefetchScalarGridSpec(
            num_scalar_prefetch=1,
            grid=(MICRO, PAIRS),
            in_specs=[content, extra]
            + [
                key_spec(n_keys, 0),
                key_spec(n_keys, 1),
                TABLE_SPEC,
                pl.BlockSpec((1, 128, 8), lambda m, j, meta: (m, 0, 0)),
            ]
            + [ANY_SPEC] * carried,
            out_specs=[
                content,
                extra,
                content,
                extra,
                pl.BlockSpec((1, 1, 8, LANES), lambda m, j, meta: (m, j, 0, 0)),
            ]
            + [ANY_SPEC] * carried,
            scratch_shapes=[
                pltpu.VMEM((n_keys, LANES), jnp.bfloat16),
                pltpu.VMEM((n_keys, LANES), jnp.bfloat16),
                pltpu.VMEM((256, n_keys), jnp.float32),
                pltpu.VMEM((256, n_keys), jnp.bfloat16),
            ]
            + [pltpu.SemaphoreType.DMA((GATHER_COPIES,))] * (2 * carried)
            + [pltpu.SemaphoreType.DMA((4,))],
        ),
        out_shape=[
            jax.ShapeDtypeStruct((MICRO * TD, D), jnp.bfloat16),
            jax.ShapeDtypeStruct((MICRO * QP, D), jnp.bfloat16),
            jax.ShapeDtypeStruct((MICRO * TD, D), jnp.float32),
            jax.ShapeDtypeStruct((MICRO * QP, D), jnp.float32),
            jax.ShapeDtypeStruct((MICRO, PAIRS, 8, LANES), jnp.float32),
        ]
        + [
            jax.ShapeDtypeStruct((8 * 4,) + shard.shape[1:], shard.dtype)
            for shard in shards
        ],
        compiler_params=host_params(2, carried),
        cost_estimate=pl.CostEstimate(
            flops=4 * pairs * LANES, bytes_accessed=16 * 1024 * 1024, transcendentals=pairs
        ),
    )(
        meta,
        queries,
        extra_q,
        key_rows,
        key_rows,
        table,
        xcol,
        *shards,
    )


def attend_back_kernel(plength, carried, *refs):
    (meta, qc, qx, k_rows, v_rows, table, xcol, xrow, lse_ref, dc, dx, full_c, full_x), refs = (
        refs[:13],
        refs[13:],
    )
    grads, refs = refs[:carried], refs[carried:]
    (dq_c, dq_x, dk_rows, dv_rows, hist), refs = refs[:5], refs[5:]
    shares, refs = refs[:carried], refs[carried:]
    keys, vals, q_all, d_all, scores, dprobs, probs_t, dscores_t, ds_p, dk_acc, dv_acc = refs[:11]
    refs = refs[11:]
    step = pl.program_id(0) * PAIRS + pl.program_id(1)
    if carried:
        net = Net()
        up, down, proj = (
            reduce_stages(net, grads[i], shares[i], refs[10 * i : 10 * i + 10])
            for i in range(carried)
        )
        hosted([(0, net.greet)], step)
        hosted(
            [
                (0, up[0]),
                (0, down[0]),
                (0, proj[0]),
                (1, up[1]),
                (4, up[2]),
                (4, down[1]),
                (6, up[3]),
                (7, down[2]),
                (7, proj[1]),
                (9, down[3]),
                (9, proj[2]),
                (9, up[4]),
                (10, proj[3]),
                (10, up[5]),
            ],
            step,
        )
    own_prompt, base, side = place(plength)
    mapped = meta[pl.program_id(0)]
    blocks = plength // 128
    at_k1 = 2 * plength + 256
    n_keys = 2 * plength + 512
    fill_keys(keys, k_rows, own_prompt, mapped, plength)
    fill_keys(vals, v_rows, own_prompt, mapped, plength)
    row = lax.broadcasted_iota(jnp.int32, (128, 128), 0)
    col = lax.broadcasted_iota(jnp.int32, (128, 128), 1)
    tab_a = jnp.broadcast_to(table[0, 0:1, :], (128, 128))
    tab_b = jnp.broadcast_to(table[0, 1:2, :], (128, 128))
    scale = jnp.asarray(0.125, jnp.bfloat16)

    p_at, x_at, c1_at, c0_at = 0, 256, 384, 640
    q_all[0:256] = head_stack(qc[0:PD] * scale)
    q_all[256:384] = head_stack(qx[...] * scale)
    q_all[384:640] = head_stack(qc[PD + 128 : PD + 256] * scale)
    q_all[640:896] = head_stack(qc[PD : PD + 128] * scale)
    d_all[0:256] = head_stack(dc[0:PD])
    d_all[256:384] = head_stack(dx[...])
    d_all[384:640] = head_stack(dc[PD + 128 : PD + 256])
    d_all[640:896] = head_stack(dc[PD : PD + 128])

    ones_lane = lax.broadcasted_iota(jnp.int32, (8, LANES), 1)
    ones_row = lax.broadcasted_iota(jnp.int32, (8, LANES), 0)
    pick = jnp.where((ones_lane < HD) == (ones_row == 0), 1.0, 0.0)
    pick = jnp.where(ones_row < 2, pick, 0.0)

    def deltas(upstream, context):
        product = upstream.astype(jnp.float32) * context
        return lax.dot_general(
            pick,
            product,
            (((1,), (1,)), ((), ())),
            precision=PRECISE,
            preferred_element_type=jnp.float32,
        )

    delta_p = deltas(dc[0:PD], full_c[0:PD])
    delta_0 = deltas(dc[PD : PD + 128], full_c[PD : PD + 128])
    delta_1 = deltas(dc[PD + 128 : PD + 256], full_c[PD + 128 : PD + 256])
    delta_x = deltas(dx[...], full_x[...])
    delta_x = jnp.concatenate([delta_x[0:1], delta_x[1:2]], axis=1)

    def block_back(first, plan, at_col, halves):
        count = len(plan)
        width = 128 * len(halves)
        span = slice(first, first + 128 * count)
        cols = slice(at_col, at_col + width)
        scores[0 : 128 * count, 0:width] = dot_nt(keys[span], q_all[cols])
        dprobs[0 : 128 * count, 0:width] = dot_nt(vals[span], d_all[cols])
        for half, (tables, lse_row, delta) in enumerate(halves):
            lane = slice(128 * half, 128 * half + 128)
            out_lane = slice(at_col + 128 * half, at_col + 128 * half + 128)
            lse = lse_ref[0, 0, lse_row : lse_row + 1, :]
            for at, (index, visible) in enumerate(plan):
                rows = slice(128 * at, 128 * at + 128)
                out_rows = slice(first + 128 * at, first + 128 * at + 128)
                s = scores[rows, lane]
                if index is not None:
                    bias = lookup(tables[0], index)
                    if len(tables) > 1:
                        bias = jnp.where(col < QP, bias, lookup(tables[1], index))
                    s = s + bias
                if visible is not None:
                    s = jnp.where(visible, s, MASKED)
                p = jnp.exp(s - lse)
                ds = p * (dprobs[rows, lane] - delta)
                probs_t[out_rows, out_lane] = p.astype(jnp.bfloat16)
                dscores_t[out_rows, out_lane] = ds.astype(jnp.bfloat16)
                yield half, at, ds

    extra_a = jnp.where(
        (xcol[0, :, 3:4] == lax.broadcasted_iota(jnp.int32, (128, TD), 1))
        & (lax.broadcasted_iota(jnp.int32, (128, TD), 0) < QP),
        1.0,
        0.0,
    ).astype(jnp.bfloat16)
    extra_b = jnp.where(
        (xcol[0, :, 3:4] == lax.broadcasted_iota(jnp.int32, (128, TD), 1))
        & (lax.broadcasted_iota(jnp.int32, (128, TD), 0) >= QP),
        1.0,
        0.0,
    ).astype(jnp.bfloat16)
    spread = (extra_a, extra_b)

    pos = xrow[0, 0:1, :]
    lim_p = xrow[0, 1:2, :]
    lim_c = xrow[0, 2:3, :]
    plan = []
    for b in range(blocks):
        key = row + 128 * b
        plan.append((near_index(pos - key), key < lim_p))
    in_cont = jnp.broadcast_to(lim_c > 0, (128, 128))
    for b in range(blocks - 1):
        plan.append((None, in_cont))
    plan.append((near_index(pos - (row + 128 * (blocks - 1))), in_cont))
    for b in range(2):
        for offset in (1 - side, side):
            key = plength + 2 * (row + 128 * b) + offset
            plan.append((near_index(pos - key), key < lim_c))
    for _ in block_back(0, plan, x_at, [((tab_a, tab_b), 6, delta_x)]):
        pass

    def spread_block(head, key_at, content_at):
        return dot_nn(
            dscores_t[pl.ds(key_at, 128), x_at : x_at + 128],
            spread[head][:, content_at : content_at + 128],
        )

    turn = (col + row) % 128
    turn_half = (col + row // 2) % 128

    def fold(block):
        return jnp.sum(block.reshape(16, 8, LANES), axis=0)

    plan = []
    for b in range(blocks):
        d = base + col - (row + 128 * b)
        plan.append((near_index(d), d >= 0))
    halves = [((tab_a,), 0, delta_p[0:1]), ((tab_b,), 3, delta_p[1:2])]
    for half, at, ds in block_back(0, plan, p_at, halves):
        ds_p[128 * at : 128 * at + 128, 128 * half : 128 * half + 128] = ds
    before = jnp.maximum(base - 128, 0)
    base_at = pl.multiple_of(base, 128)
    before_at = pl.multiple_of(before, 128)
    for head in range(2):
        lane = slice(128 * head, 128 * head + 128)
        here = ds_p[pl.ds(base_at, 128), lane] + spread_block(head, base_at, 0)
        prior = ds_p[pl.ds(before_at, 128), lane] + spread_block(head, before_at, 0)
        prior = jnp.where(base > 0, prior, 0.0)
        both = jnp.where(col >= row, here, prior)
        hist[0, 0, 32 * head : 32 * head + 8] = fold(lookup(both, turn))

    last = 128 + 2 * col + side - row
    near_d = 2 * (col - row) + 2 * side - 1
    own_d = 2 * (col - row)
    far = (None, None)
    plan_0 = [far] * (blocks - 1) + [
        (near_index(last), None),
        (near_index(near_d), near_d >= 0),
        (near_index(own_d), own_d >= 0),
    ]
    plan_1 = [far] * blocks + [
        (near_index(near_d + 256), None),
        (near_index(own_d + 256), None),
        (near_index(near_d), near_d >= 0),
        (near_index(own_d), own_d >= 0),
    ]
    halves = [((tab_a,), 1, delta_0[0:1]), ((tab_b,), 4, delta_0[1:2])]
    near_sum = {}
    own_sum = {}
    last_key = 2 * plength - 128
    for half, at, ds in block_back(plength, plan_0, c0_at, halves):
        if at == blocks - 1:
            ds = ds + spread_block(half, last_key, PD)
            ds = jnp.where(col < 64, ds, 0.0)
            hist[0, 0, 32 * half + 8 : 32 * half + 16] = fold(lookup(ds, turn_half))
        if at == blocks:
            ds = ds + spread_block(half, 2 * plength, PD)
            near_sum[half] = jnp.where(col >= row, ds, 0.0)
        if at == blocks + 1:
            ds = ds + spread_block(half, 2 * plength + 128, PD)
            own_sum[half] = jnp.where(col >= row, ds, 0.0)
    for half in range(2):
        lane = slice(128 * half, 128 * half + 128)
        ds_p[0:128, lane] = near_sum[half]
        ds_p[128:256, lane] = own_sum[half]
    halves = [((tab_a,), 2, delta_1[0:1]), ((tab_b,), 5, delta_1[1:2])]
    for half, at, ds in block_back(plength, plan_1, c1_at, halves):
        lane = slice(128 * half, 128 * half + 128)
        if at == blocks:
            ds = ds + spread_block(half, 2 * plength, PD + 128)
            ds_p[0:128, lane] = ds_p[0:128, lane] + jnp.where(col < row, ds, 0.0)
        if at == blocks + 1:
            ds = ds + spread_block(half, 2 * plength + 128, PD + 128)
            ds_p[128:256, lane] = ds_p[128:256, lane] + jnp.where(col < row, ds, 0.0)
        if at == blocks + 2:
            ds = ds + spread_block(half, at_k1, PD + 128)
            ds = ds_p[0:128, lane] + jnp.where(col >= row, ds, 0.0)
            hist[0, 0, 32 * half + 16 : 32 * half + 24] = fold(lookup(ds, turn))
        if at == blocks + 3:
            ds = ds + spread_block(half, at_k1 + 128, PD + 128)
            ds = ds_p[128:256, lane] + jnp.where(col >= row, ds, 0.0)
            hist[0, 0, 32 * half + 24 : 32 * half + 32] = fold(lookup(ds, turn))

    own = slice(0, plength)
    middle = slice(plength, at_k1)
    end = slice(at_k1, n_keys)
    for acc, left, right in ((dk_acc, dscores_t, q_all), (dv_acc, probs_t, d_all)):
        acc[own] = dot_nn(left[own, 0:384], right[0:384])
        acc[middle] = dot_nn(left[middle, 256:896], right[256:896])
        acc[end] = dot_nn(left[end, 256:640], right[256:640])

    dq_c[0:PD] = (
        head_merge(dot_tn(dscores_t[own, p_at : p_at + 256], keys[own])) * 0.125
    ).astype(jnp.bfloat16)
    dq_c[PD : PD + 128] = (
        head_merge(dot_tn(dscores_t[middle, c0_at : c0_at + 256], keys[middle])) * 0.125
    ).astype(jnp.bfloat16)
    cont = slice(plength, n_keys)
    dq_c[PD + 128 : PD + 256] = (
        head_merge(dot_tn(dscores_t[cont, c1_at : c1_at + 256], keys[cont])) * 0.125
    ).astype(jnp.bfloat16)
    out = dot_tn(dscores_t[:, x_at : x_at + 128], keys[...])
    lane = lax.broadcasted_iota(jnp.int32, (QP, LANES), 1)
    dq_x[...] = (jnp.where(lane < HD, out[0:QP], out[QP:]) * 0.125).astype(jnp.bfloat16)

    for out_ref, acc in ((dk_rows, dk_acc), (dv_rows, dv_acc)):
        for p in range(2):
            mine = jnp.where(own_prompt == p, acc[own], 0.0)
            other = jnp.where(mapped == p, acc[plength : 2 * plength], 0.0)
            out_ref[p * plength : (p + 1) * plength] = (mine + other).astype(jnp.bfloat16)
        out_ref[2 * plength :] = acc[2 * plength :].astype(jnp.bfloat16)
    if carried:
        rest = (down[4], proj[4], up[6], down[5], proj[5], down[6], proj[6])
        hosted([(11, s) for s in rest], step)


def attend_back(meta, queries, extra_q, key_rows, table, xcol, xrow, lse, dc, dx, fc, fx, grads):
    carried = len(grads)
    n_keys = key_rows.shape[0] // MICRO
    plength = (n_keys - 2 * CH) // 2
    content = pl.BlockSpec((TD, LANES), pair_column(0))
    extra = pl.BlockSpec((QP, LANES), pair_column(0))
    own_row = plength + 2 * CH
    pairs = MICRO * PAIRS * 2 * (128 * plength + 256 * own_row) + MICRO * PAIRS * 128 * n_keys
    return pl.pallas_call(
        functools.partial(attend_back_kernel, plength, carried),
        name="attend_back",
        grid_spec=pltpu.PrefetchScalarGridSpec(
            num_scalar_prefetch=1,
            grid=(MICRO, PAIRS),
            in_specs=[content, extra]
            + [
                key_spec(n_keys, 0),
                key_spec(n_keys, 1),
                TABLE_SPEC,
                pl.BlockSpec((1, 128, 8), lambda m, j, meta: (m, 0, 0)),
                pl.BlockSpec((1, 8, 128), lambda m, j, meta: (m, 0, 0)),
                pl.BlockSpec((1, 1, 8, LANES), lambda m, j, meta: (m, j, 0, 0)),
                content,
                extra,
                content,
                extra,
            ]
            + [ANY_SPEC] * carried,
            out_specs=[
                content,
                extra,
                key_spec(n_keys, 0),
                key_spec(n_keys, 0),
                pl.BlockSpec((1, 1, 64, LANES), lambda m, j, meta: (m, j, 0, 0)),
            ]
            + [ANY_SPEC] * carried,
            scratch_shapes=[
                pltpu.VMEM((n_keys, LANES), jnp.bfloat16),
                pltpu.VMEM((n_keys, LANES), jnp.bfloat16),
                pltpu.VMEM((896, LANES), jnp.bfloat16),
                pltpu.VMEM((896, LANES), jnp.bfloat16),
                pltpu.VMEM((n_keys, 256), jnp.float32),
                pltpu.VMEM((n_keys, 256), jnp.float32),
                pltpu.VMEM((n_keys, 896), jnp.bfloat16),
                pltpu.VMEM((n_keys, 896), jnp.bfloat16),
                pltpu.VMEM((plength, 256), jnp.float32),
                pltpu.VMEM((n_keys, LANES), jnp.float32),
                pltpu.VMEM((n_keys, LANES), jnp.float32),
            ]
            + [
                buffer
                for grad in grads
                for buffer in reduce_buffers(4 * grad.shape[3], grad.shape[4])
            ],
        ),
        out_shape=[
            jax.ShapeDtypeStruct((MICRO * TD, D), jnp.bfloat16),
            jax.ShapeDtypeStruct((MICRO * QP, D), jnp.bfloat16),
            jax.ShapeDtypeStruct((MICRO * n_keys, D), jnp.bfloat16),
            jax.ShapeDtypeStruct((MICRO * n_keys, D), jnp.bfloat16),
            jax.ShapeDtypeStruct((MICRO, PAIRS, 64, LANES), jnp.float32),
        ]
        + [jax.ShapeDtypeStruct(grad.shape[2:], grad.dtype) for grad in grads],
        compiler_params=host_params(3, carried),
        cost_estimate=pl.CostEstimate(
            flops=10 * pairs * LANES, bytes_accessed=32 * 1024 * 1024, transcendentals=pairs
        ),
    )(
        meta,
        queries,
        extra_q,
        key_rows,
        key_rows,
        table,
        xcol,
        xrow,
        lse,
        dc,
        dx,
        fc,
        fx,
        *grads,
    )


def from_partner(block, axis):
    count = lax.axis_size(axis)
    return lax.ppermute(block, axis, [(i, i ^ 1) for i in range(count)])


def layer_norm(value, gain, shift):
    centred = value - jnp.mean(value, axis=-1, keepdims=True)
    inverse = lax.rsqrt(jnp.mean(centred * centred, axis=-1, keepdims=True) + 1e-05)
    normed = centred * inverse
    return (normed * gain + shift, normed, inverse)


def norm_back(upstream, normed, inverse, gain):
    scaled = upstream * gain
    inner = (
        scaled
        - jnp.mean(scaled, axis=-1, keepdims=True)
        - normed * jnp.mean(scaled * normed, axis=-1, keepdims=True)
    )
    return (inverse * inner, jnp.sum(upstream * normed, axis=0), jnp.sum(upstream, axis=0))


def gelu_slope(hidden):
    return (
        0.5 * (1.0 + lax.erf(hidden * 0.7071067811865476))
        + hidden * jnp.exp(-0.5 * hidden * hidden) * 0.3989422804014327
    )


def pad_rows(block):
    return jnp.pad(block, ((0, 0), (0, QP - block.shape[1]), (0, 0))).reshape(MICRO * QP, D)


def table_gradient(hist, rel_bucket, buckets, side, heads):
    summed = jnp.sum(hist, axis=0).reshape(PAIRS, 2, 4, 8, LANES)
    prompt = jnp.sum(summed[:, :, 0], axis=2)
    even = jnp.sum(summed[:, :, 1, 0::2], axis=2)
    odd = jnp.sum(summed[:, :, 1, 1::2], axis=2)
    near = jnp.sum(summed[:, :, 2], axis=2)
    own = jnp.sum(summed[:, :, 3], axis=2)
    lanes = jnp.arange(LANES, dtype=jnp.int32)
    signed = jnp.where(lanes < 64, lanes, lanes - 128)
    distance = jnp.stack(
        [
            lanes,
            128 + side + 2 * signed,
            127 + side + 2 * signed,
            2 * lanes + 2 * side - 1,
            2 * lanes,
        ]
    ).reshape(-1)
    hot = (distance[:, None] == lanes[None, :]) & (lanes[None, :] < LANES - 1)
    parts = jnp.stack([prompt, even, odd, near, own], axis=2).reshape(heads, 5 * LANES)
    close = jnp.dot(parts, hot.astype(jnp.float32), precision=PRECISE)
    close = jnp.where(
        lanes[None, :] == LANES - 1, -jnp.sum(close, axis=1, keepdims=True), close
    )
    bucket_hot = (rel_bucket[:, None] == jnp.arange(buckets, dtype=jnp.int32)[None, :]).astype(
        jnp.float32
    )
    return jnp.dot(bucket_hot.T, close.T, precision=PRECISE)


def on_device(
    content_in,
    query_in,
    pred_order,
    cont_prompt,
    rel_bucket,
    w_query,
    b_query,
    w_key,
    w_value,
    b_value,
    w_out,
    b_out,
    ln1_gain,
    ln1_bias,
    w_up,
    b_up,
    w_down,
    b_down,
    ln2_gain,
    ln2_bias,
    bias_table,
    cot_content,
    cot_query,
):
    devices = lax.axis_size("fsdp")
    halfway = devices // 2
    own_rank = lax.axis_index("fsdp")
    plength = PD * halfway
    heads = bias_table.shape[1]
    extra_rows = query_in.shape[1]
    prompt_base = own_rank % halfway * PD
    cont_index = own_rank // 2
    side = own_rank % 2

    own_links = lax.axis_size("grp") == 4 and devices == 8

    def gather(entry):
        return lax.all_gather(entry, "fsdp", axis=0, tiled=True)

    def quarters(entry):
        return entry.reshape(4, -1, entry.shape[1])

    n_keys = 2 * plength + 2 * CH
    shard = b_query.shape[0]
    up_size = b_up.shape[0]
    vectors = jnp.concatenate(
        [b_query, b_value, b_out, b_down, ln1_gain, ln1_bias, ln2_gain, ln2_bias, b_up]
    )
    qkv_shard = jnp.concatenate([w_query, w_key, w_value], axis=1)
    if own_links:
        vector_shard = jnp.pad(vectors, (0, 32 * 256 - vectors.shape[0])).reshape(4, 8, 256)
        qkv_weight, all_vectors, keys_x = gather_first(
            quarters(qkv_shard), vector_shard, content_in
        )
        qkv_weight = qkv_weight.reshape(-1, qkv_shard.shape[1])
        all_vectors = all_vectors.reshape(devices, -1)
        carried = tuple(quarters(shard) for shard in (w_up, w_down, w_out))
    else:
        qkv_weight, all_vectors = gather(qkv_shard), gather(vectors[None])
        up_weight, down_weight, out_weight = gather(w_up), gather(w_down), gather(w_out)
        carried = ()
        prompt_x = lax.all_gather(content_in[:, :PD], "fsdp", axis=1, tiled=True)
        near_x = from_partner(content_in[:, PD:], "fsdp").reshape(MICRO, 2, 1, 128, D)
        own_x = content_in[:, PD:].reshape(MICRO, 2, 1, 128, D)
        cont_x = jnp.concatenate([near_x, own_x], axis=2).reshape(MICRO, 2 * CH, D)
        keys_x = jnp.concatenate([prompt_x, cont_x], axis=1)
    keys_x = keys_x.reshape(MICRO * n_keys, D)
    query_weight, kv_weight = qkv_weight[:, :D], qkv_weight[:, D:]
    singles = [
        all_vectors[:, shard * i : shard * i + shard].reshape(-1).astype(jnp.float32)
        for i in range(8)
    ]
    (
        query_bias,
        value_bias,
        out_bias,
        down_bias,
        gain_one,
        shift_one,
        gain_two,
        shift_two,
    ) = singles
    up_bias = all_vectors[:, 8 * shard : 8 * shard + up_size].reshape(-1).astype(jnp.float32)

    prompt_map = cont_prompt[:, 0, :]
    prompt_ref = jnp.sum(
        jnp.where(
            jnp.arange(prompt_map.shape[1], dtype=jnp.int32)[None, :] == cont_index, prompt_map, 0
        ),
        axis=1,
    )
    meta = prompt_ref.astype(jnp.int32)
    order = jnp.pad(pred_order[:, 0, :], ((0, 0), (0, QP - extra_rows)), constant_values=-1)
    real = order >= 0
    in_prompt = order < PD
    position = jnp.where(
        in_prompt, prompt_base + order, plength + 2 * (order - PD) + side
    )
    limit_p = jnp.where(real & in_prompt, jnp.maximum(position, 1), -1)
    limit_c = jnp.where(real & ~in_prompt, position, -1)
    info = jnp.stack([position, limit_p, limit_c, order], axis=1)
    info = jnp.concatenate([info, info], axis=2)
    xrow = jnp.pad(info, ((0, 0), (0, 4), (0, 0))).astype(jnp.int32)
    xcol = jnp.swapaxes(xrow, 1, 2)
    dist = bias_table.astype(jnp.float32)[rel_bucket].T
    dist = dist - dist[:, LANES - 1 :]
    table = jnp.pad(dist.reshape(PAIRS, 2, LANES), ((0, 0), (0, 6), (0, 0)))

    tokens_x = content_in.reshape(MICRO * TD, D)
    extra_x = pad_rows(query_in)
    x_all = jnp.concatenate([tokens_x, extra_x])
    kv_bias = jnp.concatenate([jnp.zeros((D,), jnp.float32), value_bias])
    key_rows = (
        jnp.dot(keys_x, kv_weight, preferred_element_type=jnp.float32) + kv_bias
    ).astype(jnp.bfloat16)
    q_all = (
        jnp.dot(x_all, query_weight, preferred_element_type=jnp.float32) + query_bias
    ).astype(jnp.bfloat16)
    queries = q_all[: MICRO * TD]
    extra_q = q_all[MICRO * TD :]

    ctx_c, ctx_x, full_c, full_x, lse, *gathered = attend(
        meta, queries, extra_q, key_rows, table, xcol, carried
    )
    if own_links:
        up_weight, down_weight, out_weight = (
            entry.reshape(-1, entry.shape[2]) for entry in gathered
        )
    context = jnp.concatenate([ctx_c, ctx_x])
    first, normed_one, inverse_one = layer_norm(
        x_all.astype(jnp.float32)
        + jnp.dot(context, out_weight, preferred_element_type=jnp.float32)
        + out_bias,
        gain_one,
        shift_one,
    )
    first_b = first.astype(jnp.bfloat16)
    hidden = jnp.dot(first_b, up_weight, preferred_element_type=jnp.float32) + up_bias
    active = jax.nn.gelu(hidden, approximate=False).astype(jnp.bfloat16)
    final, normed_two, inverse_two = layer_norm(
        first + jnp.dot(active, down_weight, preferred_element_type=jnp.float32) + down_bias,
        gain_two,
        shift_two,
    )
    rows_c = MICRO * TD
    out_content = final[:rows_c].reshape(MICRO, TD, D)
    out_query = final[rows_c:].reshape(MICRO, QP, D)[:, :extra_rows]

    upstream = jnp.concatenate(
        [cot_content.reshape(rows_c, D), pad_rows(cot_query)]
    ).astype(jnp.float32)
    dres_two, dgain_two, dshift_two = norm_back(upstream, normed_two, inverse_two, gain_two)
    dbias_down = jnp.sum(dres_two, axis=0)
    dres_two_b = dres_two.astype(jnp.bfloat16)
    dweight_down = dot_tn(active, dres_two_b)
    dactive = dot_nt(dres_two_b, down_weight).astype(jnp.bfloat16)
    dhidden = (dactive.astype(jnp.float32) * gelu_slope(hidden)).astype(jnp.bfloat16)
    dbias_up = jnp.sum(dhidden.astype(jnp.float32), axis=0)
    dweight_up = dot_tn(first_b, dhidden)
    dfirst = dres_two + dot_nt(dhidden, up_weight)
    dres_one, dgain_one, dshift_one = norm_back(dfirst, normed_one, inverse_one, gain_one)
    dbias_out = jnp.sum(dres_one, axis=0)
    dres_one_b = dres_one.astype(jnp.bfloat16)
    dweight_out = dot_tn(context, dres_one_b)
    dcontext = dot_nt(dres_one_b, out_weight).astype(jnp.bfloat16)

    def by_quarter(grad):
        grad = grad.astype(jnp.bfloat16)
        return grad.reshape(4, 2, 4, grad.shape[0] // 32, grad.shape[1])

    to_reduce = ()
    if own_links:
        to_reduce = tuple(by_quarter(g) for g in (dweight_up, dweight_down, dweight_out))
    dq_c, dq_x, dk_rows, dv_rows, hist, *reduced = attend_back(
        meta,
        queries,
        extra_q,
        key_rows,
        table,
        xcol,
        xrow,
        lse,
        dcontext[:rows_c],
        dcontext[rows_c:],
        full_c,
        full_x,
        to_reduce,
    )
    dkv_rows = jnp.concatenate([dk_rows, dv_rows], axis=1)
    dq_all = jnp.concatenate([dq_c, dq_x])
    dweight_query = dot_tn(x_all, dq_all)
    dbias_query = jnp.sum(dq_all.astype(jnp.float32), axis=0)
    dweight_kv = dot_tn(keys_x, dkv_rows)
    dbias_value = jnp.sum(dv_rows.astype(jnp.float32), axis=0)
    dkeys_x = dot_nt(dkv_rows, kv_weight).reshape(MICRO, n_keys, D)
    dtable = table_gradient(hist, rel_bucket, bias_table.shape[0], side, heads)
    small = jnp.concatenate(
        [
            entry.reshape(devices, -1)
            for entry in (
                dbias_query,
                dbias_value,
                dbias_out,
                dbias_down,
                dgain_one,
                dshift_one,
                dgain_two,
                dshift_two,
                dbias_up,
                dtable,
            )
        ],
        axis=1,
    ).astype(jnp.bfloat16)
    dprompts = dkeys_x[:, : 2 * plength].astype(jnp.bfloat16)
    dcont = dkeys_x[:, 2 * plength :].reshape(MICRO, 2, 2, 128, D)
    dnear = dcont[:, :, 0].astype(jnp.bfloat16)
    dweight_qkv = jnp.concatenate(
        [dweight_query.astype(jnp.bfloat16), dweight_kv.astype(jnp.bfloat16)], axis=1
    )
    small_size = small.shape[1]
    if own_links:
        small = jnp.pad(small, ((0, 0), (0, 32 * 256 - small_size)))
        t_qkv, t_small, from_prompts, from_near = reduce_last(
            by_quarter(dweight_qkv),
            small.reshape(4, 2, 4, 8, 256),
            dprompts.reshape(MICRO, 4, 2, PD, D),
            dnear,
        )
        t_up, t_down, t_out = reduced
        shares = (t_down, t_up, t_out, t_qkv, t_small)
        totals = [
            entry.reshape(-1, entry.shape[-1]).astype(jnp.float32) for entry in shares
        ]
    else:

        def scatter(piece, dimension=0):
            return lax.psum_scatter(
                piece.astype(jnp.bfloat16), "fsdp", scatter_dimension=dimension, tiled=True
            )

        from_prompts = scatter(dprompts, 1).astype(jnp.float32)
        from_near = from_partner(dnear, "fsdp")
        shares = [
            scatter(piece)
            for piece in (dweight_down, dweight_up, dweight_out, dweight_qkv, small)
        ]
        totals = [lax.psum(entry, "grp").astype(jnp.float32) for entry in shares]
    dcont = (dcont[:, :, 1] + from_near.astype(jnp.float32)).reshape(MICRO, CH, D)
    dx_all = dres_one + dot_nt(dq_all, query_weight)
    grad_content = dx_all[:rows_c].reshape(MICRO, TD, D) + jnp.concatenate(
        [from_prompts, dcont], axis=1
    )
    grad_query = dx_all[rows_c:].reshape(MICRO, QP, D)[:, :extra_rows]
    t_down, t_up, t_out, t_qkv, t_small = totals
    t_small = t_small.reshape(-1)[:small_size]
    pieces = [t_small[shard * i : shard * i + shard] for i in range(8)]
    up_at = 8 * shard
    t_table = t_small[up_at + up_size :].reshape(-1, heads)
    return (
        out_content,
        out_query,
        grad_content,
        grad_query,
        t_qkv[:, :D],
        pieces[0],
        t_qkv[:, D : 2 * D],
        t_qkv[:, 2 * D :],
        pieces[1],
        t_out,
        pieces[2],
        pieces[4],
        pieces[5],
        t_up,
        t_small[up_at : up_at + up_size],
        t_down,
        pieces[3],
        pieces[6],
        pieces[7],
        t_table,
    )


def solution(mesh):
    rows = P(None, ("grp", "fsdp"), None)
    matrix = P("fsdp", None)
    vector = P("fsdp")
    in_specs = (
        rows,
        rows,
        rows,
        P(None, "grp", None),
        P(),
        matrix,
        vector,
        matrix,
        matrix,
        vector,
        matrix,
        vector,
        vector,
        vector,
        matrix,
        vector,
        matrix,
        vector,
        vector,
        vector,
        P(),
        rows,
        rows,
    )
    out_specs = (
        rows,
        rows,
        rows,
        rows,
        matrix,
        vector,
        matrix,
        matrix,
        vector,
        matrix,
        vector,
        vector,
        vector,
        matrix,
        vector,
        matrix,
        vector,
        vector,
        vector,
        matrix,
    )
    return jax.shard_map(
        on_device, mesh=mesh, in_specs=in_specs, out_specs=out_specs, check_vma=False
    )
```

```python
import functools

import jax
import jax.numpy as jnp
from jax import lax
from jax.experimental import pallas as pl
from jax.experimental.pallas import tpu as pltpu
from jax.sharding import PartitionSpec as P

D = 768
PD = 128
CH = 256
MICRO = 2
TD = 384
QP = 64
HD = 64
LANES = 128
PAIRS = D // LANES

PRECISE = lax.Precision.HIGHEST
MASKED = -1e30
VMEM_LIMIT = 56 * 1024 * 1024


def dot_nt(left, right):
    return lax.dot_general(
        left, right, (((1,), (1,)), ((), ())), preferred_element_type=jnp.float32
    )


def dot_tn(left, right):
    return lax.dot_general(
        left, right, (((0,), (0,)), ((), ())), preferred_element_type=jnp.float32
    )


def dot_nn(left, right):
    return jnp.dot(left, right, preferred_element_type=jnp.float32)


def head_stack(block):
    lane = lax.broadcasted_iota(jnp.int32, block.shape, 1)
    zero = jnp.zeros_like(block)
    return jnp.concatenate(
        [jnp.where(lane < HD, block, zero), jnp.where(lane < HD, zero, block)], axis=0
    )


def head_merge(stacked):
    rows = stacked.shape[0] // 2
    lane = lax.broadcasted_iota(jnp.int32, (rows, LANES), 1)
    return jnp.where(lane < HD, stacked[:rows], stacked[rows:])


def lookup(table, index):
    return jnp.take_along_axis(table, index, axis=1, mode="promise_in_bounds")


def near_index(distance):
    return jnp.clip(distance, 0, LANES - 1)


def fill_keys(scratch, rows_ref, own_prompt, mapped, plength):
    own_at = pl.multiple_of(own_prompt * plength, 128)
    scratch[0:plength] = rows_ref[pl.ds(own_at, plength), :]
    scratch[plength : 2 * plength] = jnp.where(
        mapped == 0, rows_ref[0:plength], rows_ref[plength : 2 * plength]
    )
    scratch[2 * plength :] = rows_ref[2 * plength :]


MESH = pl.DeviceIdType.MESH
ANY_SPEC = pl.BlockSpec(memory_space=pl.ANY)


class Net:
    def __init__(self):
        self.g = lax.axis_index("grp")
        self.f = lax.axis_index("fsdp")
        self.x = self.g % 2
        self.y = self.g // 2
        self.z = self.f // 2
        self.c = self.f % 2
        self.gx = self.g + 1 - 2 * self.x
        self.gy = self.g + 2 - 4 * self.y
        self.mate = self.f + 1 - 2 * self.c
        self.z_of = [
            self.z + 1 - 2 * (self.z % 2),
            (self.z + 2) % 4,
            3 - self.z,
        ]
        self.f_of = [2 * other + self.c for other in self.z_of]
        self.to_x = (self.gx, self.f)
        self.to_y = (self.gy, self.f)
        self.to_mate = (self.g, self.mate)
        self.to_z = [(self.g, other) for other in self.f_of]

    def greet(self):
        barrier = pltpu.get_barrier_semaphore()
        everyone = [self.to_x, self.to_y, self.to_mate] + self.to_z
        for device in everyone:
            pl.semaphore_signal(barrier, inc=1, device_id=device, device_id_type=MESH)
        pl.semaphore_wait(barrier, len(everyone))


class Copies:
    def __init__(self, sends, recvs):
        self.sends = sends
        self.recvs = recvs
        self.used = 0
        self.all = []

    def to(self, device, src, dst):
        copy = pltpu.make_async_remote_copy(
            src_ref=src,
            dst_ref=dst,
            send_sem=self.sends.at[self.used],
            recv_sem=self.recvs.at[self.used],
            device_id=device,
            device_id_type=MESH,
        )
        self.used += 1
        self.all.append(copy)
        return copy

    def finish(self):
        for copy in self.all:
            copy.wait_send()


def start(copies):
    for copy in copies:
        copy.start()


def arrive(copies):
    for copy in copies:
        copy.wait_recv()


GATHER_COPIES = 19


def gather_stages(net, copies, local_sem, shard, full):
    part, width = shard.shape[1:]
    half = width // 2

    def rows(owner, quarter):
        return 4 * owner + quarter

    def whole(owner):
        return pl.ds(4 * owner, 4)

    local = pltpu.make_async_copy(shard, full.at[whole(net.f)], local_sem)
    mine = shard.at[net.g]
    along_z = [copies.to(device, mine, full.at[rows(net.f, net.g)]) for device in net.to_z]
    to_mate = [copies.to(net.to_mate, shard, full.at[whole(net.f)])]
    to_x, to_y, on_x, on_y, later = [], [], [], [], []
    for owner in net.f_of:
        got = full.at[rows(owner, net.g)]
        to_x.append(copies.to(net.to_x, got, got))
        to_y.append(copies.to(net.to_y, got, got))
        left = full.at[rows(owner, net.gx), :, pl.ds(0, half)]
        on_y.append(copies.to(net.to_y, left, left))
        right = full.at[rows(owner, net.gy), :, pl.ds(half, half)]
        on_x.append(copies.to(net.to_x, right, right))
        shared = full.at[whole(owner)]
        later.append(copies.to(net.to_mate, shared, shared))

    def begin():
        local.start()
        start(along_z)
        start(to_mate)

    def plane():
        arrive(along_z)
        start(to_x + to_y)

    def corners():
        arrive(to_x + to_y)
        start(on_y + on_x)

    def mates():
        arrive(on_y + on_x)
        start(later)

    def end():
        arrive(to_mate + later)
        local.wait()
        for copy in along_z + to_mate + to_x + to_y + on_x + on_y + later:
            copy.wait_send()

    return [begin, plane, corners, mates, end]


REDUCE_COPIES = 19


def reduce_buffers(size, width):
    part, half = size // 4, width // 2
    return [
        pltpu.VMEM((4, 4, part, width), jnp.bfloat16),
        pltpu.VMEM((4, 4, part, width), jnp.bfloat16),
        pltpu.VMEM((4, 2, part, half), jnp.bfloat16),
        pltpu.VMEM((4, 2, part, half), jnp.bfloat16),
        pltpu.VMEM((2, 4, part, half), jnp.bfloat16),
        pltpu.VMEM((2, 3, part, half), jnp.bfloat16),
        pltpu.VMEM((2, 4, part, half), jnp.bfloat16),
        pltpu.SemaphoreType.DMA((2,)),
        pltpu.SemaphoreType.DMA((REDUCE_COPIES,)),
        pltpu.SemaphoreType.DMA((REDUCE_COPIES,)),
    ]


def reduce_stages(net, grad, share, buffers):
    own, other, side_a, side_b, line, along, done, local_sem, sends, recvs = buffers
    copies = Copies(sends, recvs)
    half = grad.shape[4] // 2
    left, right = pl.ds(0, half), pl.ds(half, half)
    load = pltpu.make_async_copy(grad.at[:, net.c], own, local_sem.at[0])
    to_mate = [copies.to(net.to_mate, grad.at[:, 1 - net.c], other)]
    first = []
    for i in range(2):
        first.append(
            copies.to(net.to_x, own.at[:, 2 * i + 1 - net.x, :, left], side_a.at[:, i])
        )
        first.append(
            copies.to(net.to_y, own.at[:, 2 - 2 * net.y + i, :, right], side_b.at[:, i])
        )
    second = [
        copies.to(net.to_y, side_a.at[:, 1 - net.y], line.at[0]),
        copies.to(net.to_x, side_b.at[:, 1 - net.x], line.at[1]),
    ]
    third = []
    for k in range(3):
        for h in range(2):
            third.append(
                copies.to(net.to_z[k], line.at[h, net.z_of[k]], along.at[h, k])
            )
    fourth = []
    fifth = []
    for h in range(2):
        fourth.append(copies.to(net.to_x, done.at[h, net.g], done.at[h, net.g]))
        fourth.append(copies.to(net.to_y, done.at[h, net.g], done.at[h, net.g]))
    fifth.append(copies.to(net.to_y, done.at[0, net.gx], done.at[0, net.gx]))
    fifth.append(copies.to(net.to_x, done.at[1, net.gy], done.at[1, net.gy]))
    store = [
        pltpu.make_async_copy(done.at[0], share.at[:, :, left], local_sem.at[0]),
        pltpu.make_async_copy(done.at[1], share.at[:, :, right], local_sem.at[1]),
    ]

    def begin():
        load.start()
        start(to_mate)

    def plane():
        load.wait()
        arrive(to_mate)

        @pl.loop(0, 16)
        def _(i):
            zi, qi = i // 4, i % 4
            own[zi, qi] = own[zi, qi] + other[zi, qi]

        start(first)

    def cross():
        arrive(first)

        @pl.loop(0, 8)
        def _(i):
            zi, qi = i // 2, i % 2
            side_a[zi, qi] = side_a[zi, qi] + own[zi, 2 * qi + net.x, :, 0:half]
            side_b[zi, qi] = side_b[zi, qi] + own[zi, 2 * net.y + qi, :, half : 2 * half]

        start(second)

    def column():
        arrive(second)

        @pl.loop(0, 4)
        def _(zi):
            line[0, zi] = line[0, zi] + side_a[zi, net.y]
            line[1, zi] = line[1, zi] + side_b[zi, net.x]

        start(third)

    def spread():
        arrive(third)

        @pl.loop(0, 2)
        def _(h):
            total = line[h, net.z].astype(jnp.float32)
            for k in range(3):
                total = total + along[h, k].astype(jnp.float32)
            done[h, net.g] = total.astype(jnp.bfloat16)

        start(fourth)

    def corners():
        arrive(fourth)
        start(fifth)

    def end():
        arrive(fifth)
        start(store)
        for copy in store:
            copy.wait()
        copies.finish()

    return [begin, plane, cross, column, spread, corners, end]


def gather_first_kernel(
    w_ref, v_ref, x_ref, w_full, v_full, keys_x, w_s, w_r, v_s, v_r, x_s, x_r, local_sem
):
    net = Net()
    net.greet()
    weights = gather_stages(net, Copies(w_s, w_r), local_sem.at[0], w_ref, w_full)
    vectors = gather_stages(net, Copies(v_s, v_r), local_sem.at[1], v_ref, v_full)
    plength = PD * 4
    at = 2 * plength

    def block(owner):
        return pl.ds(pl.multiple_of(owner * PD, 128), PD)

    prompt = x_ref.at[:, pl.ds(0, PD)]
    cont = [x_ref.at[:, pl.ds(PD + 128 * i, 128)] for i in range(2)]
    near = [keys_x.at[:, pl.ds(at + 256 * i, 128)] for i in range(2)]
    here = [keys_x.at[:, pl.ds(at + 256 * i + 128, 128)] for i in range(2)]
    copies = Copies(x_s, x_r)
    local = [pltpu.make_async_copy(prompt, keys_x.at[:, block(net.f)], local_sem.at[2])]
    local += [
        pltpu.make_async_copy(cont[i], here[i], local_sem.at[3 + i]) for i in range(2)
    ]
    to_mate = [copies.to(net.to_mate, prompt, keys_x.at[:, block(net.f)])]
    to_mate += [copies.to(net.to_mate, cont[i], near[i]) for i in range(2)]
    along_z = [copies.to(device, prompt, keys_x.at[:, block(net.f)]) for device in net.to_z]
    later = [
        copies.to(net.to_mate, keys_x.at[:, block(owner)], keys_x.at[:, block(owner)])
        for owner in net.f_of
    ]
    weights[0]()
    vectors[0]()
    start(local)
    start(to_mate)
    weights[1]()
    start(along_z)
    vectors[1]()
    weights[2]()
    vectors[2]()
    weights[3]()
    vectors[3]()
    arrive(along_z)
    start(later)
    weights[4]()
    vectors[4]()
    arrive(to_mate + later)
    for copy in local:
        copy.wait()
    copies.finish()


def gather_first(w_shard, v_shard, content_in):
    def sems(count):
        return [pltpu.SemaphoreType.DMA((count,))] * 2

    return pl.pallas_call(
        gather_first_kernel,
        name="gather_first",
        in_specs=[ANY_SPEC] * 3,
        out_specs=[ANY_SPEC] * 3,
        out_shape=[
            jax.ShapeDtypeStruct((8 * 4,) + w_shard.shape[1:], jnp.bfloat16),
            jax.ShapeDtypeStruct((8 * 4,) + v_shard.shape[1:], jnp.bfloat16),
            jax.ShapeDtypeStruct((MICRO, 8 * PD + 2 * CH, D), jnp.bfloat16),
        ],
        scratch_shapes=sems(GATHER_COPIES)
        + sems(GATHER_COPIES)
        + sems(9)
        + [pltpu.SemaphoreType.DMA((5,))],
        compiler_params=pltpu.CompilerParams(collective_id=1, has_side_effects=True),
    )(w_shard, v_shard, content_in)


def hosted(plan, step):
    for at, stage in plan:

        @pl.when(step == at)
        def _():
            stage()


def place(plength):
    rank = lax.axis_index("fsdp")
    halfway = plength // PD
    return rank // halfway, rank % halfway * PD, rank % 2


def attend_kernel(plength, carried, *refs):
    (meta, qc, qx, k_rows, v_rows, table, xcol), refs = refs[:7], refs[7:]
    shards, refs = refs[:carried], refs[carried:]
    (ctx_c, ctx_x, full_c, full_x, lse_ref), refs = refs[:5], refs[5:]
    fulls, refs = refs[:carried], refs[carried:]
    keys, vals, scores, probs = refs[:4]
    step = pl.program_id(0) * PAIRS + pl.program_id(1)
    stages = []
    if carried:
        net = Net()
        for i in range(carried):
            sends, recvs = refs[4 + 2 * i : 6 + 2 * i]
            stages.append(
                gather_stages(
                    net, Copies(sends, recvs), refs[-1].at[i], shards[i], fulls[i]
                )
            )
        up, down, proj = stages
        hosted([(0, net.greet)], step)
        hosted(
            [
                (0, up[0]),
                (3, up[1]),
                (3, down[0]),
                (6, up[2]),
                (7, down[1]),
                (7, proj[0]),
                (8, up[3]),
                (8, proj[1]),
                (10, down[2]),
                (10, proj[2]),
            ],
            step,
        )
    own_prompt, base, side = place(plength)
    mapped = meta[pl.program_id(0)]
    blocks = plength // 128
    fill_keys(keys, k_rows, own_prompt, mapped, plength)
    fill_keys(vals, v_rows, own_prompt, mapped, plength)
    row = lax.broadcasted_iota(jnp.int32, (128, 128), 0)
    col = lax.broadcasted_iota(jnp.int32, (128, 128), 1)
    tab_a = jnp.broadcast_to(table[0, 0:1, :], (128, 128))
    tab_b = jnp.broadcast_to(table[0, 1:2, :], (128, 128))
    tab_x = jnp.where(row < QP, tab_a, tab_b)
    lse_ref[...] = jnp.zeros_like(lse_ref)

    def solve(stack, first, plan, tables, lse_rows):
        count = len(plan)
        span = slice(first, first + 128 * count)
        halves = len(tables)
        width = 128 * count
        scores[0 : 128 * halves, 0:width] = dot_nt(stack, keys[span])
        for half in range(halves):
            rows = slice(128 * half, 128 * half + 128)
            peak = None
            for at, (index, visible) in enumerate(plan):
                cols = slice(128 * at, 128 * at + 128)
                s = scores[rows, cols]
                if index is not None:
                    s = s + lookup(tables[half], index)
                if visible is not None:
                    s = jnp.where(visible, s, MASKED)
                if index is not None or visible is not None:
                    scores[rows, cols] = s
                peak = s if peak is None else jnp.maximum(peak, s)
            top = jnp.max(peak, axis=1, keepdims=True)
            total = None
            for at in range(count):
                cols = slice(128 * at, 128 * at + 128)
                p = jnp.exp(scores[rows, cols] - top)
                total = p if total is None else total + p
                probs[rows, cols] = p.astype(jnp.bfloat16)
            total = jnp.sum(total, axis=1, keepdims=True)
            log_total = top + jnp.log(total)
            lse_ref[0, 0, lse_rows[half] : lse_rows[half] + 1, :] = jnp.transpose(
                jnp.broadcast_to(log_total, (128, 128))
            )[0:1, :]
            scores[rows, 0:128] = jnp.broadcast_to(1.0 / total, (128, 128))
        out = dot_nn(probs[0 : 128 * halves, 0:width], vals[span])
        return out * scores[0 : 128 * halves, 0:128]

    scale = jnp.asarray(0.125, jnp.bfloat16)
    q_p = head_stack(qc[0:PD] * scale)
    q_0 = head_stack(qc[PD : PD + 128] * scale)
    q_1 = head_stack(qc[PD + 128 : PD + 256] * scale)
    q_x = head_stack(qx[...] * scale)

    plan_p = []
    for b in range(blocks):
        d = base + row - (col + 128 * b)
        plan_p.append((near_index(d), d >= 0))
    out = head_merge(solve(q_p, 0, plan_p, (tab_a, tab_b), (0, 3)))
    ctx_c[0:PD] = out.astype(jnp.bfloat16)
    full_c[0:PD] = out

    far = (None, None)
    last = 128 + 2 * row + side - col
    near_d = 2 * (row - col) + 2 * side - 1
    own_d = 2 * (row - col)
    plan_0 = [far] * (blocks - 1) + [
        (near_index(last), None),
        (near_index(near_d), near_d >= 0),
        (near_index(own_d), own_d >= 0),
    ]
    out = head_merge(solve(q_0, plength, plan_0, (tab_a, tab_b), (1, 4)))
    ctx_c[PD : PD + 128] = out.astype(jnp.bfloat16)
    full_c[PD : PD + 128] = out
    plan_1 = [far] * blocks + [
        (near_index(near_d + 256), None),
        (near_index(own_d + 256), None),
        (near_index(near_d), near_d >= 0),
        (near_index(own_d), own_d >= 0),
    ]
    out = head_merge(solve(q_1, plength, plan_1, (tab_a, tab_b), (2, 5)))
    ctx_c[PD + 128 : PD + 256] = out.astype(jnp.bfloat16)
    full_c[PD + 128 : PD + 256] = out

    pos = jnp.broadcast_to(xcol[0, :, 0:1], (128, 128))
    lim_p = jnp.broadcast_to(xcol[0, :, 1:2], (128, 128))
    lim_c = jnp.broadcast_to(xcol[0, :, 2:3], (128, 128))
    plan_x = []
    for b in range(blocks):
        key = col + 128 * b
        plan_x.append((near_index(pos - key), key < lim_p))
    in_cont = lim_c > 0
    for b in range(blocks - 1):
        plan_x.append((None, in_cont))
    key = col + 128 * (blocks - 1)
    plan_x.append((near_index(pos - key), in_cont))
    for b in range(2):
        for offset in (1 - side, side):
            key = plength + 2 * (col + 128 * b) + offset
            plan_x.append((near_index(pos - key), key < lim_c))
    out = solve(q_x, 0, plan_x, (tab_x,), (6,))
    lane = lax.broadcasted_iota(jnp.int32, (QP, LANES), 1)
    out = jnp.where(lane < HD, out[0:QP], out[QP:])
    ctx_x[...] = out.astype(jnp.bfloat16)
    full_x[...] = out
    if carried:
        hosted([(11, s) for s in (down[3], proj[3], up[4], down[4], proj[4])], step)


def pair_column(shift):
    return lambda m, j, meta: (m, shift * PAIRS + j)


def key_spec(n_keys, shift):
    return pl.BlockSpec((n_keys, LANES), lambda m, j, meta: (m, shift * PAIRS + j))


TABLE_SPEC = pl.BlockSpec((1, 8, LANES), lambda m, j, meta: (j, 0, 0))


def host_params(collective_id, carried):
    if carried:
        return pltpu.CompilerParams(
            vmem_limit_bytes=VMEM_LIMIT, collective_id=collective_id, has_side_effects=True
        )
    return pltpu.CompilerParams(vmem_limit_bytes=VMEM_LIMIT)


def attend(meta, queries, extra_q, key_rows, table, xcol, shards):
    carried = len(shards)
    n_keys = key_rows.shape[0] // MICRO
    plength = (n_keys - 2 * CH) // 2
    content = pl.BlockSpec((TD, LANES), pair_column(0))
    extra = pl.BlockSpec((QP, LANES), pair_column(0))
    own_row = plength + 2 * CH
    pairs = MICRO * PAIRS * 2 * (128 * plength + 256 * own_row) + MICRO * PAIRS * 128 * n_keys
    return pl.pallas_call(
        functools.partial(attend_kernel, plength, carried),
        name="attend",
        grid_spec=pltpu.PrefetchScalarGridSpec(
            num_scalar_prefetch=1,
            grid=(MICRO, PAIRS),
            in_specs=[content, extra]
            + [
                key_spec(n_keys, 0),
                key_spec(n_keys, 1),
                TABLE_SPEC,
                pl.BlockSpec((1, 128, 8), lambda m, j, meta: (m, 0, 0)),
            ]
            + [ANY_SPEC] * carried,
            out_specs=[
                content,
                extra,
                content,
                extra,
                pl.BlockSpec((1, 1, 8, LANES), lambda m, j, meta: (m, j, 0, 0)),
            ]
            + [ANY_SPEC] * carried,
            scratch_shapes=[
                pltpu.VMEM((n_keys, LANES), jnp.bfloat16),
                pltpu.VMEM((n_keys, LANES), jnp.bfloat16),
                pltpu.VMEM((256, n_keys), jnp.float32),
                pltpu.VMEM((256, n_keys), jnp.bfloat16),
            ]
            + [pltpu.SemaphoreType.DMA((GATHER_COPIES,))] * (2 * carried)
            + [pltpu.SemaphoreType.DMA((4,))],
        ),
        out_shape=[
            jax.ShapeDtypeStruct((MICRO * TD, D), jnp.bfloat16),
            jax.ShapeDtypeStruct((MICRO * QP, D), jnp.bfloat16),
            jax.ShapeDtypeStruct((MICRO * TD, D), jnp.float32),
            jax.ShapeDtypeStruct((MICRO * QP, D), jnp.float32),
            jax.ShapeDtypeStruct((MICRO, PAIRS, 8, LANES), jnp.float32),
        ]
        + [
            jax.ShapeDtypeStruct((8 * 4,) + shard.shape[1:], shard.dtype)
            for shard in shards
        ],
        compiler_params=host_params(2, carried),
        cost_estimate=pl.CostEstimate(
            flops=4 * pairs * LANES, bytes_accessed=16 * 1024 * 1024, transcendentals=pairs
        ),
    )(
        meta,
        queries,
        extra_q,
        key_rows,
        key_rows,
        table,
        xcol,
        *shards,
    )


def attend_back_kernel(plength, carried, *refs):
    (meta, qc, qx, k_rows, v_rows, table, xcol, xrow, lse_ref, dc, dx, full_c, full_x), refs = (
        refs[:13],
        refs[13:],
    )
    grads, refs = refs[:carried], refs[carried:]
    (dq_c, dq_x, dk_rows, dv_rows, hist), refs = refs[:5], refs[5:]
    shares, refs = refs[:carried], refs[carried:]
    keys, vals, q_all, d_all, scores, dprobs, probs_t, dscores_t, ds_p, dk_acc, dv_acc = refs[:11]
    refs = refs[11:]
    step = pl.program_id(0) * PAIRS + pl.program_id(1)
    if carried:
        net = Net()
        up, down, proj = (
            reduce_stages(net, grads[i], shares[i], refs[10 * i : 10 * i + 10])
            for i in range(carried)
        )
        hosted([(0, net.greet)], step)
        hosted(
            [
                (0, up[0]),
                (0, down[0]),
                (0, proj[0]),
                (1, up[1]),
                (4, up[2]),
                (4, down[1]),
                (6, up[3]),
                (7, down[2]),
                (7, proj[1]),
                (9, down[3]),
                (9, proj[2]),
                (9, up[4]),
                (10, proj[3]),
                (10, up[5]),
            ],
            step,
        )
    own_prompt, base, side = place(plength)
    mapped = meta[pl.program_id(0)]
    blocks = plength // 128
    at_k1 = 2 * plength + 256
    n_keys = 2 * plength + 512
    fill_keys(keys, k_rows, own_prompt, mapped, plength)
    fill_keys(vals, v_rows, own_prompt, mapped, plength)
    row = lax.broadcasted_iota(jnp.int32, (128, 128), 0)
    col = lax.broadcasted_iota(jnp.int32, (128, 128), 1)
    tab_a = jnp.broadcast_to(table[0, 0:1, :], (128, 128))
    tab_b = jnp.broadcast_to(table[0, 1:2, :], (128, 128))
    scale = jnp.asarray(0.125, jnp.bfloat16)

    p_at, x_at, c1_at, c0_at = 0, 256, 384, 640
    q_all[0:256] = head_stack(qc[0:PD] * scale)
    q_all[256:384] = head_stack(qx[...] * scale)
    q_all[384:640] = head_stack(qc[PD + 128 : PD + 256] * scale)
    q_all[640:896] = head_stack(qc[PD : PD + 128] * scale)
    d_all[0:256] = head_stack(dc[0:PD])
    d_all[256:384] = head_stack(dx[...])
    d_all[384:640] = head_stack(dc[PD + 128 : PD + 256])
    d_all[640:896] = head_stack(dc[PD : PD + 128])

    ones_lane = lax.broadcasted_iota(jnp.int32, (8, LANES), 1)
    ones_row = lax.broadcasted_iota(jnp.int32, (8, LANES), 0)
    pick = jnp.where((ones_lane < HD) == (ones_row == 0), 1.0, 0.0)
    pick = jnp.where(ones_row < 2, pick, 0.0)

    def deltas(upstream, context):
        product = upstream.astype(jnp.float32) * context
        return lax.dot_general(
            pick,
            product,
            (((1,), (1,)), ((), ())),
            precision=PRECISE,
            preferred_element_type=jnp.float32,
        )

    delta_p = deltas(dc[0:PD], full_c[0:PD])
    delta_0 = deltas(dc[PD : PD + 128], full_c[PD : PD + 128])
    delta_1 = deltas(dc[PD + 128 : PD + 256], full_c[PD + 128 : PD + 256])
    delta_x = deltas(dx[...], full_x[...])
    delta_x = jnp.concatenate([delta_x[0:1], delta_x[1:2]], axis=1)

    def block_back(first, plan, at_col, halves):
        count = len(plan)
        width = 128 * len(halves)
        span = slice(first, first + 128 * count)
        cols = slice(at_col, at_col + width)
        scores[0 : 128 * count, 0:width] = dot_nt(keys[span], q_all[cols])
        dprobs[0 : 128 * count, 0:width] = dot_nt(vals[span], d_all[cols])
        for half, (tables, lse_row, delta) in enumerate(halves):
            lane = slice(128 * half, 128 * half + 128)
            out_lane = slice(at_col + 128 * half, at_col + 128 * half + 128)
            lse = lse_ref[0, 0, lse_row : lse_row + 1, :]
            for at, (index, visible) in enumerate(plan):
                rows = slice(128 * at, 128 * at + 128)
                out_rows = slice(first + 128 * at, first + 128 * at + 128)
                s = scores[rows, lane]
                if index is not None:
                    bias = lookup(tables[0], index)
                    if len(tables) > 1:
                        bias = jnp.where(col < QP, bias, lookup(tables[1], index))
                    s = s + bias
                if visible is not None:
                    s = jnp.where(visible, s, MASKED)
                p = jnp.exp(s - lse)
                ds = p * (dprobs[rows, lane] - delta)
                probs_t[out_rows, out_lane] = p.astype(jnp.bfloat16)
                dscores_t[out_rows, out_lane] = ds.astype(jnp.bfloat16)
                yield half, at, ds

    extra_a = jnp.where(
        (xcol[0, :, 3:4] == lax.broadcasted_iota(jnp.int32, (128, TD), 1))
        & (lax.broadcasted_iota(jnp.int32, (128, TD), 0) < QP),
        1.0,
        0.0,
    ).astype(jnp.bfloat16)
    extra_b = jnp.where(
        (xcol[0, :, 3:4] == lax.broadcasted_iota(jnp.int32, (128, TD), 1))
        & (lax.broadcasted_iota(jnp.int32, (128, TD), 0) >= QP),
        1.0,
        0.0,
    ).astype(jnp.bfloat16)
    spread = (extra_a, extra_b)

    pos = xrow[0, 0:1, :]
    lim_p = xrow[0, 1:2, :]
    lim_c = xrow[0, 2:3, :]
    plan = []
    for b in range(blocks):
        key = row + 128 * b
        plan.append((near_index(pos - key), key < lim_p))
    in_cont = jnp.broadcast_to(lim_c > 0, (128, 128))
    for b in range(blocks - 1):
        plan.append((None, in_cont))
    plan.append((near_index(pos - (row + 128 * (blocks - 1))), in_cont))
    for b in range(2):
        for offset in (1 - side, side):
            key = plength + 2 * (row + 128 * b) + offset
            plan.append((near_index(pos - key), key < lim_c))
    for _ in block_back(0, plan, x_at, [((tab_a, tab_b), 6, delta_x)]):
        pass

    def spread_block(head, key_at, content_at):
        return dot_nn(
            dscores_t[pl.ds(key_at, 128), x_at : x_at + 128],
            spread[head][:, content_at : content_at + 128],
        )

    turn = (col + row) % 128
    turn_half = (col + row // 2) % 128

    def fold(block):
        return jnp.sum(block.reshape(16, 8, LANES), axis=0)

    plan = []
    for b in range(blocks):
        d = base + col - (row + 128 * b)
        plan.append((near_index(d), d >= 0))
    halves = [((tab_a,), 0, delta_p[0:1]), ((tab_b,), 3, delta_p[1:2])]
    for half, at, ds in block_back(0, plan, p_at, halves):
        ds_p[128 * at : 128 * at + 128, 128 * half : 128 * half + 128] = ds
    before = jnp.maximum(base - 128, 0)
    base_at = pl.multiple_of(base, 128)
    before_at = pl.multiple_of(before, 128)
    for head in range(2):
        lane = slice(128 * head, 128 * head + 128)
        here = ds_p[pl.ds(base_at, 128), lane] + spread_block(head, base_at, 0)
        prior = ds_p[pl.ds(before_at, 128), lane] + spread_block(head, before_at, 0)
        prior = jnp.where(base > 0, prior, 0.0)
        both = jnp.where(col >= row, here, prior)
        hist[0, 0, 32 * head : 32 * head + 8] = fold(lookup(both, turn))

    last = 128 + 2 * col + side - row
    near_d = 2 * (col - row) + 2 * side - 1
    own_d = 2 * (col - row)
    far = (None, None)
    plan_0 = [far] * (blocks - 1) + [
        (near_index(last), None),
        (near_index(near_d), near_d >= 0),
        (near_index(own_d), own_d >= 0),
    ]
    plan_1 = [far] * blocks + [
        (near_index(near_d + 256), None),
        (near_index(own_d + 256), None),
        (near_index(near_d), near_d >= 0),
        (near_index(own_d), own_d >= 0),
    ]
    halves = [((tab_a,), 1, delta_0[0:1]), ((tab_b,), 4, delta_0[1:2])]
    near_sum = {}
    own_sum = {}
    last_key = 2 * plength - 128
    for half, at, ds in block_back(plength, plan_0, c0_at, halves):
        if at == blocks - 1:
            ds = ds + spread_block(half, last_key, PD)
            ds = jnp.where(col < 64, ds, 0.0)
            hist[0, 0, 32 * half + 8 : 32 * half + 16] = fold(lookup(ds, turn_half))
        if at == blocks:
            ds = ds + spread_block(half, 2 * plength, PD)
            near_sum[half] = jnp.where(col >= row, ds, 0.0)
        if at == blocks + 1:
            ds = ds + spread_block(half, 2 * plength + 128, PD)
            own_sum[half] = jnp.where(col >= row, ds, 0.0)
    for half in range(2):
        lane = slice(128 * half, 128 * half + 128)
        ds_p[0:128, lane] = near_sum[half]
        ds_p[128:256, lane] = own_sum[half]
    halves = [((tab_a,), 2, delta_1[0:1]), ((tab_b,), 5, delta_1[1:2])]
    for half, at, ds in block_back(plength, plan_1, c1_at, halves):
        lane = slice(128 * half, 128 * half + 128)
        if at == blocks:
            ds = ds + spread_block(half, 2 * plength, PD + 128)
            ds_p[0:128, lane] = ds_p[0:128, lane] + jnp.where(col < row, ds, 0.0)
        if at == blocks + 1:
            ds = ds + spread_block(half, 2 * plength + 128, PD + 128)
            ds_p[128:256, lane] = ds_p[128:256, lane] + jnp.where(col < row, ds, 0.0)
        if at == blocks + 2:
            ds = ds + spread_block(half, at_k1, PD + 128)
            ds = ds_p[0:128, lane] + jnp.where(col >= row, ds, 0.0)
            hist[0, 0, 32 * half + 16 : 32 * half + 24] = fold(lookup(ds, turn))
        if at == blocks + 3:
            ds = ds + spread_block(half, at_k1 + 128, PD + 128)
            ds = ds_p[128:256, lane] + jnp.where(col >= row, ds, 0.0)
            hist[0, 0, 32 * half + 24 : 32 * half + 32] = fold(lookup(ds, turn))

    own = slice(0, plength)
    middle = slice(plength, at_k1)
    end = slice(at_k1, n_keys)
    for acc, left, right in ((dk_acc, dscores_t, q_all), (dv_acc, probs_t, d_all)):
        acc[own] = dot_nn(left[own, 0:384], right[0:384])
        acc[middle] = dot_nn(left[middle, 256:896], right[256:896])
        acc[end] = dot_nn(left[end, 256:640], right[256:640])

    dq_c[0:PD] = (
        head_merge(dot_tn(dscores_t[own, p_at : p_at + 256], keys[own])) * 0.125
    ).astype(jnp.bfloat16)
    dq_c[PD : PD + 128] = (
        head_merge(dot_tn(dscores_t[middle, c0_at : c0_at + 256], keys[middle])) * 0.125
    ).astype(jnp.bfloat16)
    cont = slice(plength, n_keys)
    dq_c[PD + 128 : PD + 256] = (
        head_merge(dot_tn(dscores_t[cont, c1_at : c1_at + 256], keys[cont])) * 0.125
    ).astype(jnp.bfloat16)
    out = dot_tn(dscores_t[:, x_at : x_at + 128], keys[...])
    lane = lax.broadcasted_iota(jnp.int32, (QP, LANES), 1)
    dq_x[...] = (jnp.where(lane < HD, out[0:QP], out[QP:]) * 0.125).astype(jnp.bfloat16)

    for out_ref, acc in ((dk_rows, dk_acc), (dv_rows, dv_acc)):
        for p in range(2):
            mine = jnp.where(own_prompt == p, acc[own], 0.0)
            other = jnp.where(mapped == p, acc[plength : 2 * plength], 0.0)
            out_ref[p * plength : (p + 1) * plength] = (mine + other).astype(jnp.bfloat16)
        out_ref[2 * plength :] = acc[2 * plength :].astype(jnp.bfloat16)
    if carried:
        rest = (down[4], proj[4], up[6], down[5], proj[5], down[6], proj[6])
        hosted([(11, s) for s in rest], step)


def attend_back(meta, queries, extra_q, key_rows, table, xcol, xrow, lse, dc, dx, fc, fx, grads):
    carried = len(grads)
    n_keys = key_rows.shape[0] // MICRO
    plength = (n_keys - 2 * CH) // 2
    content = pl.BlockSpec((TD, LANES), pair_column(0))
    extra = pl.BlockSpec((QP, LANES), pair_column(0))
    own_row = plength + 2 * CH
    pairs = MICRO * PAIRS * 2 * (128 * plength + 256 * own_row) + MICRO * PAIRS * 128 * n_keys
    return pl.pallas_call(
        functools.partial(attend_back_kernel, plength, carried),
        name="attend_back",
        grid_spec=pltpu.PrefetchScalarGridSpec(
            num_scalar_prefetch=1,
            grid=(MICRO, PAIRS),
            in_specs=[content, extra]
            + [
                key_spec(n_keys, 0),
                key_spec(n_keys, 1),
                TABLE_SPEC,
                pl.BlockSpec((1, 128, 8), lambda m, j, meta: (m, 0, 0)),
                pl.BlockSpec((1, 8, 128), lambda m, j, meta: (m, 0, 0)),
                pl.BlockSpec((1, 1, 8, LANES), lambda m, j, meta: (m, j, 0, 0)),
                content,
                extra,
                content,
                extra,
            ]
            + [ANY_SPEC] * carried,
            out_specs=[
                content,
                extra,
                key_spec(n_keys, 0),
                key_spec(n_keys, 0),
                pl.BlockSpec((1, 1, 64, LANES), lambda m, j, meta: (m, j, 0, 0)),
            ]
            + [ANY_SPEC] * carried,
            scratch_shapes=[
                pltpu.VMEM((n_keys, LANES), jnp.bfloat16),
                pltpu.VMEM((n_keys, LANES), jnp.bfloat16),
                pltpu.VMEM((896, LANES), jnp.bfloat16),
                pltpu.VMEM((896, LANES), jnp.bfloat16),
                pltpu.VMEM((n_keys, 256), jnp.float32),
                pltpu.VMEM((n_keys, 256), jnp.float32),
                pltpu.VMEM((n_keys, 896), jnp.bfloat16),
                pltpu.VMEM((n_keys, 896), jnp.bfloat16),
                pltpu.VMEM((plength, 256), jnp.float32),
                pltpu.VMEM((n_keys, LANES), jnp.float32),
                pltpu.VMEM((n_keys, LANES), jnp.float32),
            ]
            + [
                buffer
                for grad in grads
                for buffer in reduce_buffers(4 * grad.shape[3], grad.shape[4])
            ],
        ),
        out_shape=[
            jax.ShapeDtypeStruct((MICRO * TD, D), jnp.bfloat16),
            jax.ShapeDtypeStruct((MICRO * QP, D), jnp.bfloat16),
            jax.ShapeDtypeStruct((MICRO * n_keys, D), jnp.bfloat16),
            jax.ShapeDtypeStruct((MICRO * n_keys, D), jnp.bfloat16),
            jax.ShapeDtypeStruct((MICRO, PAIRS, 64, LANES), jnp.float32),
        ]
        + [jax.ShapeDtypeStruct(grad.shape[2:], grad.dtype) for grad in grads],
        compiler_params=host_params(3, carried),
        cost_estimate=pl.CostEstimate(
            flops=10 * pairs * LANES, bytes_accessed=32 * 1024 * 1024, transcendentals=pairs
        ),
    )(
        meta,
        queries,
        extra_q,
        key_rows,
        key_rows,
        table,
        xcol,
        xrow,
        lse,
        dc,
        dx,
        fc,
        fx,
        *grads,
    )


def from_partner(block, axis):
    count = lax.axis_size(axis)
    return lax.ppermute(block, axis, [(i, i ^ 1) for i in range(count)])


TAIL_RATE = 0.24
TAIL = (
    0.08952757299725976,
    0.1555125511021828,
    -0.15404562880205064,
    0.6255850035411683,
    -0.6460658211054147,
    0.554571568104313,
    -0.12508524614530675,
)


def gelu_parts(hidden):
    bell = jnp.exp(-0.5 * hidden * hidden)
    t = 1.0 / (1.0 + TAIL_RATE * jnp.abs(hidden))
    poly = TAIL[-1]
    for term in TAIL[-2::-1]:
        poly = poly * t + term
    tail = poly * t * bell
    cdf = jnp.where(hidden < 0.0, tail, 1.0 - tail)
    return hidden * cdf, cdf + hidden * bell * 0.3989422804014327


TILE = 448
GRAD_STEPS = 9


def fold_rows(term):
    return jnp.sum(term.reshape(-1, 8, term.shape[1]), axis=0)


def middle_kernel(
    x,
    ctx,
    cot,
    w_out,
    w_up_ref,
    w_down_ref,
    vec,
    up_bias,
    out_c,
    out_x,
    dres,
    dctx_c,
    dctx_x,
    g_down,
    g_up,
    g_out,
    sums_out,
    act,
    dhid,
    slope,
    first_b,
    dres_two_b,
    dres_one_b,
    norm_one,
    inverse_one,
    work,
    outs,
    dctx,
    sums,
    sems,
    w_up,
    w_down,
    load_sems,
):
    step = pl.program_id(0)
    load_up = pltpu.make_async_copy(w_up_ref, w_up, load_sems.at[0])
    load_down = pltpu.make_async_copy(w_down_ref, w_down, load_sems.at[1])
    width = w_up.shape[1]
    rows_c = out_c.shape[0]
    tiles = x.shape[0] // TILE
    out_bias, gain_one, shift_one = vec[0:1], vec[1:2], vec[2:3]
    down_bias, gain_two, shift_two = vec[3:4], vec[4:5], vec[5:6]
    split = rows_c - TILE
    moves = [
        [
            (outs.at[pl.ds(0, TILE)], out_c.at[pl.ds(0, TILE)]),
            (dctx.at[pl.ds(0, TILE)], dctx_c.at[pl.ds(0, TILE)]),
        ],
        [
            (outs.at[pl.ds(TILE, split)], out_c.at[pl.ds(TILE, split)]),
            (dctx.at[pl.ds(TILE, split)], dctx_c.at[pl.ds(TILE, split)]),
            (outs.at[pl.ds(rows_c, 2 * QP)], out_x),
            (dctx.at[pl.ds(rows_c, 2 * QP)], dctx_x),
        ],
    ]
    count = 0
    for group in moves:
        for i, (src, dst) in enumerate(group):
            group[i] = pltpu.make_async_copy(src, dst, sems.at[count])
            count += 1

    def mean(value):
        return jnp.mean(value, axis=-1, keepdims=True)

    @pl.when(step == 0)
    def _():
        load_up.start()
        load_down.start()
        sums[...] = jnp.zeros_like(sums)

    @pl.when(step < tiles)
    def _():
        base = pl.multiple_of(step * TILE, 64)
        rows = pl.ds(base, TILE)
        work[...] = dot_nn(ctx[rows], w_out[...])

        value = x[rows].astype(jnp.float32) + work[...] + out_bias
        centred = value - mean(value)
        inverse = lax.rsqrt(mean(centred * centred) + 1e-05)
        normed = centred * inverse
        norm_one[...] = normed
        inverse_one[...] = jnp.broadcast_to(inverse, (TILE, LANES))
        first_b[rows] = (normed * gain_one + shift_one).astype(jnp.bfloat16)

        @pl.when(step == 0)
        def _():
            load_up.wait()

        parts = 12
        block = width // parts

        def lift(c):
            cols = slice(block * c, block * c + block)
            slope[:, cols] = dot_nn(first_b[rows], w_up[:, cols])

        lift(0)
        for c in range(parts):
            cols = slice(block * c, block * c + block)
            if c + 1 < parts:
                lift(c + 1)
            active, gradient = gelu_parts(slope[:, cols] + up_bias[0:1, cols])
            act[rows, cols] = active.astype(jnp.bfloat16)
            slope[:, cols] = gradient

        @pl.when(step == 0)
        def _():
            load_down.wait()

        work[...] = dot_nn(act[rows], w_down[...])

        value = norm_one[...] * gain_one + shift_one + work[...] + down_bias
        centred = value - mean(value)
        inverse = lax.rsqrt(mean(centred * centred) + 1e-05)
        normed = centred * inverse
        outs[rows] = normed * gain_two + shift_two
        upstream = cot[rows].astype(jnp.float32)
        scaled = upstream * gain_two
        grad = inverse * (scaled - mean(scaled) - normed * mean(scaled * normed))
        work[...] = grad
        dres_two_b[rows] = grad.astype(jnp.bfloat16)
        for k, term in enumerate((upstream * normed, upstream, grad)):
            sums[8 * k : 8 * k + 8, 0:D] += fold_rows(term)

        block = width // 12
        for c in range(12):
            cols = slice(block * c, block * c + block)
            dact = dot_nt(dres_two_b[rows], w_down[cols]).astype(jnp.bfloat16)
            grad = dact.astype(jnp.float32) * slope[:, cols]
            grad_b = grad.astype(jnp.bfloat16)
            dhid[rows, cols] = grad_b
            sums[48:56, cols] += jnp.sum(
                grad_b.astype(jnp.float32).reshape(TILE // 8, 8, block), axis=0
            )
        work[...] += dot_nt(dhid[rows], w_up[...])

        normed = norm_one[...]
        inverse = inverse_one[:, 0:1]
        upstream = work[...]
        scaled = upstream * gain_one
        grad = inverse * (scaled - mean(scaled) - normed * mean(scaled * normed))
        dres[...] = grad
        dres_one_b[rows] = grad.astype(jnp.bfloat16)
        for k, term in enumerate((upstream * normed, upstream, grad)):
            sums[24 + 8 * k : 32 + 8 * k, 0:D] += fold_rows(term)

        dctx[rows] = dot_nt(dres_one_b[rows], w_out[...]).astype(jnp.bfloat16)

    for tile in range(2):

        @pl.when(step == tile)
        def _():
            for copy in moves[tile]:
                copy.start()

    quarter = width // 4
    for c in range(4):
        cols = slice(quarter * c, quarter * c + quarter)

        @pl.when(step == tiles + c)
        def _():
            g_down[...] = dot_tn(act[:, cols], dres_two_b[...]).astype(jnp.bfloat16)

        @pl.when(step == tiles + 4 + c)
        def _():
            g_up[...] = dot_tn(first_b[...], dhid[:, cols]).astype(jnp.bfloat16)

    @pl.when(step == tiles + 8)
    def _():
        g_out[...] = dot_tn(ctx[...], dres_one_b[...]).astype(jnp.bfloat16)
        for k in range(7):
            sums_out[k : k + 1] = jnp.sum(sums[8 * k : 8 * k + 8], axis=0, keepdims=True)
        sums_out[7:8] = jnp.zeros_like(sums_out[7:8])
        for group in moves:
            for copy in group:
                copy.wait()


def middle(x, ctx, cot, w_out, w_up, w_down, vec, up_bias):
    rows = x.shape[0]
    rows_c = MICRO * TD
    width = w_up.shape[1]
    tiles = rows // TILE
    quarter = width // 4
    def once(array):
        return pl.BlockSpec(array.shape, lambda s: (0, 0), pipeline_mode=pl.Buffered(1))

    bf, f32 = jnp.bfloat16, jnp.float32
    return pl.pallas_call(
        middle_kernel,
        name="middle",
        grid=(tiles + GRAD_STEPS,),
        in_specs=[
            once(x),
            once(ctx),
            once(cot),
            once(w_out),
            ANY_SPEC,
            ANY_SPEC,
            once(vec),
            once(up_bias),
        ],
        out_specs=[
            ANY_SPEC,
            ANY_SPEC,
            pl.BlockSpec((TILE, D), lambda s: (jnp.minimum(s, tiles - 1), 0)),
            ANY_SPEC,
            ANY_SPEC,
            pl.BlockSpec((quarter, D), lambda s: (jnp.clip(s - tiles, 0, 3), 0)),
            pl.BlockSpec((D, quarter), lambda s: (0, jnp.clip(s - tiles - 4, 0, 3))),
            pl.BlockSpec((D, D), lambda s: (0, 0)),
            pl.BlockSpec((8, width), lambda s: (0, 0)),
        ],
        out_shape=[
            jax.ShapeDtypeStruct((rows_c, D), f32),
            jax.ShapeDtypeStruct((rows - rows_c, D), f32),
            jax.ShapeDtypeStruct((rows, D), f32),
            jax.ShapeDtypeStruct((rows_c, D), bf),
            jax.ShapeDtypeStruct((rows - rows_c, D), bf),
            jax.ShapeDtypeStruct((width, D), bf),
            jax.ShapeDtypeStruct((D, width), bf),
            jax.ShapeDtypeStruct((D, D), bf),
            jax.ShapeDtypeStruct((8, width), f32),
        ],
        scratch_shapes=[
            pltpu.VMEM((rows, width), bf),
            pltpu.VMEM((rows, width), bf),
            pltpu.VMEM((TILE, width), f32),
            pltpu.VMEM((rows, D), bf),
            pltpu.VMEM((rows, D), bf),
            pltpu.VMEM((rows, D), bf),
            pltpu.VMEM((TILE, D), f32),
            pltpu.VMEM((TILE, LANES), f32),
            pltpu.VMEM((TILE, D), f32),
            pltpu.VMEM((rows, D), f32),
            pltpu.VMEM((rows, D), bf),
            pltpu.VMEM((56, width), f32),
            pltpu.SemaphoreType.DMA((6,)),
            pltpu.VMEM(w_up.shape, bf),
            pltpu.VMEM(w_down.shape, bf),
            pltpu.SemaphoreType.DMA((2,)),
        ],
        compiler_params=pltpu.CompilerParams(vmem_limit_bytes=60 * 1024 * 1024),
        cost_estimate=pl.CostEstimate(
            flops=2 * rows * D * (6 * width + 3 * D),
            bytes_accessed=40 * 1024 * 1024,
            transcendentals=2 * rows * width,
        ),
    )(x, ctx, cot, w_out, w_up, w_down, vec, up_bias)


SMALL_ROWS = 32


def table_rows(hist, buckets_of, side):
    lane = lax.broadcasted_iota(jnp.int32, (LANES, LANES), 0)
    target = lax.broadcasted_iota(jnp.int32, (LANES, LANES), 1)
    signed = jnp.where(lane < 64, lane, lane - 128)
    distances = (
        lane,
        128 + side + 2 * signed,
        127 + side + 2 * signed,
        2 * lane + 2 * side - 1,
        2 * lane,
    )
    kinds = [[] for _ in distances]
    row = lax.broadcasted_iota(jnp.int32, (8, LANES), 0)
    for pair in range(PAIRS):
        for head in range(2):
            block = [
                sum(hist[m, pair, 32 * head + 8 * k : 32 * head + 8 * k + 8] for m in range(MICRO))
                for k in range(4)
            ]
            picks = (
                block[0],
                jnp.where(row % 2 == 0, block[1], 0.0),
                jnp.where(row % 2 == 0, 0.0, block[1]),
                block[2],
                block[3],
            )
            for kind, pick in zip(kinds, picks):
                kind.append(jnp.sum(pick, axis=0, keepdims=True))
    pad = [jnp.zeros((16 - 2 * PAIRS, LANES), jnp.float32)]
    close = jnp.zeros((16, LANES), jnp.float32)
    for kind, distance in zip(kinds, distances):
        hot = jnp.where((distance == target) & (target < LANES - 1), 1.0, 0.0)
        close = close + jnp.dot(
            jnp.concatenate(kind + pad, axis=0),
            hot,
            precision=PRECISE,
            preferred_element_type=jnp.float32,
        )
    last = lax.broadcasted_iota(jnp.int32, (16, LANES), 1) == LANES - 1
    close = jnp.where(last, -jnp.sum(close, axis=1, keepdims=True), close)
    bucket_hot = jnp.where(lane == buckets_of[0:1], 1.0, 0.0)
    return lax.dot_general(
        close,
        bucket_hot,
        (((1,), (1,)), ((), ())),
        precision=PRECISE,
        preferred_element_type=jnp.float32,
    )


def finish_kernel(
    dq_c,
    dq_x,
    dk,
    dv,
    keys_x,
    x_c,
    x_q,
    w_qkv,
    dres,
    hist,
    buckets_of,
    sums,
    w_share,
    small_out,
    grad_c,
    grad_q,
    *scratch,
):
    w_buf = scratch[:10]
    (
        grads,
        prompts,
        theirs,
        along,
        nears,
        near_got,
        owns,
        out_c,
        small,
        x_s,
        x_r,
        sm_s,
        sm_r,
        sem,
    ) = scratch[10:]
    net = Net()
    net.greet()
    weights = reduce_stages(net, grads, w_share, w_buf)
    copies = Copies(x_s, x_r)
    to_mate = [
        copies.to(net.to_mate, prompts.at[:, :, 1 - net.c], theirs),
        copies.to(net.to_mate, nears, near_got),
    ]
    third = [
        copies.to(net.to_z[k], prompts.at[:, net.z_of[k], net.c], along.at[k]) for k in range(3)
    ]
    hops = Copies(sm_s, sm_r)
    partners = [net.to_mate, net.to_x, net.to_y, net.to_z[0], net.to_z[1]]
    butterfly = [
        hops.to(partner, small.at[i], small.at[i + 1]) for i, partner in enumerate(partners)
    ]

    def hop(i):
        butterfly[i].wait_recv()
        small[i + 1] = small[i + 1] + small[i]
        if i + 1 < len(butterfly):
            butterfly[i + 1].start()

    n_keys = dk.shape[0] // MICRO
    n_prompt = n_keys - 2 * CH

    for m in range(MICRO):
        for part in range(n_prompt // 512):
            rows = slice(m * n_keys + 512 * part, m * n_keys + 512 * part + 512)
            value = dot_nt(dk[rows], w_qkv[:, D : 2 * D]) + dot_nt(dv[rows], w_qkv[:, 2 * D :])
            for i in range(4):
                owner = 4 * part + i
                prompts[m, owner // 2, owner % 2] = value[128 * i : 128 * i + 128].astype(
                    jnp.bfloat16
                )
        rows = slice(m * n_keys + n_prompt, (m + 1) * n_keys)
        value = dot_nt(dk[rows], w_qkv[:, D : 2 * D]) + dot_nt(dv[rows], w_qkv[:, 2 * D :])
        for i in range(2):
            nears[m, i] = value[256 * i : 256 * i + 128].astype(jnp.bfloat16)
            owns[m, i] = value[256 * i + 128 : 256 * i + 256]
    start(to_mate)

    def put(value, shift):
        part = D // 32
        for owner in range(8):
            for q in range(4):
                at = (4 * owner + q) * part
                grads[owner // 2, owner % 2, q, :, shift : shift + D] = value[
                    at : at + part
                ].astype(jnp.bfloat16)

    put(dot_tn(keys_x[...], dk[...]), D)
    put(dot_tn(keys_x[...], dv[...]), 2 * D)
    put(dot_tn(x_c[...], dq_c[...]) + dot_tn(x_q[...], dq_x[...]), 0)
    weights[0]()

    small[0] = jnp.zeros_like(small[0])
    sum_q = jnp.sum(dq_c[...].astype(jnp.float32), axis=0, keepdims=True)
    sum_q = sum_q + jnp.sum(dq_x[...].astype(jnp.float32), axis=0, keepdims=True)
    small[0, 0:1] = sum_q
    small[0, 1:2] = jnp.sum(dv[...].astype(jnp.float32), axis=0, keepdims=True)
    for i in range(6):
        small[0, 2 + i : 3 + i] = sums[i : i + 1, 0:D]
    for i in range(4):
        small[0, 8 + i : 9 + i] = sums[6:7, D * i : D * i + D]
    small[0, 16:32, 0:LANES] = table_rows(hist, buckets_of, net.c)
    butterfly[0].start()

    arrive(to_mate)

    @pl.loop(0, 8)
    def _(i):
        m, zi = i // 4, i % 4
        prompts[m, zi, net.c] = prompts[m, zi, net.c] + theirs[m, zi]

    start(third)
    weights[1]()
    hop(0)
    rows_c = x_c.shape[0]
    out_c[0:rows_c] = dres[0:rows_c] + dot_nt(dq_c[...], w_qkv[:, 0:D])
    out_c[rows_c:] = dres[rows_c:] + dot_nt(dq_x[...], w_qkv[:, 0:D])
    for m in range(MICRO):
        for i in range(2):
            rows = slice(m * TD + PD + 128 * i, m * TD + PD + 128 * i + 128)
            out_c[rows] = out_c[rows] + owns[m, i] + near_got[m, i].astype(jnp.float32)
    hop(1)
    weights[2]()
    hop(2)
    weights[3]()
    hop(3)
    arrive(third)
    for m in range(MICRO):
        total = prompts[m, net.z, net.c].astype(jnp.float32)
        for k in range(3):
            total = total + along[k, m].astype(jnp.float32)
        rows = slice(m * TD, m * TD + PD)
        out_c[rows] = out_c[rows] + total
    stores = [
        pltpu.make_async_copy(out_c.at[pl.ds(0, rows_c)], grad_c, sem.at[0]),
        pltpu.make_async_copy(out_c.at[pl.ds(rows_c, 2 * QP)], grad_q, sem.at[1]),
    ]
    start(stores)
    hop(4)
    keep = pltpu.make_async_copy(small.at[5], small_out, sem.at[2])
    keep.start()
    for i in range(4, 7):
        weights[i]()
    for copy in stores + [keep]:
        copy.wait()
    copies.finish()
    hops.finish()


def finish(dq_c, dq_x, dk, dv, keys_x, x_c, x_q, w_qkv, dres, hist, buckets_of, sums):
    whole = pl.BlockSpec(memory_space=pltpu.VMEM)
    bf, f32 = jnp.bfloat16, jnp.float32
    rows_c, rows_x = x_c.shape[0], x_q.shape[0]
    part, width = D // 32, w_qkv.shape[1]
    return pl.pallas_call(
        finish_kernel,
        name="finish",
        in_specs=[whole] * 12,
        out_specs=[ANY_SPEC] * 4,
        out_shape=[
            jax.ShapeDtypeStruct((4, part, width), bf),
            jax.ShapeDtypeStruct((SMALL_ROWS, D), f32),
            jax.ShapeDtypeStruct((rows_c, D), f32),
            jax.ShapeDtypeStruct((rows_x, D), f32),
        ],
        scratch_shapes=reduce_buffers(4 * part, width)
        + [
            pltpu.VMEM((4, 2, 4, part, width), bf),
            pltpu.VMEM((MICRO, 4, 2, PD, D), bf),
            pltpu.VMEM((MICRO, 4, PD, D), bf),
            pltpu.VMEM((3, MICRO, PD, D), bf),
            pltpu.VMEM((MICRO, 2, 128, D), bf),
            pltpu.VMEM((MICRO, 2, 128, D), bf),
            pltpu.VMEM((MICRO, 2, 128, D), f32),
            pltpu.VMEM((rows_c + rows_x, D), f32),
            pltpu.VMEM((6, SMALL_ROWS, D), f32),
            pltpu.SemaphoreType.DMA((5,)),
            pltpu.SemaphoreType.DMA((5,)),
            pltpu.SemaphoreType.DMA((5,)),
            pltpu.SemaphoreType.DMA((5,)),
            pltpu.SemaphoreType.DMA((3,)),
        ],
        compiler_params=pltpu.CompilerParams(
            collective_id=4, has_side_effects=True, vmem_limit_bytes=60 * 1024 * 1024
        ),
    )(dq_c, dq_x, dk, dv, keys_x, x_c, x_q, w_qkv, dres, hist, buckets_of, sums)


def pad_rows(block):
    return jnp.pad(block, ((0, 0), (0, QP - block.shape[1]), (0, 0))).reshape(MICRO * QP, D)


def table_gradient(hist, rel_bucket, buckets, side, heads):
    summed = jnp.sum(hist, axis=0).reshape(PAIRS, 2, 4, 8, LANES)
    prompt = jnp.sum(summed[:, :, 0], axis=2)
    even = jnp.sum(summed[:, :, 1, 0::2], axis=2)
    odd = jnp.sum(summed[:, :, 1, 1::2], axis=2)
    near = jnp.sum(summed[:, :, 2], axis=2)
    own = jnp.sum(summed[:, :, 3], axis=2)
    lanes = jnp.arange(LANES, dtype=jnp.int32)
    signed = jnp.where(lanes < 64, lanes, lanes - 128)
    distance = jnp.stack(
        [
            lanes,
            128 + side + 2 * signed,
            127 + side + 2 * signed,
            2 * lanes + 2 * side - 1,
            2 * lanes,
        ]
    ).reshape(-1)
    hot = (distance[:, None] == lanes[None, :]) & (lanes[None, :] < LANES - 1)
    parts = jnp.stack([prompt, even, odd, near, own], axis=2).reshape(heads, 5 * LANES)
    close = jnp.dot(parts, hot.astype(jnp.float32), precision=PRECISE)
    close = jnp.where(
        lanes[None, :] == LANES - 1, -jnp.sum(close, axis=1, keepdims=True), close
    )
    bucket_hot = (rel_bucket[:, None] == jnp.arange(buckets, dtype=jnp.int32)[None, :]).astype(
        jnp.float32
    )
    return jnp.dot(bucket_hot.T, close.T, precision=PRECISE)


def on_device(
    content_in,
    query_in,
    pred_order,
    cont_prompt,
    rel_bucket,
    w_query,
    b_query,
    w_key,
    w_value,
    b_value,
    w_out,
    b_out,
    ln1_gain,
    ln1_bias,
    w_up,
    b_up,
    w_down,
    b_down,
    ln2_gain,
    ln2_bias,
    bias_table,
    cot_content,
    cot_query,
):
    devices = lax.axis_size("fsdp")
    halfway = devices // 2
    own_rank = lax.axis_index("fsdp")
    plength = PD * halfway
    heads = bias_table.shape[1]
    extra_rows = query_in.shape[1]
    prompt_base = own_rank % halfway * PD
    cont_index = own_rank // 2
    side = own_rank % 2

    own_links = lax.axis_size("grp") == 4 and devices == 8

    def gather(entry):
        return lax.all_gather(entry, "fsdp", axis=0, tiled=True)

    def quarters(entry):
        return entry.reshape(4, -1, entry.shape[1])

    n_keys = 2 * plength + 2 * CH
    shard = b_query.shape[0]
    up_size = b_up.shape[0]
    vectors = jnp.concatenate(
        [b_query, b_value, b_out, b_down, ln1_gain, ln1_bias, ln2_gain, ln2_bias, b_up]
    )
    qkv_shard = jnp.concatenate([w_query, w_key, w_value], axis=1)
    if own_links:
        vector_shard = jnp.pad(vectors, (0, 32 * 256 - vectors.shape[0])).reshape(4, 8, 256)
        qkv_weight, all_vectors, keys_x = gather_first(
            quarters(qkv_shard), vector_shard, content_in
        )
        qkv_weight = qkv_weight.reshape(-1, qkv_shard.shape[1])
        all_vectors = all_vectors.reshape(devices, -1)
        carried = tuple(quarters(shard) for shard in (w_up, w_down, w_out))
    else:
        qkv_weight, all_vectors = gather(qkv_shard), gather(vectors[None])
        up_weight, down_weight, out_weight = gather(w_up), gather(w_down), gather(w_out)
        carried = ()
        prompt_x = lax.all_gather(content_in[:, :PD], "fsdp", axis=1, tiled=True)
        near_x = from_partner(content_in[:, PD:], "fsdp").reshape(MICRO, 2, 1, 128, D)
        own_x = content_in[:, PD:].reshape(MICRO, 2, 1, 128, D)
        cont_x = jnp.concatenate([near_x, own_x], axis=2).reshape(MICRO, 2 * CH, D)
        keys_x = jnp.concatenate([prompt_x, cont_x], axis=1)
    keys_x = keys_x.reshape(MICRO * n_keys, D)
    query_weight, kv_weight = qkv_weight[:, :D], qkv_weight[:, D:]
    singles = [
        all_vectors[:, shard * i : shard * i + shard].reshape(-1).astype(jnp.float32)
        for i in range(8)
    ]
    (
        query_bias,
        value_bias,
        out_bias,
        down_bias,
        gain_one,
        shift_one,
        gain_two,
        shift_two,
    ) = singles
    up_bias = all_vectors[:, 8 * shard : 8 * shard + up_size].reshape(-1).astype(jnp.float32)

    prompt_map = cont_prompt[:, 0, :]
    prompt_ref = jnp.sum(
        jnp.where(
            jnp.arange(prompt_map.shape[1], dtype=jnp.int32)[None, :] == cont_index, prompt_map, 0
        ),
        axis=1,
    )
    meta = prompt_ref.astype(jnp.int32)
    order = jnp.pad(pred_order[:, 0, :], ((0, 0), (0, QP - extra_rows)), constant_values=-1)
    real = order >= 0
    in_prompt = order < PD
    position = jnp.where(
        in_prompt, prompt_base + order, plength + 2 * (order - PD) + side
    )
    limit_p = jnp.where(real & in_prompt, jnp.maximum(position, 1), -1)
    limit_c = jnp.where(real & ~in_prompt, position, -1)
    info = jnp.stack([position, limit_p, limit_c, order], axis=1)
    info = jnp.concatenate([info, info], axis=2)
    xrow = jnp.pad(info, ((0, 0), (0, 4), (0, 0))).astype(jnp.int32)
    xcol = jnp.swapaxes(xrow, 1, 2)
    dist = bias_table.astype(jnp.float32)[rel_bucket].T
    dist = dist - dist[:, LANES - 1 :]
    table = jnp.pad(dist.reshape(PAIRS, 2, LANES), ((0, 0), (0, 6), (0, 0)))

    tokens_x = content_in.reshape(MICRO * TD, D)
    extra_x = pad_rows(query_in)
    x_all = jnp.concatenate([tokens_x, extra_x])
    kv_bias = jnp.concatenate([jnp.zeros((D,), jnp.float32), value_bias])
    key_rows = (
        jnp.dot(keys_x, kv_weight, preferred_element_type=jnp.float32) + kv_bias
    ).astype(jnp.bfloat16)
    q_all = (
        jnp.dot(x_all, query_weight, preferred_element_type=jnp.float32) + query_bias
    ).astype(jnp.bfloat16)
    queries = q_all[: MICRO * TD]
    extra_q = q_all[MICRO * TD :]

    ctx_c, ctx_x, full_c, full_x, lse, *gathered = attend(
        meta, queries, extra_q, key_rows, table, xcol, carried
    )
    if own_links:
        up_weight, down_weight, out_weight = (
            entry.reshape(-1, entry.shape[2]) for entry in gathered
        )
    rows_c = MICRO * TD
    context = jnp.concatenate([ctx_c, ctx_x])
    upstream = jnp.concatenate([cot_content.reshape(rows_c, D), pad_rows(cot_query)])
    vec = jnp.stack([out_bias, gain_one, shift_one, down_bias, gain_two, shift_two])
    (
        out_content,
        out_query,
        dres_one,
        dctx_c,
        dctx_x,
        dweight_down,
        dweight_up,
        dweight_out,
        sums,
    ) = middle(
        x_all, context, upstream, out_weight, up_weight, down_weight, vec, up_bias[None]
    )
    out_content = out_content.reshape(MICRO, TD, D)
    out_query = out_query.reshape(MICRO, QP, D)[:, :extra_rows]

    def by_quarter(grad):
        grad = grad.astype(jnp.bfloat16)
        return grad.reshape(4, 2, 4, grad.shape[0] // 32, grad.shape[1])

    to_reduce = ()
    if own_links:
        to_reduce = tuple(by_quarter(g) for g in (dweight_up, dweight_down, dweight_out))
    dq_c, dq_x, dk_rows, dv_rows, hist, *reduced = attend_back(
        meta,
        queries,
        extra_q,
        key_rows,
        table,
        xcol,
        xrow,
        lse,
        dctx_c,
        dctx_x,
        full_c,
        full_x,
        to_reduce,
    )
    if own_links:
        t_qkv, small, grad_content, grad_query = finish(
            dq_c,
            dq_x,
            dk_rows,
            dv_rows,
            keys_x,
            tokens_x,
            extra_x,
            qkv_weight,
            dres_one,
            hist,
            jnp.broadcast_to(rel_bucket[None], (8, LANES)),
            sums,
        )
        grad_content = grad_content.reshape(MICRO, TD, D)
        grad_query = grad_query.reshape(MICRO, QP, D)[:, :extra_rows]
        t_up, t_down, t_out = reduced
        shares = (t_down, t_up, t_out, t_qkv)
        t_down, t_up, t_out, t_qkv = [
            entry.reshape(-1, entry.shape[-1]).astype(jnp.float32) for entry in shares
        ]
        pieces = lax.dynamic_slice_in_dim(small[:8], own_rank * shard, shard, 1)
        t_bup = lax.dynamic_index_in_dim(
            small[8:12].reshape(devices, up_size), own_rank, 0, keepdims=False
        )
        t_table = lax.dynamic_slice_in_dim(
            small[16 : 16 + heads, : bias_table.shape[0]],
            own_rank * (bias_table.shape[0] // devices),
            bias_table.shape[0] // devices,
            1,
        ).T
    else:
        dgain_two, dshift_two, dbias_down, dgain_one, dshift_one, dbias_out = sums[:6, :D]
        dbias_up = sums[6]
        dkv_rows = jnp.concatenate([dk_rows, dv_rows], axis=1)
        dq_all = jnp.concatenate([dq_c, dq_x])
        dbias_query = jnp.sum(dq_all.astype(jnp.float32), axis=0)
        dbias_value = jnp.sum(dv_rows.astype(jnp.float32), axis=0)
        dkeys_x = dot_nt(dkv_rows, kv_weight).reshape(MICRO, n_keys, D)
        dtable = table_gradient(hist, rel_bucket, bias_table.shape[0], side, heads)
        small = jnp.concatenate(
            [
                entry.reshape(devices, -1)
                for entry in (
                    dbias_query,
                    dbias_value,
                    dgain_two,
                    dshift_two,
                    dbias_down,
                    dgain_one,
                    dshift_one,
                    dbias_out,
                    dbias_up,
                    dtable,
                )
            ],
            axis=1,
        ).astype(jnp.bfloat16)
        dprompts = dkeys_x[:, : 2 * plength].astype(jnp.bfloat16)
        dcont = dkeys_x[:, 2 * plength :].reshape(MICRO, 2, 2, 128, D)
        dnear = dcont[:, :, 0].astype(jnp.bfloat16)
        dweight_qkv = jnp.concatenate(
            [dot_tn(x_all, dq_all), dot_tn(keys_x, dkv_rows)], axis=1
        )

        def scatter(piece, dimension=0):
            return lax.psum_scatter(
                piece.astype(jnp.bfloat16), "fsdp", scatter_dimension=dimension, tiled=True
            )

        from_prompts = scatter(dprompts, 1).astype(jnp.float32)
        from_near = from_partner(dnear, "fsdp")
        shares = [
            scatter(piece)
            for piece in (dweight_down, dweight_up, dweight_out, dweight_qkv, small)
        ]
        t_down, t_up, t_out, t_qkv, t_small = [
            lax.psum(entry, "grp").astype(jnp.float32) for entry in shares
        ]
        dcont = (dcont[:, :, 1] + from_near.astype(jnp.float32)).reshape(MICRO, CH, D)
        dx_all = dres_one + dot_nt(dq_all, query_weight)
        grad_content = dx_all[:rows_c].reshape(MICRO, TD, D) + jnp.concatenate(
            [from_prompts, dcont], axis=1
        )
        grad_query = dx_all[rows_c:].reshape(MICRO, QP, D)[:, :extra_rows]
        t_small = t_small.reshape(-1)
        pieces = [t_small[shard * i : shard * i + shard] for i in range(8)]
        up_at = 8 * shard
        t_bup = t_small[up_at : up_at + up_size]
        t_table = t_small[up_at + up_size :].reshape(-1, heads)
    return (
        out_content,
        out_query,
        grad_content,
        grad_query,
        t_qkv[:, :D],
        pieces[0],
        t_qkv[:, D : 2 * D],
        t_qkv[:, 2 * D :],
        pieces[1],
        t_out,
        pieces[7],
        pieces[5],
        pieces[6],
        t_up,
        t_bup,
        t_down,
        pieces[4],
        pieces[2],
        pieces[3],
        t_table,
    )


def solution(mesh):
    rows = P(None, ("grp", "fsdp"), None)
    matrix = P("fsdp", None)
    vector = P("fsdp")
    in_specs = (
        rows,
        rows,
        rows,
        P(None, "grp", None),
        P(),
        matrix,
        vector,
        matrix,
        matrix,
        vector,
        matrix,
        vector,
        vector,
        vector,
        matrix,
        vector,
        matrix,
        vector,
        vector,
        vector,
        P(),
        rows,
        rows,
    )
    out_specs = (
        rows,
        rows,
        rows,
        rows,
        matrix,
        vector,
        matrix,
        matrix,
        vector,
        matrix,
        vector,
        vector,
        vector,
        matrix,
        vector,
        matrix,
        vector,
        vector,
        vector,
        matrix,
    )
    return jax.shard_map(
        on_device, mesh=mesh, in_specs=in_specs, out_specs=out_specs, check_vma=False
    )
```

```python
import functools

import jax
import jax.numpy as jnp
from jax import lax
from jax.experimental import pallas as pl
from jax.experimental.pallas import tpu as pltpu
from jax.sharding import PartitionSpec as P

D = 768
PD = 128
CH = 256
MICRO = 2
TD = 384
QP = 64
HD = 64
LANES = 128
PAIRS = D // LANES

PRECISE = lax.Precision.HIGHEST
MASKED = -1e30
VMEM_LIMIT = 56 * 1024 * 1024


def dot_nt(left, right):
    return lax.dot_general(
        left, right, (((1,), (1,)), ((), ())), preferred_element_type=jnp.float32
    )


def dot_tn(left, right):
    return lax.dot_general(
        left, right, (((0,), (0,)), ((), ())), preferred_element_type=jnp.float32
    )


def dot_nn(left, right):
    return jnp.dot(left, right, preferred_element_type=jnp.float32)


def head_stack(block):
    lane = lax.broadcasted_iota(jnp.int32, block.shape, 1)
    zero = jnp.zeros_like(block)
    return jnp.concatenate(
        [jnp.where(lane < HD, block, zero), jnp.where(lane < HD, zero, block)], axis=0
    )


def head_merge(stacked):
    rows = stacked.shape[0] // 2
    lane = lax.broadcasted_iota(jnp.int32, (rows, LANES), 1)
    return jnp.where(lane < HD, stacked[:rows], stacked[rows:])


def lookup(table, index):
    return jnp.take_along_axis(table, index, axis=1, mode="promise_in_bounds")


def near_index(distance):
    return jnp.clip(distance, 0, LANES - 1)


def fill_keys(scratch, rows_ref, own_prompt, mapped, plength):
    own_at = pl.multiple_of(own_prompt * plength, 128)
    scratch[0:plength] = rows_ref[pl.ds(own_at, plength), :]
    scratch[plength : 2 * plength] = jnp.where(
        mapped == 0, rows_ref[0:plength], rows_ref[plength : 2 * plength]
    )
    scratch[2 * plength :] = rows_ref[2 * plength :]


MESH = pl.DeviceIdType.MESH
ANY_SPEC = pl.BlockSpec(memory_space=pl.ANY)


class Net:
    def __init__(self):
        self.g = lax.axis_index("grp")
        self.f = lax.axis_index("fsdp")
        self.x = self.g % 2
        self.y = self.g // 2
        self.z = self.f // 2
        self.c = self.f % 2
        self.gx = self.g + 1 - 2 * self.x
        self.gy = self.g + 2 - 4 * self.y
        self.mate = self.f + 1 - 2 * self.c
        self.z_of = [
            self.z + 1 - 2 * (self.z % 2),
            (self.z + 2) % 4,
            3 - self.z,
        ]
        self.f_of = [2 * other + self.c for other in self.z_of]
        self.to_x = (self.gx, self.f)
        self.to_y = (self.gy, self.f)
        self.to_mate = (self.g, self.mate)
        self.to_z = [(self.g, other) for other in self.f_of]

    def greet(self):
        barrier = pltpu.get_barrier_semaphore()
        everyone = [self.to_x, self.to_y, self.to_mate] + self.to_z
        for device in everyone:
            pl.semaphore_signal(barrier, inc=1, device_id=device, device_id_type=MESH)
        pl.semaphore_wait(barrier, len(everyone))


class Copies:
    def __init__(self, sends, recvs):
        self.sends = sends
        self.recvs = recvs
        self.used = 0
        self.all = []

    def to(self, device, src, dst):
        copy = pltpu.make_async_remote_copy(
            src_ref=src,
            dst_ref=dst,
            send_sem=self.sends.at[self.used],
            recv_sem=self.recvs.at[self.used],
            device_id=device,
            device_id_type=MESH,
        )
        self.used += 1
        self.all.append(copy)
        return copy

    def finish(self):
        for copy in self.all:
            copy.wait_send()


def start(copies):
    for copy in copies:
        copy.start()


def arrive(copies):
    for copy in copies:
        copy.wait_recv()


GATHER_COPIES = 19


def gather_stages(net, copies, local_sem, shard, full):
    part, width = shard.shape[1:]
    half = width // 2

    def rows(owner, quarter):
        return 4 * owner + quarter

    def whole(owner):
        return pl.ds(4 * owner, 4)

    local = pltpu.make_async_copy(shard, full.at[whole(net.f)], local_sem)
    mine = shard.at[net.g]
    along_z = [copies.to(device, mine, full.at[rows(net.f, net.g)]) for device in net.to_z[:2]]
    passed = full.at[rows(net.f_of[1], net.g)]
    relay = copies.to(net.to_z[0], passed, passed)
    to_mate = [copies.to(net.to_mate, shard, full.at[whole(net.f)])]
    to_x, to_y, on_x, on_y, later = [], [], [], [], []
    for owner in net.f_of:
        got = full.at[rows(owner, net.g)]
        to_x.append(copies.to(net.to_x, got, got))
        to_y.append(copies.to(net.to_y, got, got))
        left = full.at[rows(owner, net.gx), :, pl.ds(0, half)]
        on_y.append(copies.to(net.to_y, left, left))
        right = full.at[rows(owner, net.gy), :, pl.ds(half, half)]
        on_x.append(copies.to(net.to_x, right, right))
        shared = full.at[whole(owner)]
        later.append(copies.to(net.to_mate, shared, shared))

    def begin():
        local.start()
        start(along_z)
        start(to_mate)

    def onward():
        along_z[1].wait_recv()
        relay.start()

    def plane():
        arrive([along_z[0], relay])
        start(to_x + to_y)

    def corners():
        arrive(to_x + to_y)
        start(on_y + on_x)

    def mates():
        arrive(on_y + on_x)
        start(later)

    def end():
        arrive(to_mate + later)
        local.wait()
        copies.finish()

    return [begin, onward, plane, corners, mates, end]


REDUCE_COPIES = 19


def reduce_buffers(size, width):
    part, half = size // 4, width // 2
    return [
        pltpu.VMEM((4, 4, part, width), jnp.bfloat16),
        pltpu.VMEM((4, 4, part, width), jnp.bfloat16),
        pltpu.VMEM((4, 2, part, half), jnp.bfloat16),
        pltpu.VMEM((4, 2, part, half), jnp.bfloat16),
        pltpu.VMEM((2, 4, part, half), jnp.bfloat16),
        pltpu.VMEM((2, 3, part, half), jnp.bfloat16),
        pltpu.VMEM((2, 4, part, half), jnp.bfloat16),
        pltpu.SemaphoreType.DMA((2,)),
        pltpu.SemaphoreType.DMA((REDUCE_COPIES,)),
        pltpu.SemaphoreType.DMA((REDUCE_COPIES,)),
    ]


def reduce_stages(net, grad, share, buffers):
    own, other, side_a, side_b, line, along, done, local_sem, sends, recvs = buffers
    copies = Copies(sends, recvs)
    half = grad.shape[4] // 2
    left, right = pl.ds(0, half), pl.ds(half, half)
    load = pltpu.make_async_copy(grad.at[:, net.c], own, local_sem.at[0])
    to_mate = [copies.to(net.to_mate, grad.at[:, 1 - net.c], other)]
    first = []
    for i in range(2):
        first.append(
            copies.to(net.to_x, own.at[:, 2 * i + 1 - net.x, :, left], side_a.at[:, i])
        )
        first.append(
            copies.to(net.to_y, own.at[:, 2 - 2 * net.y + i, :, right], side_b.at[:, i])
        )
    second = [
        copies.to(net.to_y, side_a.at[:, 1 - net.y], line.at[0]),
        copies.to(net.to_x, side_b.at[:, 1 - net.x], line.at[1]),
    ]
    third = []
    for h in range(2):
        third.append(copies.to(net.to_z[0], line.at[h, net.z_of[2]], along.at[h, 0]))
        third.append(copies.to(net.to_z[0], line.at[h, net.z_of[0]], along.at[h, 1]))
    relay = [copies.to(net.to_z[1], line.at[h, net.z_of[1]], along.at[h, 2]) for h in range(2)]
    fourth = []
    fifth = []
    for h in range(2):
        fourth.append(copies.to(net.to_x, done.at[h, net.g], done.at[h, net.g]))
        fourth.append(copies.to(net.to_y, done.at[h, net.g], done.at[h, net.g]))
    fifth.append(copies.to(net.to_y, done.at[0, net.gx], done.at[0, net.gx]))
    fifth.append(copies.to(net.to_x, done.at[1, net.gy], done.at[1, net.gy]))
    store = [
        pltpu.make_async_copy(done.at[0], share.at[:, :, left], local_sem.at[0]),
        pltpu.make_async_copy(done.at[1], share.at[:, :, right], local_sem.at[1]),
    ]

    def begin():
        load.start()
        start(to_mate)

    def plane():
        load.wait()
        arrive(to_mate)

        @pl.loop(0, 16)
        def _(i):
            zi, qi = i // 4, i % 4
            own[zi, qi] = own[zi, qi] + other[zi, qi]

        start(first)

    def cross():
        arrive(first)

        @pl.loop(0, 8)
        def _(i):
            zi, qi = i // 2, i % 2
            side_a[zi, qi] = side_a[zi, qi] + own[zi, 2 * qi + net.x, :, 0:half]
            side_b[zi, qi] = side_b[zi, qi] + own[zi, 2 * net.y + qi, :, half : 2 * half]

        start(second)

    def column():
        arrive(second)

        @pl.loop(0, 4)
        def _(zi):
            line[0, zi] = line[0, zi] + side_a[zi, net.y]
            line[1, zi] = line[1, zi] + side_b[zi, net.x]

        start(third)

    def onward():
        arrive(third[0::2])

        @pl.loop(0, 2)
        def _(h):
            line[h, net.z_of[1]] = line[h, net.z_of[1]] + along[h, 0]

        start(relay)

    def spread():
        arrive(third[1::2] + relay)

        @pl.loop(0, 2)
        def _(h):
            total = line[h, net.z].astype(jnp.float32)
            for k in range(1, 3):
                total = total + along[h, k].astype(jnp.float32)
            done[h, net.g] = total.astype(jnp.bfloat16)

        start(fourth)

    def corners():
        arrive(fourth)
        start(fifth)

    def end():
        arrive(fifth)
        start(store)
        for copy in store:
            copy.wait()
        copies.finish()

    return [begin, plane, cross, column, onward, spread, corners, end]


ROW_COPIES = 9


def rows_stages(net, copies, local_sems, x_ref, keys_x):
    at = 8 * PD

    def block(owner):
        return keys_x.at[pl.ds(pl.multiple_of(owner * PD, 128), PD)]

    prompt = x_ref.at[pl.ds(0, PD)]
    cont = [x_ref.at[pl.ds(PD + 128 * i, 128)] for i in range(2)]
    local = [pltpu.make_async_copy(prompt, block(net.f), local_sems.at[0])]
    to_mate = [copies.to(net.to_mate, prompt, block(net.f))]
    for i in range(2):
        near = keys_x.at[pl.ds(at + 256 * i, 128)]
        here = keys_x.at[pl.ds(at + 256 * i + 128, 128)]
        local.append(pltpu.make_async_copy(cont[i], here, local_sems.at[1 + i]))
        to_mate.append(copies.to(net.to_mate, cont[i], near))
    along_z = [copies.to(device, prompt, block(net.f)) for device in net.to_z[:2]]
    relay = copies.to(net.to_z[0], block(net.f_of[1]), block(net.f_of[1]))
    later = [copies.to(net.to_mate, block(owner), block(owner)) for owner in net.f_of]

    def begin():
        start(local)
        start(to_mate)

    def column():
        start(along_z)

    def onward():
        along_z[1].wait_recv()
        relay.start()

    def mates():
        arrive([along_z[0], relay])
        start(later)

    def end():
        arrive(to_mate + later)
        for copy in local:
            copy.wait()
        copies.finish()

    return [begin, column, onward, mates, end]


def gather_first_kernel(*refs):
    shards, x_ref, fulls, keys_x = refs[:4], refs[4], refs[5:9], refs[9]
    sems, local_sem, row_sems = refs[10:20], refs[20], refs[21]
    net = Net()
    net.greet()
    parts = [
        gather_stages(
            net, Copies(sems[2 * i], sems[2 * i + 1]), local_sem.at[i], shards[i], fulls[i]
        )
        for i in range(4)
    ]
    rows = rows_stages(net, Copies(sems[8], sems[9]), row_sems, x_ref.at[0], keys_x)
    for part in parts:
        part[0]()
    rows[0]()
    for part in parts:
        part[1]()
    rows[1]()
    for part in parts:
        part[2]()
    for part in parts:
        part[3]()
    rows[2]()
    for part in parts:
        part[4]()
    rows[3]()
    for part in parts:
        part[5]()
    rows[4]()


def gather_first(shards, content_in):
    return pl.pallas_call(
        gather_first_kernel,
        name="gather_first",
        in_specs=[ANY_SPEC] * 5,
        out_specs=[ANY_SPEC] * 5,
        out_shape=[jax.ShapeDtypeStruct((8 * 4,) + s.shape[1:], jnp.bfloat16) for s in shards]
        + [jax.ShapeDtypeStruct((8 * PD + 2 * CH, D), jnp.bfloat16)],
        scratch_shapes=[pltpu.SemaphoreType.DMA((GATHER_COPIES,))] * 8
        + [pltpu.SemaphoreType.DMA((ROW_COPIES,))] * 2
        + [pltpu.SemaphoreType.DMA((4,)), pltpu.SemaphoreType.DMA((3,))],
        compiler_params=pltpu.CompilerParams(collective_id=1, has_side_effects=True),
    )(*shards, content_in)


def halves_of(ref):
    rows, columns = ref.shape[-2:]
    rest = (slice(None),) * (len(ref.shape) - 2)
    if columns > rows * 16:
        cut = columns // 2
        return [ref.at[rest + (slice(None), pl.ds(cut * i, cut))] for i in range(2)]
    cut = rows // 2
    return [ref.at[rest + (pl.ds(cut * i, cut),)] for i in range(2)]


def hosted(plan, step):
    for at, stage in plan:

        @pl.when(step == at)
        def _():
            stage()


def place(plength):
    rank = lax.axis_index("fsdp")
    halfway = plength // PD
    return rank // halfway, rank % halfway * PD, rank % 2


def attend_kernel(plength, carried, *refs):
    (meta, x_c, x_q, w_q, w_k, w_v, bias, table, xcol, first_rows, other), refs = (
        refs[:11],
        refs[11:],
    )
    shards, refs = refs[:carried], refs[carried:]
    (ctx_c, ctx_x, full_c, full_x, lse_ref, qc, qx, k_rows, v_rows), refs = refs[:9], refs[9:]
    second_rows = other
    if carried:
        second_rows, refs = refs[0], refs[1:]
    fulls, refs = refs[:carried], refs[carried:]
    keys, vals, scores, probs, x_keys, load_sem = refs[:6]
    refs = refs[6:]
    step = pl.program_id(0) * PAIRS + pl.program_id(1)
    if carried:
        net = Net()
        pieces = []
        for i in range(2):
            pieces += list(zip(halves_of(shards[i]), halves_of(fulls[i])))
        pieces.append((shards[2], fulls[2]))
        one, two, three, four, proj = (
            gather_stages(
                net, Copies(refs[2 * i], refs[2 * i + 1]), refs[12].at[i], src, dst
            )
            for i, (src, dst) in enumerate(pieces)
        )
        rows = rows_stages(
            net, Copies(refs[10], refs[11]), refs[13], other.at[1], second_rows
        )
        hosted([(0, net.greet)], step)
        hosted(
            [
                (0, rows[0]),
                (0, rows[1]),
                (2, one[0]),
                (2, proj[0]),
                (3, rows[2]),
                (3, two[0]),
                (4, one[1]),
                (4, proj[1]),
                (5, rows[3]),
                (6, rows[4]),
                (6, one[2]),
                (6, proj[2]),
                (6, two[1]),
                (6, three[0]),
                (7, two[2]),
                (7, four[0]),
                (8, one[3]),
                (8, proj[3]),
                (8, three[1]),
                (9, three[2]),
                (9, four[1]),
                (10, one[4]),
                (10, proj[4]),
                (10, two[3]),
                (10, four[2]),
                (11, three[3]),
            ],
            step,
        )
    for m, source in enumerate((first_rows, second_rows)):

        @pl.when(step == m * PAIRS)
        def _():
            load = pltpu.make_async_copy(source, x_keys, load_sem)
            load.start()
            load.wait()

    w_kv = jnp.concatenate([w_k[...], w_v[...]], axis=1)
    for at in range(0, x_keys.shape[0], 512):
        part = slice(at, at + 512)
        value = dot_nn(x_keys[part], w_kv)
        k_rows[part] = value[:, :LANES].astype(jnp.bfloat16)
        v_rows[part] = (value[:, LANES:] + bias[1:2]).astype(jnp.bfloat16)
    qc[...] = (dot_nn(x_c[...], w_q[...]) + bias[0:1]).astype(jnp.bfloat16)
    qx[...] = (dot_nn(x_q[...], w_q[...]) + bias[0:1]).astype(jnp.bfloat16)
    own_prompt, base, side = place(plength)
    mapped = meta[pl.program_id(0)]
    blocks = plength // 128
    fill_keys(keys, k_rows, own_prompt, mapped, plength)
    fill_keys(vals, v_rows, own_prompt, mapped, plength)
    row = lax.broadcasted_iota(jnp.int32, (128, 128), 0)
    col = lax.broadcasted_iota(jnp.int32, (128, 128), 1)
    tab_a = jnp.broadcast_to(table[0, 0:1, :], (128, 128))
    tab_b = jnp.broadcast_to(table[0, 1:2, :], (128, 128))
    tab_x = jnp.where(row < QP, tab_a, tab_b)
    lse_ref[...] = jnp.zeros_like(lse_ref)

    def solve(stack, first, plan, tables, lse_rows):
        count = len(plan)
        span = slice(first, first + 128 * count)
        halves = len(tables)
        width = 128 * count
        scores[0 : 128 * halves, 0:width] = dot_nt(stack, keys[span])
        for half in range(halves):
            rows = slice(128 * half, 128 * half + 128)
            peak = None
            for at, (index, visible) in enumerate(plan):
                cols = slice(128 * at, 128 * at + 128)
                s = scores[rows, cols]
                if index is not None:
                    s = s + lookup(tables[half], index)
                if visible is not None:
                    s = jnp.where(visible, s, MASKED)
                if index is not None or visible is not None:
                    scores[rows, cols] = s
                peak = s if peak is None else jnp.maximum(peak, s)
            top = jnp.max(peak, axis=1, keepdims=True)
            total = None
            for at in range(count):
                cols = slice(128 * at, 128 * at + 128)
                p = jnp.exp(scores[rows, cols] - top)
                total = p if total is None else total + p
                probs[rows, cols] = p.astype(jnp.bfloat16)
            total = jnp.sum(total, axis=1, keepdims=True)
            log_total = top + jnp.log(total)
            lse_ref[0, 0, lse_rows[half] : lse_rows[half] + 1, :] = jnp.transpose(
                jnp.broadcast_to(log_total, (128, 128))
            )[0:1, :]
            scores[rows, 0:128] = jnp.broadcast_to(1.0 / total, (128, 128))
        out = dot_nn(probs[0 : 128 * halves, 0:width], vals[span])
        return out * scores[0 : 128 * halves, 0:128]

    scale = jnp.asarray(0.125, jnp.bfloat16)
    q_p = head_stack(qc[0:PD] * scale)
    q_0 = head_stack(qc[PD : PD + 128] * scale)
    q_1 = head_stack(qc[PD + 128 : PD + 256] * scale)
    q_x = head_stack(qx[...] * scale)

    plan_p = []
    for b in range(blocks):
        d = base + row - (col + 128 * b)
        plan_p.append((near_index(d), d >= 0))
    out = head_merge(solve(q_p, 0, plan_p, (tab_a, tab_b), (0, 3)))
    ctx_c[0:PD] = out.astype(jnp.bfloat16)
    full_c[0:PD] = out

    far = (None, None)
    last = 128 + 2 * row + side - col
    near_d = 2 * (row - col) + 2 * side - 1
    own_d = 2 * (row - col)
    plan_0 = [far] * (blocks - 1) + [
        (near_index(last), None),
        (near_index(near_d), near_d >= 0),
        (near_index(own_d), own_d >= 0),
    ]
    out = head_merge(solve(q_0, plength, plan_0, (tab_a, tab_b), (1, 4)))
    ctx_c[PD : PD + 128] = out.astype(jnp.bfloat16)
    full_c[PD : PD + 128] = out
    plan_1 = [far] * blocks + [
        (near_index(near_d + 256), None),
        (near_index(own_d + 256), None),
        (near_index(near_d), near_d >= 0),
        (near_index(own_d), own_d >= 0),
    ]
    out = head_merge(solve(q_1, plength, plan_1, (tab_a, tab_b), (2, 5)))
    ctx_c[PD + 128 : PD + 256] = out.astype(jnp.bfloat16)
    full_c[PD + 128 : PD + 256] = out

    pos = jnp.broadcast_to(xcol[0, :, 0:1], (128, 128))
    lim_p = jnp.broadcast_to(xcol[0, :, 1:2], (128, 128))
    lim_c = jnp.broadcast_to(xcol[0, :, 2:3], (128, 128))
    plan_x = []
    for b in range(blocks):
        key = col + 128 * b
        plan_x.append((near_index(pos - key), key < lim_p))
    in_cont = lim_c > 0
    for b in range(blocks - 1):
        plan_x.append((None, in_cont))
    key = col + 128 * (blocks - 1)
    plan_x.append((near_index(pos - key), in_cont))
    for b in range(2):
        for offset in (1 - side, side):
            key = plength + 2 * (col + 128 * b) + offset
            plan_x.append((near_index(pos - key), key < lim_c))
    out = solve(q_x, 0, plan_x, (tab_x,), (6,))
    lane = lax.broadcasted_iota(jnp.int32, (QP, LANES), 1)
    out = jnp.where(lane < HD, out[0:QP], out[QP:])
    ctx_x[...] = out.astype(jnp.bfloat16)
    full_x[...] = out
    if carried:
        rest = (four[3], two[4], three[4], four[4], one[5], proj[5], two[5], three[5], four[5])
        hosted([(11, stage) for stage in rest], step)


def pair_column():
    return lambda m, j, meta: (m, j)


def key_spec(n_keys):
    return pl.BlockSpec((n_keys, LANES), lambda m, j, meta: (m, j))


TABLE_SPEC = pl.BlockSpec((1, 8, LANES), lambda m, j, meta: (j, 0, 0))


def host_params(collective_id, carried):
    if carried:
        return pltpu.CompilerParams(
            vmem_limit_bytes=VMEM_LIMIT, collective_id=collective_id, has_side_effects=True
        )
    return pltpu.CompilerParams(vmem_limit_bytes=VMEM_LIMIT)


def attend(meta, x_c, x_q, weights, bias, table, xcol, first_rows, other, shards):
    carried = len(shards)
    n_keys = first_rows.shape[0]
    plength = (n_keys - 2 * CH) // 2
    content = pl.BlockSpec((TD, LANES), pair_column())
    extra = pl.BlockSpec((QP, LANES), pair_column())
    own_row = plength + 2 * CH
    pairs = MICRO * PAIRS * 2 * (128 * plength + 256 * own_row) + MICRO * PAIRS * 128 * n_keys
    return pl.pallas_call(
        functools.partial(attend_kernel, plength, carried),
        name="attend",
        grid_spec=pltpu.PrefetchScalarGridSpec(
            num_scalar_prefetch=1,
            grid=(MICRO, PAIRS),
            in_specs=[
                pl.BlockSpec((TD, D), lambda m, j, meta: (m, 0)),
                pl.BlockSpec((QP, D), lambda m, j, meta: (m, 0)),
            ]
            + [pl.BlockSpec((D, LANES), lambda m, j, meta: (0, j))] * 3
            + [
                pl.BlockSpec((8, LANES), lambda m, j, meta: (0, j)),
                TABLE_SPEC,
                pl.BlockSpec((1, 128, 8), lambda m, j, meta: (m, 0, 0)),
                ANY_SPEC,
                ANY_SPEC,
            ]
            + [ANY_SPEC] * carried,
            out_specs=[
                content,
                extra,
                content,
                extra,
                pl.BlockSpec((1, 1, 8, LANES), lambda m, j, meta: (m, j, 0, 0)),
                content,
                extra,
                key_spec(n_keys),
                key_spec(n_keys),
            ]
            + [ANY_SPEC] * (carried + 1 if carried else 0),
            scratch_shapes=[
                pltpu.VMEM((n_keys, LANES), jnp.bfloat16),
                pltpu.VMEM((n_keys, LANES), jnp.bfloat16),
                pltpu.VMEM((256, n_keys), jnp.float32),
                pltpu.VMEM((256, n_keys), jnp.bfloat16),
            ]
            + [pltpu.VMEM((n_keys, D), jnp.bfloat16), pltpu.SemaphoreType.DMA]
            + (
                [pltpu.SemaphoreType.DMA((GATHER_COPIES,))] * 10
                + [pltpu.SemaphoreType.DMA((ROW_COPIES,))] * 2
                + [pltpu.SemaphoreType.DMA((5,)), pltpu.SemaphoreType.DMA((3,))]
                if carried
                else []
            ),
        ),
        out_shape=[
            jax.ShapeDtypeStruct((MICRO * TD, D), jnp.bfloat16),
            jax.ShapeDtypeStruct((MICRO * QP, D), jnp.bfloat16),
            jax.ShapeDtypeStruct((MICRO * TD, D), jnp.float32),
            jax.ShapeDtypeStruct((MICRO * QP, D), jnp.float32),
            jax.ShapeDtypeStruct((MICRO, PAIRS, 8, LANES), jnp.float32),
            jax.ShapeDtypeStruct((MICRO * TD, D), jnp.bfloat16),
            jax.ShapeDtypeStruct((MICRO * QP, D), jnp.bfloat16),
            jax.ShapeDtypeStruct((MICRO * n_keys, D), jnp.bfloat16),
            jax.ShapeDtypeStruct((MICRO * n_keys, D), jnp.bfloat16),
        ]
        + ([jax.ShapeDtypeStruct((n_keys, D), jnp.bfloat16)] if carried else [])
        + [
            jax.ShapeDtypeStruct((8 * 4,) + shard.shape[1:], shard.dtype)
            for shard in shards
        ],
        compiler_params=host_params(2, carried),
        cost_estimate=pl.CostEstimate(
            flops=4 * pairs * LANES, bytes_accessed=16 * 1024 * 1024, transcendentals=pairs
        ),
    )(
        meta,
        x_c,
        x_q,
        *weights,
        bias,
        table,
        xcol,
        first_rows,
        other,
        *shards,
    )


def attend_back_kernel(plength, carried, *refs):
    (meta, qc, qx, k_rows, v_rows, table, xcol, xrow, lse_ref, dc, dx, full_c, full_x), refs = (
        refs[:13],
        refs[13:],
    )
    grads, refs = refs[:carried], refs[carried:]
    (dq_c, dq_x, dk_rows, dv_rows, hist), refs = refs[:5], refs[5:]
    shares, refs = refs[:carried], refs[carried:]
    keys, vals, q_all, d_all, scores, dprobs, probs_t, dscores_t, ds_p, dk_acc, dv_acc = refs[:11]
    refs = refs[11:]
    step = pl.program_id(0) * PAIRS + pl.program_id(1)
    if carried:
        net = Net()
        pieces = list(zip(halves_of(grads[0]), halves_of(shares[0])))
        pieces.append((grads[1], shares[1]))
        one, two, proj = (
            reduce_stages(net, src, dst, refs[10 * i : 10 * i + 10])
            for i, (src, dst) in enumerate(pieces)
        )
        hosted([(0, net.greet)], step)
        hosted(
            [
                (0, one[0]),
                (0, two[0]),
                (0, proj[0]),
                (1, one[1]),
                (2, two[1]),
                (3, proj[1]),
                (4, one[2]),
                (5, two[2]),
                (6, proj[2]),
                (6, one[3]),
                (7, two[3]),
                (8, proj[3]),
                (8, one[4]),
                (9, two[4]),
                (10, proj[4]),
                (10, one[5]),
                (11, two[5]),
                (11, proj[5]),
                (11, one[6]),
            ],
            step,
        )
    own_prompt, base, side = place(plength)
    mapped = meta[pl.program_id(0)]
    blocks = plength // 128
    at_k1 = 2 * plength + 256
    n_keys = 2 * plength + 512
    fill_keys(keys, k_rows, own_prompt, mapped, plength)
    fill_keys(vals, v_rows, own_prompt, mapped, plength)
    row = lax.broadcasted_iota(jnp.int32, (128, 128), 0)
    col = lax.broadcasted_iota(jnp.int32, (128, 128), 1)
    tab_a = jnp.broadcast_to(table[0, 0:1, :], (128, 128))
    tab_b = jnp.broadcast_to(table[0, 1:2, :], (128, 128))
    scale = jnp.asarray(0.125, jnp.bfloat16)

    p_at, x_at, c1_at, c0_at = 0, 256, 384, 640
    q_all[0:256] = head_stack(qc[0:PD] * scale)
    q_all[256:384] = head_stack(qx[...] * scale)
    q_all[384:640] = head_stack(qc[PD + 128 : PD + 256] * scale)
    q_all[640:896] = head_stack(qc[PD : PD + 128] * scale)
    d_all[0:256] = head_stack(dc[0:PD])
    d_all[256:384] = head_stack(dx[...])
    d_all[384:640] = head_stack(dc[PD + 128 : PD + 256])
    d_all[640:896] = head_stack(dc[PD : PD + 128])

    ones_lane = lax.broadcasted_iota(jnp.int32, (8, LANES), 1)
    ones_row = lax.broadcasted_iota(jnp.int32, (8, LANES), 0)
    pick = jnp.where((ones_lane < HD) == (ones_row == 0), 1.0, 0.0)
    pick = jnp.where(ones_row < 2, pick, 0.0)

    def deltas(upstream, context):
        product = upstream.astype(jnp.float32) * context
        return lax.dot_general(
            pick,
            product,
            (((1,), (1,)), ((), ())),
            precision=PRECISE,
            preferred_element_type=jnp.float32,
        )

    delta_p = deltas(dc[0:PD], full_c[0:PD])
    delta_0 = deltas(dc[PD : PD + 128], full_c[PD : PD + 128])
    delta_1 = deltas(dc[PD + 128 : PD + 256], full_c[PD + 128 : PD + 256])
    delta_x = deltas(dx[...], full_x[...])
    delta_x = jnp.concatenate([delta_x[0:1], delta_x[1:2]], axis=1)

    def block_back(first, plan, at_col, halves):
        count = len(plan)
        width = 128 * len(halves)
        span = slice(first, first + 128 * count)
        cols = slice(at_col, at_col + width)
        scores[0 : 128 * count, 0:width] = dot_nt(keys[span], q_all[cols])
        dprobs[0 : 128 * count, 0:width] = dot_nt(vals[span], d_all[cols])
        for half, (tables, lse_row, delta) in enumerate(halves):
            lane = slice(128 * half, 128 * half + 128)
            out_lane = slice(at_col + 128 * half, at_col + 128 * half + 128)
            lse = lse_ref[0, 0, lse_row : lse_row + 1, :]
            for at, (index, visible) in enumerate(plan):
                rows = slice(128 * at, 128 * at + 128)
                out_rows = slice(first + 128 * at, first + 128 * at + 128)
                s = scores[rows, lane]
                if index is not None:
                    bias = lookup(tables[0], index)
                    if len(tables) > 1:
                        bias = jnp.where(col < QP, bias, lookup(tables[1], index))
                    s = s + bias
                if visible is not None:
                    s = jnp.where(visible, s, MASKED)
                p = jnp.exp(s - lse)
                ds = p * (dprobs[rows, lane] - delta)
                probs_t[out_rows, out_lane] = p.astype(jnp.bfloat16)
                dscores_t[out_rows, out_lane] = ds.astype(jnp.bfloat16)
                yield half, at, ds

    extra_a = jnp.where(
        (xcol[0, :, 3:4] == lax.broadcasted_iota(jnp.int32, (128, TD), 1))
        & (lax.broadcasted_iota(jnp.int32, (128, TD), 0) < QP),
        1.0,
        0.0,
    ).astype(jnp.bfloat16)
    extra_b = jnp.where(
        (xcol[0, :, 3:4] == lax.broadcasted_iota(jnp.int32, (128, TD), 1))
        & (lax.broadcasted_iota(jnp.int32, (128, TD), 0) >= QP),
        1.0,
        0.0,
    ).astype(jnp.bfloat16)
    spread = (extra_a, extra_b)

    pos = xrow[0, 0:1, :]
    lim_p = xrow[0, 1:2, :]
    lim_c = xrow[0, 2:3, :]
    plan = []
    for b in range(blocks):
        key = row + 128 * b
        plan.append((near_index(pos - key), key < lim_p))
    in_cont = jnp.broadcast_to(lim_c > 0, (128, 128))
    for b in range(blocks - 1):
        plan.append((None, in_cont))
    plan.append((near_index(pos - (row + 128 * (blocks - 1))), in_cont))
    for b in range(2):
        for offset in (1 - side, side):
            key = plength + 2 * (row + 128 * b) + offset
            plan.append((near_index(pos - key), key < lim_c))
    for _ in block_back(0, plan, x_at, [((tab_a, tab_b), 6, delta_x)]):
        pass

    def spread_block(head, key_at, content_at):
        return dot_nn(
            dscores_t[pl.ds(key_at, 128), x_at : x_at + 128],
            spread[head][:, content_at : content_at + 128],
        )

    turn = (col + row) % 128
    turn_half = (col + row // 2) % 128

    def fold(block):
        return jnp.sum(block.reshape(16, 8, LANES), axis=0)

    plan = []
    for b in range(blocks):
        d = base + col - (row + 128 * b)
        plan.append((near_index(d), d >= 0))
    halves = [((tab_a,), 0, delta_p[0:1]), ((tab_b,), 3, delta_p[1:2])]
    for half, at, ds in block_back(0, plan, p_at, halves):
        ds_p[128 * at : 128 * at + 128, 128 * half : 128 * half + 128] = ds
    before = jnp.maximum(base - 128, 0)
    base_at = pl.multiple_of(base, 128)
    before_at = pl.multiple_of(before, 128)
    for head in range(2):
        lane = slice(128 * head, 128 * head + 128)
        here = ds_p[pl.ds(base_at, 128), lane] + spread_block(head, base_at, 0)
        prior = ds_p[pl.ds(before_at, 128), lane] + spread_block(head, before_at, 0)
        prior = jnp.where(base > 0, prior, 0.0)
        both = jnp.where(col >= row, here, prior)
        hist[0, 0, 32 * head : 32 * head + 8] = fold(lookup(both, turn))

    last = 128 + 2 * col + side - row
    near_d = 2 * (col - row) + 2 * side - 1
    own_d = 2 * (col - row)
    far = (None, None)
    plan_0 = [far] * (blocks - 1) + [
        (near_index(last), None),
        (near_index(near_d), near_d >= 0),
        (near_index(own_d), own_d >= 0),
    ]
    plan_1 = [far] * blocks + [
        (near_index(near_d + 256), None),
        (near_index(own_d + 256), None),
        (near_index(near_d), near_d >= 0),
        (near_index(own_d), own_d >= 0),
    ]
    halves = [((tab_a,), 1, delta_0[0:1]), ((tab_b,), 4, delta_0[1:2])]
    near_sum = {}
    own_sum = {}
    last_key = 2 * plength - 128
    for half, at, ds in block_back(plength, plan_0, c0_at, halves):
        if at == blocks - 1:
            ds = ds + spread_block(half, last_key, PD)
            ds = jnp.where(col < 64, ds, 0.0)
            hist[0, 0, 32 * half + 8 : 32 * half + 16] = fold(lookup(ds, turn_half))
        if at == blocks:
            ds = ds + spread_block(half, 2 * plength, PD)
            near_sum[half] = jnp.where(col >= row, ds, 0.0)
        if at == blocks + 1:
            ds = ds + spread_block(half, 2 * plength + 128, PD)
            own_sum[half] = jnp.where(col >= row, ds, 0.0)
    for half in range(2):
        lane = slice(128 * half, 128 * half + 128)
        ds_p[0:128, lane] = near_sum[half]
        ds_p[128:256, lane] = own_sum[half]
    halves = [((tab_a,), 2, delta_1[0:1]), ((tab_b,), 5, delta_1[1:2])]
    for half, at, ds in block_back(plength, plan_1, c1_at, halves):
        lane = slice(128 * half, 128 * half + 128)
        if at == blocks:
            ds = ds + spread_block(half, 2 * plength, PD + 128)
            ds_p[0:128, lane] = ds_p[0:128, lane] + jnp.where(col < row, ds, 0.0)
        if at == blocks + 1:
            ds = ds + spread_block(half, 2 * plength + 128, PD + 128)
            ds_p[128:256, lane] = ds_p[128:256, lane] + jnp.where(col < row, ds, 0.0)
        if at == blocks + 2:
            ds = ds + spread_block(half, at_k1, PD + 128)
            ds = ds_p[0:128, lane] + jnp.where(col >= row, ds, 0.0)
            hist[0, 0, 32 * half + 16 : 32 * half + 24] = fold(lookup(ds, turn))
        if at == blocks + 3:
            ds = ds + spread_block(half, at_k1 + 128, PD + 128)
            ds = ds_p[128:256, lane] + jnp.where(col >= row, ds, 0.0)
            hist[0, 0, 32 * half + 24 : 32 * half + 32] = fold(lookup(ds, turn))

    own = slice(0, plength)
    middle = slice(plength, at_k1)
    end = slice(at_k1, n_keys)
    for acc, left, right in ((dk_acc, dscores_t, q_all), (dv_acc, probs_t, d_all)):
        acc[own] = dot_nn(left[own, 0:384], right[0:384])
        acc[middle] = dot_nn(left[middle, 256:896], right[256:896])
        acc[end] = dot_nn(left[end, 256:640], right[256:640])

    dq_c[0:PD] = (
        head_merge(dot_tn(dscores_t[own, p_at : p_at + 256], keys[own])) * 0.125
    ).astype(jnp.bfloat16)
    dq_c[PD : PD + 128] = (
        head_merge(dot_tn(dscores_t[middle, c0_at : c0_at + 256], keys[middle])) * 0.125
    ).astype(jnp.bfloat16)
    cont = slice(plength, n_keys)
    dq_c[PD + 128 : PD + 256] = (
        head_merge(dot_tn(dscores_t[cont, c1_at : c1_at + 256], keys[cont])) * 0.125
    ).astype(jnp.bfloat16)
    out = dot_tn(dscores_t[:, x_at : x_at + 128], keys[...])
    lane = lax.broadcasted_iota(jnp.int32, (QP, LANES), 1)
    dq_x[...] = (jnp.where(lane < HD, out[0:QP], out[QP:]) * 0.125).astype(jnp.bfloat16)

    for out_ref, acc in ((dk_rows, dk_acc), (dv_rows, dv_acc)):
        for p in range(2):
            mine = jnp.where(own_prompt == p, acc[own], 0.0)
            other = jnp.where(mapped == p, acc[plength : 2 * plength], 0.0)
            out_ref[p * plength : (p + 1) * plength] = (mine + other).astype(jnp.bfloat16)
        out_ref[2 * plength :] = acc[2 * plength :].astype(jnp.bfloat16)
    if carried:
        rest = (two[6], proj[6], one[7], two[7], proj[7])
        hosted([(11, stage) for stage in rest], step)


def attend_back(
    meta, queries, extra_q, k_rows, v_rows, table, xcol, xrow, lse, dc, dx, fc, fx, grads
):
    carried = len(grads)
    sizes, kept = [], []
    if carried:
        part, width = grads[0].shape[3:]
        tall, narrow = grads[1].shape[3:]
        sizes = [(4 * part, width // 2)] * 2 + [(4 * tall, narrow)]
        kept = [jax.ShapeDtypeStruct((4,) + grad.shape[3:], jnp.bfloat16) for grad in grads]
    n_keys = k_rows.shape[0] // MICRO
    plength = (n_keys - 2 * CH) // 2
    content = pl.BlockSpec((TD, LANES), pair_column())
    extra = pl.BlockSpec((QP, LANES), pair_column())
    own_row = plength + 2 * CH
    pairs = MICRO * PAIRS * 2 * (128 * plength + 256 * own_row) + MICRO * PAIRS * 128 * n_keys
    return pl.pallas_call(
        functools.partial(attend_back_kernel, plength, carried),
        name="attend_back",
        grid_spec=pltpu.PrefetchScalarGridSpec(
            num_scalar_prefetch=1,
            grid=(MICRO, PAIRS),
            in_specs=[content, extra]
            + [
                key_spec(n_keys),
                key_spec(n_keys),
                TABLE_SPEC,
                pl.BlockSpec((1, 128, 8), lambda m, j, meta: (m, 0, 0)),
                pl.BlockSpec((1, 8, 128), lambda m, j, meta: (m, 0, 0)),
                pl.BlockSpec((1, 1, 8, LANES), lambda m, j, meta: (m, j, 0, 0)),
                content,
                extra,
                content,
                extra,
            ]
            + [ANY_SPEC] * carried,
            out_specs=[
                content,
                extra,
                key_spec(n_keys),
                key_spec(n_keys),
                pl.BlockSpec((1, 1, 64, LANES), lambda m, j, meta: (m, j, 0, 0)),
            ]
            + [ANY_SPEC] * carried,
            scratch_shapes=[
                pltpu.VMEM((n_keys, LANES), jnp.bfloat16),
                pltpu.VMEM((n_keys, LANES), jnp.bfloat16),
                pltpu.VMEM((896, LANES), jnp.bfloat16),
                pltpu.VMEM((896, LANES), jnp.bfloat16),
                pltpu.VMEM((n_keys, 256), jnp.float32),
                pltpu.VMEM((n_keys, 256), jnp.float32),
                pltpu.VMEM((n_keys, 896), jnp.bfloat16),
                pltpu.VMEM((n_keys, 896), jnp.bfloat16),
                pltpu.VMEM((plength, 256), jnp.float32),
                pltpu.VMEM((n_keys, LANES), jnp.float32),
                pltpu.VMEM((n_keys, LANES), jnp.float32),
            ]
            + [buffer for size in sizes for buffer in reduce_buffers(*size)],
        ),
        out_shape=[
            jax.ShapeDtypeStruct((MICRO * TD, D), jnp.bfloat16),
            jax.ShapeDtypeStruct((MICRO * QP, D), jnp.bfloat16),
            jax.ShapeDtypeStruct((MICRO * n_keys, D), jnp.bfloat16),
            jax.ShapeDtypeStruct((MICRO * n_keys, D), jnp.bfloat16),
            jax.ShapeDtypeStruct((MICRO, PAIRS, 64, LANES), jnp.float32),
        ]
        + kept,
        compiler_params=host_params(3, carried),
        cost_estimate=pl.CostEstimate(
            flops=10 * pairs * LANES, bytes_accessed=32 * 1024 * 1024, transcendentals=pairs
        ),
    )(
        meta,
        queries,
        extra_q,
        k_rows,
        v_rows,
        table,
        xcol,
        xrow,
        lse,
        dc,
        dx,
        fc,
        fx,
        *grads,
    )


def from_partner(block, axis):
    count = lax.axis_size(axis)
    return lax.ppermute(block, axis, [(i, i ^ 1) for i in range(count)])


TAIL_RATE = 0.24
TAIL = (
    0.08952757299725976,
    0.1555125511021828,
    -0.15404562880205064,
    0.6255850035411683,
    -0.6460658211054147,
    0.554571568104313,
    -0.12508524614530675,
)


def gelu_parts(hidden):
    bell = jnp.exp(-0.5 * hidden * hidden)
    t = 1.0 / (1.0 + TAIL_RATE * jnp.abs(hidden))
    poly = TAIL[-1]
    for term in TAIL[-2::-1]:
        poly = poly * t + term
    tail = poly * t * bell
    cdf = jnp.where(hidden < 0.0, tail, 1.0 - tail)
    return hidden * cdf, cdf + hidden * bell * 0.3989422804014327


TILE = 448
GRAD_STEPS = 9


def fold_rows(term):
    return jnp.sum(term.reshape(-1, 8, term.shape[1]), axis=0)


def middle_kernel(
    x,
    ctx,
    cot,
    w_out,
    w_up_ref,
    w_down_ref,
    vec,
    up_bias,
    out_c,
    out_x,
    dres,
    dctx_c,
    dctx_x,
    g_down,
    g_up,
    g_out,
    sums_out,
    act,
    dhid,
    slope,
    first_b,
    dres_two_b,
    dres_one_b,
    norm_one,
    inverse_one,
    work,
    outs,
    dctx,
    sums,
    sems,
    w_up,
    w_down,
    load_sems,
):
    step = pl.program_id(0)
    load_up = pltpu.make_async_copy(w_up_ref, w_up, load_sems.at[0])
    load_down = pltpu.make_async_copy(w_down_ref, w_down, load_sems.at[1])
    width = w_up.shape[1]
    rows_c = out_c.shape[0]
    tiles = x.shape[0] // TILE
    out_bias, gain_one, shift_one = vec[0:1], vec[1:2], vec[2:3]
    down_bias, gain_two, shift_two = vec[3:4], vec[4:5], vec[5:6]
    split = rows_c - TILE
    moves = [
        [
            (outs.at[pl.ds(0, TILE)], out_c.at[pl.ds(0, TILE)]),
            (dctx.at[pl.ds(0, TILE)], dctx_c.at[pl.ds(0, TILE)]),
        ],
        [
            (outs.at[pl.ds(TILE, split)], out_c.at[pl.ds(TILE, split)]),
            (dctx.at[pl.ds(TILE, split)], dctx_c.at[pl.ds(TILE, split)]),
            (outs.at[pl.ds(rows_c, 2 * QP)], out_x),
            (dctx.at[pl.ds(rows_c, 2 * QP)], dctx_x),
        ],
    ]
    count = 0
    for group in moves:
        for i, (src, dst) in enumerate(group):
            group[i] = pltpu.make_async_copy(src, dst, sems.at[count])
            count += 1

    def mean(value):
        return jnp.mean(value, axis=-1, keepdims=True)

    @pl.when(step == 0)
    def _():
        load_up.start()
        load_down.start()
        sums[...] = jnp.zeros_like(sums)

    @pl.when(step < tiles)
    def _():
        base = pl.multiple_of(step * TILE, 64)
        rows = pl.ds(base, TILE)
        work[...] = dot_nn(ctx[rows], w_out[...])

        value = x[rows].astype(jnp.float32) + work[...] + out_bias
        centred = value - mean(value)
        inverse = lax.rsqrt(mean(centred * centred) + 1e-05)
        normed = centred * inverse
        norm_one[...] = normed
        inverse_one[...] = jnp.broadcast_to(inverse, (TILE, LANES))
        first_b[rows] = (normed * gain_one + shift_one).astype(jnp.bfloat16)

        @pl.when(step == 0)
        def _():
            load_up.wait()

        parts = 12
        block = width // parts

        def lift(c):
            cols = slice(block * c, block * c + block)
            slope[:, cols] = dot_nn(first_b[rows], w_up[:, cols])

        lift(0)
        for c in range(parts):
            cols = slice(block * c, block * c + block)
            if c + 1 < parts:
                lift(c + 1)
            active, gradient = gelu_parts(slope[:, cols] + up_bias[0:1, cols])
            act[rows, cols] = active.astype(jnp.bfloat16)
            slope[:, cols] = gradient

        @pl.when(step == 0)
        def _():
            load_down.wait()

        work[...] = dot_nn(act[rows], w_down[...])

        value = norm_one[...] * gain_one + shift_one + work[...] + down_bias
        centred = value - mean(value)
        inverse = lax.rsqrt(mean(centred * centred) + 1e-05)
        normed = centred * inverse
        outs[rows] = normed * gain_two + shift_two
        upstream = cot[rows].astype(jnp.float32)
        scaled = upstream * gain_two
        grad = inverse * (scaled - mean(scaled) - normed * mean(scaled * normed))
        work[...] = grad
        dres_two_b[rows] = grad.astype(jnp.bfloat16)
        for k, term in enumerate((upstream * normed, upstream, grad)):
            sums[8 * k : 8 * k + 8, 0:D] += fold_rows(term)

        block = width // 12
        for c in range(12):
            cols = slice(block * c, block * c + block)
            dact = dot_nt(dres_two_b[rows], w_down[cols]).astype(jnp.bfloat16)
            grad = dact.astype(jnp.float32) * slope[:, cols]
            grad_b = grad.astype(jnp.bfloat16)
            dhid[rows, cols] = grad_b
            sums[48:56, cols] += jnp.sum(
                grad_b.astype(jnp.float32).reshape(TILE // 8, 8, block), axis=0
            )
        work[...] += dot_nt(dhid[rows], w_up[...])

        normed = norm_one[...]
        inverse = inverse_one[:, 0:1]
        upstream = work[...]
        scaled = upstream * gain_one
        grad = inverse * (scaled - mean(scaled) - normed * mean(scaled * normed))
        dres[...] = grad
        dres_one_b[rows] = grad.astype(jnp.bfloat16)
        for k, term in enumerate((upstream * normed, upstream, grad)):
            sums[24 + 8 * k : 32 + 8 * k, 0:D] += fold_rows(term)

        dctx[rows] = dot_nt(dres_one_b[rows], w_out[...]).astype(jnp.bfloat16)

    for tile in range(2):

        @pl.when(step == tile)
        def _():
            for copy in moves[tile]:
                copy.start()

    quarter = width // 4
    for c in range(4):
        cols = slice(quarter * c, quarter * c + quarter)

        @pl.when(step == tiles + c)
        def _():
            g_down[...] = dot_tn(act[:, cols], dres_two_b[...]).astype(jnp.bfloat16)

        @pl.when(step == tiles + 4 + c)
        def _():
            g_up[...] = dot_tn(first_b[...], dhid[:, cols]).astype(jnp.bfloat16)

    @pl.when(step == tiles + 8)
    def _():
        g_out[...] = dot_tn(ctx[...], dres_one_b[...]).astype(jnp.bfloat16)
        for k in range(7):
            sums_out[k : k + 1] = jnp.sum(sums[8 * k : 8 * k + 8], axis=0, keepdims=True)
        sums_out[7:8] = jnp.zeros_like(sums_out[7:8])
        for group in moves:
            for copy in group:
                copy.wait()


def middle(x, ctx, cot, w_out, w_up, w_down, vec, up_bias):
    rows = x.shape[0]
    rows_c = MICRO * TD
    width = w_up.shape[1]
    tiles = rows // TILE
    quarter = width // 4
    def once(array):
        return pl.BlockSpec(array.shape, lambda s: (0, 0), pipeline_mode=pl.Buffered(1))

    bf, f32 = jnp.bfloat16, jnp.float32
    return pl.pallas_call(
        middle_kernel,
        name="middle",
        grid=(tiles + GRAD_STEPS,),
        in_specs=[
            once(x),
            once(ctx),
            once(cot),
            once(w_out),
            ANY_SPEC,
            ANY_SPEC,
            once(vec),
            once(up_bias),
        ],
        out_specs=[
            ANY_SPEC,
            ANY_SPEC,
            pl.BlockSpec((TILE, D), lambda s: (jnp.minimum(s, tiles - 1), 0)),
            ANY_SPEC,
            ANY_SPEC,
            pl.BlockSpec((quarter, D), lambda s: (jnp.clip(s - tiles, 0, 3), 0)),
            pl.BlockSpec((D, quarter), lambda s: (0, jnp.clip(s - tiles - 4, 0, 3))),
            pl.BlockSpec((D, D), lambda s: (0, 0)),
            pl.BlockSpec((8, width), lambda s: (0, 0)),
        ],
        out_shape=[
            jax.ShapeDtypeStruct((rows_c, D), f32),
            jax.ShapeDtypeStruct((rows - rows_c, D), f32),
            jax.ShapeDtypeStruct((rows, D), f32),
            jax.ShapeDtypeStruct((rows_c, D), bf),
            jax.ShapeDtypeStruct((rows - rows_c, D), bf),
            jax.ShapeDtypeStruct((width, D), bf),
            jax.ShapeDtypeStruct((D, width), bf),
            jax.ShapeDtypeStruct((D, D), bf),
            jax.ShapeDtypeStruct((8, width), f32),
        ],
        scratch_shapes=[
            pltpu.VMEM((rows, width), bf),
            pltpu.VMEM((rows, width), bf),
            pltpu.VMEM((TILE, width), f32),
            pltpu.VMEM((rows, D), bf),
            pltpu.VMEM((rows, D), bf),
            pltpu.VMEM((rows, D), bf),
            pltpu.VMEM((TILE, D), f32),
            pltpu.VMEM((TILE, LANES), f32),
            pltpu.VMEM((TILE, D), f32),
            pltpu.VMEM((rows, D), f32),
            pltpu.VMEM((rows, D), bf),
            pltpu.VMEM((56, width), f32),
            pltpu.SemaphoreType.DMA((6,)),
            pltpu.VMEM(w_up.shape, bf),
            pltpu.VMEM(w_down.shape, bf),
            pltpu.SemaphoreType.DMA((2,)),
        ],
        compiler_params=pltpu.CompilerParams(vmem_limit_bytes=60 * 1024 * 1024),
        cost_estimate=pl.CostEstimate(
            flops=2 * rows * D * (6 * width + 3 * D),
            bytes_accessed=40 * 1024 * 1024,
            transcendentals=2 * rows * width,
        ),
    )(x, ctx, cot, w_out, w_up, w_down, vec, up_bias)


SMALL_ROWS = 32


def table_rows(hist, buckets_of, side):
    lane = lax.broadcasted_iota(jnp.int32, (LANES, LANES), 0)
    target = lax.broadcasted_iota(jnp.int32, (LANES, LANES), 1)
    signed = jnp.where(lane < 64, lane, lane - 128)
    distances = (
        lane,
        128 + side + 2 * signed,
        127 + side + 2 * signed,
        2 * lane + 2 * side - 1,
        2 * lane,
    )
    kinds = [[] for _ in distances]
    row = lax.broadcasted_iota(jnp.int32, (8, LANES), 0)
    for pair in range(PAIRS):
        for head in range(2):
            block = [
                sum(hist[m, pair, 32 * head + 8 * k : 32 * head + 8 * k + 8] for m in range(MICRO))
                for k in range(4)
            ]
            picks = (
                block[0],
                jnp.where(row % 2 == 0, block[1], 0.0),
                jnp.where(row % 2 == 0, 0.0, block[1]),
                block[2],
                block[3],
            )
            for kind, pick in zip(kinds, picks):
                kind.append(jnp.sum(pick, axis=0, keepdims=True))
    pad = [jnp.zeros((16 - 2 * PAIRS, LANES), jnp.float32)]
    close = jnp.zeros((16, LANES), jnp.float32)
    for kind, distance in zip(kinds, distances):
        hot = jnp.where((distance == target) & (target < LANES - 1), 1.0, 0.0)
        close = close + jnp.dot(
            jnp.concatenate(kind + pad, axis=0),
            hot,
            precision=PRECISE,
            preferred_element_type=jnp.float32,
        )
    last = lax.broadcasted_iota(jnp.int32, (16, LANES), 1) == LANES - 1
    close = jnp.where(last, -jnp.sum(close, axis=1, keepdims=True), close)
    bucket_hot = jnp.where(lane == buckets_of[0:1], 1.0, 0.0)
    return lax.dot_general(
        close,
        bucket_hot,
        (((1,), (1,)), ((), ())),
        precision=PRECISE,
        preferred_element_type=jnp.float32,
    )


def finish_kernel(
    dq_c,
    dq_x,
    dk,
    dv,
    keys_0,
    keys_1,
    x_c,
    x_q,
    w_q,
    w_k,
    w_v,
    dres,
    hist,
    buckets_of,
    sums,
    d_ref,
    q_share,
    k_share,
    v_share,
    d_share,
    small_out,
    grad_c,
    grad_q,
    *scratch,
):
    shares = (q_share, k_share, v_share, d_share)
    buffers = [scratch[10 * i : 10 * i + 10] for i in range(4)]
    (
        grads,
        prompts,
        theirs,
        along,
        nears,
        near_got,
        owns,
        out_c,
        small,
        x_s,
        x_r,
        sm_s,
        sm_r,
        sem,
    ) = scratch[40:]
    net = Net()
    net.greet()
    sources = [grads.at[i] for i in range(3)] + [d_ref]
    one, two, three, down = (
        reduce_stages(net, sources[i], shares[i], buffers[i]) for i in range(4)
    )
    down[0]()
    copies = Copies(x_s, x_r)
    to_mate = [
        copies.to(net.to_mate, prompts.at[m, :, 1 - net.c], theirs.at[m]) for m in range(MICRO)
    ]
    swap = copies.to(net.to_mate, nears, near_got)
    third, relay = [], []
    for m in range(MICRO):
        third.append(
            [
                copies.to(net.to_z[0], prompts.at[m, net.z_of[2], net.c], along.at[0, m]),
                copies.to(net.to_z[0], prompts.at[m, net.z_of[0], net.c], along.at[1, m]),
            ]
        )
        passed = prompts.at[m, net.z_of[1], net.c]
        relay.append(copies.to(net.to_z[1], passed, along.at[2, m]))
    hops = Copies(sm_s, sm_r)
    partners = [net.to_mate, net.to_x, net.to_y, net.to_z[0], net.to_z[1]]
    butterfly = [
        hops.to(partner, small.at[i], small.at[i + 1]) for i, partner in enumerate(partners)
    ]

    def hop(i):
        butterfly[i].wait_recv()
        small[i + 1] = small[i + 1] + small[i]
        if i + 1 < len(butterfly):
            butterfly[i + 1].start()

    n_keys = dk.shape[0] // MICRO
    n_prompt = n_keys - 2 * CH

    def put(value, which):
        part = D // 32
        for owner in range(8):
            for q in range(4):
                at = (4 * owner + q) * part
                grads[which, owner // 2, owner % 2, q] = value[at : at + part].astype(
                    jnp.bfloat16
                )

    def back(rows):
        return dot_nt(dk[rows], w_k[...]) + dot_nt(dv[rows], w_v[...])

    def onward(m):
        to_mate[m].wait_recv()

        @pl.loop(0, 4)
        def _(zi):
            prompts[m, zi, net.c] = prompts[m, zi, net.c] + theirs[m, zi]

        start(third[m])

    def onto(m):
        third[m][0].wait_recv()
        prompts[m, net.z_of[1], net.c] = prompts[m, net.z_of[1], net.c] + along[0, m]
        relay[m].start()

    for m in range(MICRO):
        for part in range(n_prompt // 512):
            value = back(slice(m * n_keys + 512 * part, m * n_keys + 512 * part + 512))
            for i in range(4):
                owner = 4 * part + i
                prompts[m, owner // 2, owner % 2] = value[128 * i : 128 * i + 128].astype(
                    jnp.bfloat16
                )
        to_mate[m].start()
        if m == 0:
            down[1]()
    put(dot_tn(x_c[...], dq_c[...]) + dot_tn(x_q[...], dq_x[...]), 0)
    one[0]()
    onward(0)
    put(dot_tn(keys_0[...], dk[:n_keys]) + dot_tn(keys_1[...], dk[n_keys:]), 1)
    two[0]()
    onward(1)
    one[1]()
    put(dot_tn(keys_0[...], dv[:n_keys]) + dot_tn(keys_1[...], dv[n_keys:]), 2)
    three[0]()
    two[1]()
    onto(0)
    down[2]()

    small[0] = jnp.zeros_like(small[0])
    sum_q = jnp.sum(dq_c[...].astype(jnp.float32), axis=0, keepdims=True)
    sum_q = sum_q + jnp.sum(dq_x[...].astype(jnp.float32), axis=0, keepdims=True)
    small[0, 0:1] = sum_q
    small[0, 1:2] = jnp.sum(dv[...].astype(jnp.float32), axis=0, keepdims=True)
    for i in range(6):
        small[0, 2 + i : 3 + i] = sums[i : i + 1, 0:D]
    for i in range(4):
        small[0, 8 + i : 9 + i] = sums[6:7, D * i : D * i + D]
    small[0, 16:32, 0:LANES] = table_rows(hist, buckets_of, net.c)
    butterfly[0].start()
    three[1]()
    one[2]()
    for m in range(MICRO):
        value = back(slice(m * n_keys + n_prompt, (m + 1) * n_keys))
        for i in range(2):
            nears[m, i] = value[256 * i : 256 * i + 128].astype(jnp.bfloat16)
            owns[m, i] = value[256 * i + 128 : 256 * i + 256]
    swap.start()
    onto(1)
    two[2]()
    hop(0)
    rows_c = x_c.shape[0]
    out_c[0:rows_c] = dres[0:rows_c] + dot_nt(dq_c[...], w_q[...])
    out_c[rows_c:] = dres[rows_c:] + dot_nt(dq_x[...], w_q[...])
    down[3]()
    one[3]()
    three[2]()
    hop(1)
    two[3]()
    one[4]()
    swap.wait_recv()
    for m in range(MICRO):
        for i in range(2):
            rows = slice(m * TD + PD + 128 * i, m * TD + PD + 128 * i + 128)
            out_c[rows] = out_c[rows] + owns[m, i] + near_got[m, i].astype(jnp.float32)
    three[3]()
    hop(2)
    two[4]()
    down[4]()
    one[5]()
    hop(3)
    three[4]()
    two[5]()
    for m in range(MICRO):
        arrive([third[m][1], relay[m]])
        total = prompts[m, net.z, net.c].astype(jnp.float32)
        for k in range(1, 3):
            total = total + along[k, m].astype(jnp.float32)
        rows = slice(m * TD, m * TD + PD)
        out_c[rows] = out_c[rows] + total
    stores = [
        pltpu.make_async_copy(out_c.at[pl.ds(0, rows_c)], grad_c, sem.at[0]),
        pltpu.make_async_copy(out_c.at[pl.ds(rows_c, 2 * QP)], grad_q, sem.at[1]),
    ]
    start(stores)
    one[6]()
    down[5]()
    three[5]()
    hop(4)
    keep = pltpu.make_async_copy(small.at[5], small_out, sem.at[2])
    keep.start()
    two[6]()
    one[7]()
    down[6]()
    three[6]()
    two[7]()
    down[7]()
    three[7]()
    for copy in stores + [keep]:
        copy.wait()
    copies.finish()
    hops.finish()


def finish(
    dq_c,
    dq_x,
    dk,
    dv,
    keys_x,
    x_c,
    x_q,
    weights,
    dres,
    hist,
    buckets_of,
    sums,
    down_grad,
):
    whole = pl.BlockSpec(memory_space=pltpu.VMEM)
    bf, f32 = jnp.bfloat16, jnp.float32
    rows_c, rows_x = x_c.shape[0], x_q.shape[0]
    part, tall = D // 32, down_grad.shape[3]
    return pl.pallas_call(
        finish_kernel,
        name="finish",
        in_specs=[whole] * 15 + [ANY_SPEC],
        out_specs=[ANY_SPEC] * 7,
        out_shape=[
            jax.ShapeDtypeStruct((4, part, D), bf),
            jax.ShapeDtypeStruct((4, part, D), bf),
            jax.ShapeDtypeStruct((4, part, D), bf),
            jax.ShapeDtypeStruct((4, tall, D), bf),
            jax.ShapeDtypeStruct((SMALL_ROWS, D), f32),
            jax.ShapeDtypeStruct((rows_c, D), f32),
            jax.ShapeDtypeStruct((rows_x, D), f32),
        ],
        scratch_shapes=reduce_buffers(4 * part, D) * 3
        + reduce_buffers(4 * tall, D)
        + [
            pltpu.VMEM((3, 4, 2, 4, part, D), bf),
            pltpu.VMEM((MICRO, 4, 2, PD, D), bf),
            pltpu.VMEM((MICRO, 4, PD, D), bf),
            pltpu.VMEM((3, MICRO, PD, D), bf),
            pltpu.VMEM((MICRO, 2, 128, D), bf),
            pltpu.VMEM((MICRO, 2, 128, D), bf),
            pltpu.VMEM((MICRO, 2, 128, D), f32),
            pltpu.VMEM((rows_c + rows_x, D), f32),
            pltpu.VMEM((6, SMALL_ROWS, D), f32),
            pltpu.SemaphoreType.DMA((9,)),
            pltpu.SemaphoreType.DMA((9,)),
            pltpu.SemaphoreType.DMA((5,)),
            pltpu.SemaphoreType.DMA((5,)),
            pltpu.SemaphoreType.DMA((3,)),
        ],
        compiler_params=pltpu.CompilerParams(
            collective_id=4, has_side_effects=True, vmem_limit_bytes=60 * 1024 * 1024
        ),
    )(dq_c, dq_x, dk, dv, *keys_x, x_c, x_q, *weights, dres, hist, buckets_of, sums, down_grad)


def pad_rows(block):
    return jnp.pad(block, ((0, 0), (0, QP - block.shape[1]), (0, 0))).reshape(MICRO * QP, D)


def table_gradient(hist, rel_bucket, buckets, side, heads):
    summed = jnp.sum(hist, axis=0).reshape(PAIRS, 2, 4, 8, LANES)
    prompt = jnp.sum(summed[:, :, 0], axis=2)
    even = jnp.sum(summed[:, :, 1, 0::2], axis=2)
    odd = jnp.sum(summed[:, :, 1, 1::2], axis=2)
    near = jnp.sum(summed[:, :, 2], axis=2)
    own = jnp.sum(summed[:, :, 3], axis=2)
    lanes = jnp.arange(LANES, dtype=jnp.int32)
    signed = jnp.where(lanes < 64, lanes, lanes - 128)
    distance = jnp.stack(
        [
            lanes,
            128 + side + 2 * signed,
            127 + side + 2 * signed,
            2 * lanes + 2 * side - 1,
            2 * lanes,
        ]
    ).reshape(-1)
    hot = (distance[:, None] == lanes[None, :]) & (lanes[None, :] < LANES - 1)
    parts = jnp.stack([prompt, even, odd, near, own], axis=2).reshape(heads, 5 * LANES)
    close = jnp.dot(parts, hot.astype(jnp.float32), precision=PRECISE)
    close = jnp.where(
        lanes[None, :] == LANES - 1, -jnp.sum(close, axis=1, keepdims=True), close
    )
    bucket_hot = (rel_bucket[:, None] == jnp.arange(buckets, dtype=jnp.int32)[None, :]).astype(
        jnp.float32
    )
    return jnp.dot(bucket_hot.T, close.T, precision=PRECISE)


def on_device(
    content_in,
    query_in,
    pred_order,
    cont_prompt,
    rel_bucket,
    w_query,
    b_query,
    w_key,
    w_value,
    b_value,
    w_out,
    b_out,
    ln1_gain,
    ln1_bias,
    w_up,
    b_up,
    w_down,
    b_down,
    ln2_gain,
    ln2_bias,
    bias_table,
    cot_content,
    cot_query,
):
    devices = lax.axis_size("fsdp")
    halfway = devices // 2
    own_rank = lax.axis_index("fsdp")
    plength = PD * halfway
    heads = bias_table.shape[1]
    extra_rows = query_in.shape[1]
    prompt_base = own_rank % halfway * PD
    cont_index = own_rank // 2
    side = own_rank % 2

    own_links = lax.axis_size("grp") == 4 and devices == 8

    def gather(entry):
        return lax.all_gather(entry, "fsdp", axis=0, tiled=True)

    def quarters(entry):
        return entry.reshape(4, -1, entry.shape[1])

    n_keys = 2 * plength + 2 * CH
    shard = b_query.shape[0]
    up_size = b_up.shape[0]
    vectors = jnp.stack(
        [b_query, b_value, b_out, b_down, ln1_gain, ln1_bias, ln2_gain, ln2_bias]
        + [b_up[shard * i : shard * i + shard] for i in range(up_size // shard)]
    )
    tokens_x = content_in.reshape(MICRO * TD, D)
    extra_x = pad_rows(query_in)
    if own_links:
        lines = vectors.shape[0]
        vector_shard = jnp.pad(vectors, ((0, 32 - lines), (0, 256 - shard))).reshape(4, 8, 256)
        *qkv_weights, all_vectors, first_rows = gather_first(
            [quarters(w_query), quarters(w_key), quarters(w_value), vector_shard], content_in
        )
        qkv_weights = [entry.reshape(-1, D) for entry in qkv_weights]
        all_vectors = all_vectors.reshape(devices, 32, 256)[:, :lines, :shard]
        other = content_in
        carried = tuple(quarters(shard) for shard in (w_up, w_down, w_out))
    else:
        qkv_weights = [gather(w_query), gather(w_key), gather(w_value)]
        all_vectors = gather(vectors[None])
        up_weight, down_weight, out_weight = gather(w_up), gather(w_down), gather(w_out)
        carried = ()
        prompt_x = lax.all_gather(content_in[:, :PD], "fsdp", axis=1, tiled=True)
        near_x = from_partner(content_in[:, PD:], "fsdp").reshape(MICRO, 2, 1, 128, D)
        own_x = content_in[:, PD:].reshape(MICRO, 2, 1, 128, D)
        cont_x = jnp.concatenate([near_x, own_x], axis=2).reshape(MICRO, 2 * CH, D)
        first_rows, other = jnp.concatenate([prompt_x, cont_x], axis=1)
    singles = [
        all_vectors[:, i].reshape(-1).astype(jnp.float32)
        for i in range(8)
    ]
    (
        query_bias,
        value_bias,
        out_bias,
        down_bias,
        gain_one,
        shift_one,
        gain_two,
        shift_two,
    ) = singles
    up_bias = all_vectors[:, 8:].reshape(-1).astype(jnp.float32)

    prompt_map = cont_prompt[:, 0, :]
    prompt_ref = jnp.sum(
        jnp.where(
            jnp.arange(prompt_map.shape[1], dtype=jnp.int32)[None, :] == cont_index, prompt_map, 0
        ),
        axis=1,
    )
    meta = prompt_ref.astype(jnp.int32)
    order = jnp.pad(pred_order[:, 0, :], ((0, 0), (0, QP - extra_rows)), constant_values=-1)
    real = order >= 0
    in_prompt = order < PD
    position = jnp.where(
        in_prompt, prompt_base + order, plength + 2 * (order - PD) + side
    )
    limit_p = jnp.where(real & in_prompt, jnp.maximum(position, 1), -1)
    limit_c = jnp.where(real & ~in_prompt, position, -1)
    info = jnp.stack([position, limit_p, limit_c, order], axis=1)
    info = jnp.concatenate([info, info], axis=2)
    xrow = jnp.pad(info, ((0, 0), (0, 4), (0, 0))).astype(jnp.int32)
    xcol = jnp.swapaxes(xrow, 1, 2)
    dist = bias_table.astype(jnp.float32)[rel_bucket].T
    dist = dist - dist[:, LANES - 1 :]
    table = jnp.pad(dist.reshape(PAIRS, 2, LANES), ((0, 0), (0, 6), (0, 0)))

    x_all = jnp.concatenate([tokens_x, extra_x])
    bias = jnp.pad(jnp.stack([query_bias, value_bias]), ((0, 6), (0, 0)))
    ctx_c, ctx_x, full_c, full_x, lse, queries, extra_q, k_rows, v_rows, *gathered = attend(
        meta, tokens_x, extra_x, qkv_weights, bias, table, xcol, first_rows, other, carried
    )
    keys_x = (first_rows, other)
    if own_links:
        keys_x = (first_rows, gathered[0])
        up_weight, down_weight, out_weight = (
            entry.reshape(-1, entry.shape[2]) for entry in gathered[1:]
        )
    rows_c = MICRO * TD
    context = jnp.concatenate([ctx_c, ctx_x])
    upstream = jnp.concatenate([cot_content.reshape(rows_c, D), pad_rows(cot_query)])
    vec = jnp.stack([out_bias, gain_one, shift_one, down_bias, gain_two, shift_two])
    (
        out_content,
        out_query,
        dres_one,
        dctx_c,
        dctx_x,
        dweight_down,
        dweight_up,
        dweight_out,
        sums,
    ) = middle(
        x_all, context, upstream, out_weight, up_weight, down_weight, vec, up_bias[None]
    )
    out_content = out_content.reshape(MICRO, TD, D)
    out_query = out_query.reshape(MICRO, QP, D)[:, :extra_rows]

    def by_quarter(grad):
        grad = grad.astype(jnp.bfloat16)
        return grad.reshape(4, 2, 4, grad.shape[0] // 32, grad.shape[1])

    to_reduce = ()
    if own_links:
        to_reduce = (by_quarter(dweight_up), by_quarter(dweight_out))
    dq_c, dq_x, dk_rows, dv_rows, hist, *reduced = attend_back(
        meta,
        queries,
        extra_q,
        k_rows,
        v_rows,
        table,
        xcol,
        xrow,
        lse,
        dctx_c,
        dctx_x,
        full_c,
        full_x,
        to_reduce,
    )
    if own_links:
        *t_qkv, t_down, small, grad_content, grad_query = finish(
            dq_c,
            dq_x,
            dk_rows,
            dv_rows,
            keys_x,
            tokens_x,
            extra_x,
            qkv_weights,
            dres_one,
            hist,
            jnp.broadcast_to(rel_bucket[None], (8, LANES)),
            sums,
            by_quarter(dweight_down),
        )
        grad_content = grad_content.reshape(MICRO, TD, D)
        grad_query = grad_query.reshape(MICRO, QP, D)[:, :extra_rows]
        t_up, t_out = reduced
        shares = (t_down, t_up, t_out, *t_qkv)
        t_down, t_up, t_out, *t_qkv = [
            entry.reshape(-1, entry.shape[-1]).astype(jnp.float32) for entry in shares
        ]
        pieces = lax.dynamic_slice_in_dim(small[:8], own_rank * shard, shard, 1)
        t_bup = lax.dynamic_index_in_dim(
            small[8:12].reshape(devices, up_size), own_rank, 0, keepdims=False
        )
        t_table = lax.dynamic_slice_in_dim(
            small[16 : 16 + heads, : bias_table.shape[0]],
            own_rank * (bias_table.shape[0] // devices),
            bias_table.shape[0] // devices,
            1,
        ).T
    else:
        dgain_two, dshift_two, dbias_down, dgain_one, dshift_one, dbias_out = sums[:6, :D]
        dbias_up = sums[6]
        dkv_rows = jnp.concatenate([dk_rows, dv_rows], axis=1)
        dq_all = jnp.concatenate([dq_c, dq_x])
        dbias_query = jnp.sum(dq_all.astype(jnp.float32), axis=0)
        dbias_value = jnp.sum(dv_rows.astype(jnp.float32), axis=0)
        query_weight, key_weight, value_weight = qkv_weights
        kv_weight = jnp.concatenate([key_weight, value_weight], axis=1)
        keys_x = jnp.concatenate(keys_x)
        dkeys_x = dot_nt(dkv_rows, kv_weight).reshape(MICRO, n_keys, D)
        dtable = table_gradient(hist, rel_bucket, bias_table.shape[0], side, heads)
        small = jnp.concatenate(
            [
                entry.reshape(devices, -1)
                for entry in (
                    dbias_query,
                    dbias_value,
                    dgain_two,
                    dshift_two,
                    dbias_down,
                    dgain_one,
                    dshift_one,
                    dbias_out,
                    dbias_up,
                    dtable,
                )
            ],
            axis=1,
        ).astype(jnp.bfloat16)
        dprompts = dkeys_x[:, : 2 * plength].astype(jnp.bfloat16)
        dcont = dkeys_x[:, 2 * plength :].reshape(MICRO, 2, 2, 128, D)
        dnear = dcont[:, :, 0].astype(jnp.bfloat16)
        dweight_qkv = jnp.concatenate(
            [dot_tn(x_all, dq_all), dot_tn(keys_x, dkv_rows)], axis=1
        )

        def scatter(piece, dimension=0):
            return lax.psum_scatter(
                piece.astype(jnp.bfloat16), "fsdp", scatter_dimension=dimension, tiled=True
            )

        from_prompts = scatter(dprompts, 1).astype(jnp.float32)
        from_near = from_partner(dnear, "fsdp")
        shares = [
            scatter(piece)
            for piece in (dweight_down, dweight_up, dweight_out, dweight_qkv, small)
        ]
        t_down, t_up, t_out, t_qkv, t_small = [
            lax.psum(entry, "grp").astype(jnp.float32) for entry in shares
        ]
        t_qkv = [t_qkv[:, D * i : D * i + D] for i in range(3)]
        dcont = (dcont[:, :, 1] + from_near.astype(jnp.float32)).reshape(MICRO, CH, D)
        dx_all = dres_one + dot_nt(dq_all, query_weight)
        grad_content = dx_all[:rows_c].reshape(MICRO, TD, D) + jnp.concatenate(
            [from_prompts, dcont], axis=1
        )
        grad_query = dx_all[rows_c:].reshape(MICRO, QP, D)[:, :extra_rows]
        t_small = t_small.reshape(-1)
        pieces = [t_small[shard * i : shard * i + shard] for i in range(8)]
        up_at = 8 * shard
        t_bup = t_small[up_at : up_at + up_size]
        t_table = t_small[up_at + up_size :].reshape(-1, heads)
    return (
        out_content,
        out_query,
        grad_content,
        grad_query,
        t_qkv[0],
        pieces[0],
        t_qkv[1],
        t_qkv[2],
        pieces[1],
        t_out,
        pieces[7],
        pieces[5],
        pieces[6],
        t_up,
        t_bup,
        t_down,
        pieces[4],
        pieces[2],
        pieces[3],
        t_table,
    )


def solution(mesh):
    rows = P(None, ("grp", "fsdp"), None)
    matrix = P("fsdp", None)
    vector = P("fsdp")
    in_specs = (
        rows,
        rows,
        rows,
        P(None, "grp", None),
        P(),
        matrix,
        vector,
        matrix,
        matrix,
        vector,
        matrix,
        vector,
        vector,
        vector,
        matrix,
        vector,
        matrix,
        vector,
        vector,
        vector,
        P(),
        rows,
        rows,
    )
    out_specs = (
        rows,
        rows,
        rows,
        rows,
        matrix,
        vector,
        matrix,
        matrix,
        vector,
        matrix,
        vector,
        vector,
        vector,
        matrix,
        vector,
        matrix,
        vector,
        vector,
        vector,
        matrix,
    )
    return jax.shard_map(
        on_device, mesh=mesh, in_specs=in_specs, out_specs=out_specs, check_vma=False
    )
```

```python
import functools

import jax
import jax.numpy as jnp
from jax import lax
from jax.experimental import pallas as pl
from jax.experimental.pallas import tpu as pltpu
from jax.sharding import PartitionSpec as P

D = 768
PD = 128
CH = 256
MICRO = 2
TD = 384
QP = 64
HD = 64
LANES = 128
PAIRS = D // LANES

PRECISE = lax.Precision.HIGHEST
MASKED = -1e30
VMEM_LIMIT = 56 * 1024 * 1024


def dot_nt(left, right):
    return lax.dot_general(
        left, right, (((1,), (1,)), ((), ())), preferred_element_type=jnp.float32
    )


def dot_tn(left, right):
    return lax.dot_general(
        left, right, (((0,), (0,)), ((), ())), preferred_element_type=jnp.float32
    )


def dot_nn(left, right):
    return jnp.dot(left, right, preferred_element_type=jnp.float32)


def head_stack(block):
    lane = lax.broadcasted_iota(jnp.int32, block.shape, 1)
    zero = jnp.zeros_like(block)
    return jnp.concatenate(
        [jnp.where(lane < HD, block, zero), jnp.where(lane < HD, zero, block)], axis=0
    )


def head_merge(stacked):
    rows = stacked.shape[0] // 2
    lane = lax.broadcasted_iota(jnp.int32, (rows, LANES), 1)
    return jnp.where(lane < HD, stacked[:rows], stacked[rows:])


def lookup(table, index):
    return jnp.take_along_axis(table, index, axis=1, mode="promise_in_bounds")


def near_index(distance):
    return jnp.clip(distance, 0, LANES - 1)


def fill_keys(scratch, rows_ref, own_prompt, mapped, plength):
    own_at = pl.multiple_of(own_prompt * plength, 128)
    scratch[0:plength] = rows_ref[pl.ds(own_at, plength), :]
    scratch[plength : 2 * plength] = jnp.where(
        mapped == 0, rows_ref[0:plength], rows_ref[plength : 2 * plength]
    )
    scratch[2 * plength :] = rows_ref[2 * plength :]


MESH = pl.DeviceIdType.MESH
ANY_SPEC = pl.BlockSpec(memory_space=pl.ANY)


class Net:
    def __init__(self):
        self.g = lax.axis_index("grp")
        self.f = lax.axis_index("fsdp")
        self.x = self.g % 2
        self.y = self.g // 2
        self.z = self.f // 2
        self.c = self.f % 2
        self.gx = self.g + 1 - 2 * self.x
        self.gy = self.g + 2 - 4 * self.y
        self.mate = self.f + 1 - 2 * self.c
        self.z_of = [
            self.z + 1 - 2 * (self.z % 2),
            (self.z + 2) % 4,
            3 - self.z,
        ]
        self.f_of = [2 * other + self.c for other in self.z_of]
        self.to_x = (self.gx, self.f)
        self.to_y = (self.gy, self.f)
        self.to_mate = (self.g, self.mate)
        self.to_z = [(self.g, other) for other in self.f_of]

    def greet(self):
        barrier = pltpu.get_barrier_semaphore()
        everyone = [self.to_x, self.to_y, self.to_mate] + self.to_z
        for device in everyone:
            pl.semaphore_signal(barrier, inc=1, device_id=device, device_id_type=MESH)
        pl.semaphore_wait(barrier, len(everyone))


class Copies:
    def __init__(self, sends, recvs):
        self.sends = sends
        self.recvs = recvs
        self.used = 0
        self.all = []

    def to(self, device, src, dst):
        copy = pltpu.make_async_remote_copy(
            src_ref=src,
            dst_ref=dst,
            send_sem=self.sends.at[self.used],
            recv_sem=self.recvs.at[self.used],
            device_id=device,
            device_id_type=MESH,
        )
        self.used += 1
        self.all.append(copy)
        return copy

    def finish(self):
        for copy in self.all:
            copy.wait_send()


def start(copies):
    for copy in copies:
        copy.start()


def arrive(copies):
    for copy in copies:
        copy.wait_recv()


GATHER_COPIES = 19


def gather_stages(net, copies, local_sem, shard, full):
    part, width = shard.shape[1:]
    half = width // 2

    def rows(owner, quarter):
        return 4 * owner + quarter

    def whole(owner):
        return pl.ds(4 * owner, 4)

    local = pltpu.make_async_copy(shard, full.at[whole(net.f)], local_sem)
    mine = shard.at[net.g]
    along_z = [copies.to(device, mine, full.at[rows(net.f, net.g)]) for device in net.to_z[:2]]
    passed = full.at[rows(net.f_of[1], net.g)]
    relay = copies.to(net.to_z[0], passed, passed)
    to_mate = [copies.to(net.to_mate, shard, full.at[whole(net.f)])]
    to_x, to_y, on_x, on_y, later = [], [], [], [], []
    for owner in net.f_of:
        got = full.at[rows(owner, net.g)]
        to_x.append(copies.to(net.to_x, got, got))
        to_y.append(copies.to(net.to_y, got, got))
        left = full.at[rows(owner, net.gx), :, pl.ds(0, half)]
        on_y.append(copies.to(net.to_y, left, left))
        right = full.at[rows(owner, net.gy), :, pl.ds(half, half)]
        on_x.append(copies.to(net.to_x, right, right))
        shared = full.at[whole(owner)]
        later.append(copies.to(net.to_mate, shared, shared))

    def begin():
        local.start()
        start(along_z)
        start(to_mate)

    def onward():
        along_z[1].wait_recv()
        relay.start()

    def plane():
        arrive([along_z[0], relay])
        start(to_x + to_y)

    def corners():
        arrive(to_x + to_y)
        start(on_y + on_x)

    def mates():
        arrive(on_y + on_x)
        start(later)

    def end():
        arrive(to_mate + later)
        local.wait()
        copies.finish()

    return [begin, onward, plane, corners, mates, end]


REDUCE_COPIES = 19


def reduce_buffers(size, width):
    part, half = size // 4, width // 2
    return [
        pltpu.VMEM((4, 4, part, width), jnp.bfloat16),
        pltpu.VMEM((4, 4, part, width), jnp.bfloat16),
        pltpu.VMEM((4, 2, part, half), jnp.bfloat16),
        pltpu.VMEM((4, 2, part, half), jnp.bfloat16),
        pltpu.VMEM((2, 4, part, half), jnp.bfloat16),
        pltpu.VMEM((2, 3, part, half), jnp.bfloat16),
        pltpu.VMEM((2, 4, part, half), jnp.bfloat16),
        pltpu.VMEM((4, part, width), jnp.float32),
        pltpu.SemaphoreType.DMA((2,)),
        pltpu.SemaphoreType.DMA((REDUCE_COPIES,)),
        pltpu.SemaphoreType.DMA((REDUCE_COPIES,)),
    ]


def reduce_stages(net, grad, share, buffers):
    own, other, side_a, side_b, line, along, done, wide, local_sem, sends, recvs = buffers
    copies = Copies(sends, recvs)
    half = grad.shape[4] // 2
    left, right = pl.ds(0, half), pl.ds(half, half)
    load = pltpu.make_async_copy(grad.at[:, net.c], own, local_sem.at[0])
    to_mate = [copies.to(net.to_mate, grad.at[:, 1 - net.c], other)]
    first = []
    for i in range(2):
        first.append(
            copies.to(net.to_x, own.at[:, 2 * i + 1 - net.x, :, left], side_a.at[:, i])
        )
        first.append(
            copies.to(net.to_y, own.at[:, 2 - 2 * net.y + i, :, right], side_b.at[:, i])
        )
    second = [
        copies.to(net.to_y, side_a.at[:, 1 - net.y], line.at[0]),
        copies.to(net.to_x, side_b.at[:, 1 - net.x], line.at[1]),
    ]
    third = []
    for h in range(2):
        third.append(copies.to(net.to_z[0], line.at[h, net.z_of[2]], along.at[h, 0]))
        third.append(copies.to(net.to_z[0], line.at[h, net.z_of[0]], along.at[h, 1]))
    relay = [copies.to(net.to_z[1], line.at[h, net.z_of[1]], along.at[h, 2]) for h in range(2)]
    fourth = []
    fifth = []
    for h in range(2):
        fourth.append(copies.to(net.to_x, done.at[h, net.g], done.at[h, net.g]))
        fourth.append(copies.to(net.to_y, done.at[h, net.g], done.at[h, net.g]))
    fifth.append(copies.to(net.to_y, done.at[0, net.gx], done.at[0, net.gx]))
    fifth.append(copies.to(net.to_x, done.at[1, net.gy], done.at[1, net.gy]))
    store = pltpu.make_async_copy(wide, share, local_sem.at[1])

    def begin():
        load.start()
        start(to_mate)

    def plane():
        load.wait()
        arrive(to_mate)

        @pl.loop(0, 16)
        def _(i):
            zi, qi = i // 4, i % 4
            own[zi, qi] = own[zi, qi] + other[zi, qi]

        start(first)

    def cross():
        arrive(first)

        @pl.loop(0, 8)
        def _(i):
            zi, qi = i // 2, i % 2
            side_a[zi, qi] = side_a[zi, qi] + own[zi, 2 * qi + net.x, :, 0:half]
            side_b[zi, qi] = side_b[zi, qi] + own[zi, 2 * net.y + qi, :, half : 2 * half]

        start(second)

    def column():
        arrive(second)

        @pl.loop(0, 4)
        def _(zi):
            line[0, zi] = line[0, zi] + side_a[zi, net.y]
            line[1, zi] = line[1, zi] + side_b[zi, net.x]

        start(third)

    def onward():
        arrive(third[0::2])

        @pl.loop(0, 2)
        def _(h):
            line[h, net.z_of[1]] = line[h, net.z_of[1]] + along[h, 0]

        start(relay)

    def spread():
        arrive(third[1::2] + relay)

        @pl.loop(0, 2)
        def _(h):
            total = line[h, net.z].astype(jnp.float32)
            for k in range(1, 3):
                total = total + along[h, k].astype(jnp.float32)
            done[h, net.g] = total.astype(jnp.bfloat16)

        start(fourth)

    def corners():
        arrive(fourth)
        start(fifth)

    def end():
        arrive(fifth)

        @pl.loop(0, 4)
        def _(qi):
            for h in range(2):
                wide[qi, :, h * half : h * half + half] = done[h, qi].astype(jnp.float32)

        store.start()
        store.wait()
        copies.finish()

    return [begin, plane, cross, column, onward, spread, corners, end]


ROW_COPIES = 9


def rows_stages(net, copies, local_sems, x_ref, keys_x):
    at = 8 * PD

    def block(owner):
        return keys_x.at[pl.ds(pl.multiple_of(owner * PD, 128), PD)]

    prompt = x_ref.at[pl.ds(0, PD)]
    cont = [x_ref.at[pl.ds(PD + 128 * i, 128)] for i in range(2)]
    local = [pltpu.make_async_copy(prompt, block(net.f), local_sems.at[0])]
    to_mate = [copies.to(net.to_mate, prompt, block(net.f))]
    for i in range(2):
        near = keys_x.at[pl.ds(at + 256 * i, 128)]
        here = keys_x.at[pl.ds(at + 256 * i + 128, 128)]
        local.append(pltpu.make_async_copy(cont[i], here, local_sems.at[1 + i]))
        to_mate.append(copies.to(net.to_mate, cont[i], near))
    along_z = [copies.to(device, prompt, block(net.f)) for device in net.to_z[:2]]
    relay = copies.to(net.to_z[0], block(net.f_of[1]), block(net.f_of[1]))
    later = [copies.to(net.to_mate, block(owner), block(owner)) for owner in net.f_of]

    def begin():
        start(local)
        start(to_mate)

    def column():
        start(along_z)

    def onward():
        along_z[1].wait_recv()
        relay.start()

    def mates():
        arrive([along_z[0], relay])
        start(later)

    def end():
        arrive(to_mate + later)
        for copy in local:
            copy.wait()
        copies.finish()

    return [begin, column, onward, mates, end]


def gather_first_kernel(*refs):
    shards, x_ref, fulls, keys_x = refs[:4], refs[4], refs[5:9], refs[9]
    sems, local_sem, row_sems = refs[10:20], refs[20], refs[21]
    net = Net()
    net.greet()
    parts = [
        gather_stages(
            net, Copies(sems[2 * i], sems[2 * i + 1]), local_sem.at[i], shards[i], fulls[i]
        )
        for i in range(4)
    ]
    rows = rows_stages(net, Copies(sems[8], sems[9]), row_sems, x_ref.at[0], keys_x)
    for part in parts:
        part[0]()
    rows[0]()
    for part in parts:
        part[1]()
    rows[1]()
    for part in parts:
        part[2]()
    for part in parts:
        part[3]()
    rows[2]()
    for part in parts:
        part[4]()
    rows[3]()
    for part in parts:
        part[5]()
    rows[4]()


def gather_first(shards, content_in):
    return pl.pallas_call(
        gather_first_kernel,
        name="gather_first",
        in_specs=[ANY_SPEC] * 5,
        out_specs=[ANY_SPEC] * 5,
        out_shape=[jax.ShapeDtypeStruct((8 * 4,) + s.shape[1:], jnp.bfloat16) for s in shards]
        + [jax.ShapeDtypeStruct((8 * PD + 2 * CH, D), jnp.bfloat16)],
        scratch_shapes=[pltpu.SemaphoreType.DMA((GATHER_COPIES,))] * 8
        + [pltpu.SemaphoreType.DMA((ROW_COPIES,))] * 2
        + [pltpu.SemaphoreType.DMA((4,)), pltpu.SemaphoreType.DMA((3,))],
        compiler_params=pltpu.CompilerParams(collective_id=1, has_side_effects=True),
    )(*shards, content_in)


def halves_of(ref):
    rows, columns = ref.shape[-2:]
    rest = (slice(None),) * (len(ref.shape) - 2)
    if columns > rows * 16:
        cut = columns // 2
        return [ref.at[rest + (slice(None), pl.ds(cut * i, cut))] for i in range(2)]
    cut = rows // 2
    return [ref.at[rest + (pl.ds(cut * i, cut),)] for i in range(2)]


def hosted(plan, step):
    for at, stage in plan:

        @pl.when(step == at)
        def _():
            stage()


def place(plength):
    rank = lax.axis_index("fsdp")
    halfway = plength // PD
    return rank // halfway, rank % halfway * PD, rank % 2


def attend_kernel(plength, carried, *refs):
    (meta, x_c, x_q, w_q, w_k, w_v, bias, table, xcol, first_rows, other), refs = (
        refs[:11],
        refs[11:],
    )
    shards, refs = refs[:carried], refs[carried:]
    (ctx_c, ctx_x, full_c, full_x, lse_ref, qc, qx, k_rows, v_rows), refs = refs[:9], refs[9:]
    second_rows = other
    if carried:
        second_rows, refs = refs[0], refs[1:]
    fulls, refs = refs[:carried], refs[carried:]
    keys, vals, x_keys, load_sem = refs[:4]
    all_scores, all_probs = refs[4:8], refs[8:12]
    refs = refs[12:]
    step = pl.program_id(0) * PAIRS + pl.program_id(1)
    if carried:
        net = Net()
        pieces = []
        for i in range(2):
            pieces += list(zip(halves_of(shards[i]), halves_of(fulls[i])))
        pieces.append((shards[2], fulls[2]))
        one, two, three, four, proj = (
            gather_stages(
                net, Copies(refs[2 * i], refs[2 * i + 1]), refs[12].at[i], src, dst
            )
            for i, (src, dst) in enumerate(pieces)
        )
        rows = rows_stages(
            net, Copies(refs[10], refs[11]), refs[13], other.at[1], second_rows
        )
        hosted([(0, net.greet)], step)
        hosted(
            [
                (0, rows[0]),
                (0, rows[1]),
                (2, one[0]),
                (2, proj[0]),
                (3, rows[2]),
                (3, two[0]),
                (4, one[1]),
                (4, proj[1]),
                (5, rows[3]),
                (6, rows[4]),
                (6, one[2]),
                (6, proj[2]),
                (6, two[1]),
                (6, three[0]),
                (7, two[2]),
                (7, four[0]),
                (8, one[3]),
                (8, proj[3]),
                (8, three[1]),
                (9, three[2]),
                (9, four[1]),
                (10, one[4]),
                (10, proj[4]),
                (10, two[3]),
                (10, four[2]),
                (11, three[3]),
            ],
            step,
        )
    for m, source in enumerate((first_rows, second_rows)):

        @pl.when(step == m * PAIRS)
        def _():
            load = pltpu.make_async_copy(source, x_keys, load_sem)
            load.start()
            load.wait()

    w_kv = jnp.concatenate([w_k[...], w_v[...]], axis=1)
    for at in range(0, x_keys.shape[0], 512):
        part = slice(at, at + 512)
        value = dot_nn(x_keys[part], w_kv)
        k_rows[part] = value[:, :LANES].astype(jnp.bfloat16)
        v_rows[part] = (value[:, LANES:] + bias[1:2]).astype(jnp.bfloat16)
    qc[...] = (dot_nn(x_c[...], w_q[...]) + bias[0:1]).astype(jnp.bfloat16)
    qx[...] = (dot_nn(x_q[...], w_q[...]) + bias[0:1]).astype(jnp.bfloat16)
    own_prompt, base, side = place(plength)
    mapped = meta[pl.program_id(0)]
    blocks = plength // 128
    fill_keys(keys, k_rows, own_prompt, mapped, plength)
    fill_keys(vals, v_rows, own_prompt, mapped, plength)
    row = lax.broadcasted_iota(jnp.int32, (128, 128), 0)
    col = lax.broadcasted_iota(jnp.int32, (128, 128), 1)
    tab_a = jnp.broadcast_to(table[0, 0:1, :], (128, 128))
    tab_b = jnp.broadcast_to(table[0, 1:2, :], (128, 128))
    tab_x = jnp.where(row < QP, tab_a, tab_b)
    lse_ref[...] = jnp.zeros_like(lse_ref)

    def solve(which, stack, first, plan, tables, lse_rows):
        scores, probs = all_scores[which], all_probs[which]
        count = len(plan)
        span = slice(first, first + 128 * count)
        halves = len(tables)
        width = 128 * count
        scores[0 : 128 * halves, 0:width] = dot_nt(stack, keys[span])
        for half in range(halves):
            rows = slice(128 * half, 128 * half + 128)
            peak = None
            for at, (index, visible) in enumerate(plan):
                cols = slice(128 * at, 128 * at + 128)
                s = scores[rows, cols]
                if index is not None:
                    s = s + lookup(tables[half], index)
                if visible is not None:
                    s = jnp.where(visible, s, MASKED)
                if index is not None or visible is not None:
                    scores[rows, cols] = s
                peak = s if peak is None else jnp.maximum(peak, s)
            top = jnp.max(peak, axis=1, keepdims=True)
            total = None
            for at in range(count):
                cols = slice(128 * at, 128 * at + 128)
                p = jnp.exp(scores[rows, cols] - top)
                total = p if total is None else total + p
                probs[rows, cols] = p.astype(jnp.bfloat16)
            total = jnp.sum(total, axis=1, keepdims=True)
            log_total = top + jnp.log(total)
            lse_ref[0, 0, lse_rows[half] : lse_rows[half] + 1, :] = jnp.transpose(
                jnp.broadcast_to(log_total, (128, 128))
            )[0:1, :]
            scores[rows, 0:128] = jnp.broadcast_to(1.0 / total, (128, 128))
        out = dot_nn(probs[0 : 128 * halves, 0:width], vals[span])
        return out * scores[0 : 128 * halves, 0:128]

    scale = jnp.asarray(0.125, jnp.bfloat16)
    q_p = head_stack(qc[0:PD] * scale)
    q_0 = head_stack(qc[PD : PD + 128] * scale)
    q_1 = head_stack(qc[PD + 128 : PD + 256] * scale)
    q_x = head_stack(qx[...] * scale)

    plan_p = []
    for b in range(blocks):
        d = base + row - (col + 128 * b)
        plan_p.append((near_index(d), d >= 0))
    out = head_merge(solve(0, q_p, 0, plan_p, (tab_a, tab_b), (0, 3)))
    ctx_c[0:PD] = out.astype(jnp.bfloat16)
    full_c[0:PD] = out

    far = (None, None)
    last = 128 + 2 * row + side - col
    near_d = 2 * (row - col) + 2 * side - 1
    own_d = 2 * (row - col)
    plan_0 = [far] * (blocks - 1) + [
        (near_index(last), None),
        (near_index(near_d), near_d >= 0),
        (near_index(own_d), own_d >= 0),
    ]
    out = head_merge(solve(1, q_0, plength, plan_0, (tab_a, tab_b), (1, 4)))
    ctx_c[PD : PD + 128] = out.astype(jnp.bfloat16)
    full_c[PD : PD + 128] = out
    plan_1 = [far] * blocks + [
        (near_index(near_d + 256), None),
        (near_index(own_d + 256), None),
        (near_index(near_d), near_d >= 0),
        (near_index(own_d), own_d >= 0),
    ]
    out = head_merge(solve(2, q_1, plength, plan_1, (tab_a, tab_b), (2, 5)))
    ctx_c[PD + 128 : PD + 256] = out.astype(jnp.bfloat16)
    full_c[PD + 128 : PD + 256] = out

    pos = jnp.broadcast_to(xcol[0, :, 0:1], (128, 128))
    lim_p = jnp.broadcast_to(xcol[0, :, 1:2], (128, 128))
    lim_c = jnp.broadcast_to(xcol[0, :, 2:3], (128, 128))
    plan_x = []
    for b in range(blocks):
        key = col + 128 * b
        plan_x.append((near_index(pos - key), key < lim_p))
    in_cont = lim_c > 0
    for b in range(blocks - 1):
        plan_x.append((None, in_cont))
    key = col + 128 * (blocks - 1)
    plan_x.append((near_index(pos - key), in_cont))
    for b in range(2):
        for offset in (1 - side, side):
            key = plength + 2 * (col + 128 * b) + offset
            plan_x.append((near_index(pos - key), key < lim_c))
    out = solve(3, q_x, 0, plan_x, (tab_x,), (6,))
    lane = lax.broadcasted_iota(jnp.int32, (QP, LANES), 1)
    out = jnp.where(lane < HD, out[0:QP], out[QP:])
    ctx_x[...] = out.astype(jnp.bfloat16)
    full_x[...] = out
    if carried:
        rest = (four[3], two[4], three[4], four[4], one[5], proj[5], two[5], three[5], four[5])
        hosted([(11, stage) for stage in rest], step)


def pair_column():
    return lambda m, j, meta: (m, j)


def key_spec(n_keys):
    return pl.BlockSpec((n_keys, LANES), lambda m, j, meta: (m, j))


TABLE_SPEC = pl.BlockSpec((1, 8, LANES), lambda m, j, meta: (j, 0, 0))


def host_params(collective_id, carried):
    if carried:
        return pltpu.CompilerParams(
            vmem_limit_bytes=VMEM_LIMIT, collective_id=collective_id, has_side_effects=True
        )
    return pltpu.CompilerParams(vmem_limit_bytes=VMEM_LIMIT)


def attend(meta, x_c, x_q, weights, bias, table, xcol, first_rows, other, shards):
    carried = len(shards)
    n_keys = first_rows.shape[0]
    plength = (n_keys - 2 * CH) // 2
    groups = [(256, plength), (256, plength + 256), (256, plength + 512), (128, n_keys)]
    content = pl.BlockSpec((TD, LANES), pair_column())
    extra = pl.BlockSpec((QP, LANES), pair_column())
    own_row = plength + 2 * CH
    pairs = MICRO * PAIRS * 2 * (128 * plength + 256 * own_row) + MICRO * PAIRS * 128 * n_keys
    return pl.pallas_call(
        functools.partial(attend_kernel, plength, carried),
        name="attend",
        grid_spec=pltpu.PrefetchScalarGridSpec(
            num_scalar_prefetch=1,
            grid=(MICRO, PAIRS),
            in_specs=[
                pl.BlockSpec((TD, D), lambda m, j, meta: (m, 0)),
                pl.BlockSpec((QP, D), lambda m, j, meta: (m, 0)),
            ]
            + [pl.BlockSpec((D, LANES), lambda m, j, meta: (0, j))] * 3
            + [
                pl.BlockSpec((8, LANES), lambda m, j, meta: (0, j)),
                TABLE_SPEC,
                pl.BlockSpec((1, 128, 8), lambda m, j, meta: (m, 0, 0)),
                ANY_SPEC,
                ANY_SPEC,
            ]
            + [ANY_SPEC] * carried,
            out_specs=[
                content,
                extra,
                content,
                extra,
                pl.BlockSpec((1, 1, 8, LANES), lambda m, j, meta: (m, j, 0, 0)),
                content,
                extra,
                key_spec(n_keys),
                key_spec(n_keys),
            ]
            + [ANY_SPEC] * (carried + 1 if carried else 0),
            scratch_shapes=[
                pltpu.VMEM((n_keys, LANES), jnp.bfloat16),
                pltpu.VMEM((n_keys, LANES), jnp.bfloat16),
                pltpu.VMEM((n_keys, D), jnp.bfloat16),
                pltpu.SemaphoreType.DMA,
            ]
            + [pltpu.VMEM(group, jnp.float32) for group in groups]
            + [pltpu.VMEM(group, jnp.bfloat16) for group in groups]
            + (
                [pltpu.SemaphoreType.DMA((GATHER_COPIES,))] * 10
                + [pltpu.SemaphoreType.DMA((ROW_COPIES,))] * 2
                + [pltpu.SemaphoreType.DMA((5,)), pltpu.SemaphoreType.DMA((3,))]
                if carried
                else []
            ),
        ),
        out_shape=[
            jax.ShapeDtypeStruct((MICRO * TD, D), jnp.bfloat16),
            jax.ShapeDtypeStruct((MICRO * QP, D), jnp.bfloat16),
            jax.ShapeDtypeStruct((MICRO * TD, D), jnp.float32),
            jax.ShapeDtypeStruct((MICRO * QP, D), jnp.float32),
            jax.ShapeDtypeStruct((MICRO, PAIRS, 8, LANES), jnp.float32),
            jax.ShapeDtypeStruct((MICRO * TD, D), jnp.bfloat16),
            jax.ShapeDtypeStruct((MICRO * QP, D), jnp.bfloat16),
            jax.ShapeDtypeStruct((MICRO * n_keys, D), jnp.bfloat16),
            jax.ShapeDtypeStruct((MICRO * n_keys, D), jnp.bfloat16),
        ]
        + ([jax.ShapeDtypeStruct((n_keys, D), jnp.bfloat16)] if carried else [])
        + [
            jax.ShapeDtypeStruct((8 * 4,) + shard.shape[1:], shard.dtype)
            for shard in shards
        ],
        compiler_params=host_params(2, carried),
        cost_estimate=pl.CostEstimate(
            flops=4 * pairs * LANES, bytes_accessed=16 * 1024 * 1024, transcendentals=pairs
        ),
    )(
        meta,
        x_c,
        x_q,
        *weights,
        bias,
        table,
        xcol,
        first_rows,
        other,
        *shards,
    )


def attend_back_kernel(plength, carried, *refs):
    (meta, qc, qx, k_rows, v_rows, table, xcol, xrow, lse_ref, dc, dx, full_c, full_x), refs = (
        refs[:13],
        refs[13:],
    )
    grads, refs = refs[:carried], refs[carried:]
    (dq_c, dq_x, dk_rows, dv_rows, hist), refs = refs[:5], refs[5:]
    shares, refs = refs[:carried], refs[carried:]
    keys, vals, q_all, d_all, probs_t, dscores_t, ds_p, ds_c, dk_acc, dv_acc = refs[:10]
    all_scores, all_dprobs = refs[10:14], refs[14:18]
    refs = refs[18:]
    step = pl.program_id(0) * PAIRS + pl.program_id(1)
    if carried:
        net = Net()
        pieces = list(zip(halves_of(grads[0]), halves_of(shares[0])))
        pieces.append((grads[1], shares[1]))
        one, two, proj = (
            reduce_stages(net, src, dst, refs[11 * i : 11 * i + 11])
            for i, (src, dst) in enumerate(pieces)
        )
        hosted([(0, net.greet)], step)
        hosted(
            [
                (0, one[0]),
                (0, two[0]),
                (0, proj[0]),
                (1, one[1]),
                (2, two[1]),
                (3, proj[1]),
                (4, one[2]),
                (5, two[2]),
                (6, proj[2]),
                (6, one[3]),
                (7, two[3]),
                (8, proj[3]),
                (8, one[4]),
                (9, two[4]),
                (10, proj[4]),
                (10, one[5]),
                (11, two[5]),
                (11, proj[5]),
                (11, one[6]),
            ],
            step,
        )
    own_prompt, base, side = place(plength)
    mapped = meta[pl.program_id(0)]
    blocks = plength // 128
    at_k1 = 2 * plength + 256
    n_keys = 2 * plength + 512
    fill_keys(keys, k_rows, own_prompt, mapped, plength)
    fill_keys(vals, v_rows, own_prompt, mapped, plength)
    row = lax.broadcasted_iota(jnp.int32, (128, 128), 0)
    col = lax.broadcasted_iota(jnp.int32, (128, 128), 1)
    tab_a = jnp.broadcast_to(table[0, 0:1, :], (128, 128))
    tab_b = jnp.broadcast_to(table[0, 1:2, :], (128, 128))
    scale = jnp.asarray(0.125, jnp.bfloat16)

    p_at, x_at, c1_at, c0_at = 0, 256, 384, 640
    q_all[0:256] = head_stack(qc[0:PD] * scale)
    q_all[256:384] = head_stack(qx[...] * scale)
    q_all[384:640] = head_stack(qc[PD + 128 : PD + 256] * scale)
    q_all[640:896] = head_stack(qc[PD : PD + 128] * scale)
    d_all[0:256] = head_stack(dc[0:PD])
    d_all[256:384] = head_stack(dx[...])
    d_all[384:640] = head_stack(dc[PD + 128 : PD + 256])
    d_all[640:896] = head_stack(dc[PD : PD + 128])

    ones_lane = lax.broadcasted_iota(jnp.int32, (8, LANES), 1)
    ones_row = lax.broadcasted_iota(jnp.int32, (8, LANES), 0)
    pick = jnp.where((ones_lane < HD) == (ones_row == 0), 1.0, 0.0)
    pick = jnp.where(ones_row < 2, pick, 0.0)

    def deltas(upstream, context):
        product = upstream.astype(jnp.float32) * context
        return lax.dot_general(
            pick,
            product,
            (((1,), (1,)), ((), ())),
            precision=PRECISE,
            preferred_element_type=jnp.float32,
        )

    delta_p = deltas(dc[0:PD], full_c[0:PD])
    delta_0 = deltas(dc[PD : PD + 128], full_c[PD : PD + 128])
    delta_1 = deltas(dc[PD + 128 : PD + 256], full_c[PD + 128 : PD + 256])
    delta_x = deltas(dx[...], full_x[...])
    delta_x = jnp.concatenate([delta_x[0:1], delta_x[1:2]], axis=1)

    def block_back(which, first, plan, at_col, halves):
        scores, dprobs = all_scores[which], all_dprobs[which]
        count = len(plan)
        width = 128 * len(halves)
        span = slice(first, first + 128 * count)
        cols = slice(at_col, at_col + width)
        scores[0 : 128 * count, 0:width] = dot_nt(keys[span], q_all[cols])
        dprobs[0 : 128 * count, 0:width] = dot_nt(vals[span], d_all[cols])
        for half, (tables, lse_row, delta) in enumerate(halves):
            lane = slice(128 * half, 128 * half + 128)
            out_lane = slice(at_col + 128 * half, at_col + 128 * half + 128)
            lse = lse_ref[0, 0, lse_row : lse_row + 1, :]
            for at, (index, visible) in enumerate(plan):
                rows = slice(128 * at, 128 * at + 128)
                out_rows = slice(first + 128 * at, first + 128 * at + 128)
                s = scores[rows, lane]
                if index is not None:
                    bias = lookup(tables[0], index)
                    if len(tables) > 1:
                        bias = jnp.where(col < QP, bias, lookup(tables[1], index))
                    s = s + bias
                if visible is not None:
                    s = jnp.where(visible, s, MASKED)
                p = jnp.exp(s - lse)
                ds = p * (dprobs[rows, lane] - delta)
                probs_t[out_rows, out_lane] = p.astype(jnp.bfloat16)
                dscores_t[out_rows, out_lane] = ds.astype(jnp.bfloat16)
                yield half, at, ds

    extra_a = jnp.where(
        (xcol[0, :, 3:4] == lax.broadcasted_iota(jnp.int32, (128, TD), 1))
        & (lax.broadcasted_iota(jnp.int32, (128, TD), 0) < QP),
        1.0,
        0.0,
    ).astype(jnp.bfloat16)
    extra_b = jnp.where(
        (xcol[0, :, 3:4] == lax.broadcasted_iota(jnp.int32, (128, TD), 1))
        & (lax.broadcasted_iota(jnp.int32, (128, TD), 0) >= QP),
        1.0,
        0.0,
    ).astype(jnp.bfloat16)
    spread = (extra_a, extra_b)

    pos = xrow[0, 0:1, :]
    lim_p = xrow[0, 1:2, :]
    lim_c = xrow[0, 2:3, :]
    plan = []
    for b in range(blocks):
        key = row + 128 * b
        plan.append((near_index(pos - key), key < lim_p))
    in_cont = jnp.broadcast_to(lim_c > 0, (128, 128))
    for b in range(blocks - 1):
        plan.append((None, in_cont))
    plan.append((near_index(pos - (row + 128 * (blocks - 1))), in_cont))
    for b in range(2):
        for offset in (1 - side, side):
            key = plength + 2 * (row + 128 * b) + offset
            plan.append((near_index(pos - key), key < lim_c))
    for _ in block_back(3, 0, plan, x_at, [((tab_a, tab_b), 6, delta_x)]):
        pass

    def spread_block(head, key_at, content_at):
        return dot_nn(
            dscores_t[pl.ds(key_at, 128), x_at : x_at + 128],
            spread[head][:, content_at : content_at + 128],
        )

    turn = (col + row) % 128
    turn_half = (col + row // 2) % 128

    def fold(block):
        return jnp.sum(block.reshape(16, 8, LANES), axis=0)

    plan = []
    for b in range(blocks):
        d = base + col - (row + 128 * b)
        plan.append((near_index(d), d >= 0))
    halves = [((tab_a,), 0, delta_p[0:1]), ((tab_b,), 3, delta_p[1:2])]
    for half, at, ds in block_back(0, 0, plan, p_at, halves):
        ds_p[128 * at : 128 * at + 128, 128 * half : 128 * half + 128] = ds
    before = jnp.maximum(base - 128, 0)
    base_at = pl.multiple_of(base, 128)
    before_at = pl.multiple_of(before, 128)
    for head in range(2):
        lane = slice(128 * head, 128 * head + 128)
        here = ds_p[pl.ds(base_at, 128), lane] + spread_block(head, base_at, 0)
        prior = ds_p[pl.ds(before_at, 128), lane] + spread_block(head, before_at, 0)
        prior = jnp.where(base > 0, prior, 0.0)
        both = jnp.where(col >= row, here, prior)
        hist[0, 0, 32 * head : 32 * head + 8] = fold(lookup(both, turn))

    last = 128 + 2 * col + side - row
    near_d = 2 * (col - row) + 2 * side - 1
    own_d = 2 * (col - row)
    far = (None, None)
    plan_0 = [far] * (blocks - 1) + [
        (near_index(last), None),
        (near_index(near_d), near_d >= 0),
        (near_index(own_d), own_d >= 0),
    ]
    plan_1 = [far] * blocks + [
        (near_index(near_d + 256), None),
        (near_index(own_d + 256), None),
        (near_index(near_d), near_d >= 0),
        (near_index(own_d), own_d >= 0),
    ]
    halves = [((tab_a,), 1, delta_0[0:1]), ((tab_b,), 4, delta_0[1:2])]
    near_sum = {}
    own_sum = {}
    last_key = 2 * plength - 128
    for half, at, ds in block_back(1, plength, plan_0, c0_at, halves):
        if at == blocks - 1:
            ds = ds + spread_block(half, last_key, PD)
            ds = jnp.where(col < 64, ds, 0.0)
            hist[0, 0, 32 * half + 8 : 32 * half + 16] = fold(lookup(ds, turn_half))
        if at == blocks:
            ds = ds + spread_block(half, 2 * plength, PD)
            near_sum[half] = jnp.where(col >= row, ds, 0.0)
        if at == blocks + 1:
            ds = ds + spread_block(half, 2 * plength + 128, PD)
            own_sum[half] = jnp.where(col >= row, ds, 0.0)
    for half in range(2):
        lane = slice(128 * half, 128 * half + 128)
        ds_c[0:128, lane] = near_sum[half]
        ds_c[128:256, lane] = own_sum[half]
    halves = [((tab_a,), 2, delta_1[0:1]), ((tab_b,), 5, delta_1[1:2])]
    for half, at, ds in block_back(2, plength, plan_1, c1_at, halves):
        lane = slice(128 * half, 128 * half + 128)
        if at == blocks:
            ds = ds + spread_block(half, 2 * plength, PD + 128)
            ds_c[0:128, lane] = ds_c[0:128, lane] + jnp.where(col < row, ds, 0.0)
        if at == blocks + 1:
            ds = ds + spread_block(half, 2 * plength + 128, PD + 128)
            ds_c[128:256, lane] = ds_c[128:256, lane] + jnp.where(col < row, ds, 0.0)
        if at == blocks + 2:
            ds = ds + spread_block(half, at_k1, PD + 128)
            ds = ds_c[0:128, lane] + jnp.where(col >= row, ds, 0.0)
            hist[0, 0, 32 * half + 16 : 32 * half + 24] = fold(lookup(ds, turn))
        if at == blocks + 3:
            ds = ds + spread_block(half, at_k1 + 128, PD + 128)
            ds = ds_c[128:256, lane] + jnp.where(col >= row, ds, 0.0)
            hist[0, 0, 32 * half + 24 : 32 * half + 32] = fold(lookup(ds, turn))

    own = slice(0, plength)
    middle = slice(plength, at_k1)
    end = slice(at_k1, n_keys)
    for acc, left, right in ((dk_acc, dscores_t, q_all), (dv_acc, probs_t, d_all)):
        acc[own] = dot_nn(left[own, 0:384], right[0:384])
        acc[middle] = dot_nn(left[middle, 256:896], right[256:896])
        acc[end] = dot_nn(left[end, 256:640], right[256:640])

    dq_c[0:PD] = (
        head_merge(dot_tn(dscores_t[own, p_at : p_at + 256], keys[own])) * 0.125
    ).astype(jnp.bfloat16)
    dq_c[PD : PD + 128] = (
        head_merge(dot_tn(dscores_t[middle, c0_at : c0_at + 256], keys[middle])) * 0.125
    ).astype(jnp.bfloat16)
    cont = slice(plength, n_keys)
    dq_c[PD + 128 : PD + 256] = (
        head_merge(dot_tn(dscores_t[cont, c1_at : c1_at + 256], keys[cont])) * 0.125
    ).astype(jnp.bfloat16)
    out = dot_tn(dscores_t[:, x_at : x_at + 128], keys[...])
    lane = lax.broadcasted_iota(jnp.int32, (QP, LANES), 1)
    dq_x[...] = (jnp.where(lane < HD, out[0:QP], out[QP:]) * 0.125).astype(jnp.bfloat16)

    for out_ref, acc in ((dk_rows, dk_acc), (dv_rows, dv_acc)):
        for p in range(2):
            mine = jnp.where(own_prompt == p, acc[own], 0.0)
            other = jnp.where(mapped == p, acc[plength : 2 * plength], 0.0)
            out_ref[p * plength : (p + 1) * plength] = (mine + other).astype(jnp.bfloat16)
        out_ref[2 * plength :] = acc[2 * plength :].astype(jnp.bfloat16)
    if carried:
        rest = (two[6], proj[6], one[7], two[7], proj[7])
        hosted([(11, stage) for stage in rest], step)


def attend_back(
    meta, queries, extra_q, k_rows, v_rows, table, xcol, xrow, lse, dc, dx, fc, fx, grads
):
    carried = len(grads)
    sizes, kept = [], []
    if carried:
        part, width = grads[0].shape[3:]
        tall, narrow = grads[1].shape[3:]
        sizes = [(4 * part, width // 2)] * 2 + [(4 * tall, narrow)]
        kept = [jax.ShapeDtypeStruct((4,) + grad.shape[3:], jnp.float32) for grad in grads]
    n_keys = k_rows.shape[0] // MICRO
    plength = (n_keys - 2 * CH) // 2
    groups = [(plength, 256), (plength + 256, 256), (plength + 512, 256), (n_keys, 128)]
    content = pl.BlockSpec((TD, LANES), pair_column())
    extra = pl.BlockSpec((QP, LANES), pair_column())
    own_row = plength + 2 * CH
    pairs = MICRO * PAIRS * 2 * (128 * plength + 256 * own_row) + MICRO * PAIRS * 128 * n_keys
    return pl.pallas_call(
        functools.partial(attend_back_kernel, plength, carried),
        name="attend_back",
        grid_spec=pltpu.PrefetchScalarGridSpec(
            num_scalar_prefetch=1,
            grid=(MICRO, PAIRS),
            in_specs=[content, extra]
            + [
                key_spec(n_keys),
                key_spec(n_keys),
                TABLE_SPEC,
                pl.BlockSpec((1, 128, 8), lambda m, j, meta: (m, 0, 0)),
                pl.BlockSpec((1, 8, 128), lambda m, j, meta: (m, 0, 0)),
                pl.BlockSpec((1, 1, 8, LANES), lambda m, j, meta: (m, j, 0, 0)),
                content,
                extra,
                content,
                extra,
            ]
            + [ANY_SPEC] * carried,
            out_specs=[
                content,
                extra,
                key_spec(n_keys),
                key_spec(n_keys),
                pl.BlockSpec((1, 1, 64, LANES), lambda m, j, meta: (m, j, 0, 0)),
            ]
            + [ANY_SPEC] * carried,
            scratch_shapes=[
                pltpu.VMEM((n_keys, LANES), jnp.bfloat16),
                pltpu.VMEM((n_keys, LANES), jnp.bfloat16),
                pltpu.VMEM((896, LANES), jnp.bfloat16),
                pltpu.VMEM((896, LANES), jnp.bfloat16),
                pltpu.VMEM((n_keys, 896), jnp.bfloat16),
                pltpu.VMEM((n_keys, 896), jnp.bfloat16),
                pltpu.VMEM((plength, 256), jnp.float32),
                pltpu.VMEM((256, 256), jnp.float32),
                pltpu.VMEM((n_keys, LANES), jnp.float32),
                pltpu.VMEM((n_keys, LANES), jnp.float32),
            ]
            + [pltpu.VMEM(group, jnp.float32) for group in groups] * 2
            + [buffer for size in sizes for buffer in reduce_buffers(*size)],
        ),
        out_shape=[
            jax.ShapeDtypeStruct((MICRO * TD, D), jnp.bfloat16),
            jax.ShapeDtypeStruct((MICRO * QP, D), jnp.bfloat16),
            jax.ShapeDtypeStruct((MICRO * n_keys, D), jnp.bfloat16),
            jax.ShapeDtypeStruct((MICRO * n_keys, D), jnp.bfloat16),
            jax.ShapeDtypeStruct((MICRO, PAIRS, 64, LANES), jnp.float32),
        ]
        + kept,
        compiler_params=host_params(3, carried),
        cost_estimate=pl.CostEstimate(
            flops=10 * pairs * LANES, bytes_accessed=32 * 1024 * 1024, transcendentals=pairs
        ),
    )(
        meta,
        queries,
        extra_q,
        k_rows,
        v_rows,
        table,
        xcol,
        xrow,
        lse,
        dc,
        dx,
        fc,
        fx,
        *grads,
    )


def from_partner(block, axis):
    count = lax.axis_size(axis)
    return lax.ppermute(block, axis, [(i, i ^ 1) for i in range(count)])


TAIL_RATE = 0.24
TAIL = (
    0.08952757299725976,
    0.1555125511021828,
    -0.15404562880205064,
    0.6255850035411683,
    -0.6460658211054147,
    0.554571568104313,
    -0.12508524614530675,
)


def gelu_parts(hidden):
    bell = jnp.exp(-0.5 * hidden * hidden)
    t = 1.0 / (1.0 + TAIL_RATE * jnp.abs(hidden))
    poly = TAIL[-1]
    for term in TAIL[-2::-1]:
        poly = poly * t + term
    tail = poly * t * bell
    cdf = jnp.where(hidden < 0.0, tail, 1.0 - tail)
    return hidden * cdf, cdf + hidden * bell * 0.3989422804014327


TILE = 448
GRAD_STEPS = 9


def fold_rows(term):
    return jnp.sum(term.reshape(-1, 8, term.shape[1]), axis=0)


def middle_kernel(
    x_c,
    x_x,
    ctx_c,
    ctx_x,
    cot_c,
    cot_x,
    w_out,
    w_up_ref,
    w_down_ref,
    vec,
    up_bias,
    out_c,
    out_x,
    dres,
    dctx_c,
    dctx_x,
    g_down,
    g_up,
    g_out,
    sums_out,
    act,
    dhid,
    slope,
    first_b,
    dres_two_b,
    dres_one_b,
    norm_one,
    inverse_one,
    work,
    outs,
    dctx,
    sums,
    sems,
    w_up,
    w_down,
    x,
    ctx,
    cot,
    load_sems,
):
    step = pl.program_id(0)
    load_up = pltpu.make_async_copy(w_up_ref, w_up, load_sems.at[0])
    load_down = pltpu.make_async_copy(w_down_ref, w_down, load_sems.at[1])
    loads = []
    for content, extra, rows in ((x_c, x_x, x), (ctx_c, ctx_x, ctx), (cot_c, cot_x, cot)):
        size = content.shape[0]
        for source, at in ((content, pl.ds(0, size)), (extra, pl.ds(size, 2 * QP))):
            sem = load_sems.at[2 + len(loads)]
            loads.append(pltpu.make_async_copy(source, rows.at[at], sem))
    width = w_up.shape[1]
    rows_c = out_c.shape[0]
    tiles = x.shape[0] // TILE
    out_bias, gain_one, shift_one = vec[0:1], vec[1:2], vec[2:3]
    down_bias, gain_two, shift_two = vec[3:4], vec[4:5], vec[5:6]
    split = rows_c - TILE
    moves = [
        [
            (outs.at[pl.ds(0, TILE)], out_c.at[pl.ds(0, TILE)]),
            (dctx.at[pl.ds(0, TILE)], dctx_c.at[pl.ds(0, TILE)]),
        ],
        [
            (outs.at[pl.ds(TILE, split)], out_c.at[pl.ds(TILE, split)]),
            (dctx.at[pl.ds(TILE, split)], dctx_c.at[pl.ds(TILE, split)]),
            *[
                (outs.at[pl.ds(rows_c + QP * m, out_x.shape[1])], out_x.at[m])
                for m in range(MICRO)
            ],
            (dctx.at[pl.ds(rows_c, 2 * QP)], dctx_x),
        ],
    ]
    count = 0
    for group in moves:
        for i, (src, dst) in enumerate(group):
            group[i] = pltpu.make_async_copy(src, dst, sems.at[count])
            count += 1

    def mean(value):
        return jnp.mean(value, axis=-1, keepdims=True)

    @pl.when(step == 0)
    def _():
        start(loads[2:4] + loads[0:2])
        load_up.start()
        start(loads[4:6])
        load_down.start()
        for copy in loads[0:4]:
            copy.wait()
        sums[...] = jnp.zeros_like(sums)

    @pl.when(step < tiles)
    def _():
        base = pl.multiple_of(step * TILE, 64)
        rows = pl.ds(base, TILE)
        work[...] = dot_nn(ctx[rows], w_out[...])

        value = x[rows].astype(jnp.float32) + work[...] + out_bias
        centred = value - mean(value)
        inverse = lax.rsqrt(mean(centred * centred) + 1e-05)
        normed = centred * inverse
        norm_one[...] = normed
        inverse_one[...] = jnp.broadcast_to(inverse, (TILE, LANES))
        first_b[rows] = (normed * gain_one + shift_one).astype(jnp.bfloat16)

        @pl.when(step == 0)
        def _():
            load_up.wait()

        parts = 12
        block = width // parts

        def lift(c):
            cols = slice(block * c, block * c + block)
            slope[:, cols] = dot_nn(first_b[rows], w_up[:, cols])

        lift(0)
        for c in range(parts):
            cols = slice(block * c, block * c + block)
            if c + 1 < parts:
                lift(c + 1)
            active, gradient = gelu_parts(slope[:, cols] + up_bias[0:1, cols])
            act[rows, cols] = active.astype(jnp.bfloat16)
            slope[:, cols] = gradient

        @pl.when(step == 0)
        def _():
            load_down.wait()
            for copy in loads[4:6]:
                copy.wait()

        work[...] = dot_nn(act[rows], w_down[...])

        value = norm_one[...] * gain_one + shift_one + work[...] + down_bias
        centred = value - mean(value)
        inverse = lax.rsqrt(mean(centred * centred) + 1e-05)
        normed = centred * inverse
        outs[rows] = normed * gain_two + shift_two
        upstream = cot[rows].astype(jnp.float32)
        scaled = upstream * gain_two
        grad = inverse * (scaled - mean(scaled) - normed * mean(scaled * normed))
        work[...] = grad
        dres_two_b[rows] = grad.astype(jnp.bfloat16)
        for k, term in enumerate((upstream * normed, upstream, grad)):
            sums[8 * k : 8 * k + 8, 0:D] += fold_rows(term)

        block = width // 12
        for c in range(12):
            cols = slice(block * c, block * c + block)
            dact = dot_nt(dres_two_b[rows], w_down[cols]).astype(jnp.bfloat16)
            grad = dact.astype(jnp.float32) * slope[:, cols]
            grad_b = grad.astype(jnp.bfloat16)
            dhid[rows, cols] = grad_b
            sums[48:56, cols] += jnp.sum(
                grad_b.astype(jnp.float32).reshape(TILE // 8, 8, block), axis=0
            )
        work[...] += dot_nt(dhid[rows], w_up[...])

        normed = norm_one[...]
        inverse = inverse_one[:, 0:1]
        upstream = work[...]
        scaled = upstream * gain_one
        grad = inverse * (scaled - mean(scaled) - normed * mean(scaled * normed))
        dres[...] = grad
        dres_one_b[rows] = grad.astype(jnp.bfloat16)
        for k, term in enumerate((upstream * normed, upstream, grad)):
            sums[24 + 8 * k : 32 + 8 * k, 0:D] += fold_rows(term)

        dctx[rows] = dot_nt(dres_one_b[rows], w_out[...]).astype(jnp.bfloat16)

    for tile in range(2):

        @pl.when(step == tile)
        def _():
            for copy in moves[tile]:
                copy.start()

    quarter = width // 4
    for c in range(4):
        cols = slice(quarter * c, quarter * c + quarter)

        @pl.when(step == tiles + c)
        def _():
            g_down[...] = dot_tn(act[:, cols], dres_two_b[...]).astype(jnp.bfloat16)

        @pl.when(step == tiles + 4 + c)
        def _():
            g_up[...] = dot_tn(first_b[...], dhid[:, cols]).astype(jnp.bfloat16)

    @pl.when(step == tiles + 8)
    def _():
        g_out[...] = dot_tn(ctx[...], dres_one_b[...]).astype(jnp.bfloat16)
        for k in range(7):
            sums_out[k : k + 1] = jnp.sum(sums[8 * k : 8 * k + 8], axis=0, keepdims=True)
        sums_out[7:8] = jnp.zeros_like(sums_out[7:8])
        for group in moves:
            for copy in group:
                copy.wait()


def middle(
    x_c, x_x, ctx_c, ctx_x, cot_c, cot_x, w_out, w_up, w_down, vec, up_bias, extra_rows
):
    rows_c = x_c.shape[0]
    rows = rows_c + x_x.shape[0]
    width = w_up.shape[1]
    tiles = rows // TILE
    quarter = width // 4
    def once(array):
        return pl.BlockSpec(array.shape, lambda s: (0, 0), pipeline_mode=pl.Buffered(1))

    bf, f32 = jnp.bfloat16, jnp.float32
    return pl.pallas_call(
        middle_kernel,
        name="middle",
        grid=(tiles + GRAD_STEPS,),
        in_specs=[
            *[ANY_SPEC] * 6,
            once(w_out),
            ANY_SPEC,
            ANY_SPEC,
            once(vec),
            once(up_bias),
        ],
        out_specs=[
            ANY_SPEC,
            ANY_SPEC,
            pl.BlockSpec((TILE, D), lambda s: (jnp.minimum(s, tiles - 1), 0)),
            ANY_SPEC,
            ANY_SPEC,
            pl.BlockSpec((quarter, D), lambda s: (jnp.clip(s - tiles, 0, 3), 0)),
            pl.BlockSpec((D, quarter), lambda s: (0, jnp.clip(s - tiles - 4, 0, 3))),
            pl.BlockSpec((D, D), lambda s: (0, 0)),
            pl.BlockSpec((8, width), lambda s: (0, 0)),
        ],
        out_shape=[
            jax.ShapeDtypeStruct((rows_c, D), f32),
            jax.ShapeDtypeStruct((MICRO, extra_rows, D), f32),
            jax.ShapeDtypeStruct((rows, D), f32),
            jax.ShapeDtypeStruct((rows_c, D), bf),
            jax.ShapeDtypeStruct((rows - rows_c, D), bf),
            jax.ShapeDtypeStruct((width, D), bf),
            jax.ShapeDtypeStruct((D, width), bf),
            jax.ShapeDtypeStruct((D, D), bf),
            jax.ShapeDtypeStruct((8, width), f32),
        ],
        scratch_shapes=[
            pltpu.VMEM((rows, width), bf),
            pltpu.VMEM((rows, width), bf),
            pltpu.VMEM((TILE, width), f32),
            pltpu.VMEM((rows, D), bf),
            pltpu.VMEM((rows, D), bf),
            pltpu.VMEM((rows, D), bf),
            pltpu.VMEM((TILE, D), f32),
            pltpu.VMEM((TILE, LANES), f32),
            pltpu.VMEM((TILE, D), f32),
            pltpu.VMEM((rows, D), f32),
            pltpu.VMEM((rows, D), bf),
            pltpu.VMEM((56, width), f32),
            pltpu.SemaphoreType.DMA((7,)),
            pltpu.VMEM(w_up.shape, bf),
            pltpu.VMEM(w_down.shape, bf),
            pltpu.VMEM((rows, D), bf),
            pltpu.VMEM((rows, D), bf),
            pltpu.VMEM((rows, D), bf),
            pltpu.SemaphoreType.DMA((8,)),
        ],
        compiler_params=pltpu.CompilerParams(vmem_limit_bytes=60 * 1024 * 1024),
        cost_estimate=pl.CostEstimate(
            flops=2 * rows * D * (6 * width + 3 * D),
            bytes_accessed=40 * 1024 * 1024,
            transcendentals=2 * rows * width,
        ),
    )(x_c, x_x, ctx_c, ctx_x, cot_c, cot_x, w_out, w_up, w_down, vec, up_bias)


SMALL_ROWS = 32


def table_rows(hist, buckets_of, side):
    lane = lax.broadcasted_iota(jnp.int32, (LANES, LANES), 0)
    target = lax.broadcasted_iota(jnp.int32, (LANES, LANES), 1)
    signed = jnp.where(lane < 64, lane, lane - 128)
    distances = (
        lane,
        128 + side + 2 * signed,
        127 + side + 2 * signed,
        2 * lane + 2 * side - 1,
        2 * lane,
    )
    kinds = [[] for _ in distances]
    row = lax.broadcasted_iota(jnp.int32, (8, LANES), 0)
    for pair in range(PAIRS):
        for head in range(2):
            block = [
                sum(hist[m, pair, 32 * head + 8 * k : 32 * head + 8 * k + 8] for m in range(MICRO))
                for k in range(4)
            ]
            picks = (
                block[0],
                jnp.where(row % 2 == 0, block[1], 0.0),
                jnp.where(row % 2 == 0, 0.0, block[1]),
                block[2],
                block[3],
            )
            for kind, pick in zip(kinds, picks):
                kind.append(jnp.sum(pick, axis=0, keepdims=True))
    pad = [jnp.zeros((16 - 2 * PAIRS, LANES), jnp.float32)]
    close = jnp.zeros((16, LANES), jnp.float32)
    for kind, distance in zip(kinds, distances):
        hot = jnp.where((distance == target) & (target < LANES - 1), 1.0, 0.0)
        close = close + jnp.dot(
            jnp.concatenate(kind + pad, axis=0),
            hot,
            precision=PRECISE,
            preferred_element_type=jnp.float32,
        )
    last = lax.broadcasted_iota(jnp.int32, (16, LANES), 1) == LANES - 1
    close = jnp.where(last, -jnp.sum(close, axis=1, keepdims=True), close)
    bucket_hot = jnp.where(lane == buckets_of[0:1], 1.0, 0.0)
    return lax.dot_general(
        close,
        bucket_hot,
        (((1,), (1,)), ((), ())),
        precision=PRECISE,
        preferred_element_type=jnp.float32,
    )


def finish_kernel(
    dq_c_ref,
    dq_x,
    dk_ref,
    dv_ref,
    keys_0_ref,
    keys_1_ref,
    x_c_ref,
    x_q,
    w_q,
    w_k,
    w_v,
    dres_ref,
    hist,
    buckets_of,
    sums,
    d_ref,
    q_share,
    k_share,
    v_share,
    d_share,
    small_out,
    grad_c,
    grad_q,
    *scratch,
):
    shares = [q_share, k_share, v_share] + halves_of(d_share)
    buffers = [scratch[11 * i : 11 * i + 11] for i in range(5)]
    (
        grads,
        prompts,
        theirs,
        along,
        nears,
        near_got,
        owns,
        out_c,
        small,
        x_s,
        x_r,
        sm_s,
        sm_r,
        sem,
        dq_c,
        dk,
        dv,
        keys_0,
        keys_1,
        x_c,
        load_sem,
    ) = scratch[55:]
    net = Net()
    net.greet()
    sources = [grads.at[i] for i in range(3)] + halves_of(d_ref)
    one, two, three, down, rest = (
        reduce_stages(net, sources[i], shares[i], buffers[i]) for i in range(5)
    )
    n_keys = dk.shape[0] // MICRO
    halves = [pl.ds(m * n_keys, n_keys) for m in range(MICRO)]
    moves = []
    for half in halves:
        moves += [(dk_ref.at[half], dk.at[half]), (dv_ref.at[half], dv.at[half])]
    moves += [(x_c_ref, x_c), (dq_c_ref, dq_c), (keys_0_ref, keys_0), (keys_1_ref, keys_1)]
    moves.append((dres_ref, out_c))
    loads = [
        pltpu.make_async_copy(src, dst, load_sem.at[i]) for i, (src, dst) in enumerate(moves)
    ]
    start(loads)

    def loaded(first, last):
        for copy in loads[first:last]:
            copy.wait()

    down[0]()
    rest[0]()
    copies = Copies(x_s, x_r)
    to_mate = [
        copies.to(net.to_mate, prompts.at[m, :, 1 - net.c], theirs.at[m]) for m in range(MICRO)
    ]
    swap = copies.to(net.to_mate, nears, near_got)
    third, relay = [], []
    for m in range(MICRO):
        third.append(
            [
                copies.to(net.to_z[0], prompts.at[m, net.z_of[2], net.c], along.at[0, m]),
                copies.to(net.to_z[0], prompts.at[m, net.z_of[0], net.c], along.at[1, m]),
            ]
        )
        passed = prompts.at[m, net.z_of[1], net.c]
        relay.append(copies.to(net.to_z[1], passed, along.at[2, m]))
    hops = Copies(sm_s, sm_r)
    partners = [net.to_mate, net.to_x, net.to_y, net.to_z[0], net.to_z[1]]
    butterfly = [
        hops.to(partner, small.at[i], small.at[i + 1]) for i, partner in enumerate(partners)
    ]

    def hop(i):
        butterfly[i].wait_recv()
        small[i + 1] = small[i + 1] + small[i]
        if i + 1 < len(butterfly):
            butterfly[i + 1].start()

    n_prompt = n_keys - 2 * CH

    def put(value, which):
        part = D // 32
        for owner in range(8):
            for q in range(4):
                at = (4 * owner + q) * part
                grads[which, owner // 2, owner % 2, q] = value[at : at + part].astype(
                    jnp.bfloat16
                )

    def back(rows):
        return dot_nt(dk[rows], w_k[...]) + dot_nt(dv[rows], w_v[...])

    def onward(m):
        to_mate[m].wait_recv()

        @pl.loop(0, 4)
        def _(zi):
            prompts[m, zi, net.c] = prompts[m, zi, net.c] + theirs[m, zi]

        start(third[m])

    def onto(m):
        third[m][0].wait_recv()
        prompts[m, net.z_of[1], net.c] = prompts[m, net.z_of[1], net.c] + along[0, m]
        relay[m].start()

    def prompt_back(m):
        for part in range(n_prompt // 512):
            value = back(slice(m * n_keys + 512 * part, m * n_keys + 512 * part + 512))
            for i in range(4):
                owner = 4 * part + i
                prompts[m, owner // 2, owner % 2] = value[128 * i : 128 * i + 128].astype(
                    jnp.bfloat16
                )
        to_mate[m].start()

    loaded(0, 2)
    prompt_back(0)
    down[1]()
    rest[1]()
    loaded(2, 4)
    prompt_back(1)
    onward(0)
    loaded(4, 6)
    put(dot_tn(x_c[...], dq_c[...]) + dot_tn(x_q[...], dq_x[...]), 0)
    one[0]()
    onward(1)
    loaded(6, 8)
    put(dot_tn(keys_0[...], dk[:n_keys]) + dot_tn(keys_1[...], dk[n_keys:]), 1)
    two[0]()
    one[1]()
    down[2]()
    put(dot_tn(keys_0[...], dv[:n_keys]) + dot_tn(keys_1[...], dv[n_keys:]), 2)
    three[0]()
    two[1]()
    rest[2]()
    onto(0)
    three[1]()
    down[3]()
    one[2]()
    for m in range(MICRO):
        value = back(slice(m * n_keys + n_prompt, (m + 1) * n_keys))
        for i in range(2):
            nears[m, i] = value[256 * i : 256 * i + 128].astype(jnp.bfloat16)
            owns[m, i] = value[256 * i + 128 : 256 * i + 256]
    swap.start()
    small[0] = jnp.zeros_like(small[0])
    sum_q = jnp.sum(dq_c[...].astype(jnp.float32), axis=0, keepdims=True)
    sum_q = sum_q + jnp.sum(dq_x[...].astype(jnp.float32), axis=0, keepdims=True)
    small[0, 0:1] = sum_q
    small[0, 1:2] = jnp.sum(dv[...].astype(jnp.float32), axis=0, keepdims=True)
    for i in range(6):
        small[0, 2 + i : 3 + i] = sums[i : i + 1, 0:D]
    for i in range(4):
        small[0, 8 + i : 9 + i] = sums[6:7, D * i : D * i + D]
    small[0, 16:32, 0:LANES] = table_rows(hist, buckets_of, net.c)
    butterfly[0].start()
    rest[3]()
    onto(1)
    two[2]()
    down[4]()
    one[3]()
    hop(0)
    three[2]()
    rest[4]()
    loaded(8, 9)
    rows_c = x_c.shape[0]
    out_c[0:rows_c] = out_c[0:rows_c] + dot_nt(dq_c[...], w_q[...])
    out_c[rows_c:] = out_c[rows_c:] + dot_nt(dq_x[...], w_q[...])
    two[3]()
    down[5]()
    one[4]()
    hop(1)
    three[3]()
    rest[5]()
    two[4]()
    swap.wait_recv()
    for m in range(MICRO):
        for i in range(2):
            rows = slice(m * TD + PD + 128 * i, m * TD + PD + 128 * i + 128)
            out_c[rows] = out_c[rows] + owns[m, i] + near_got[m, i].astype(jnp.float32)
    down[6]()
    one[5]()
    hop(2)
    three[4]()
    rest[6]()
    two[5]()
    hop(3)
    down[7]()
    for m in range(MICRO):
        arrive([third[m][1], relay[m]])
        total = prompts[m, net.z, net.c].astype(jnp.float32)
        for k in range(1, 3):
            total = total + along[k, m].astype(jnp.float32)
        rows = slice(m * TD, m * TD + PD)
        out_c[rows] = out_c[rows] + total
    stores = [
        pltpu.make_async_copy(out_c.at[pl.ds(0, rows_c)], grad_c, sem.at[0]),
    ]
    for m in range(MICRO):
        rows = out_c.at[pl.ds(rows_c + QP * m, grad_q.shape[1])]
        stores.append(pltpu.make_async_copy(rows, grad_q.at[m], sem.at[1 + m]))
    start(stores)
    one[6]()
    three[5]()
    rest[7]()
    hop(4)
    keep = pltpu.make_async_copy(small.at[5], small_out, sem.at[3])
    keep.start()
    two[6]()
    one[7]()
    three[6]()
    two[7]()
    three[7]()
    for copy in stores + [keep]:
        copy.wait()
    copies.finish()
    hops.finish()


def finish(
    dq_c,
    dq_x,
    dk,
    dv,
    keys_x,
    x_c,
    x_q,
    weights,
    dres,
    hist,
    buckets_of,
    sums,
    down_grad,
    extra_rows,
):
    whole = pl.BlockSpec(memory_space=pltpu.VMEM)
    bf, f32 = jnp.bfloat16, jnp.float32
    rows_c, rows_x = x_c.shape[0], x_q.shape[0]
    part, tall = D // 32, down_grad.shape[3]
    return pl.pallas_call(
        finish_kernel,
        name="finish",
        in_specs=[ANY_SPEC, whole]
        + [ANY_SPEC] * 5
        + [whole] * 4
        + [ANY_SPEC]
        + [whole] * 3
        + [ANY_SPEC],
        out_specs=[ANY_SPEC] * 7,
        out_shape=[
            jax.ShapeDtypeStruct((4, part, D), f32),
            jax.ShapeDtypeStruct((4, part, D), f32),
            jax.ShapeDtypeStruct((4, part, D), f32),
            jax.ShapeDtypeStruct((4, tall, D), f32),
            jax.ShapeDtypeStruct((SMALL_ROWS, D), f32),
            jax.ShapeDtypeStruct((rows_c, D), f32),
            jax.ShapeDtypeStruct((MICRO, extra_rows, D), f32),
        ],
        scratch_shapes=reduce_buffers(4 * part, D) * 3
        + reduce_buffers(2 * tall, D) * 2
        + [
            pltpu.VMEM((3, 4, 2, 4, part, D), bf),
            pltpu.VMEM((MICRO, 4, 2, PD, D), bf),
            pltpu.VMEM((MICRO, 4, PD, D), bf),
            pltpu.VMEM((3, MICRO, PD, D), bf),
            pltpu.VMEM((MICRO, 2, 128, D), bf),
            pltpu.VMEM((MICRO, 2, 128, D), bf),
            pltpu.VMEM((MICRO, 2, 128, D), f32),
            pltpu.VMEM((rows_c + rows_x, D), f32),
            pltpu.VMEM((6, SMALL_ROWS, D), f32),
            pltpu.SemaphoreType.DMA((9,)),
            pltpu.SemaphoreType.DMA((9,)),
            pltpu.SemaphoreType.DMA((5,)),
            pltpu.SemaphoreType.DMA((5,)),
            pltpu.SemaphoreType.DMA((4,)),
        ]
        + [
            pltpu.VMEM(kept.shape, kept.dtype)
            for kept in (dq_c, dk, dv, *keys_x, x_c)
        ]
        + [pltpu.SemaphoreType.DMA((9,))],
        compiler_params=pltpu.CompilerParams(
            collective_id=4, has_side_effects=True, vmem_limit_bytes=60 * 1024 * 1024
        ),
    )(dq_c, dq_x, dk, dv, *keys_x, x_c, x_q, *weights, dres, hist, buckets_of, sums, down_grad)


def pad_rows(block):
    return jnp.pad(block, ((0, 0), (0, QP - block.shape[1]), (0, 0))).reshape(MICRO * QP, D)


def table_gradient(hist, rel_bucket, buckets, side, heads):
    summed = jnp.sum(hist, axis=0).reshape(PAIRS, 2, 4, 8, LANES)
    prompt = jnp.sum(summed[:, :, 0], axis=2)
    even = jnp.sum(summed[:, :, 1, 0::2], axis=2)
    odd = jnp.sum(summed[:, :, 1, 1::2], axis=2)
    near = jnp.sum(summed[:, :, 2], axis=2)
    own = jnp.sum(summed[:, :, 3], axis=2)
    lanes = jnp.arange(LANES, dtype=jnp.int32)
    signed = jnp.where(lanes < 64, lanes, lanes - 128)
    distance = jnp.stack(
        [
            lanes,
            128 + side + 2 * signed,
            127 + side + 2 * signed,
            2 * lanes + 2 * side - 1,
            2 * lanes,
        ]
    ).reshape(-1)
    hot = (distance[:, None] == lanes[None, :]) & (lanes[None, :] < LANES - 1)
    parts = jnp.stack([prompt, even, odd, near, own], axis=2).reshape(heads, 5 * LANES)
    close = jnp.dot(parts, hot.astype(jnp.float32), precision=PRECISE)
    close = jnp.where(
        lanes[None, :] == LANES - 1, -jnp.sum(close, axis=1, keepdims=True), close
    )
    bucket_hot = (rel_bucket[:, None] == jnp.arange(buckets, dtype=jnp.int32)[None, :]).astype(
        jnp.float32
    )
    return jnp.dot(bucket_hot.T, close.T, precision=PRECISE)


def on_device(
    content_in,
    query_in,
    pred_order,
    cont_prompt,
    rel_bucket,
    w_query,
    b_query,
    w_key,
    w_value,
    b_value,
    w_out,
    b_out,
    ln1_gain,
    ln1_bias,
    w_up,
    b_up,
    w_down,
    b_down,
    ln2_gain,
    ln2_bias,
    bias_table,
    cot_content,
    cot_query,
):
    devices = lax.axis_size("fsdp")
    halfway = devices // 2
    own_rank = lax.axis_index("fsdp")
    plength = PD * halfway
    heads = bias_table.shape[1]
    extra_rows = query_in.shape[1]
    prompt_base = own_rank % halfway * PD
    cont_index = own_rank // 2
    side = own_rank % 2

    own_links = lax.axis_size("grp") == 4 and devices == 8

    def gather(entry):
        return lax.all_gather(entry, "fsdp", axis=0, tiled=True)

    def quarters(entry):
        return entry.reshape(4, -1, entry.shape[1])

    n_keys = 2 * plength + 2 * CH
    shard = b_query.shape[0]
    up_size = b_up.shape[0]
    vectors = jnp.stack(
        [b_query, b_value, b_out, b_down, ln1_gain, ln1_bias, ln2_gain, ln2_bias]
        + [b_up[shard * i : shard * i + shard] for i in range(up_size // shard)]
    )
    tokens_x = content_in.reshape(MICRO * TD, D)
    extra_x = pad_rows(query_in)
    if own_links:
        lines = vectors.shape[0]
        vector_shard = jnp.pad(vectors, ((0, 32 - lines), (0, 256 - shard))).reshape(4, 8, 256)
        *qkv_weights, all_vectors, first_rows = gather_first(
            [quarters(w_query), quarters(w_key), quarters(w_value), vector_shard], content_in
        )
        qkv_weights = [entry.reshape(-1, D) for entry in qkv_weights]
        all_vectors = all_vectors.reshape(devices, 32, 256)[:, :lines, :shard]
        other = content_in
        carried = tuple(quarters(shard) for shard in (w_up, w_down, w_out))
    else:
        qkv_weights = [gather(w_query), gather(w_key), gather(w_value)]
        all_vectors = gather(vectors[None])
        up_weight, down_weight, out_weight = gather(w_up), gather(w_down), gather(w_out)
        carried = ()
        prompt_x = lax.all_gather(content_in[:, :PD], "fsdp", axis=1, tiled=True)
        near_x = from_partner(content_in[:, PD:], "fsdp").reshape(MICRO, 2, 1, 128, D)
        own_x = content_in[:, PD:].reshape(MICRO, 2, 1, 128, D)
        cont_x = jnp.concatenate([near_x, own_x], axis=2).reshape(MICRO, 2 * CH, D)
        first_rows, other = jnp.concatenate([prompt_x, cont_x], axis=1)
    singles = [
        all_vectors[:, i].reshape(-1).astype(jnp.float32)
        for i in range(8)
    ]
    (
        query_bias,
        value_bias,
        out_bias,
        down_bias,
        gain_one,
        shift_one,
        gain_two,
        shift_two,
    ) = singles
    up_bias = all_vectors[:, 8:].reshape(-1).astype(jnp.float32)

    prompt_map = cont_prompt[:, 0, :]
    prompt_ref = jnp.sum(
        jnp.where(
            jnp.arange(prompt_map.shape[1], dtype=jnp.int32)[None, :] == cont_index, prompt_map, 0
        ),
        axis=1,
    )
    meta = prompt_ref.astype(jnp.int32)
    order = jnp.pad(pred_order[:, 0, :], ((0, 0), (0, QP - extra_rows)), constant_values=-1)
    real = order >= 0
    in_prompt = order < PD
    position = jnp.where(
        in_prompt, prompt_base + order, plength + 2 * (order - PD) + side
    )
    limit_p = jnp.where(real & in_prompt, jnp.maximum(position, 1), -1)
    limit_c = jnp.where(real & ~in_prompt, position, -1)
    info = jnp.stack([position, limit_p, limit_c, order], axis=1)
    info = jnp.concatenate([info, info], axis=2)
    xrow = jnp.pad(info, ((0, 0), (0, 4), (0, 0))).astype(jnp.int32)
    xcol = jnp.swapaxes(xrow, 1, 2)
    dist = bias_table.astype(jnp.float32)[rel_bucket].T
    dist = dist - dist[:, LANES - 1 :]
    table = jnp.pad(dist.reshape(PAIRS, 2, LANES), ((0, 0), (0, 6), (0, 0)))

    bias = jnp.pad(jnp.stack([query_bias, value_bias]), ((0, 6), (0, 0)))
    ctx_c, ctx_x, full_c, full_x, lse, queries, extra_q, k_rows, v_rows, *gathered = attend(
        meta, tokens_x, extra_x, qkv_weights, bias, table, xcol, first_rows, other, carried
    )
    keys_x = (first_rows, other)
    if own_links:
        keys_x = (first_rows, gathered[0])
        up_weight, down_weight, out_weight = (
            entry.reshape(-1, entry.shape[2]) for entry in gathered[1:]
        )
    rows_c = MICRO * TD
    vec = jnp.stack([out_bias, gain_one, shift_one, down_bias, gain_two, shift_two])
    (
        out_content,
        out_query,
        dres_one,
        dctx_c,
        dctx_x,
        dweight_down,
        dweight_up,
        dweight_out,
        sums,
    ) = middle(
        tokens_x,
        extra_x,
        ctx_c,
        ctx_x,
        cot_content.reshape(rows_c, D),
        pad_rows(cot_query),
        out_weight,
        up_weight,
        down_weight,
        vec,
        up_bias[None],
        extra_rows,
    )
    out_content = out_content.reshape(MICRO, TD, D)

    def by_quarter(grad):
        grad = grad.astype(jnp.bfloat16)
        return grad.reshape(4, 2, 4, grad.shape[0] // 32, grad.shape[1])

    to_reduce = ()
    if own_links:
        to_reduce = (by_quarter(dweight_up), by_quarter(dweight_out))
    dq_c, dq_x, dk_rows, dv_rows, hist, *reduced = attend_back(
        meta,
        queries,
        extra_q,
        k_rows,
        v_rows,
        table,
        xcol,
        xrow,
        lse,
        dctx_c,
        dctx_x,
        full_c,
        full_x,
        to_reduce,
    )
    if own_links:
        *t_qkv, t_down, small, grad_content, grad_query = finish(
            dq_c,
            dq_x,
            dk_rows,
            dv_rows,
            keys_x,
            tokens_x,
            extra_x,
            qkv_weights,
            dres_one,
            hist,
            jnp.broadcast_to(rel_bucket[None], (8, LANES)),
            sums,
            by_quarter(dweight_down),
            extra_rows,
        )
        grad_content = grad_content.reshape(MICRO, TD, D)
        t_up, t_out = reduced
        shares = (t_down, t_up, t_out, *t_qkv)
        t_down, t_up, t_out, *t_qkv = [
            entry.reshape(-1, entry.shape[-1]) for entry in shares
        ]
        pieces = lax.dynamic_slice_in_dim(small[:8], own_rank * shard, shard, 1)
        t_bup = lax.dynamic_index_in_dim(
            small[8:12].reshape(devices, up_size), own_rank, 0, keepdims=False
        )
        t_table = lax.dynamic_slice_in_dim(
            small[16 : 16 + heads, : bias_table.shape[0]],
            own_rank * (bias_table.shape[0] // devices),
            bias_table.shape[0] // devices,
            1,
        ).T
    else:
        dgain_two, dshift_two, dbias_down, dgain_one, dshift_one, dbias_out = sums[:6, :D]
        dbias_up = sums[6]
        dkv_rows = jnp.concatenate([dk_rows, dv_rows], axis=1)
        dq_all = jnp.concatenate([dq_c, dq_x])
        dbias_query = jnp.sum(dq_all.astype(jnp.float32), axis=0)
        dbias_value = jnp.sum(dv_rows.astype(jnp.float32), axis=0)
        query_weight, key_weight, value_weight = qkv_weights
        kv_weight = jnp.concatenate([key_weight, value_weight], axis=1)
        keys_x = jnp.concatenate(keys_x)
        dkeys_x = dot_nt(dkv_rows, kv_weight).reshape(MICRO, n_keys, D)
        dtable = table_gradient(hist, rel_bucket, bias_table.shape[0], side, heads)
        small = jnp.concatenate(
            [
                entry.reshape(devices, -1)
                for entry in (
                    dbias_query,
                    dbias_value,
                    dgain_two,
                    dshift_two,
                    dbias_down,
                    dgain_one,
                    dshift_one,
                    dbias_out,
                    dbias_up,
                    dtable,
                )
            ],
            axis=1,
        ).astype(jnp.bfloat16)
        dprompts = dkeys_x[:, : 2 * plength].astype(jnp.bfloat16)
        dcont = dkeys_x[:, 2 * plength :].reshape(MICRO, 2, 2, 128, D)
        dnear = dcont[:, :, 0].astype(jnp.bfloat16)
        dweight_qkv = jnp.concatenate(
            [dot_tn(jnp.concatenate([tokens_x, extra_x]), dq_all), dot_tn(keys_x, dkv_rows)], axis=1
        )

        def scatter(piece, dimension=0):
            return lax.psum_scatter(
                piece.astype(jnp.bfloat16), "fsdp", scatter_dimension=dimension, tiled=True
            )

        from_prompts = scatter(dprompts, 1).astype(jnp.float32)
        from_near = from_partner(dnear, "fsdp")
        shares = [
            scatter(piece)
            for piece in (dweight_down, dweight_up, dweight_out, dweight_qkv, small)
        ]
        t_down, t_up, t_out, t_qkv, t_small = [
            lax.psum(entry, "grp").astype(jnp.float32) for entry in shares
        ]
        t_qkv = [t_qkv[:, D * i : D * i + D] for i in range(3)]
        dcont = (dcont[:, :, 1] + from_near.astype(jnp.float32)).reshape(MICRO, CH, D)
        dx_all = dres_one + dot_nt(dq_all, query_weight)
        grad_content = dx_all[:rows_c].reshape(MICRO, TD, D) + jnp.concatenate(
            [from_prompts, dcont], axis=1
        )
        grad_query = dx_all[rows_c:].reshape(MICRO, QP, D)[:, :extra_rows]
        t_small = t_small.reshape(-1)
        pieces = [t_small[shard * i : shard * i + shard] for i in range(8)]
        up_at = 8 * shard
        t_bup = t_small[up_at : up_at + up_size]
        t_table = t_small[up_at + up_size :].reshape(-1, heads)
    return (
        out_content,
        out_query,
        grad_content,
        grad_query,
        t_qkv[0],
        pieces[0],
        t_qkv[1],
        t_qkv[2],
        pieces[1],
        t_out,
        pieces[7],
        pieces[5],
        pieces[6],
        t_up,
        t_bup,
        t_down,
        pieces[4],
        pieces[2],
        pieces[3],
        t_table,
    )


def solution(mesh):
    rows = P(None, ("grp", "fsdp"), None)
    matrix = P("fsdp", None)
    vector = P("fsdp")
    in_specs = (
        rows,
        rows,
        rows,
        P(None, "grp", None),
        P(),
        matrix,
        vector,
        matrix,
        matrix,
        vector,
        matrix,
        vector,
        vector,
        vector,
        matrix,
        vector,
        matrix,
        vector,
        vector,
        vector,
        P(),
        rows,
        rows,
    )
    out_specs = (
        rows,
        rows,
        rows,
        rows,
        matrix,
        vector,
        matrix,
        matrix,
        vector,
        matrix,
        vector,
        vector,
        vector,
        matrix,
        vector,
        matrix,
        vector,
        vector,
        vector,
        matrix,
    )
    return jax.shard_map(
        on_device, mesh=mesh, in_specs=in_specs, out_specs=out_specs, check_vma=False
    )
```

```python
import functools

import jax
import jax.numpy as jnp
from jax import lax
from jax.experimental import pallas as pl
from jax.experimental.pallas import tpu as pltpu
from jax.sharding import PartitionSpec as P

D = 768
PD = 128
CH = 256
MICRO = 2
TD = 384
QP = 64
HD = 64
LANES = 128
PAIRS = D // LANES

PRECISE = lax.Precision.HIGHEST
MASKED = -1e30
VMEM_LIMIT = 56 * 1024 * 1024


def dot_nt(left, right):
    return lax.dot_general(
        left, right, (((1,), (1,)), ((), ())), preferred_element_type=jnp.float32
    )


def dot_tn(left, right):
    return lax.dot_general(
        left, right, (((0,), (0,)), ((), ())), preferred_element_type=jnp.float32
    )


def dot_nn(left, right):
    return jnp.dot(left, right, preferred_element_type=jnp.float32)


def head_stack(block):
    lane = lax.broadcasted_iota(jnp.int32, block.shape, 1)
    zero = jnp.zeros_like(block)
    return jnp.concatenate(
        [jnp.where(lane < HD, block, zero), jnp.where(lane < HD, zero, block)], axis=0
    )


def head_merge(stacked):
    rows = stacked.shape[0] // 2
    lane = lax.broadcasted_iota(jnp.int32, (rows, LANES), 1)
    return jnp.where(lane < HD, stacked[:rows], stacked[rows:])


def lookup(table, index):
    return jnp.take_along_axis(table, index, axis=1, mode="promise_in_bounds")


def near_index(distance):
    return jnp.clip(distance, 0, LANES - 1)


def fill_keys(scratch, rows_ref, own_prompt, mapped, plength):
    own_at = pl.multiple_of(own_prompt * plength, 128)
    scratch[0:plength] = rows_ref[pl.ds(own_at, plength), :]
    scratch[plength : 2 * plength] = jnp.where(
        mapped == 0, rows_ref[0:plength], rows_ref[plength : 2 * plength]
    )
    scratch[2 * plength :] = rows_ref[2 * plength :]


MESH = pl.DeviceIdType.MESH
ANY_SPEC = pl.BlockSpec(memory_space=pl.ANY)


class Net:
    def __init__(self):
        self.g = lax.axis_index("grp")
        self.f = lax.axis_index("fsdp")
        self.x = self.g % 2
        self.y = self.g // 2
        self.z = self.f // 2
        self.c = self.f % 2
        self.gx = self.g + 1 - 2 * self.x
        self.gy = self.g + 2 - 4 * self.y
        self.mate = self.f + 1 - 2 * self.c
        self.z_of = [
            self.z + 1 - 2 * (self.z % 2),
            (self.z + 2) % 4,
            3 - self.z,
        ]
        self.f_of = [2 * other + self.c for other in self.z_of]
        self.to_x = (self.gx, self.f)
        self.to_y = (self.gy, self.f)
        self.to_corner = (3 - self.g, self.f)
        self.to_mate = (self.g, self.mate)
        self.to_z = [(self.g, other) for other in self.f_of]

    def greet(self):
        barrier = pltpu.get_barrier_semaphore()
        everyone = [self.to_x, self.to_y, self.to_corner, self.to_mate] + self.to_z
        for device in everyone:
            pl.semaphore_signal(barrier, inc=1, device_id=device, device_id_type=MESH)
        pl.semaphore_wait(barrier, len(everyone))


class Copies:
    def __init__(self, sends, recvs):
        self.sends = sends
        self.recvs = recvs
        self.used = 0
        self.all = []

    def to(self, device, src, dst):
        copy = pltpu.make_async_remote_copy(
            src_ref=src,
            dst_ref=dst,
            send_sem=self.sends.at[self.used],
            recv_sem=self.recvs.at[self.used],
            device_id=device,
            device_id_type=MESH,
        )
        self.used += 1
        self.all.append(copy)
        return copy

    def finish(self):
        for copy in self.all:
            copy.wait_send()


def start(copies):
    for copy in copies:
        copy.start()


def arrive(copies):
    for copy in copies:
        copy.wait_recv()


GATHER_COPIES = 19


def gather_stages(net, copies, local_sem, shard, full):
    part, width = shard.shape[1:]
    half = width // 2

    def rows(owner, quarter):
        return 4 * owner + quarter

    def whole(owner):
        return pl.ds(4 * owner, 4)

    local = pltpu.make_async_copy(shard, full.at[whole(net.f)], local_sem)
    mine = shard.at[net.g]
    along_z = [copies.to(device, mine, full.at[rows(net.f, net.g)]) for device in net.to_z[:2]]
    passed = full.at[rows(net.f_of[1], net.g)]
    relay = copies.to(net.to_z[0], passed, passed)
    to_mate = [copies.to(net.to_mate, shard, full.at[whole(net.f)])]
    to_x, to_y, on_x, on_y, later = [], [], [], [], []
    for owner in net.f_of:
        got = full.at[rows(owner, net.g)]
        to_x.append(copies.to(net.to_x, got, got))
        to_y.append(copies.to(net.to_y, got, got))
        left = full.at[rows(owner, net.gx), :, pl.ds(0, half)]
        on_y.append(copies.to(net.to_y, left, left))
        right = full.at[rows(owner, net.gy), :, pl.ds(half, half)]
        on_x.append(copies.to(net.to_x, right, right))
        shared = full.at[whole(owner)]
        later.append(copies.to(net.to_mate, shared, shared))

    def begin():
        local.start()
        start(along_z)
        start(to_mate)

    def onward():
        along_z[1].wait_recv()
        relay.start()

    def plane():
        arrive([along_z[0], relay])
        start(to_x + to_y)

    def corners():
        arrive(to_x + to_y)
        start(on_y + on_x)

    def mates():
        arrive(on_y + on_x)
        start(later)

    def end():
        arrive(to_mate + later)
        local.wait()
        copies.finish()

    return [begin, onward, plane, corners, mates, end]


REDUCE_COPIES = 19


def reduce_buffers(size, width):
    part, half = size // 4, width // 2
    return [
        pltpu.VMEM((4, 4, part, width), jnp.bfloat16),
        pltpu.VMEM((4, 4, part, width), jnp.bfloat16),
        pltpu.VMEM((4, 2, part, half), jnp.bfloat16),
        pltpu.VMEM((4, 2, part, half), jnp.bfloat16),
        pltpu.VMEM((2, 4, part, half), jnp.bfloat16),
        pltpu.VMEM((2, 3, part, half), jnp.bfloat16),
        pltpu.VMEM((2, 4, part, half), jnp.bfloat16),
        pltpu.VMEM((4, part, width), jnp.float32),
        pltpu.SemaphoreType.DMA((2,)),
        pltpu.SemaphoreType.DMA((REDUCE_COPIES,)),
        pltpu.SemaphoreType.DMA((REDUCE_COPIES,)),
    ]


def reduce_stages(net, grad, share, buffers):
    own, other, side_a, side_b, line, along, done, wide, local_sem, sends, recvs = buffers
    copies = Copies(sends, recvs)
    half = grad.shape[4] // 2
    left, right = pl.ds(0, half), pl.ds(half, half)
    load = pltpu.make_async_copy(grad.at[:, net.c], own, local_sem.at[0])
    to_mate = [copies.to(net.to_mate, grad.at[:, 1 - net.c], other)]
    first = []
    for i in range(2):
        first.append(
            copies.to(net.to_x, own.at[:, 2 * i + 1 - net.x, :, left], side_a.at[:, i])
        )
        first.append(
            copies.to(net.to_y, own.at[:, 2 - 2 * net.y + i, :, right], side_b.at[:, i])
        )
    second = [
        copies.to(net.to_y, side_a.at[:, 1 - net.y], line.at[0]),
        copies.to(net.to_x, side_b.at[:, 1 - net.x], line.at[1]),
    ]
    third = []
    for h in range(2):
        third.append(copies.to(net.to_z[0], line.at[h, net.z_of[2]], along.at[h, 0]))
        third.append(copies.to(net.to_z[0], line.at[h, net.z_of[0]], along.at[h, 1]))
    relay = [copies.to(net.to_z[1], line.at[h, net.z_of[1]], along.at[h, 2]) for h in range(2)]
    fourth = [
        copies.to(device, done.at[h, net.g], done.at[h, net.g])
        for h in range(2)
        for device in (net.to_corner, net.to_x, net.to_y)
    ]
    store = pltpu.make_async_copy(wide, share, local_sem.at[1])

    def begin():
        load.start()
        start(to_mate)

    def plane():
        load.wait()
        arrive(to_mate)

        @pl.loop(0, 16)
        def _(i):
            zi, qi = i // 4, i % 4
            own[zi, qi] = own[zi, qi] + other[zi, qi]

        start(first)

    def cross():
        arrive(first)

        @pl.loop(0, 8)
        def _(i):
            zi, qi = i // 2, i % 2
            side_a[zi, qi] = side_a[zi, qi] + own[zi, 2 * qi + net.x, :, 0:half]
            side_b[zi, qi] = side_b[zi, qi] + own[zi, 2 * net.y + qi, :, half : 2 * half]

        start(second)

    def column():
        arrive(second)

        @pl.loop(0, 4)
        def _(zi):
            line[0, zi] = line[0, zi] + side_a[zi, net.y]
            line[1, zi] = line[1, zi] + side_b[zi, net.x]

        start(third)

    def onward():
        arrive(third[0::2])

        @pl.loop(0, 2)
        def _(h):
            line[h, net.z_of[1]] = line[h, net.z_of[1]] + along[h, 0]

        start(relay)

    def spread():
        arrive(third[1::2] + relay)

        @pl.loop(0, 2)
        def _(h):
            total = line[h, net.z].astype(jnp.float32)
            for k in range(1, 3):
                total = total + along[h, k].astype(jnp.float32)
            done[h, net.g] = total.astype(jnp.bfloat16)

        start(fourth)

    def corners():
        arrive(fourth)

    def end():

        @pl.loop(0, 4)
        def _(qi):
            for h in range(2):
                wide[qi, :, h * half : h * half + half] = done[h, qi].astype(jnp.float32)

        store.start()
        store.wait()
        copies.finish()

    return [begin, plane, cross, column, onward, spread, corners, end]


ROW_COPIES = 9


def rows_stages(net, copies, local_sems, x_ref, keys_x):
    at = 8 * PD

    def block(owner):
        return keys_x.at[pl.ds(pl.multiple_of(owner * PD, 128), PD)]

    prompt = x_ref.at[pl.ds(0, PD)]
    cont = [x_ref.at[pl.ds(PD + 128 * i, 128)] for i in range(2)]
    local = [pltpu.make_async_copy(prompt, block(net.f), local_sems.at[0])]
    to_mate = [copies.to(net.to_mate, prompt, block(net.f))]
    for i in range(2):
        near = keys_x.at[pl.ds(at + 256 * i, 128)]
        here = keys_x.at[pl.ds(at + 256 * i + 128, 128)]
        local.append(pltpu.make_async_copy(cont[i], here, local_sems.at[1 + i]))
        to_mate.append(copies.to(net.to_mate, cont[i], near))
    along_z = [copies.to(device, prompt, block(net.f)) for device in net.to_z[:2]]
    relay = copies.to(net.to_z[0], block(net.f_of[1]), block(net.f_of[1]))
    later = [copies.to(net.to_mate, block(owner), block(owner)) for owner in net.f_of]

    def begin():
        start(local)
        start(to_mate)

    def column():
        start(along_z)

    def onward():
        along_z[1].wait_recv()
        relay.start()

    def mates():
        arrive([along_z[0], relay])
        start(later)

    def end():
        arrive(to_mate + later)
        for copy in local:
            copy.wait()
        copies.finish()

    return [begin, column, onward, mates, end]


def gather_first_kernel(*refs):
    shards, x_ref, fulls, keys_x = refs[:4], refs[4], refs[5:9], refs[9]
    sems, local_sem, row_sems = refs[10:20], refs[20], refs[21]
    net = Net()
    net.greet()
    parts = [
        gather_stages(
            net, Copies(sems[2 * i], sems[2 * i + 1]), local_sem.at[i], shards[i], fulls[i]
        )
        for i in range(4)
    ]
    rows = rows_stages(net, Copies(sems[8], sems[9]), row_sems, x_ref.at[0], keys_x)
    for part in parts:
        part[0]()
    rows[0]()
    for part in parts:
        part[1]()
    rows[1]()
    for part in parts:
        part[2]()
    for part in parts:
        part[3]()
    rows[2]()
    for part in parts:
        part[4]()
    rows[3]()
    for part in parts:
        part[5]()
    rows[4]()


def gather_first(shards, content_in):
    return pl.pallas_call(
        gather_first_kernel,
        name="gather_first",
        in_specs=[ANY_SPEC] * 5,
        out_specs=[ANY_SPEC] * 5,
        out_shape=[jax.ShapeDtypeStruct((8 * 4,) + s.shape[1:], jnp.bfloat16) for s in shards]
        + [jax.ShapeDtypeStruct((8 * PD + 2 * CH, D), jnp.bfloat16)],
        scratch_shapes=[pltpu.SemaphoreType.DMA((GATHER_COPIES,))] * 8
        + [pltpu.SemaphoreType.DMA((ROW_COPIES,))] * 2
        + [pltpu.SemaphoreType.DMA((4,)), pltpu.SemaphoreType.DMA((3,))],
        compiler_params=pltpu.CompilerParams(collective_id=1, has_side_effects=True),
    )(*shards, content_in)


def halves_of(ref):
    rows, columns = ref.shape[-2:]
    rest = (slice(None),) * (len(ref.shape) - 2)
    if columns > rows * 16:
        cut = columns // 2
        return [ref.at[rest + (slice(None), pl.ds(cut * i, cut))] for i in range(2)]
    cut = rows // 2
    return [ref.at[rest + (pl.ds(cut * i, cut),)] for i in range(2)]


def hosted(plan, step):
    for at, stage in plan:

        @pl.when(step == at)
        def _():
            stage()


def place(plength):
    rank = lax.axis_index("fsdp")
    halfway = plength // PD
    return rank // halfway, rank % halfway * PD, rank % 2


def attend_kernel(plength, carried, *refs):
    (meta, x_c, x_q, w_q, w_k, w_v, bias, table, xcol, first_rows, other), refs = (
        refs[:11],
        refs[11:],
    )
    shards, refs = refs[:carried], refs[carried:]
    (ctx_c, ctx_x, full_c, full_x, lse_ref, qc, qx, k_rows, v_rows), refs = refs[:9], refs[9:]
    second_rows = other
    if carried:
        second_rows, refs = refs[0], refs[1:]
    fulls, refs = refs[:carried], refs[carried:]
    keys, vals, x_keys, load_sem = refs[:4]
    all_scores, all_probs = refs[4:8], refs[8:12]
    refs = refs[12:]
    step = pl.program_id(0) * PAIRS + pl.program_id(1)
    if carried:
        net = Net()
        pieces = []
        for i in range(2):
            pieces += list(zip(halves_of(shards[i]), halves_of(fulls[i])))
        pieces.append((shards[2], fulls[2]))
        one, two, three, four, proj = (
            gather_stages(
                net, Copies(refs[2 * i], refs[2 * i + 1]), refs[12].at[i], src, dst
            )
            for i, (src, dst) in enumerate(pieces)
        )
        rows = rows_stages(
            net, Copies(refs[10], refs[11]), refs[13], other.at[1], second_rows
        )
        hosted([(0, net.greet)], step)
        hosted(
            [
                (0, rows[0]),
                (0, rows[1]),
                (2, one[0]),
                (2, proj[0]),
                (3, rows[2]),
                (3, two[0]),
                (4, one[1]),
                (4, proj[1]),
                (5, rows[3]),
                (6, rows[4]),
                (6, one[2]),
                (6, proj[2]),
                (6, two[1]),
                (6, three[0]),
                (7, two[2]),
                (7, four[0]),
                (8, one[3]),
                (8, proj[3]),
                (8, three[1]),
                (9, three[2]),
                (9, four[1]),
                (10, one[4]),
                (10, proj[4]),
                (10, two[3]),
                (10, four[2]),
                (11, three[3]),
            ],
            step,
        )
    for m, source in enumerate((first_rows, second_rows)):

        @pl.when(step == m * PAIRS)
        def _():
            load = pltpu.make_async_copy(source, x_keys, load_sem)
            load.start()
            load.wait()

    w_kv = jnp.concatenate([w_k[...], w_v[...]], axis=1)
    for at in range(0, x_keys.shape[0], 512):
        part = slice(at, at + 512)
        value = dot_nn(x_keys[part], w_kv)
        k_rows[part] = value[:, :LANES].astype(jnp.bfloat16)
        v_rows[part] = (value[:, LANES:] + bias[1:2]).astype(jnp.bfloat16)
    qc[...] = (dot_nn(x_c[...], w_q[...]) + bias[0:1]).astype(jnp.bfloat16)
    qx[...] = (dot_nn(x_q[...], w_q[...]) + bias[0:1]).astype(jnp.bfloat16)
    own_prompt, base, side = place(plength)
    mapped = meta[pl.program_id(0)]
    blocks = plength // 128
    fill_keys(keys, k_rows, own_prompt, mapped, plength)
    fill_keys(vals, v_rows, own_prompt, mapped, plength)
    row = lax.broadcasted_iota(jnp.int32, (128, 128), 0)
    col = lax.broadcasted_iota(jnp.int32, (128, 128), 1)
    tab_a = jnp.broadcast_to(table[0, 0:1, :], (128, 128))
    tab_b = jnp.broadcast_to(table[0, 1:2, :], (128, 128))
    tab_x = jnp.where(row < QP, tab_a, tab_b)
    lse_ref[...] = jnp.zeros_like(lse_ref)

    def solve(which, stack, first, plan, tables, lse_rows):
        scores, probs = all_scores[which], all_probs[which]
        count = len(plan)
        span = slice(first, first + 128 * count)
        halves = len(tables)
        width = 128 * count
        scores[0 : 128 * halves, 0:width] = dot_nt(stack, keys[span])
        for half in range(halves):
            rows = slice(128 * half, 128 * half + 128)
            peak = None
            for at, (index, visible) in enumerate(plan):
                cols = slice(128 * at, 128 * at + 128)
                s = scores[rows, cols]
                if index is not None:
                    s = s + lookup(tables[half], index)
                if visible is not None:
                    s = jnp.where(visible, s, MASKED)
                if index is not None or visible is not None:
                    scores[rows, cols] = s
                peak = s if peak is None else jnp.maximum(peak, s)
            top = jnp.max(peak, axis=1, keepdims=True)
            total = None
            for at in range(count):
                cols = slice(128 * at, 128 * at + 128)
                p = jnp.exp(scores[rows, cols] - top)
                total = p if total is None else total + p
                probs[rows, cols] = p.astype(jnp.bfloat16)
            total = jnp.sum(total, axis=1, keepdims=True)
            log_total = top + jnp.log(total)
            lse_ref[0, 0, lse_rows[half] : lse_rows[half] + 1, :] = jnp.transpose(
                jnp.broadcast_to(log_total, (128, 128))
            )[0:1, :]
            scores[rows, 0:128] = jnp.broadcast_to(1.0 / total, (128, 128))
        out = dot_nn(probs[0 : 128 * halves, 0:width], vals[span])
        return out * scores[0 : 128 * halves, 0:128]

    scale = jnp.asarray(0.125, jnp.bfloat16)
    q_p = head_stack(qc[0:PD] * scale)
    q_0 = head_stack(qc[PD : PD + 128] * scale)
    q_1 = head_stack(qc[PD + 128 : PD + 256] * scale)
    q_x = head_stack(qx[...] * scale)

    plan_p = []
    for b in range(blocks):
        d = base + row - (col + 128 * b)
        plan_p.append((near_index(d), d >= 0))
    out = head_merge(solve(0, q_p, 0, plan_p, (tab_a, tab_b), (0, 3)))
    ctx_c[0:PD] = out.astype(jnp.bfloat16)
    full_c[0:PD] = out

    far = (None, None)
    last = 128 + 2 * row + side - col
    near_d = 2 * (row - col) + 2 * side - 1
    own_d = 2 * (row - col)
    plan_0 = [far] * (blocks - 1) + [
        (near_index(last), None),
        (near_index(near_d), near_d >= 0),
        (near_index(own_d), own_d >= 0),
    ]
    out = head_merge(solve(1, q_0, plength, plan_0, (tab_a, tab_b), (1, 4)))
    ctx_c[PD : PD + 128] = out.astype(jnp.bfloat16)
    full_c[PD : PD + 128] = out
    plan_1 = [far] * blocks + [
        (near_index(near_d + 256), None),
        (near_index(own_d + 256), None),
        (near_index(near_d), near_d >= 0),
        (near_index(own_d), own_d >= 0),
    ]
    out = head_merge(solve(2, q_1, plength, plan_1, (tab_a, tab_b), (2, 5)))
    ctx_c[PD + 128 : PD + 256] = out.astype(jnp.bfloat16)
    full_c[PD + 128 : PD + 256] = out

    pos = jnp.broadcast_to(xcol[0, :, 0:1], (128, 128))
    lim_p = jnp.broadcast_to(xcol[0, :, 1:2], (128, 128))
    lim_c = jnp.broadcast_to(xcol[0, :, 2:3], (128, 128))
    plan_x = []
    for b in range(blocks):
        key = col + 128 * b
        plan_x.append((near_index(pos - key), key < lim_p))
    in_cont = lim_c > 0
    for b in range(blocks - 1):
        plan_x.append((None, in_cont))
    key = col + 128 * (blocks - 1)
    plan_x.append((near_index(pos - key), in_cont))
    for b in range(2):
        for offset in (1 - side, side):
            key = plength + 2 * (col + 128 * b) + offset
            plan_x.append((near_index(pos - key), key < lim_c))
    out = solve(3, q_x, 0, plan_x, (tab_x,), (6,))
    lane = lax.broadcasted_iota(jnp.int32, (QP, LANES), 1)
    out = jnp.where(lane < HD, out[0:QP], out[QP:])
    ctx_x[...] = out.astype(jnp.bfloat16)
    full_x[...] = out
    if carried:
        rest = (four[3], two[4], three[4], four[4], one[5], proj[5], two[5], three[5], four[5])
        hosted([(11, stage) for stage in rest], step)


def pair_column():
    return lambda m, j, meta: (m, j)


def key_spec(n_keys):
    return pl.BlockSpec((n_keys, LANES), lambda m, j, meta: (m, j))


TABLE_SPEC = pl.BlockSpec((1, 8, LANES), lambda m, j, meta: (j, 0, 0))


def host_params(collective_id, carried):
    if carried:
        return pltpu.CompilerParams(
            vmem_limit_bytes=VMEM_LIMIT, collective_id=collective_id, has_side_effects=True
        )
    return pltpu.CompilerParams(vmem_limit_bytes=VMEM_LIMIT)


def attend(meta, x_c, x_q, weights, bias, table, xcol, first_rows, other, shards):
    carried = len(shards)
    n_keys = first_rows.shape[0]
    plength = (n_keys - 2 * CH) // 2
    groups = [(256, plength), (256, plength + 256), (256, plength + 512), (128, n_keys)]
    content = pl.BlockSpec((TD, LANES), pair_column())
    extra = pl.BlockSpec((QP, LANES), pair_column())
    own_row = plength + 2 * CH
    pairs = MICRO * PAIRS * 2 * (128 * plength + 256 * own_row) + MICRO * PAIRS * 128 * n_keys
    return pl.pallas_call(
        functools.partial(attend_kernel, plength, carried),
        name="attend",
        grid_spec=pltpu.PrefetchScalarGridSpec(
            num_scalar_prefetch=1,
            grid=(MICRO, PAIRS),
            in_specs=[
                pl.BlockSpec((TD, D), lambda m, j, meta: (m, 0)),
                pl.BlockSpec((QP, D), lambda m, j, meta: (m, 0)),
            ]
            + [pl.BlockSpec((D, LANES), lambda m, j, meta: (0, j))] * 3
            + [
                pl.BlockSpec((8, LANES), lambda m, j, meta: (0, j)),
                TABLE_SPEC,
                pl.BlockSpec((1, 128, 8), lambda m, j, meta: (m, 0, 0)),
                ANY_SPEC,
                ANY_SPEC,
            ]
            + [ANY_SPEC] * carried,
            out_specs=[
                content,
                extra,
                content,
                extra,
                pl.BlockSpec((1, 1, 8, LANES), lambda m, j, meta: (m, j, 0, 0)),
                content,
                extra,
                key_spec(n_keys),
                key_spec(n_keys),
            ]
            + [ANY_SPEC] * (carried + 1 if carried else 0),
            scratch_shapes=[
                pltpu.VMEM((n_keys, LANES), jnp.bfloat16),
                pltpu.VMEM((n_keys, LANES), jnp.bfloat16),
                pltpu.VMEM((n_keys, D), jnp.bfloat16),
                pltpu.SemaphoreType.DMA,
            ]
            + [pltpu.VMEM(group, jnp.float32) for group in groups]
            + [pltpu.VMEM(group, jnp.bfloat16) for group in groups]
            + (
                [pltpu.SemaphoreType.DMA((GATHER_COPIES,))] * 10
                + [pltpu.SemaphoreType.DMA((ROW_COPIES,))] * 2
                + [pltpu.SemaphoreType.DMA((5,)), pltpu.SemaphoreType.DMA((3,))]
                if carried
                else []
            ),
        ),
        out_shape=[
            jax.ShapeDtypeStruct((MICRO * TD, D), jnp.bfloat16),
            jax.ShapeDtypeStruct((MICRO * QP, D), jnp.bfloat16),
            jax.ShapeDtypeStruct((MICRO * TD, D), jnp.float32),
            jax.ShapeDtypeStruct((MICRO * QP, D), jnp.float32),
            jax.ShapeDtypeStruct((MICRO, PAIRS, 8, LANES), jnp.float32),
            jax.ShapeDtypeStruct((MICRO * TD, D), jnp.bfloat16),
            jax.ShapeDtypeStruct((MICRO * QP, D), jnp.bfloat16),
            jax.ShapeDtypeStruct((MICRO * n_keys, D), jnp.bfloat16),
            jax.ShapeDtypeStruct((MICRO * n_keys, D), jnp.bfloat16),
        ]
        + ([jax.ShapeDtypeStruct((n_keys, D), jnp.bfloat16)] if carried else [])
        + [
            jax.ShapeDtypeStruct((8 * 4,) + shard.shape[1:], shard.dtype)
            for shard in shards
        ],
        compiler_params=host_params(2, carried),
        cost_estimate=pl.CostEstimate(
            flops=4 * pairs * LANES, bytes_accessed=16 * 1024 * 1024, transcendentals=pairs
        ),
    )(
        meta,
        x_c,
        x_q,
        *weights,
        bias,
        table,
        xcol,
        first_rows,
        other,
        *shards,
    )


def attend_back_kernel(plength, carried, *refs):
    (meta, qc, qx, k_rows, v_rows, table, xcol, xrow, lse_ref, dc, dx, full_c, full_x), refs = (
        refs[:13],
        refs[13:],
    )
    grads, refs = refs[:carried], refs[carried:]
    (dq_c, dq_x, dk_rows, dv_rows, hist), refs = refs[:5], refs[5:]
    shares, refs = refs[:carried], refs[carried:]
    keys, vals, q_all, d_all, probs_t, dscores_t, ds_p, ds_c, dk_acc, dv_acc = refs[:10]
    all_scores, all_dprobs = refs[10:14], refs[14:18]
    refs = refs[18:]
    step = pl.program_id(0) * PAIRS + pl.program_id(1)
    if carried:
        net = Net()
        pieces = list(zip(halves_of(grads[0]), halves_of(shares[0])))
        pieces.append((grads[1], shares[1]))
        one, two, proj = (
            reduce_stages(net, src, dst, refs[11 * i : 11 * i + 11])
            for i, (src, dst) in enumerate(pieces)
        )
        hosted([(0, net.greet)], step)
        hosted(
            [
                (0, one[0]),
                (0, two[0]),
                (0, proj[0]),
                (1, one[1]),
                (2, two[1]),
                (3, proj[1]),
                (4, one[2]),
                (5, two[2]),
                (6, proj[2]),
                (6, one[3]),
                (7, two[3]),
                (8, proj[3]),
                (8, one[4]),
                (9, two[4]),
                (10, proj[4]),
                (10, one[5]),
                (11, two[5]),
                (11, proj[5]),
                (11, one[6]),
            ],
            step,
        )
    own_prompt, base, side = place(plength)
    mapped = meta[pl.program_id(0)]
    blocks = plength // 128
    at_k1 = 2 * plength + 256
    n_keys = 2 * plength + 512
    fill_keys(keys, k_rows, own_prompt, mapped, plength)
    fill_keys(vals, v_rows, own_prompt, mapped, plength)
    row = lax.broadcasted_iota(jnp.int32, (128, 128), 0)
    col = lax.broadcasted_iota(jnp.int32, (128, 128), 1)
    tab_a = jnp.broadcast_to(table[0, 0:1, :], (128, 128))
    tab_b = jnp.broadcast_to(table[0, 1:2, :], (128, 128))
    scale = jnp.asarray(0.125, jnp.bfloat16)

    p_at, x_at, c1_at, c0_at = 0, 256, 384, 640
    q_all[0:256] = head_stack(qc[0:PD] * scale)
    q_all[256:384] = head_stack(qx[...] * scale)
    q_all[384:640] = head_stack(qc[PD + 128 : PD + 256] * scale)
    q_all[640:896] = head_stack(qc[PD : PD + 128] * scale)
    d_all[0:256] = head_stack(dc[0:PD])
    d_all[256:384] = head_stack(dx[...])
    d_all[384:640] = head_stack(dc[PD + 128 : PD + 256])
    d_all[640:896] = head_stack(dc[PD : PD + 128])

    ones_lane = lax.broadcasted_iota(jnp.int32, (8, LANES), 1)
    ones_row = lax.broadcasted_iota(jnp.int32, (8, LANES), 0)
    pick = jnp.where((ones_lane < HD) == (ones_row == 0), 1.0, 0.0)
    pick = jnp.where(ones_row < 2, pick, 0.0)

    def deltas(upstream, context):
        product = upstream.astype(jnp.float32) * context
        return lax.dot_general(
            pick,
            product,
            (((1,), (1,)), ((), ())),
            precision=PRECISE,
            preferred_element_type=jnp.float32,
        )

    delta_p = deltas(dc[0:PD], full_c[0:PD])
    delta_0 = deltas(dc[PD : PD + 128], full_c[PD : PD + 128])
    delta_1 = deltas(dc[PD + 128 : PD + 256], full_c[PD + 128 : PD + 256])
    delta_x = deltas(dx[...], full_x[...])
    delta_x = jnp.concatenate([delta_x[0:1], delta_x[1:2]], axis=1)

    def block_back(which, first, plan, at_col, halves):
        scores, dprobs = all_scores[which], all_dprobs[which]
        count = len(plan)
        width = 128 * len(halves)
        span = slice(first, first + 128 * count)
        cols = slice(at_col, at_col + width)
        scores[0 : 128 * count, 0:width] = dot_nt(keys[span], q_all[cols])
        dprobs[0 : 128 * count, 0:width] = dot_nt(vals[span], d_all[cols])
        for half, (tables, lse_row, delta) in enumerate(halves):
            lane = slice(128 * half, 128 * half + 128)
            out_lane = slice(at_col + 128 * half, at_col + 128 * half + 128)
            lse = lse_ref[0, 0, lse_row : lse_row + 1, :]
            for at, (index, visible) in enumerate(plan):
                rows = slice(128 * at, 128 * at + 128)
                out_rows = slice(first + 128 * at, first + 128 * at + 128)
                s = scores[rows, lane]
                if index is not None:
                    bias = lookup(tables[0], index)
                    if len(tables) > 1:
                        bias = jnp.where(col < QP, bias, lookup(tables[1], index))
                    s = s + bias
                if visible is not None:
                    s = jnp.where(visible, s, MASKED)
                p = jnp.exp(s - lse)
                ds = p * (dprobs[rows, lane] - delta)
                probs_t[out_rows, out_lane] = p.astype(jnp.bfloat16)
                dscores_t[out_rows, out_lane] = ds.astype(jnp.bfloat16)
                yield half, at, ds

    extra_a = jnp.where(
        (xcol[0, :, 3:4] == lax.broadcasted_iota(jnp.int32, (128, TD), 1))
        & (lax.broadcasted_iota(jnp.int32, (128, TD), 0) < QP),
        1.0,
        0.0,
    ).astype(jnp.bfloat16)
    extra_b = jnp.where(
        (xcol[0, :, 3:4] == lax.broadcasted_iota(jnp.int32, (128, TD), 1))
        & (lax.broadcasted_iota(jnp.int32, (128, TD), 0) >= QP),
        1.0,
        0.0,
    ).astype(jnp.bfloat16)
    spread = (extra_a, extra_b)

    pos = xrow[0, 0:1, :]
    lim_p = xrow[0, 1:2, :]
    lim_c = xrow[0, 2:3, :]
    plan = []
    for b in range(blocks):
        key = row + 128 * b
        plan.append((near_index(pos - key), key < lim_p))
    in_cont = jnp.broadcast_to(lim_c > 0, (128, 128))
    for b in range(blocks - 1):
        plan.append((None, in_cont))
    plan.append((near_index(pos - (row + 128 * (blocks - 1))), in_cont))
    for b in range(2):
        for offset in (1 - side, side):
            key = plength + 2 * (row + 128 * b) + offset
            plan.append((near_index(pos - key), key < lim_c))
    for _ in block_back(3, 0, plan, x_at, [((tab_a, tab_b), 6, delta_x)]):
        pass

    def spread_block(head, key_at, content_at):
        return dot_nn(
            dscores_t[pl.ds(key_at, 128), x_at : x_at + 128],
            spread[head][:, content_at : content_at + 128],
        )

    turn = (col + row) % 128
    turn_half = (col + row // 2) % 128

    def fold(block):
        return jnp.sum(block.reshape(16, 8, LANES), axis=0)

    plan = []
    for b in range(blocks):
        d = base + col - (row + 128 * b)
        plan.append((near_index(d), d >= 0))
    halves = [((tab_a,), 0, delta_p[0:1]), ((tab_b,), 3, delta_p[1:2])]
    for half, at, ds in block_back(0, 0, plan, p_at, halves):
        ds_p[128 * at : 128 * at + 128, 128 * half : 128 * half + 128] = ds
    before = jnp.maximum(base - 128, 0)
    base_at = pl.multiple_of(base, 128)
    before_at = pl.multiple_of(before, 128)
    for head in range(2):
        lane = slice(128 * head, 128 * head + 128)
        here = ds_p[pl.ds(base_at, 128), lane] + spread_block(head, base_at, 0)
        prior = ds_p[pl.ds(before_at, 128), lane] + spread_block(head, before_at, 0)
        prior = jnp.where(base > 0, prior, 0.0)
        both = jnp.where(col >= row, here, prior)
        hist[0, 0, 32 * head : 32 * head + 8] = fold(lookup(both, turn))

    last = 128 + 2 * col + side - row
    near_d = 2 * (col - row) + 2 * side - 1
    own_d = 2 * (col - row)
    far = (None, None)
    plan_0 = [far] * (blocks - 1) + [
        (near_index(last), None),
        (near_index(near_d), near_d >= 0),
        (near_index(own_d), own_d >= 0),
    ]
    plan_1 = [far] * blocks + [
        (near_index(near_d + 256), None),
        (near_index(own_d + 256), None),
        (near_index(near_d), near_d >= 0),
        (near_index(own_d), own_d >= 0),
    ]
    halves = [((tab_a,), 1, delta_0[0:1]), ((tab_b,), 4, delta_0[1:2])]
    near_sum = {}
    own_sum = {}
    last_key = 2 * plength - 128
    for half, at, ds in block_back(1, plength, plan_0, c0_at, halves):
        if at == blocks - 1:
            ds = ds + spread_block(half, last_key, PD)
            ds = jnp.where(col < 64, ds, 0.0)
            hist[0, 0, 32 * half + 8 : 32 * half + 16] = fold(lookup(ds, turn_half))
        if at == blocks:
            ds = ds + spread_block(half, 2 * plength, PD)
            near_sum[half] = jnp.where(col >= row, ds, 0.0)
        if at == blocks + 1:
            ds = ds + spread_block(half, 2 * plength + 128, PD)
            own_sum[half] = jnp.where(col >= row, ds, 0.0)
    for half in range(2):
        lane = slice(128 * half, 128 * half + 128)
        ds_c[0:128, lane] = near_sum[half]
        ds_c[128:256, lane] = own_sum[half]
    halves = [((tab_a,), 2, delta_1[0:1]), ((tab_b,), 5, delta_1[1:2])]
    for half, at, ds in block_back(2, plength, plan_1, c1_at, halves):
        lane = slice(128 * half, 128 * half + 128)
        if at == blocks:
            ds = ds + spread_block(half, 2 * plength, PD + 128)
            ds_c[0:128, lane] = ds_c[0:128, lane] + jnp.where(col < row, ds, 0.0)
        if at == blocks + 1:
            ds = ds + spread_block(half, 2 * plength + 128, PD + 128)
            ds_c[128:256, lane] = ds_c[128:256, lane] + jnp.where(col < row, ds, 0.0)
        if at == blocks + 2:
            ds = ds + spread_block(half, at_k1, PD + 128)
            ds = ds_c[0:128, lane] + jnp.where(col >= row, ds, 0.0)
            hist[0, 0, 32 * half + 16 : 32 * half + 24] = fold(lookup(ds, turn))
        if at == blocks + 3:
            ds = ds + spread_block(half, at_k1 + 128, PD + 128)
            ds = ds_c[128:256, lane] + jnp.where(col >= row, ds, 0.0)
            hist[0, 0, 32 * half + 24 : 32 * half + 32] = fold(lookup(ds, turn))

    own = slice(0, plength)
    middle = slice(plength, at_k1)
    end = slice(at_k1, n_keys)
    for acc, left, right in ((dk_acc, dscores_t, q_all), (dv_acc, probs_t, d_all)):
        acc[own] = dot_nn(left[own, 0:384], right[0:384])
        acc[middle] = dot_nn(left[middle, 256:896], right[256:896])
        acc[end] = dot_nn(left[end, 256:640], right[256:640])

    dq_c[0:PD] = (
        head_merge(dot_tn(dscores_t[own, p_at : p_at + 256], keys[own])) * 0.125
    ).astype(jnp.bfloat16)
    dq_c[PD : PD + 128] = (
        head_merge(dot_tn(dscores_t[middle, c0_at : c0_at + 256], keys[middle])) * 0.125
    ).astype(jnp.bfloat16)
    cont = slice(plength, n_keys)
    dq_c[PD + 128 : PD + 256] = (
        head_merge(dot_tn(dscores_t[cont, c1_at : c1_at + 256], keys[cont])) * 0.125
    ).astype(jnp.bfloat16)
    out = dot_tn(dscores_t[:, x_at : x_at + 128], keys[...])
    lane = lax.broadcasted_iota(jnp.int32, (QP, LANES), 1)
    dq_x[...] = (jnp.where(lane < HD, out[0:QP], out[QP:]) * 0.125).astype(jnp.bfloat16)

    for out_ref, acc in ((dk_rows, dk_acc), (dv_rows, dv_acc)):
        for p in range(2):
            mine = jnp.where(own_prompt == p, acc[own], 0.0)
            other = jnp.where(mapped == p, acc[plength : 2 * plength], 0.0)
            out_ref[p * plength : (p + 1) * plength] = (mine + other).astype(jnp.bfloat16)
        out_ref[2 * plength :] = acc[2 * plength :].astype(jnp.bfloat16)
    if carried:
        rest = (two[6], proj[6], one[7], two[7], proj[7])
        hosted([(11, stage) for stage in rest], step)


def attend_back(
    meta, queries, extra_q, k_rows, v_rows, table, xcol, xrow, lse, dc, dx, fc, fx, grads
):
    carried = len(grads)
    sizes, kept = [], []
    if carried:
        part, width = grads[0].shape[3:]
        tall, narrow = grads[1].shape[3:]
        sizes = [(4 * part, width // 2)] * 2 + [(4 * tall, narrow)]
        kept = [jax.ShapeDtypeStruct((4,) + grad.shape[3:], jnp.float32) for grad in grads]
    n_keys = k_rows.shape[0] // MICRO
    plength = (n_keys - 2 * CH) // 2
    groups = [(plength, 256), (plength + 256, 256), (plength + 512, 256), (n_keys, 128)]
    content = pl.BlockSpec((TD, LANES), pair_column())
    extra = pl.BlockSpec((QP, LANES), pair_column())
    own_row = plength + 2 * CH
    pairs = MICRO * PAIRS * 2 * (128 * plength + 256 * own_row) + MICRO * PAIRS * 128 * n_keys
    return pl.pallas_call(
        functools.partial(attend_back_kernel, plength, carried),
        name="attend_back",
        grid_spec=pltpu.PrefetchScalarGridSpec(
            num_scalar_prefetch=1,
            grid=(MICRO, PAIRS),
            in_specs=[content, extra]
            + [
                key_spec(n_keys),
                key_spec(n_keys),
                TABLE_SPEC,
                pl.BlockSpec((1, 128, 8), lambda m, j, meta: (m, 0, 0)),
                pl.BlockSpec((1, 8, 128), lambda m, j, meta: (m, 0, 0)),
                pl.BlockSpec((1, 1, 8, LANES), lambda m, j, meta: (m, j, 0, 0)),
                content,
                extra,
                content,
                extra,
            ]
            + [ANY_SPEC] * carried,
            out_specs=[
                content,
                extra,
                key_spec(n_keys),
                key_spec(n_keys),
                pl.BlockSpec((1, 1, 64, LANES), lambda m, j, meta: (m, j, 0, 0)),
            ]
            + [ANY_SPEC] * carried,
            scratch_shapes=[
                pltpu.VMEM((n_keys, LANES), jnp.bfloat16),
                pltpu.VMEM((n_keys, LANES), jnp.bfloat16),
                pltpu.VMEM((896, LANES), jnp.bfloat16),
                pltpu.VMEM((896, LANES), jnp.bfloat16),
                pltpu.VMEM((n_keys, 896), jnp.bfloat16),
                pltpu.VMEM((n_keys, 896), jnp.bfloat16),
                pltpu.VMEM((plength, 256), jnp.float32),
                pltpu.VMEM((256, 256), jnp.float32),
                pltpu.VMEM((n_keys, LANES), jnp.float32),
                pltpu.VMEM((n_keys, LANES), jnp.float32),
            ]
            + [pltpu.VMEM(group, jnp.float32) for group in groups] * 2
            + [buffer for size in sizes for buffer in reduce_buffers(*size)],
        ),
        out_shape=[
            jax.ShapeDtypeStruct((MICRO * TD, D), jnp.bfloat16),
            jax.ShapeDtypeStruct((MICRO * QP, D), jnp.bfloat16),
            jax.ShapeDtypeStruct((MICRO * n_keys, D), jnp.bfloat16),
            jax.ShapeDtypeStruct((MICRO * n_keys, D), jnp.bfloat16),
            jax.ShapeDtypeStruct((MICRO, PAIRS, 64, LANES), jnp.float32),
        ]
        + kept,
        compiler_params=host_params(3, carried),
        cost_estimate=pl.CostEstimate(
            flops=10 * pairs * LANES, bytes_accessed=32 * 1024 * 1024, transcendentals=pairs
        ),
    )(
        meta,
        queries,
        extra_q,
        k_rows,
        v_rows,
        table,
        xcol,
        xrow,
        lse,
        dc,
        dx,
        fc,
        fx,
        *grads,
    )


def from_partner(block, axis):
    count = lax.axis_size(axis)
    return lax.ppermute(block, axis, [(i, i ^ 1) for i in range(count)])


TAIL_RATE = 0.24
TAIL = (
    0.08952757299725976,
    0.1555125511021828,
    -0.15404562880205064,
    0.6255850035411683,
    -0.6460658211054147,
    0.554571568104313,
    -0.12508524614530675,
)


def gelu_parts(hidden):
    bell = jnp.exp(-0.5 * hidden * hidden)
    t = 1.0 / (1.0 + TAIL_RATE * jnp.abs(hidden))
    poly = TAIL[-1]
    for term in TAIL[-2::-1]:
        poly = poly * t + term
    tail = poly * t * bell
    cdf = jnp.where(hidden < 0.0, tail, 1.0 - tail)
    return hidden * cdf, cdf + hidden * bell * 0.3989422804014327


TILE = 448
GRAD_STEPS = 9


def fold_rows(term):
    return jnp.sum(term.reshape(-1, 8, term.shape[1]), axis=0)


def middle_kernel(
    x_c,
    x_x,
    ctx_c,
    ctx_x,
    cot_c,
    cot_x,
    w_out,
    w_up_ref,
    w_down_ref,
    vec,
    up_bias,
    out_c,
    out_x,
    dres,
    dctx_c,
    dctx_x,
    g_down,
    g_up,
    g_out,
    sums_out,
    act,
    dhid,
    slope,
    first_b,
    dres_two_b,
    dres_one_b,
    norm_one,
    inverse_one,
    work,
    outs,
    dctx,
    sums,
    sems,
    w_up,
    w_down,
    x,
    ctx,
    cot,
    load_sems,
):
    step = pl.program_id(0)
    load_up = pltpu.make_async_copy(w_up_ref, w_up, load_sems.at[0])
    load_down = pltpu.make_async_copy(w_down_ref, w_down, load_sems.at[1])
    loads = []
    for content, extra, rows in ((x_c, x_x, x), (ctx_c, ctx_x, ctx), (cot_c, cot_x, cot)):
        size = content.shape[0]
        for source, at in ((content, pl.ds(0, size)), (extra, pl.ds(size, 2 * QP))):
            sem = load_sems.at[2 + len(loads)]
            loads.append(pltpu.make_async_copy(source, rows.at[at], sem))
    width = w_up.shape[1]
    rows_c = out_c.shape[0]
    tiles = x.shape[0] // TILE
    out_bias, gain_one, shift_one = vec[0:1], vec[1:2], vec[2:3]
    down_bias, gain_two, shift_two = vec[3:4], vec[4:5], vec[5:6]
    split = rows_c - TILE
    moves = [
        [
            (outs.at[pl.ds(0, TILE)], out_c.at[pl.ds(0, TILE)]),
            (dctx.at[pl.ds(0, TILE)], dctx_c.at[pl.ds(0, TILE)]),
        ],
        [
            (outs.at[pl.ds(TILE, split)], out_c.at[pl.ds(TILE, split)]),
            (dctx.at[pl.ds(TILE, split)], dctx_c.at[pl.ds(TILE, split)]),
            *[
                (outs.at[pl.ds(rows_c + QP * m, out_x.shape[1])], out_x.at[m])
                for m in range(MICRO)
            ],
            (dctx.at[pl.ds(rows_c, 2 * QP)], dctx_x),
        ],
    ]
    count = 0
    for group in moves:
        for i, (src, dst) in enumerate(group):
            group[i] = pltpu.make_async_copy(src, dst, sems.at[count])
            count += 1

    def mean(value):
        return jnp.mean(value, axis=-1, keepdims=True)

    @pl.when(step == 0)
    def _():
        start(loads[2:4] + loads[0:2])
        load_up.start()
        start(loads[4:6])
        load_down.start()
        for copy in loads[0:4]:
            copy.wait()
        sums[...] = jnp.zeros_like(sums)

    @pl.when(step < tiles)
    def _():
        base = pl.multiple_of(step * TILE, 64)
        rows = pl.ds(base, TILE)
        work[...] = dot_nn(ctx[rows], w_out[...])

        value = x[rows].astype(jnp.float32) + work[...] + out_bias
        centred = value - mean(value)
        inverse = lax.rsqrt(mean(centred * centred) + 1e-05)
        normed = centred * inverse
        norm_one[...] = normed
        inverse_one[...] = jnp.broadcast_to(inverse, (TILE, LANES))
        first_b[rows] = (normed * gain_one + shift_one).astype(jnp.bfloat16)

        @pl.when(step == 0)
        def _():
            load_up.wait()

        parts = 12
        block = width // parts

        def lift(c):
            cols = slice(block * c, block * c + block)
            slope[:, cols] = dot_nn(first_b[rows], w_up[:, cols])

        lift(0)
        for c in range(parts):
            cols = slice(block * c, block * c + block)
            if c + 1 < parts:
                lift(c + 1)
            active, gradient = gelu_parts(slope[:, cols] + up_bias[0:1, cols])
            act[rows, cols] = active.astype(jnp.bfloat16)
            slope[:, cols] = gradient

        @pl.when(step == 0)
        def _():
            load_down.wait()
            for copy in loads[4:6]:
                copy.wait()

        work[...] = dot_nn(act[rows], w_down[...])

        value = norm_one[...] * gain_one + shift_one + work[...] + down_bias
        centred = value - mean(value)
        inverse = lax.rsqrt(mean(centred * centred) + 1e-05)
        normed = centred * inverse
        outs[rows] = normed * gain_two + shift_two
        upstream = cot[rows].astype(jnp.float32)
        scaled = upstream * gain_two
        grad = inverse * (scaled - mean(scaled) - normed * mean(scaled * normed))
        work[...] = grad
        dres_two_b[rows] = grad.astype(jnp.bfloat16)
        for k, term in enumerate((upstream * normed, upstream, grad)):
            sums[8 * k : 8 * k + 8, 0:D] += fold_rows(term)

        block = width // 12
        for c in range(12):
            cols = slice(block * c, block * c + block)
            dact = dot_nt(dres_two_b[rows], w_down[cols]).astype(jnp.bfloat16)
            grad = dact.astype(jnp.float32) * slope[:, cols]
            grad_b = grad.astype(jnp.bfloat16)
            dhid[rows, cols] = grad_b
            sums[48:56, cols] += jnp.sum(
                grad_b.astype(jnp.float32).reshape(TILE // 8, 8, block), axis=0
            )
        work[...] += dot_nt(dhid[rows], w_up[...])

        normed = norm_one[...]
        inverse = inverse_one[:, 0:1]
        upstream = work[...]
        scaled = upstream * gain_one
        grad = inverse * (scaled - mean(scaled) - normed * mean(scaled * normed))
        dres[...] = grad
        dres_one_b[rows] = grad.astype(jnp.bfloat16)
        for k, term in enumerate((upstream * normed, upstream, grad)):
            sums[24 + 8 * k : 32 + 8 * k, 0:D] += fold_rows(term)

        dctx[rows] = dot_nt(dres_one_b[rows], w_out[...]).astype(jnp.bfloat16)

    for tile in range(2):

        @pl.when(step == tile)
        def _():
            for copy in moves[tile]:
                copy.start()

    quarter = width // 4
    for c in range(4):
        cols = slice(quarter * c, quarter * c + quarter)

        @pl.when(step == tiles + c)
        def _():
            g_down[...] = dot_tn(act[:, cols], dres_two_b[...]).astype(jnp.bfloat16)

        @pl.when(step == tiles + 4 + c)
        def _():
            g_up[...] = dot_tn(first_b[...], dhid[:, cols]).astype(jnp.bfloat16)

    @pl.when(step == tiles + 8)
    def _():
        g_out[...] = dot_tn(ctx[...], dres_one_b[...]).astype(jnp.bfloat16)
        for k in range(7):
            sums_out[k : k + 1] = jnp.sum(sums[8 * k : 8 * k + 8], axis=0, keepdims=True)
        sums_out[7:8] = jnp.zeros_like(sums_out[7:8])
        for group in moves:
            for copy in group:
                copy.wait()


def middle(
    x_c, x_x, ctx_c, ctx_x, cot_c, cot_x, w_out, w_up, w_down, vec, up_bias, extra_rows
):
    rows_c = x_c.shape[0]
    rows = rows_c + x_x.shape[0]
    width = w_up.shape[1]
    tiles = rows // TILE
    quarter = width // 4
    def once(array):
        return pl.BlockSpec(array.shape, lambda s: (0, 0), pipeline_mode=pl.Buffered(1))

    bf, f32 = jnp.bfloat16, jnp.float32
    return pl.pallas_call(
        middle_kernel,
        name="middle",
        grid=(tiles + GRAD_STEPS,),
        in_specs=[
            *[ANY_SPEC] * 6,
            once(w_out),
            ANY_SPEC,
            ANY_SPEC,
            once(vec),
            once(up_bias),
        ],
        out_specs=[
            ANY_SPEC,
            ANY_SPEC,
            pl.BlockSpec((TILE, D), lambda s: (jnp.minimum(s, tiles - 1), 0)),
            ANY_SPEC,
            ANY_SPEC,
            pl.BlockSpec((quarter, D), lambda s: (jnp.clip(s - tiles, 0, 3), 0)),
            pl.BlockSpec((D, quarter), lambda s: (0, jnp.clip(s - tiles - 4, 0, 3))),
            pl.BlockSpec((D, D), lambda s: (0, 0)),
            pl.BlockSpec((8, width), lambda s: (0, 0)),
        ],
        out_shape=[
            jax.ShapeDtypeStruct((rows_c, D), f32),
            jax.ShapeDtypeStruct((MICRO, extra_rows, D), f32),
            jax.ShapeDtypeStruct((rows, D), f32),
            jax.ShapeDtypeStruct((rows_c, D), bf),
            jax.ShapeDtypeStruct((rows - rows_c, D), bf),
            jax.ShapeDtypeStruct((width, D), bf),
            jax.ShapeDtypeStruct((D, width), bf),
            jax.ShapeDtypeStruct((D, D), bf),
            jax.ShapeDtypeStruct((8, width), f32),
        ],
        scratch_shapes=[
            pltpu.VMEM((rows, width), bf),
            pltpu.VMEM((rows, width), bf),
            pltpu.VMEM((TILE, width), f32),
            pltpu.VMEM((rows, D), bf),
            pltpu.VMEM((rows, D), bf),
            pltpu.VMEM((rows, D), bf),
            pltpu.VMEM((TILE, D), f32),
            pltpu.VMEM((TILE, LANES), f32),
            pltpu.VMEM((TILE, D), f32),
            pltpu.VMEM((rows, D), f32),
            pltpu.VMEM((rows, D), bf),
            pltpu.VMEM((56, width), f32),
            pltpu.SemaphoreType.DMA((7,)),
            pltpu.VMEM(w_up.shape, bf),
            pltpu.VMEM(w_down.shape, bf),
            pltpu.VMEM((rows, D), bf),
            pltpu.VMEM((rows, D), bf),
            pltpu.VMEM((rows, D), bf),
            pltpu.SemaphoreType.DMA((8,)),
        ],
        compiler_params=pltpu.CompilerParams(vmem_limit_bytes=60 * 1024 * 1024),
        cost_estimate=pl.CostEstimate(
            flops=2 * rows * D * (6 * width + 3 * D),
            bytes_accessed=40 * 1024 * 1024,
            transcendentals=2 * rows * width,
        ),
    )(x_c, x_x, ctx_c, ctx_x, cot_c, cot_x, w_out, w_up, w_down, vec, up_bias)


SMALL_ROWS = 32


def table_rows(hist, buckets_of, side):
    lane = lax.broadcasted_iota(jnp.int32, (LANES, LANES), 0)
    target = lax.broadcasted_iota(jnp.int32, (LANES, LANES), 1)
    signed = jnp.where(lane < 64, lane, lane - 128)
    distances = (
        lane,
        128 + side + 2 * signed,
        127 + side + 2 * signed,
        2 * lane + 2 * side - 1,
        2 * lane,
    )
    kinds = [[] for _ in distances]
    row = lax.broadcasted_iota(jnp.int32, (8, LANES), 0)
    for pair in range(PAIRS):
        for head in range(2):
            block = [
                sum(hist[m, pair, 32 * head + 8 * k : 32 * head + 8 * k + 8] for m in range(MICRO))
                for k in range(4)
            ]
            picks = (
                block[0],
                jnp.where(row % 2 == 0, block[1], 0.0),
                jnp.where(row % 2 == 0, 0.0, block[1]),
                block[2],
                block[3],
            )
            for kind, pick in zip(kinds, picks):
                kind.append(jnp.sum(pick, axis=0, keepdims=True))
    pad = [jnp.zeros((16 - 2 * PAIRS, LANES), jnp.float32)]
    close = jnp.zeros((16, LANES), jnp.float32)
    for kind, distance in zip(kinds, distances):
        hot = jnp.where((distance == target) & (target < LANES - 1), 1.0, 0.0)
        close = close + jnp.dot(
            jnp.concatenate(kind + pad, axis=0),
            hot,
            precision=PRECISE,
            preferred_element_type=jnp.float32,
        )
    last = lax.broadcasted_iota(jnp.int32, (16, LANES), 1) == LANES - 1
    close = jnp.where(last, -jnp.sum(close, axis=1, keepdims=True), close)
    bucket_hot = jnp.where(lane == buckets_of[0:1], 1.0, 0.0)
    return lax.dot_general(
        close,
        bucket_hot,
        (((1,), (1,)), ((), ())),
        precision=PRECISE,
        preferred_element_type=jnp.float32,
    )


def finish_kernel(
    dq_c_ref,
    dq_x,
    dk_ref,
    dv_ref,
    keys_0_ref,
    keys_1_ref,
    x_c_ref,
    x_q,
    w_q,
    w_k,
    w_v,
    dres_ref,
    hist,
    buckets_of,
    sums,
    d_ref,
    q_share,
    k_share,
    v_share,
    d_share,
    small_out,
    grad_c,
    grad_q,
    *scratch,
):
    shares = [q_share, k_share, v_share] + halves_of(d_share)
    buffers = [scratch[11 * i : 11 * i + 11] for i in range(5)]
    (
        grads,
        prompts,
        theirs,
        along,
        nears,
        near_got,
        owns,
        out_c,
        small,
        x_s,
        x_r,
        sm_s,
        sm_r,
        sem,
        dq_c,
        dk,
        dv,
        keys_0,
        keys_1,
        x_c,
        load_sem,
    ) = scratch[55:]
    net = Net()
    net.greet()
    sources = [grads.at[i] for i in range(3)] + halves_of(d_ref)
    one, two, three, down, rest = (
        reduce_stages(net, sources[i], shares[i], buffers[i]) for i in range(5)
    )
    n_keys = dk.shape[0] // MICRO
    halves = [pl.ds(m * n_keys, n_keys) for m in range(MICRO)]
    moves = []
    for half in halves:
        moves += [(dk_ref.at[half], dk.at[half]), (dv_ref.at[half], dv.at[half])]
    moves += [(x_c_ref, x_c), (dq_c_ref, dq_c), (keys_0_ref, keys_0), (keys_1_ref, keys_1)]
    moves.append((dres_ref, out_c))
    loads = [
        pltpu.make_async_copy(src, dst, load_sem.at[i]) for i, (src, dst) in enumerate(moves)
    ]
    start(loads)

    def loaded(first, last):
        for copy in loads[first:last]:
            copy.wait()

    down[0]()
    rest[0]()
    copies = Copies(x_s, x_r)
    to_mate = [
        copies.to(net.to_mate, prompts.at[m, :, 1 - net.c], theirs.at[m]) for m in range(MICRO)
    ]
    swap = copies.to(net.to_mate, nears, near_got)
    third, relay = [], []
    for m in range(MICRO):
        third.append(
            [
                copies.to(net.to_z[0], prompts.at[m, net.z_of[2], net.c], along.at[0, m]),
                copies.to(net.to_z[0], prompts.at[m, net.z_of[0], net.c], along.at[1, m]),
            ]
        )
        passed = prompts.at[m, net.z_of[1], net.c]
        relay.append(copies.to(net.to_z[1], passed, along.at[2, m]))
    hops = Copies(sm_s, sm_r)
    partners = [net.to_mate, net.to_x, net.to_y, net.to_z[0], net.to_z[1]]
    butterfly = [
        hops.to(partner, small.at[i], small.at[i + 1]) for i, partner in enumerate(partners)
    ]

    def hop(i):
        butterfly[i].wait_recv()
        small[i + 1] = small[i + 1] + small[i]
        if i + 1 < len(butterfly):
            butterfly[i + 1].start()

    n_prompt = n_keys - 2 * CH

    def put(value, which):
        part = D // 32
        for owner in range(8):
            for q in range(4):
                at = (4 * owner + q) * part
                grads[which, owner // 2, owner % 2, q] = value[at : at + part].astype(
                    jnp.bfloat16
                )

    def back(rows):
        return dot_nt(dk[rows], w_k[...]) + dot_nt(dv[rows], w_v[...])

    def onward(m):
        to_mate[m].wait_recv()

        @pl.loop(0, 4)
        def _(zi):
            prompts[m, zi, net.c] = prompts[m, zi, net.c] + theirs[m, zi]

        start(third[m])

    def onto(m):
        third[m][0].wait_recv()
        prompts[m, net.z_of[1], net.c] = prompts[m, net.z_of[1], net.c] + along[0, m]
        relay[m].start()

    def prompt_back(m):
        for part in range(n_prompt // 512):
            value = back(slice(m * n_keys + 512 * part, m * n_keys + 512 * part + 512))
            for i in range(4):
                owner = 4 * part + i
                prompts[m, owner // 2, owner % 2] = value[128 * i : 128 * i + 128].astype(
                    jnp.bfloat16
                )
        to_mate[m].start()

    loaded(0, 2)
    prompt_back(0)
    down[1]()
    rest[1]()
    loaded(2, 4)
    prompt_back(1)
    onward(0)
    loaded(4, 6)
    put(dot_tn(x_c[...], dq_c[...]) + dot_tn(x_q[...], dq_x[...]), 0)
    one[0]()
    onward(1)
    loaded(6, 8)
    put(dot_tn(keys_0[...], dk[:n_keys]) + dot_tn(keys_1[...], dk[n_keys:]), 1)
    two[0]()
    one[1]()
    down[2]()
    put(dot_tn(keys_0[...], dv[:n_keys]) + dot_tn(keys_1[...], dv[n_keys:]), 2)
    three[0]()
    two[1]()
    rest[2]()
    onto(0)
    three[1]()
    down[3]()
    one[2]()
    for m in range(MICRO):
        value = back(slice(m * n_keys + n_prompt, (m + 1) * n_keys))
        for i in range(2):
            nears[m, i] = value[256 * i : 256 * i + 128].astype(jnp.bfloat16)
            owns[m, i] = value[256 * i + 128 : 256 * i + 256]
    swap.start()
    small[0] = jnp.zeros_like(small[0])
    sum_q = jnp.sum(dq_c[...].astype(jnp.float32), axis=0, keepdims=True)
    sum_q = sum_q + jnp.sum(dq_x[...].astype(jnp.float32), axis=0, keepdims=True)
    small[0, 0:1] = sum_q
    small[0, 1:2] = jnp.sum(dv[...].astype(jnp.float32), axis=0, keepdims=True)
    for i in range(6):
        small[0, 2 + i : 3 + i] = sums[i : i + 1, 0:D]
    for i in range(4):
        small[0, 8 + i : 9 + i] = sums[6:7, D * i : D * i + D]
    small[0, 16:32, 0:LANES] = table_rows(hist, buckets_of, net.c)
    butterfly[0].start()
    rest[3]()
    onto(1)
    two[2]()
    down[4]()
    one[3]()
    hop(0)
    three[2]()
    rest[4]()
    loaded(8, 9)
    rows_c = x_c.shape[0]
    out_c[0:rows_c] = out_c[0:rows_c] + dot_nt(dq_c[...], w_q[...])
    out_c[rows_c:] = out_c[rows_c:] + dot_nt(dq_x[...], w_q[...])
    two[3]()
    down[5]()
    one[4]()
    hop(1)
    three[3]()
    rest[5]()
    two[4]()
    swap.wait_recv()
    for m in range(MICRO):
        for i in range(2):
            rows = slice(m * TD + PD + 128 * i, m * TD + PD + 128 * i + 128)
            out_c[rows] = out_c[rows] + owns[m, i] + near_got[m, i].astype(jnp.float32)
    down[6]()
    one[5]()
    hop(2)
    three[4]()
    rest[6]()
    two[5]()
    hop(3)
    down[7]()
    for m in range(MICRO):
        arrive([third[m][1], relay[m]])
        total = prompts[m, net.z, net.c].astype(jnp.float32)
        for k in range(1, 3):
            total = total + along[k, m].astype(jnp.float32)
        rows = slice(m * TD, m * TD + PD)
        out_c[rows] = out_c[rows] + total
    stores = [
        pltpu.make_async_copy(out_c.at[pl.ds(0, rows_c)], grad_c, sem.at[0]),
    ]
    for m in range(MICRO):
        rows = out_c.at[pl.ds(rows_c + QP * m, grad_q.shape[1])]
        stores.append(pltpu.make_async_copy(rows, grad_q.at[m], sem.at[1 + m]))
    start(stores)
    one[6]()
    three[5]()
    rest[7]()
    hop(4)
    keep = pltpu.make_async_copy(small.at[5], small_out, sem.at[3])
    keep.start()
    two[6]()
    one[7]()
    three[6]()
    two[7]()
    three[7]()
    for copy in stores + [keep]:
        copy.wait()
    copies.finish()
    hops.finish()


def finish(
    dq_c,
    dq_x,
    dk,
    dv,
    keys_x,
    x_c,
    x_q,
    weights,
    dres,
    hist,
    buckets_of,
    sums,
    down_grad,
    extra_rows,
):
    whole = pl.BlockSpec(memory_space=pltpu.VMEM)
    bf, f32 = jnp.bfloat16, jnp.float32
    rows_c, rows_x = x_c.shape[0], x_q.shape[0]
    part, tall = D // 32, down_grad.shape[3]
    return pl.pallas_call(
        finish_kernel,
        name="finish",
        in_specs=[ANY_SPEC, whole]
        + [ANY_SPEC] * 5
        + [whole] * 4
        + [ANY_SPEC]
        + [whole] * 3
        + [ANY_SPEC],
        out_specs=[ANY_SPEC] * 7,
        out_shape=[
            jax.ShapeDtypeStruct((4, part, D), f32),
            jax.ShapeDtypeStruct((4, part, D), f32),
            jax.ShapeDtypeStruct((4, part, D), f32),
            jax.ShapeDtypeStruct((4, tall, D), f32),
            jax.ShapeDtypeStruct((SMALL_ROWS, D), f32),
            jax.ShapeDtypeStruct((rows_c, D), f32),
            jax.ShapeDtypeStruct((MICRO, extra_rows, D), f32),
        ],
        scratch_shapes=reduce_buffers(4 * part, D) * 3
        + reduce_buffers(2 * tall, D) * 2
        + [
            pltpu.VMEM((3, 4, 2, 4, part, D), bf),
            pltpu.VMEM((MICRO, 4, 2, PD, D), bf),
            pltpu.VMEM((MICRO, 4, PD, D), bf),
            pltpu.VMEM((3, MICRO, PD, D), bf),
            pltpu.VMEM((MICRO, 2, 128, D), bf),
            pltpu.VMEM((MICRO, 2, 128, D), bf),
            pltpu.VMEM((MICRO, 2, 128, D), f32),
            pltpu.VMEM((rows_c + rows_x, D), f32),
            pltpu.VMEM((6, SMALL_ROWS, D), f32),
            pltpu.SemaphoreType.DMA((9,)),
            pltpu.SemaphoreType.DMA((9,)),
            pltpu.SemaphoreType.DMA((5,)),
            pltpu.SemaphoreType.DMA((5,)),
            pltpu.SemaphoreType.DMA((4,)),
        ]
        + [
            pltpu.VMEM(kept.shape, kept.dtype)
            for kept in (dq_c, dk, dv, *keys_x, x_c)
        ]
        + [pltpu.SemaphoreType.DMA((9,))],
        compiler_params=pltpu.CompilerParams(
            collective_id=4, has_side_effects=True, vmem_limit_bytes=60 * 1024 * 1024
        ),
    )(dq_c, dq_x, dk, dv, *keys_x, x_c, x_q, *weights, dres, hist, buckets_of, sums, down_grad)


def pad_rows(block):
    return jnp.pad(block, ((0, 0), (0, QP - block.shape[1]), (0, 0))).reshape(MICRO * QP, D)


def table_gradient(hist, rel_bucket, buckets, side, heads):
    summed = jnp.sum(hist, axis=0).reshape(PAIRS, 2, 4, 8, LANES)
    prompt = jnp.sum(summed[:, :, 0], axis=2)
    even = jnp.sum(summed[:, :, 1, 0::2], axis=2)
    odd = jnp.sum(summed[:, :, 1, 1::2], axis=2)
    near = jnp.sum(summed[:, :, 2], axis=2)
    own = jnp.sum(summed[:, :, 3], axis=2)
    lanes = jnp.arange(LANES, dtype=jnp.int32)
    signed = jnp.where(lanes < 64, lanes, lanes - 128)
    distance = jnp.stack(
        [
            lanes,
            128 + side + 2 * signed,
            127 + side + 2 * signed,
            2 * lanes + 2 * side - 1,
            2 * lanes,
        ]
    ).reshape(-1)
    hot = (distance[:, None] == lanes[None, :]) & (lanes[None, :] < LANES - 1)
    parts = jnp.stack([prompt, even, odd, near, own], axis=2).reshape(heads, 5 * LANES)
    close = jnp.dot(parts, hot.astype(jnp.float32), precision=PRECISE)
    close = jnp.where(
        lanes[None, :] == LANES - 1, -jnp.sum(close, axis=1, keepdims=True), close
    )
    bucket_hot = (rel_bucket[:, None] == jnp.arange(buckets, dtype=jnp.int32)[None, :]).astype(
        jnp.float32
    )
    return jnp.dot(bucket_hot.T, close.T, precision=PRECISE)


def on_device(
    content_in,
    query_in,
    pred_order,
    cont_prompt,
    rel_bucket,
    w_query,
    b_query,
    w_key,
    w_value,
    b_value,
    w_out,
    b_out,
    ln1_gain,
    ln1_bias,
    w_up,
    b_up,
    w_down,
    b_down,
    ln2_gain,
    ln2_bias,
    bias_table,
    cot_content,
    cot_query,
):
    devices = lax.axis_size("fsdp")
    halfway = devices // 2
    own_rank = lax.axis_index("fsdp")
    plength = PD * halfway
    heads = bias_table.shape[1]
    extra_rows = query_in.shape[1]
    prompt_base = own_rank % halfway * PD
    cont_index = own_rank // 2
    side = own_rank % 2

    own_links = lax.axis_size("grp") == 4 and devices == 8

    def gather(entry):
        return lax.all_gather(entry, "fsdp", axis=0, tiled=True)

    def quarters(entry):
        return entry.reshape(4, -1, entry.shape[1])

    n_keys = 2 * plength + 2 * CH
    shard = b_query.shape[0]
    up_size = b_up.shape[0]
    vectors = jnp.stack(
        [b_query, b_value, b_out, b_down, ln1_gain, ln1_bias, ln2_gain, ln2_bias]
        + [b_up[shard * i : shard * i + shard] for i in range(up_size // shard)]
    )
    tokens_x = content_in.reshape(MICRO * TD, D)
    extra_x = pad_rows(query_in)
    if own_links:
        lines = vectors.shape[0]
        vector_shard = jnp.pad(vectors, ((0, 32 - lines), (0, 256 - shard))).reshape(4, 8, 256)
        *qkv_weights, all_vectors, first_rows = gather_first(
            [quarters(w_query), quarters(w_key), quarters(w_value), vector_shard], content_in
        )
        qkv_weights = [entry.reshape(-1, D) for entry in qkv_weights]
        all_vectors = all_vectors.reshape(devices, 32, 256)[:, :lines, :shard]
        other = content_in
        carried = tuple(quarters(shard) for shard in (w_up, w_down, w_out))
    else:
        qkv_weights = [gather(w_query), gather(w_key), gather(w_value)]
        all_vectors = gather(vectors[None])
        up_weight, down_weight, out_weight = gather(w_up), gather(w_down), gather(w_out)
        carried = ()
        prompt_x = lax.all_gather(content_in[:, :PD], "fsdp", axis=1, tiled=True)
        near_x = from_partner(content_in[:, PD:], "fsdp").reshape(MICRO, 2, 1, 128, D)
        own_x = content_in[:, PD:].reshape(MICRO, 2, 1, 128, D)
        cont_x = jnp.concatenate([near_x, own_x], axis=2).reshape(MICRO, 2 * CH, D)
        first_rows, other = jnp.concatenate([prompt_x, cont_x], axis=1)
    singles = [
        all_vectors[:, i].reshape(-1).astype(jnp.float32)
        for i in range(8)
    ]
    (
        query_bias,
        value_bias,
        out_bias,
        down_bias,
        gain_one,
        shift_one,
        gain_two,
        shift_two,
    ) = singles
    up_bias = all_vectors[:, 8:].reshape(-1).astype(jnp.float32)

    prompt_map = cont_prompt[:, 0, :]
    prompt_ref = jnp.sum(
        jnp.where(
            jnp.arange(prompt_map.shape[1], dtype=jnp.int32)[None, :] == cont_index, prompt_map, 0
        ),
        axis=1,
    )
    meta = prompt_ref.astype(jnp.int32)
    order = jnp.pad(pred_order[:, 0, :], ((0, 0), (0, QP - extra_rows)), constant_values=-1)
    real = order >= 0
    in_prompt = order < PD
    position = jnp.where(
        in_prompt, prompt_base + order, plength + 2 * (order - PD) + side
    )
    limit_p = jnp.where(real & in_prompt, jnp.maximum(position, 1), -1)
    limit_c = jnp.where(real & ~in_prompt, position, -1)
    info = jnp.stack([position, limit_p, limit_c, order], axis=1)
    info = jnp.concatenate([info, info], axis=2)
    xrow = jnp.pad(info, ((0, 0), (0, 4), (0, 0))).astype(jnp.int32)
    xcol = jnp.swapaxes(xrow, 1, 2)
    dist = bias_table.astype(jnp.float32)[rel_bucket].T
    dist = dist - dist[:, LANES - 1 :]
    table = jnp.pad(dist.reshape(PAIRS, 2, LANES), ((0, 0), (0, 6), (0, 0)))

    bias = jnp.pad(jnp.stack([query_bias, value_bias]), ((0, 6), (0, 0)))
    ctx_c, ctx_x, full_c, full_x, lse, queries, extra_q, k_rows, v_rows, *gathered = attend(
        meta, tokens_x, extra_x, qkv_weights, bias, table, xcol, first_rows, other, carried
    )
    keys_x = (first_rows, other)
    if own_links:
        keys_x = (first_rows, gathered[0])
        up_weight, down_weight, out_weight = (
            entry.reshape(-1, entry.shape[2]) for entry in gathered[1:]
        )
    rows_c = MICRO * TD
    vec = jnp.stack([out_bias, gain_one, shift_one, down_bias, gain_two, shift_two])
    (
        out_content,
        out_query,
        dres_one,
        dctx_c,
        dctx_x,
        dweight_down,
        dweight_up,
        dweight_out,
        sums,
    ) = middle(
        tokens_x,
        extra_x,
        ctx_c,
        ctx_x,
        cot_content.reshape(rows_c, D),
        pad_rows(cot_query),
        out_weight,
        up_weight,
        down_weight,
        vec,
        up_bias[None],
        extra_rows,
    )
    out_content = out_content.reshape(MICRO, TD, D)

    def by_quarter(grad):
        grad = grad.astype(jnp.bfloat16)
        return grad.reshape(4, 2, 4, grad.shape[0] // 32, grad.shape[1])

    to_reduce = ()
    if own_links:
        to_reduce = (by_quarter(dweight_up), by_quarter(dweight_out))
    dq_c, dq_x, dk_rows, dv_rows, hist, *reduced = attend_back(
        meta,
        queries,
        extra_q,
        k_rows,
        v_rows,
        table,
        xcol,
        xrow,
        lse,
        dctx_c,
        dctx_x,
        full_c,
        full_x,
        to_reduce,
    )
    if own_links:
        *t_qkv, t_down, small, grad_content, grad_query = finish(
            dq_c,
            dq_x,
            dk_rows,
            dv_rows,
            keys_x,
            tokens_x,
            extra_x,
            qkv_weights,
            dres_one,
            hist,
            jnp.broadcast_to(rel_bucket[None], (8, LANES)),
            sums,
            by_quarter(dweight_down),
            extra_rows,
        )
        grad_content = grad_content.reshape(MICRO, TD, D)
        t_up, t_out = reduced
        shares = (t_down, t_up, t_out, *t_qkv)
        t_down, t_up, t_out, *t_qkv = [
            entry.reshape(-1, entry.shape[-1]) for entry in shares
        ]
        pieces = lax.dynamic_slice_in_dim(small[:8], own_rank * shard, shard, 1)
        t_bup = lax.dynamic_index_in_dim(
            small[8:12].reshape(devices, up_size), own_rank, 0, keepdims=False
        )
        t_table = lax.dynamic_slice_in_dim(
            small[16 : 16 + heads, : bias_table.shape[0]],
            own_rank * (bias_table.shape[0] // devices),
            bias_table.shape[0] // devices,
            1,
        ).T
    else:
        dgain_two, dshift_two, dbias_down, dgain_one, dshift_one, dbias_out = sums[:6, :D]
        dbias_up = sums[6]
        dkv_rows = jnp.concatenate([dk_rows, dv_rows], axis=1)
        dq_all = jnp.concatenate([dq_c, dq_x])
        dbias_query = jnp.sum(dq_all.astype(jnp.float32), axis=0)
        dbias_value = jnp.sum(dv_rows.astype(jnp.float32), axis=0)
        query_weight, key_weight, value_weight = qkv_weights
        kv_weight = jnp.concatenate([key_weight, value_weight], axis=1)
        keys_x = jnp.concatenate(keys_x)
        dkeys_x = dot_nt(dkv_rows, kv_weight).reshape(MICRO, n_keys, D)
        dtable = table_gradient(hist, rel_bucket, bias_table.shape[0], side, heads)
        small = jnp.concatenate(
            [
                entry.reshape(devices, -1)
                for entry in (
                    dbias_query,
                    dbias_value,
                    dgain_two,
                    dshift_two,
                    dbias_down,
                    dgain_one,
                    dshift_one,
                    dbias_out,
                    dbias_up,
                    dtable,
                )
            ],
            axis=1,
        ).astype(jnp.bfloat16)
        dprompts = dkeys_x[:, : 2 * plength].astype(jnp.bfloat16)
        dcont = dkeys_x[:, 2 * plength :].reshape(MICRO, 2, 2, 128, D)
        dnear = dcont[:, :, 0].astype(jnp.bfloat16)
        dweight_qkv = jnp.concatenate(
            [dot_tn(jnp.concatenate([tokens_x, extra_x]), dq_all), dot_tn(keys_x, dkv_rows)], axis=1
        )

        def scatter(piece, dimension=0):
            return lax.psum_scatter(
                piece.astype(jnp.bfloat16), "fsdp", scatter_dimension=dimension, tiled=True
            )

        from_prompts = scatter(dprompts, 1).astype(jnp.float32)
        from_near = from_partner(dnear, "fsdp")
        shares = [
            scatter(piece)
            for piece in (dweight_down, dweight_up, dweight_out, dweight_qkv, small)
        ]
        t_down, t_up, t_out, t_qkv, t_small = [
            lax.psum(entry, "grp").astype(jnp.float32) for entry in shares
        ]
        t_qkv = [t_qkv[:, D * i : D * i + D] for i in range(3)]
        dcont = (dcont[:, :, 1] + from_near.astype(jnp.float32)).reshape(MICRO, CH, D)
        dx_all = dres_one + dot_nt(dq_all, query_weight)
        grad_content = dx_all[:rows_c].reshape(MICRO, TD, D) + jnp.concatenate(
            [from_prompts, dcont], axis=1
        )
        grad_query = dx_all[rows_c:].reshape(MICRO, QP, D)[:, :extra_rows]
        t_small = t_small.reshape(-1)
        pieces = [t_small[shard * i : shard * i + shard] for i in range(8)]
        up_at = 8 * shard
        t_bup = t_small[up_at : up_at + up_size]
        t_table = t_small[up_at + up_size :].reshape(-1, heads)
    return (
        out_content,
        out_query,
        grad_content,
        grad_query,
        t_qkv[0],
        pieces[0],
        t_qkv[1],
        t_qkv[2],
        pieces[1],
        t_out,
        pieces[7],
        pieces[5],
        pieces[6],
        t_up,
        t_bup,
        t_down,
        pieces[4],
        pieces[2],
        pieces[3],
        t_table,
    )


def solution(mesh):
    rows = P(None, ("grp", "fsdp"), None)
    matrix = P("fsdp", None)
    vector = P("fsdp")
    in_specs = (
        rows,
        rows,
        rows,
        P(None, "grp", None),
        P(),
        matrix,
        vector,
        matrix,
        matrix,
        vector,
        matrix,
        vector,
        vector,
        vector,
        matrix,
        vector,
        matrix,
        vector,
        vector,
        vector,
        P(),
        rows,
        rows,
    )
    out_specs = (
        rows,
        rows,
        rows,
        rows,
        matrix,
        vector,
        matrix,
        matrix,
        vector,
        matrix,
        vector,
        vector,
        vector,
        matrix,
        vector,
        matrix,
        vector,
        vector,
        vector,
        matrix,
    )
    return jax.shard_map(
        on_device, mesh=mesh, in_specs=in_specs, out_specs=out_specs, check_vma=False
    )
```
